32 devices in a mesh: wide: 8 (over y, x, core), tp: 4 (over z).
Axes of the slice: x: 2, y: 2, z: 4, core: 2. Of those that a mesh axis runs over, the one named last changes fastest.
Arguments:
- hidden_in: bfloat16 [8, 1024, 1024], P('tp', 'wide'), may hold values from -6 to 6
- lengths: int32 [8], replicated, may hold values from 256 to 1024, as said below
- pre_gain: bfloat16 [1024], P('wide'), may hold values from 0.5 to 1.5
- pre_shift: bfloat16 [1024], P('wide'), may hold values from -1.796875 to 1.796875
- w_query: bfloat16 [1024, 1024], P('wide', 'tp'), may hold values from -0.1875 to 0.1875
- w_key: bfloat16 [1024, 1024], P('wide', 'tp'), may hold values from -0.1875 to 0.1875
- w_value: bfloat16 [1024, 1024], P('wide', 'tp'), may hold values from -0.1875 to 0.1875
- b_query: bfloat16 [16, 64], P('tp', 'wide'), may hold values from -1.796875 to 1.796875
- b_value: bfloat16 [16, 64], P('tp', 'wide'), may hold values from -1.796875 to 1.796875
- w_dense: bfloat16 [1024, 1024], P('tp', 'wide'), may hold values from -0.75 to 0.75
- b_dense: bfloat16 [1024], P('wide'), may hold values from -1.796875 to 1.796875
- mid_gain: bfloat16 [1024], P('wide'), may hold values from 0.5 to 1.5
- mid_shift: bfloat16 [1024], P('wide'), may hold values from -1.796875 to 1.796875
- w_up: bfloat16 [1024, 4096], P('wide', 'tp'), may hold values from -0.1875 to 0.1875
- b_up: bfloat16 [16, 256], P('tp', 'wide'), may hold values from -1.796875 to 1.796875
- w_down: bfloat16 [4096, 1024], P('tp', 'wide'), may hold values from -0.09375 to 0.09375
- b_down: bfloat16 [1024], P('wide'), may hold values from -1.796875 to 1.796875
- cotangent: bfloat16 [8, 1024, 1024], P('tp', 'wide'), may hold values from -6 to 6
Outputs:
- output: bfloat16 [8, 1024, 1024], P('tp', 'wide')
- grad_in: bfloat16 [8, 1024, 1024], P('tp', 'wide')
- grad_pre_gain: float32 [1024], P('wide')
- grad_pre_shift: float32 [1024], P('wide')
- grad_w_query: float32 [1024, 1024], P('wide', 'tp')
- grad_w_key: float32 [1024, 1024], P('wide', 'tp')
- grad_w_value: float32 [1024, 1024], P('wide', 'tp')
- grad_b_query: float32 [16, 64], P('tp', 'wide')
- grad_b_value: float32 [16, 64], P('tp', 'wide')
- grad_w_dense: float32 [1024, 1024], P('tp', 'wide')
- grad_b_dense: float32 [1024], P('wide')
- grad_mid_gain: float32 [1024], P('wide')
- grad_mid_shift: float32 [1024], P('wide')
- grad_w_up: float32 [1024, 4096], P('wide', 'tp')
- grad_b_up: float32 [16, 256], P('tp', 'wide')
- grad_w_down: float32 [4096, 1024], P('tp', 'wide')
- grad_b_down: float32 [1024], P('wide')
The draws below stay inside these ranges and needn't reach their ends.
Inputs may be any that keep to these rules, and one draw needn't show every extreme that they name: lengths[s] tokens fill the leading positions of slot s; some slot is full and some holds exactly 256 tokens.
All inputs are finite; a program needn't handle non-finite values.
Results may differ from the reference program's by a relative error of at most 0.02.
Values may be sent and summed in bfloat16 or wider, within the bound.
A program may use at most 192 MiB of HBM per device.

```python
import jax
import jax.numpy as jnp
from jax import lax

D = 1024
HEADS = 16
FF = 4096
HEAD = 64
SLOTS = 8
SLOT_LEN = 1024
MIN_LEN = 256


def draw_lengths(key, part):
    drawn = jax.random.randint(jax.random.fold_in(key, 11), (SLOTS,), MIN_LEN, SLOT_LEN + 1)
    longest = jax.random.randint(jax.random.fold_in(key, 12), (), 0, SLOTS)
    offset = jax.random.randint(jax.random.fold_in(key, 13), (), 1, SLOTS)
    shortest = (longest + offset) % SLOTS
    places = jnp.arange(SLOTS)
    drawn = jnp.where(places == shortest, MIN_LEN, drawn)
    return jnp.where(places == longest, SLOT_LEN, drawn).astype(jnp.int32)


def raised(array, own_key, source, target, shards_of, factor):
    owner, partner = [(jnp.arange(array.shape[dim]) // (array.shape[dim] // shards_of)).reshape([-1 if axis == dim else 1 for axis in range(array.ndim)]) for dim in (source, target)]
    chosen = jax.random.permutation(own_key, shards_of)[partner]
    strong = (owner == chosen) | (owner == (partner + shards_of // 2) % shards_of)
    return jnp.where(strong, factor * array, array)


def shard_levels(rng, dims, pieces, low, top_value):
    gain, own = 1.0, jax.random.fold_in(rng, 6)
    for dim, shards_of in pieces:
        heights = jnp.exp(jax.random.uniform(jax.random.fold_in(own, dim), (shards_of,), jnp.float32, low / len(pieces), top_value / len(pieces)))
        gain = gain * jnp.repeat(heights, dims[dim] // shards_of).reshape([-1 if axis == dim else 1 for axis in range(len(dims))])
    return gain


def gaussian(stream_key, shape, scale, bound, cuts=(), kind=jnp.bfloat16):
    values = jax.random.normal(stream_key, shape, jnp.float32) * scale
    if len(cuts) > 0:
        values = shard_levels(stream_key, shape, cuts, -0.22, 0.18) * values
    return jnp.clip(values, min=-bound, max=bound).astype(kind)


def bell_draw_with(rng, extent, deviation, most, split, heavy, kind=jnp.bfloat16):
    values = deviation * jax.random.normal(rng, extent, jnp.float32)
    if split:
        values = values * shard_levels(rng, extent, split, -0.22, 0.18)
    return jnp.clip(raised(values, jax.random.fold_in(rng, 3), *heavy), -most, most).astype(kind)


def setup_inputs(seed: int = 0) -> dict:
    arg_keys = jax.random.split(jax.random.key(seed), 19)
    hidden_in = gaussian(arg_keys[0], (SLOTS, SLOT_LEN, D), 1.0, 6.0, ((0, 4), (1, 8)))
    lengths = draw_lengths(jax.random.fold_in(arg_keys[18], 71), 0)
    pre_gain = jnp.clip(1.0 + 0.1 * jax.random.normal(arg_keys[2], (D,), jnp.float32), 0.5, 1.5).astype(jnp.bfloat16)
    pre_shift = gaussian(arg_keys[3], (D,), 0.3, 1.796875, ((0, 8),))
    w_query = gaussian(arg_keys[4], (D, D), D ** -0.5, 0.1875, ((0, 8), (1, 4)))
    w_key = gaussian(arg_keys[5], (D, D), D ** -0.5, 0.1875, ((0, 8), (1, 4)))
    w_value = gaussian(arg_keys[6], (D, D), D ** -0.5, 0.1875, ((0, 8), (1, 4)))
    b_query = gaussian(arg_keys[7], (HEADS, HEAD), 0.3, 1.796875, ((0, 4), (1, 8)))
    b_value = gaussian(arg_keys[8], (HEADS, HEAD), 0.3, 1.796875, ((0, 4), (1, 8)))
    w_dense = gaussian(arg_keys[9], (D, D), (D // 16) ** -0.5, 0.75, ((0, 4), (1, 8)))
    b_dense = gaussian(arg_keys[10], (D,), 0.3, 1.796875, ((0, 8),))
    mid_gain = jnp.clip(1.0 + 0.1 * jax.random.normal(arg_keys[11], (D,), jnp.float32), 0.5, 1.5).astype(jnp.bfloat16)
    mid_shift = gaussian(arg_keys[12], (D,), 0.3, 1.796875, ((0, 8),))
    w_up = gaussian(arg_keys[13], (D, FF), D ** -0.5, 0.1875, ((0, 8), (1, 4)))
    b_up = gaussian(arg_keys[14], (HEADS, FF // HEADS), 0.3, 1.796875, ((0, 4), (1, 8)))
    w_down = gaussian(arg_keys[15], (FF, D), FF ** -0.5, 0.09375, ((0, 4), (1, 8)))
    b_down = gaussian(arg_keys[16], (D,), 0.3, 1.796875, ((0, 8),))
    cotangent = bell_draw_with(arg_keys[17], (SLOTS, SLOT_LEN, D), 1.0, 6.0, ((0, 4), (1, 8)), (1, 2, 8, 2.0))
    return {"hidden_in": hidden_in, "lengths": lengths, "pre_gain": pre_gain, "pre_shift": pre_shift, "w_query": w_query, "w_key": w_key, "w_value": w_value, "b_query": b_query, "b_value": b_value, "w_dense": w_dense, "b_dense": b_dense, "mid_gain": mid_gain, "mid_shift": mid_shift, "w_up": w_up, "b_up": b_up, "w_down": w_down, "b_down": b_down, "cotangent": cotangent}


@jax.custom_vjp
def low(v):
    return lax.optimization_barrier(v.astype(jnp.bfloat16)).astype(jnp.float32)

@jax.custom_vjp
def low_back(v):
    return v

def low_keep(v):
    return (low(v), None)

def low_pass(kept, grad):
    return (grad,)

def back_keep(v):
    return (v, None)

def back_low(kept, grad):
    return (low(grad),)
low.defvjp(low_keep, low_pass)
low_back.defvjp(back_keep, back_low)

def rounded(values):
    return low(low_back(values))

def norm_rows(values, gain_vec, shift_vec):
    middle = lax.optimization_barrier(jnp.mean(values, axis=-1, keepdims=True))
    centred = values - middle
    spread = lax.optimization_barrier(jnp.mean(centred * centred, axis=-1, keepdims=True))
    return centred * lax.rsqrt(spread + 1e-05) * gain_vec + shift_vec

def product(first_op, second_op):
    return jnp.dot(first_op, second_op, precision=lax.Precision.HIGHEST)

def attend_slot(query_rows, key_rows, value_rows, slot_length):
    places = jnp.arange(SLOT_LEN, dtype=jnp.int32)
    slopes = jnp.exp2(-0.5 * (jnp.arange(HEADS, dtype=jnp.int32).astype(jnp.float32) + 1.0))
    distance = (places[:, None] - places[None, :]).astype(jnp.float32)
    allowed = (places[None, :] <= places[:, None]) & (places[None, :] < slot_length)
    scores = jnp.einsum('ihd,jhd->hij', query_rows, key_rows, precision=lax.Precision.HIGHEST) * 0.125
    scores = low_back(scores - slopes[:, None, None] * distance[None])
    masked = jnp.where(allowed[None], scores, -jnp.inf)
    totals = jax.nn.logsumexp(masked, axis=-1, keepdims=True)
    probabilities = jnp.exp(masked - totals)
    return jnp.einsum('hij,jhd->ihd', low(probabilities), value_rows, precision=lax.Precision.HIGHEST)

def slot_layer(slot_length, hidden, pre_gain, pre_shift, w_query, w_key, w_value, b_query, b_value, w_dense, b_dense, mid_gain, mid_shift, w_up, b_up, w_down, b_down):
    places = jnp.arange(SLOT_LEN, dtype=jnp.int32)
    validity = (places < slot_length).astype(jnp.float32)
    normed = low(norm_rows(hidden, pre_gain, pre_shift))
    head_shape = (SLOT_LEN, HEADS, HEAD)
    queries = rounded(product(normed, w_query) + b_query.reshape(D)).reshape(head_shape)
    keys_proj = rounded(product(normed, w_key)).reshape(head_shape)
    values_proj = rounded(product(normed, w_value) + b_value.reshape(D)).reshape(head_shape)
    attended = attend_slot(queries, keys_proj, values_proj, slot_length)
    attention = rounded(attended.reshape(SLOT_LEN, D))
    residual = hidden + low_back(product(attention, w_dense)) + b_dense
    second = low(norm_rows(residual, mid_gain, mid_shift))
    pre_act = low_back(product(second, w_up) + b_up.reshape(FF))
    activated = low(jax.nn.gelu(pre_act, approximate=True))
    down_out = low_back(product(activated, w_down))
    return validity[:, None] * (residual + down_out + b_down)

def reference(hidden_in, lengths, pre_gain, pre_shift, w_query, w_key, w_value, b_query, b_value, w_dense, b_dense, mid_gain, mid_shift, w_up, b_up, w_down, b_down, cotangent):
    weights = tuple((weight_arg.astype(jnp.float32) for weight_arg in (pre_gain, pre_shift, w_query, w_key, w_value, b_query, b_value, w_dense, b_dense, mid_gain, mid_shift, w_up, b_up, w_down, b_down)))
    starting = tuple((jnp.zeros_like(weight_arg) for weight_arg in weights))

    def one_slot(running, inputs):
        slot_hidden, slot_length, slot_cot = inputs

        def run_slot(hidden, *params):
            return slot_layer(slot_length, hidden, *params)
        result, pullback = jax.vjp(run_slot, slot_hidden.astype(jnp.float32), *weights)
        cotangents = pullback(slot_cot.astype(jnp.float32))
        running = jax.tree.map(jnp.add, running, tuple(cotangents[1:]))
        return (running, (result.astype(jnp.bfloat16), cotangents[0].astype(jnp.bfloat16)))
    totals, (output, grad_in) = lax.scan(one_slot, starting, (hidden_in, lengths, cotangent))
    return (output, grad_in, totals[0], totals[1], totals[2], totals[3], totals[4], totals[5], totals[6], totals[7], totals[8], totals[9], totals[10], totals[11], totals[12], totals[13], totals[14])
```

```python
import functools
import math

import jax
import jax.numpy as jnp
from jax import lax
from jax.experimental import pallas as pl
from jax.experimental.pallas import tpu as pltpu
from jax.sharding import PartitionSpec as P

HEAD = 64
MESH = pl.DeviceIdType.MESH


def norm_rows(values, gain_vec, shift_vec):
    middle = jnp.mean(values, axis=-1, keepdims=True)
    centred = values - middle
    spread = jnp.mean(centred * centred, axis=-1, keepdims=True)
    return centred * lax.rsqrt(spread + 1e-05) * gain_vec + shift_vec


def flatten_rows(tensor):
    return tensor.reshape(-1, tensor.shape[-1])


def row_product(first_op, second_op):
    return jnp.dot(first_op, second_op, preferred_element_type=jnp.float32)


def inner_rows(first_op, second_op):
    return lax.dot_general(
        flatten_rows(first_op),
        flatten_rows(second_op),
        (((0,), (0,)), ((), ())),
        preferred_element_type=jnp.float32,
    )


def times_transposed(first_op, second_op):
    return lax.dot_general(
        first_op,
        second_op,
        (((first_op.ndim - 1,), (1,)), ((), ())),
        preferred_element_type=jnp.float32,
    )


def activate(values):
    return jax.nn.gelu(values, approximate=True)


def masked_scores(query_blk, key_blk, lengths_blk, slopes, distance, causal_mask, key_places):
    raw_scores = (
        jnp.einsum("gihd,gjhd->ghij", query_blk, key_blk, preferred_element_type=jnp.float32)
        * 0.125
    )
    raw_scores = raw_scores - slopes[None, :, None, None] * distance[None, None]
    allowed = causal_mask[None] & (key_places[None, None, :] < lengths_blk[:, None, None])
    return jnp.where(allowed[:, None], raw_scores, -jnp.inf)


def per_device(
    hidden_in,
    lengths,
    pre_gain,
    pre_shift,
    w_query,
    w_key,
    w_value,
    b_query,
    b_value,
    w_dense,
    b_dense,
    mid_gain,
    mid_shift,
    w_up,
    b_up,
    w_down,
    b_down,
    cotangent,
):
    local_slots, block_len, _unused = hidden_in.shape
    heads_dev = b_query.shape[0]
    head_width = heads_dev * HEAD
    slot_total = local_slots * lax.axis_size("tp")
    slot_len = block_len * lax.axis_size("wide")
    wide_at = lax.axis_index("wide")
    tp_at = lax.axis_index("tp")
    vec_part = pre_gain.shape[0]
    (
        gain_one,
        shift_one,
        query_w,
        key_w,
        value_w,
        query_b,
        value_b,
        dense_w,
        dense_b,
        gain_two,
        shift_two,
        up_w,
        up_b,
        down_w,
        down_b,
    ) = (
        lax.all_gather(pre_gain, "wide", axis=0, tiled=True),
        lax.all_gather(pre_shift, "wide", axis=0, tiled=True),
        lax.all_gather(w_query, "wide", axis=0, tiled=True),
        lax.all_gather(w_key, "wide", axis=0, tiled=True),
        lax.all_gather(w_value, "wide", axis=0, tiled=True),
        lax.all_gather(b_query, "wide", axis=1, tiled=True),
        lax.all_gather(b_value, "wide", axis=1, tiled=True),
        lax.all_gather(w_dense, "wide", axis=1, tiled=True),
        lax.all_gather(b_dense, "wide", axis=0, tiled=True),
        lax.all_gather(mid_gain, "wide", axis=0, tiled=True),
        lax.all_gather(mid_shift, "wide", axis=0, tiled=True),
        lax.all_gather(w_up, "wide", axis=0, tiled=True),
        lax.all_gather(b_up, "wide", axis=1, tiled=True),
        lax.all_gather(w_down, "wide", axis=1, tiled=True),
        lax.all_gather(b_down, "wide", axis=0, tiled=True),
    )
    gain_one = gain_one.astype(jnp.float32)
    shift_one = shift_one.astype(jnp.float32)
    gain_two = gain_two.astype(jnp.float32)
    shift_two = shift_two.astype(jnp.float32)
    query_places = wide_at * block_len + jnp.arange(block_len, dtype=jnp.int32)
    key_places = jnp.arange(slot_len, dtype=jnp.int32)
    distance = (query_places[:, None] - key_places[None, :]).astype(jnp.float32)
    causal_mask = key_places[None, :] <= query_places[:, None]
    head_index = tp_at * heads_dev + jnp.arange(heads_dev, dtype=jnp.int32)
    slopes = jnp.exp2(-0.5 * (head_index.astype(jnp.float32) + 1.0))
    own_lengths = lax.dynamic_slice_in_dim(lengths, tp_at * local_slots, local_slots, 0)
    validity = (query_places[None, :] < own_lengths[:, None]).astype(jnp.float32)
    group_size = math.gcd(slot_total, max(1, 512 // block_len))
    group_count = slot_total // group_size
    grouped_lengths = lengths.reshape(group_count, group_size)
    hidden = hidden_in.astype(jnp.float32)

    def query_view(tensor):
        return tensor.reshape(group_count, group_size, block_len, heads_dev, HEAD)

    def pair_view(tensor):
        return tensor.reshape(group_count, group_size, slot_len, 2, heads_dev, HEAD)

    def forward_group(inputs):
        query_blk, pair_blk, lengths_blk = inputs
        masked = masked_scores(
            query_blk, pair_blk[:, :, 0], lengths_blk, slopes, distance, causal_mask, key_places
        )
        highest = jnp.max(masked, axis=-1, keepdims=True)
        totals = highest + jnp.log(jnp.sum(jnp.exp(masked - highest), axis=-1, keepdims=True))
        probabilities = jnp.exp(masked - totals).astype(jnp.bfloat16)
        summed = jnp.einsum(
            "ghij,gjhd->gihd", probabilities, pair_blk[:, :, 1], preferred_element_type=jnp.float32
        )
        return (totals[..., 0], summed)

    def attention_forward(hidden_rows):
        normed_f, norm_back = jax.vjp(norm_rows, hidden_rows, gain_one, shift_one)
        normed = normed_f.astype(jnp.bfloat16)
        normed_all = lax.all_gather(normed, "tp", axis=0, tiled=True)
        queries = (
            row_product(normed_all, query_w) + query_b.reshape(head_width).astype(jnp.float32)
        ).astype(jnp.bfloat16)
        keys_now = row_product(normed_all, key_w).astype(jnp.bfloat16)
        values_now = (
            row_product(normed_all, value_w) + value_b.reshape(head_width).astype(jnp.float32)
        ).astype(jnp.bfloat16)
        pairs = jnp.concatenate([keys_now, values_now], axis=-1)
        pairs_all = lax.all_gather(pairs, "wide", axis=1, tiled=True)
        totals, summed = lax.map(
            forward_group, (query_view(queries), pair_view(pairs_all), grouped_lengths)
        )
        return (
            normed_all,
            queries,
            pairs_all,
            totals,
            summed.reshape(slot_total, block_len, head_width),
            norm_back,
        )

    forward_parts = attention_forward(hidden)
    attention = forward_parts[4].astype(jnp.bfloat16)
    branch = lax.psum_scatter(
        row_product(attention, dense_w).astype(jnp.bfloat16), "tp", scatter_dimension=0, tiled=True
    ).astype(jnp.float32)
    residual = hidden + branch + dense_b.astype(jnp.float32)
    second_f, second_back = jax.vjp(norm_rows, residual, gain_two, shift_two)
    second = second_f.astype(jnp.bfloat16)
    grad_output = validity[:, :, None] * cotangent.astype(jnp.float32)
    grad_down = grad_output.astype(jnp.bfloat16)
    second_all, grad_down_all = (
        lax.all_gather(second, "tp", axis=0, tiled=True),
        lax.all_gather(grad_down, "tp", axis=0, tiled=True),
    )
    pre_act = row_product(second_all, up_w) + up_b.reshape(-1).astype(jnp.float32)
    act_value, act_back = jax.vjp(activate, pre_act)
    activated = act_value.astype(jnp.bfloat16)
    down_out = lax.psum_scatter(
        row_product(activated, down_w).astype(jnp.bfloat16), "tp", scatter_dimension=0, tiled=True
    ).astype(jnp.float32)
    grad_act = times_transposed(grad_down_all, down_w)
    grad_pre = act_back(grad_act)[0].astype(jnp.bfloat16)
    grad_up = inner_rows(second_all, grad_pre)
    grad_up_b = jnp.sum(flatten_rows(grad_pre), axis=0, dtype=jnp.float32).reshape(up_b.shape)
    grad_down_w = inner_rows(activated, grad_down_all)
    grad_second = lax.psum_scatter(
        times_transposed(grad_pre, up_w), "tp", scatter_dimension=0, tiled=True
    )
    output = (validity[:, :, None] * (residual + down_out + down_b.astype(jnp.float32))).astype(
        jnp.bfloat16
    )
    grad_resid_norm, grad_gain_two, grad_shift_two = second_back(grad_second)
    grad_resid = grad_output + grad_resid_norm
    grad_branch = grad_resid.astype(jnp.bfloat16)
    hidden_again, grad_branch = lax.optimization_barrier((hidden, grad_branch))
    forward_parts = attention_forward(hidden_again)
    normed_all, queries, pairs_all, totals, summed, norm_back = forward_parts
    attention_back = summed.astype(jnp.bfloat16)
    branch_all = lax.all_gather(grad_branch, "tp", axis=0, tiled=True)
    grad_dense_w = inner_rows(attention_back, branch_all)
    grad_attention = times_transposed(branch_all, dense_w).astype(jnp.bfloat16)

    def backward_group(inputs):
        query_blk, pair_blk, lengths_blk, totals_blk, grad_blk = inputs
        masked = masked_scores(
            query_blk, pair_blk[:, :, 0], lengths_blk, slopes, distance, causal_mask, key_places
        )
        probabilities = jnp.exp(masked - totals_blk[..., None])
        grad_probs = jnp.einsum(
            "gihd,gjhd->ghij", grad_blk, pair_blk[:, :, 1], preferred_element_type=jnp.float32
        )
        row_delta = jnp.sum(probabilities * grad_probs, axis=-1, keepdims=True)
        grad_scores = (probabilities * (grad_probs - row_delta)).astype(jnp.bfloat16)
        grad_query = (
            jnp.einsum(
                "ghij,gjhd->gihd",
                grad_scores,
                pair_blk[:, :, 0],
                preferred_element_type=jnp.float32,
            )
            * 0.125
        )
        grad_key = (
            jnp.einsum(
                "ghij,gihd->gjhd", grad_scores, query_blk, preferred_element_type=jnp.float32
            )
            * 0.125
        )
        grad_value = jnp.einsum(
            "ghij,gihd->gjhd",
            probabilities.astype(jnp.bfloat16),
            grad_blk,
            preferred_element_type=jnp.float32,
        )
        return (grad_query, jnp.stack([grad_key, grad_value], axis=2))

    grad_query_all, grad_pairs = lax.map(
        backward_group,
        (
            query_view(queries),
            pair_view(pairs_all),
            grouped_lengths,
            totals,
            query_view(grad_attention),
        ),
    )
    grad_pairs_local = lax.psum_scatter(
        grad_pairs.reshape(slot_total, slot_len, 2 * head_width).astype(jnp.bfloat16),
        "wide",
        scatter_dimension=1,
        tiled=True,
    ).astype(jnp.float32)
    grad_queries = grad_query_all.reshape(slot_total, block_len, head_width).astype(jnp.bfloat16)
    grad_keys = grad_pairs_local[:, :, :head_width].astype(jnp.bfloat16)
    grad_values = grad_pairs_local[:, :, head_width:].astype(jnp.bfloat16)
    grad_query_w = inner_rows(normed_all, grad_queries)
    grad_key_w = inner_rows(normed_all, grad_keys)
    grad_value_w = inner_rows(normed_all, grad_values)
    grad_query_b = jnp.sum(flatten_rows(grad_queries), axis=0, dtype=jnp.float32).reshape(
        heads_dev, HEAD
    )
    grad_value_b = jnp.sum(flatten_rows(grad_values), axis=0, dtype=jnp.float32).reshape(
        heads_dev, HEAD
    )
    grad_normed = lax.psum_scatter(
        (
            times_transposed(grad_queries, query_w)
            + times_transposed(grad_keys, key_w)
            + times_transposed(grad_values, value_w)
        ).astype(jnp.bfloat16),
        "tp",
        scatter_dimension=0,
        tiled=True,
    ).astype(jnp.float32)
    grad_hidden_norm, grad_gain_one, grad_shift_one = norm_back(grad_normed)
    grad_in = (grad_resid + grad_hidden_norm).astype(jnp.bfloat16)
    (
        sum_query_w,
        sum_key_w,
        sum_value_w,
        sum_query_b,
        sum_value_b,
        sum_dense_w,
        sum_up_w,
        sum_up_b,
        sum_down_w,
    ) = (
        lax.psum_scatter(
            grad_query_w.astype(jnp.bfloat16), "wide", scatter_dimension=0, tiled=True
        ).astype(jnp.float32),
        lax.psum_scatter(
            grad_key_w.astype(jnp.bfloat16), "wide", scatter_dimension=0, tiled=True
        ).astype(jnp.float32),
        lax.psum_scatter(
            grad_value_w.astype(jnp.bfloat16), "wide", scatter_dimension=0, tiled=True
        ).astype(jnp.float32),
        lax.psum_scatter(
            grad_query_b.astype(jnp.bfloat16), "wide", scatter_dimension=1, tiled=True
        ).astype(jnp.float32),
        lax.psum_scatter(
            grad_value_b.astype(jnp.bfloat16), "wide", scatter_dimension=1, tiled=True
        ).astype(jnp.float32),
        lax.psum_scatter(
            grad_dense_w.astype(jnp.bfloat16), "wide", scatter_dimension=1, tiled=True
        ).astype(jnp.float32),
        lax.psum_scatter(
            grad_up.astype(jnp.bfloat16), "wide", scatter_dimension=0, tiled=True
        ).astype(jnp.float32),
        lax.psum_scatter(
            grad_up_b.astype(jnp.bfloat16), "wide", scatter_dimension=1, tiled=True
        ).astype(jnp.float32),
        lax.psum_scatter(
            grad_down_w.astype(jnp.bfloat16), "wide", scatter_dimension=1, tiled=True
        ).astype(jnp.float32),
    )
    grad_dense_b = jnp.sum(grad_resid, axis=(0, 1))
    grad_down_b = jnp.sum(grad_output, axis=(0, 1))
    sum_gain_one, sum_shift_one, sum_dense_b, sum_gain_two, sum_shift_two, sum_down_b = lax.psum(
        (grad_gain_one, grad_shift_one, grad_dense_b, grad_gain_two, grad_shift_two, grad_down_b),
        ("wide", "tp"),
    )

    def own_part(tensor):
        return lax.dynamic_slice_in_dim(tensor, wide_at * vec_part, vec_part, 0)

    return (
        output,
        grad_in,
        own_part(sum_gain_one),
        own_part(sum_shift_one),
        sum_query_w,
        sum_key_w,
        sum_value_w,
        sum_query_b,
        sum_value_b,
        sum_dense_w,
        own_part(sum_dense_b),
        own_part(sum_gain_two),
        own_part(sum_shift_two),
        sum_up_w,
        sum_up_b,
        sum_down_w,
        own_part(sum_down_b),
    )


BF = jnp.bfloat16
F32 = jnp.float32
LOG2E = 1.4426950408889634
NEG = -1e30
BLK = 128


def hbm():
    return pl.BlockSpec(memory_space=pl.ANY)


def vmem():
    return pl.BlockSpec(memory_space=pltpu.VMEM)


def square_places():
    own = lax.axis_index("wide")
    core = own % 2
    col = (own // 2) % 2
    row = own // 4
    pair = own + 1 - 2 * core
    along_x = own + 2 - 4 * col
    along_y = own + 4 - 8 * row
    return own, pair, along_x, along_y, along_x + along_y - own


def greet(targets):
    barrier = pltpu.get_barrier_semaphore()
    for target in targets:
        pl.semaphore_signal(barrier, inc=1, device_id=target, device_id_type=MESH)
    pl.semaphore_wait(barrier, len(targets))


def remote(src, dst, send_sem, recv_sem, target):
    return pltpu.make_async_remote_copy(
        src_ref=src,
        dst_ref=dst,
        send_sem=send_sem,
        recv_sem=recv_sem,
        device_id=target,
        device_id_type=MESH,
    )


class SquareGather:
    SENDS = 13

    def __init__(self, src, dst, send, recv, local):
        own, pair, ax, ay, dg = square_places()

        def place(slot, dev):
            return dst.at[slot, pl.ds(pl.multiple_of(dev * BLK, BLK), BLK)]

        def both(dev):
            return dst.at[:, pl.ds(pl.multiple_of(dev * BLK, BLK), BLK)]

        to_x, to_y, to_p = {"wide": ax}, {"wide": ay}, {"wide": pair}
        self.local = pltpu.make_async_copy(src, both(own), local)
        copies = {}
        copies["x0"] = remote(src.at[0], place(0, own), send.at[0], recv.at[0], to_x)
        copies["x1"] = remote(src.at[1], place(1, own), send.at[1], recv.at[1], to_x)
        copies["y0"] = remote(src.at[0], place(0, own), send.at[2], recv.at[2], to_y)
        copies["y1"] = remote(src.at[1], place(1, own), send.at[3], recv.at[3], to_y)
        copies["d0"] = remote(place(0, ay), place(0, ay), send.at[4], recv.at[4], to_x)
        copies["d1"] = remote(place(1, ax), place(1, ax), send.at[5], recv.at[5], to_y)
        copies["p"] = remote(src, both(own), send.at[6], recv.at[6], to_p)
        for index, (name, slot, dev) in enumerate(
            (("x0", 0, ax), ("x1", 1, ax), ("y0", 0, ay), ("y1", 1, ay), ("d0", 0, dg), ("d1", 1, dg))
        ):
            copies["p" + name] = remote(
                place(slot, dev), place(slot, dev), send.at[7 + index], recv.at[7 + index], to_p
            )
        self.copies = copies

    def start(self):
        for name in ("y0", "x1", "x0", "y1", "p"):
            self.copies[name].start()
        self.local.start()

    def pass_on(self, arrived, sends):
        self.copies[arrived].wait_recv()
        for name in sends:
            self.copies[name].start()

    def first(self):
        self.pass_on("y0", ("d0", "py0"))
        self.pass_on("x1", ("d1", "px1"))

    def second(self):
        self.pass_on("x0", ("px0",))
        self.pass_on("y1", ("py1",))

    def third(self):
        self.pass_on("d0", ("pd0",))
        self.pass_on("d1", ("pd1",))

    def finish(self):
        for name in ("p", "px0", "px1", "py0", "py1", "pd0", "pd1"):
            self.copies[name].wait_recv()
        for copy in self.copies.values():
            copy.wait_send()
        self.local.wait()


def wide_square(own_places):
    _own, pair, ax, ay, _dg = own_places
    return [{"wide": pair}, {"wide": ax}, {"wide": ay}]


def gather_body(count, *refs):
    srcs, dsts = refs[:count], refs[count : 2 * count]
    send, recv, local = refs[2 * count :]
    greet(wide_square(square_places()))
    parts = [
        SquareGather(srcs[i], dsts[i], send.at[i], recv.at[i], local.at[i]) for i in range(count)
    ]
    for part in parts:
        part.start()
    for part in parts:
        part.first()
    for part in parts:
        part.second()
    for part in parts:
        part.third()
    for part in parts:
        part.finish()


def square_gather(*arrays):
    count = len(arrays)
    width = arrays[0].shape[-1]
    shape = jax.ShapeDtypeStruct((2, 8 * BLK, width), arrays[0].dtype)
    return pl.pallas_call(
        functools.partial(gather_body, count),
        out_shape=[shape] * count,
        in_specs=[vmem()] * count,
        out_specs=[hbm()] * count,
        scratch_shapes=[
            pltpu.SemaphoreType.DMA((count, SquareGather.SENDS)),
            pltpu.SemaphoreType.DMA((count, SquareGather.SENDS)),
            pltpu.SemaphoreType.DMA((count,)),
        ],
        compiler_params=pltpu.CompilerParams(collective_id=count, has_side_effects=True),
        name="square_gather" + str(count),
    )(*arrays)


def add_rows(dst, first, second, third=None):
    step = 16

    def body(index, carry):
        rows = pl.ds(pl.multiple_of(index * step, step), step)
        total = first[rows].astype(F32) + second[rows].astype(F32)
        if third is not None:
            total = total + third[rows].astype(F32)
        dst[rows] = total.astype(dst.dtype)
        return carry

    lax.fori_loop(0, BLK // step, body, 0)


class SquareScatter:
    SENDS = 14

    def __init__(self, src, out, from_pair, summed, from_x, from_y, send, recv):
        own, pair, ax, ay, dg = square_places()
        shift = pair - own
        to_x, to_y, to_p = {"wide": ax}, {"wide": ay}, {"wide": pair}
        self.src, self.out = src, out
        self.from_pair, self.summed, self.from_x, self.from_y = from_pair, summed, from_x, from_y
        self.dests = (dg, ax, ay, own)

        self.order = ((0, 0), (0, 1), (1, 0), (2, 1), (2, 0), (1, 1), (3, 0), (3, 1))
        self.pair_copies = {}
        for index, (chip, slot) in enumerate(self.order):
            self.pair_copies[chip, slot] = remote(
                self.block(slot, self.dests[chip] + shift),
                from_pair.at[chip, slot],
                send.at[index],
                recv.at[index],
                to_p,
            )
        self.dx = remote(summed.at[0, 0], from_x.at[0], send.at[8], recv.at[8], to_x)
        self.dy = remote(summed.at[0, 1], from_y.at[0], send.at[9], recv.at[9], to_y)
        self.xx = remote(summed.at[1, 0], from_x.at[1], send.at[10], recv.at[10], to_x)
        self.yy = remote(summed.at[2, 1], from_y.at[1], send.at[11], recv.at[11], to_y)
        self.ty = remote(summed.at[2, 0], from_y.at[2], send.at[12], recv.at[12], to_y)
        self.tx = remote(summed.at[1, 1], from_x.at[2], send.at[13], recv.at[13], to_x)

    def block(self, slot, dev):
        return self.src.at[slot, pl.ds(pl.multiple_of(dev * BLK, BLK), BLK)]

    def start(self):
        for key in self.order:
            self.pair_copies[key].start()

    def pair_sum(self, chip, slot):
        self.pair_copies[chip, slot].wait_recv()
        add_rows(
            self.summed.at[chip, slot],
            self.block(slot, self.dests[chip]),
            self.from_pair.at[chip, slot],
        )

    def first(self):
        self.pair_sum(0, 0)
        self.dx.start()
        self.pair_sum(0, 1)
        self.dy.start()
        self.pair_sum(1, 0)
        self.xx.start()
        self.pair_sum(2, 1)
        self.yy.start()

    def middle(self):
        self.pair_copies[2, 0].wait_recv()
        self.dx.wait_recv()
        _own, _pair, _ax, ay, _dg = square_places()
        add_rows(
            self.summed.at[2, 0], self.block(0, ay), self.from_pair.at[2, 0], self.from_x.at[0]
        )
        self.ty.start()
        self.pair_copies[1, 1].wait_recv()
        self.dy.wait_recv()
        add_rows(
            self.summed.at[1, 1],
            self.block(1, self.dests[1]),
            self.from_pair.at[1, 1],
            self.from_y.at[0],
        )
        self.tx.start()

    def own_sums(self):
        self.pair_sum(3, 0)
        self.pair_sum(3, 1)

    def finish(self):
        self.xx.wait_recv()
        self.ty.wait_recv()
        add_rows(self.out.at[0], self.summed.at[3, 0], self.from_x.at[1], self.from_y.at[2])
        self.yy.wait_recv()
        self.tx.wait_recv()
        add_rows(self.out.at[1], self.summed.at[3, 1], self.from_y.at[1], self.from_x.at[2])
        for copy in self.pair_copies.values():
            copy.wait_send()
        for copy in (self.dx, self.dy, self.xx, self.yy, self.ty, self.tx):
            copy.wait_send()


def scatter_scratch(count, width):
    return [
        pltpu.VMEM((count, 4, 2, BLK, width), BF),
        pltpu.VMEM((count, 4, 2, BLK, width), BF),
        pltpu.VMEM((count, 3, BLK, width), BF),
        pltpu.VMEM((count, 3, BLK, width), BF),
        pltpu.SemaphoreType.DMA((count, SquareScatter.SENDS)),
        pltpu.SemaphoreType.DMA((count, SquareScatter.SENDS)),
    ]


def scatter_parts(srcs, outs, scratch):
    return [
        SquareScatter(srcs[i], outs[i], *[buffer.at[i] for buffer in scratch])
        for i in range(len(srcs))
    ]


def scatter_body(count, *refs):
    srcs, outs = refs[:count], refs[count : 2 * count]
    greet(wide_square(square_places()))
    parts = scatter_parts(srcs, outs, refs[2 * count :])
    for part in parts:
        part.start()
    for part in parts:
        part.first()
    for part in parts:
        part.middle()
    for part in parts:
        part.own_sums()
    for part in parts:
        part.finish()


def square_scatter(*arrays):
    count = len(arrays)
    width = arrays[0].shape[-1]
    shape = jax.ShapeDtypeStruct((2, BLK, width), F32)
    return pl.pallas_call(
        functools.partial(scatter_body, count),
        out_shape=[shape] * count,
        in_specs=[vmem()] * count,
        out_specs=[vmem()] * count,
        scratch_shapes=scatter_scratch(count, width),
        compiler_params=pltpu.CompilerParams(collective_id=4 + count, has_side_effects=True),
        name="square_scatter" + str(count),
    )(*arrays)


def wide_others(own):
    return [{"wide": (own + step) % 8} for step in range(1, 8)]


def first_body(
    depth,
    hidden,
    attn_w,
    ffn_w,
    vec,
    hidden_all,
    attn_all,
    ffn_all,
    vec_all,
    attn_z,
    vec_z,
    send,
    recv,
    local,
    z_send,
    z_recv,
    a_send,
    a_recv,
    f_send,
    f_recv,
    v_send,
    v_recv,
    own_sems,
):
    own, pair, ax, ay, dg = square_places()
    layer = lax.axis_index("tp")
    greet(wide_others(own) + [{"tp": (layer + step) % depth} for step in range(1, depth)])
    gather = SquareGather(hidden, hidden_all, send, recv, local.at[0])
    gather.start()

    def up_copies(step):
        index = layer - step + 1
        sem = step - 1
        src_w = attn_w if step == 1 else attn_z.at[index]
        src_v = vec if step == 1 else vec_z.at[index]
        up = {"tp": layer + 1}
        return (
            remote(src_w, attn_z.at[index], z_send.at[0, sem], z_recv.at[0, sem], up),
            remote(src_v, vec_z.at[index], z_send.at[1, sem], z_recv.at[1, sem], up),
        )

    def down_copies(step):
        index = layer + step - 1
        sem = step - 1
        src_w = attn_w if step == 1 else attn_z.at[index]
        src_v = vec if step == 1 else vec_z.at[index]
        down = {"tp": layer - 1}
        return (
            remote(src_w, attn_z.at[index], z_send.at[2, sem], z_recv.at[2, sem], down),
            remote(src_v, vec_z.at[index], z_send.at[3, sem], z_recv.at[3, sem], down),
        )

    def z_start(step):
        @pl.when((layer < depth - 1) & (layer - step + 1 >= 0))
        def _():
            for copy in up_copies(step):
                copy.start()

        @pl.when((layer > 0) & (layer + step - 1 < depth))
        def _():
            for copy in down_copies(step):
                copy.start()

    def z_arrive(step):
        @pl.when(layer - step >= 0)
        def _():
            for copy in up_copies(step):
                copy.wait_recv()

        @pl.when(layer + step < depth)
        def _():
            for copy in down_copies(step):
                copy.wait_recv()

    def z_sent(step):
        @pl.when((layer < depth - 1) & (layer - step + 1 >= 0))
        def _():
            for copy in up_copies(step):
                copy.wait_send()

        @pl.when((layer > 0) & (layer + step - 1 < depth))
        def _():
            for copy in down_copies(step):
                copy.wait_send()

    z_start(1)
    own_z = [
        pltpu.make_async_copy(attn_w, attn_z.at[layer], own_sems.at[0]),
        pltpu.make_async_copy(vec, vec_z.at[layer], own_sems.at[1]),
    ]
    for copy in own_z:
        copy.start()
    gather.first()
    ffn_own = pltpu.make_async_copy(ffn_w.at[own], ffn_all.at[:, own], own_sems.at[2])
    ffn_own.start()
    ffn_copies = []
    for step in range(1, 8):
        there = (own + step) % 8
        ffn_copies.append(
            remote(
                ffn_w.at[there],
                ffn_all.at[:, own],
                f_send.at[step - 1],
                f_recv.at[step - 1],
                {"wide": there},
            )
        )
    for copy in ffn_copies:
        copy.start()
    z_arrive(1)
    if depth > 2:
        z_start(2)
    gather.second()
    if depth > 2:
        z_arrive(2)
    if depth > 3:
        z_start(3)
    gather.third()
    if depth > 3:
        z_arrive(3)
    for copy in own_z:
        copy.wait()
    per_layer = 8 // depth
    attn_own = pltpu.make_async_copy(
        attn_z.at[own // per_layer, own % per_layer], attn_all.at[:, own], own_sems.at[3]
    )
    attn_own.start()
    vec_own = pltpu.make_async_copy(vec_z, vec_all.at[own], own_sems.at[4])
    vec_own.start()
    late = []
    for step in range(1, 8):
        there = (own + step) % 8
        late.append(
            remote(vec_z, vec_all.at[own], v_send.at[step - 1], v_recv.at[step - 1], {"wide": there})
        )
        late.append(
            remote(
                attn_z.at[there // per_layer, there % per_layer],
                attn_all.at[:, own],
                a_send.at[step - 1],
                a_recv.at[step - 1],
                {"wide": there},
            )
        )
    for copy in late:
        copy.start()
    gather.finish()
    for copy in ffn_copies + late:
        copy.wait_recv()
    for copy in ffn_copies + late:
        copy.wait_send()
    ffn_own.wait()
    attn_own.wait()
    vec_own.wait()
    for step in range(1, depth):
        z_sent(step)


def first_exchange(depth, hidden, attn_w, ffn_w, vec):
    width = hidden.shape[-1]
    dma = pltpu.SemaphoreType.DMA
    return pl.pallas_call(
        functools.partial(first_body, depth),
        out_shape=[
            jax.ShapeDtypeStruct((2, 8 * BLK, width), BF),
            jax.ShapeDtypeStruct((4, 8, BLK, BLK), BF),
            jax.ShapeDtypeStruct((2, 8, BLK, BLK), BF),
            jax.ShapeDtypeStruct((8, depth) + vec.shape, F32),
        ],
        in_specs=[vmem()] * 4,
        out_specs=[hbm(), hbm(), hbm(), vmem()],
        scratch_shapes=[
            pltpu.VMEM((depth,) + attn_w.shape, BF),
            pltpu.VMEM((depth,) + vec.shape, F32),
            dma((SquareGather.SENDS,)),
            dma((SquareGather.SENDS,)),
            dma((1,)),
            dma((4, depth - 1)),
            dma((4, depth - 1)),
            dma((7,)),
            dma((7,)),
            dma((7,)),
            dma((7,)),
            dma((7,)),
            dma((7,)),
            dma((5,)),
        ],
        compiler_params=pltpu.CompilerParams(collective_id=10, has_side_effects=True),
        name="first_exchange",
    )(hidden, attn_w, ffn_w, vec)


def last_body(
    depth,
    shares,
    attn_g,
    ffn_g,
    rows_out,
    attn_out,
    ffn_out,
    attn_in,
    attn_z,
    from_pair,
    summed,
    from_x,
    from_y,
    s_send,
    s_recv,
    a_send,
    a_recv,
    z_send,
    z_recv,
    f_send,
    f_recv,
    own_sems,
):
    own, pair, ax, ay, dg = square_places()
    layer = lax.axis_index("tp")
    per_layer = 8 // depth
    greet(wide_others(own) + [{"tp": (layer + step) % depth} for step in range(1, depth)])
    scatter = scatter_parts(
        [shares], [rows_out], (from_pair, summed, from_x, from_y, s_send, s_recv)
    )[0]
    scatter.start()
    attn_copies = []
    for step in range(1, 8):
        there = (own + step) % 8
        attn_copies.append(
            remote(
                attn_g.at[there],
                attn_in.at[own],
                a_send.at[step - 1],
                a_recv.at[step - 1],
                {"wide": there},
            )
        )
    for copy in attn_copies:
        copy.start()
    own_copy = pltpu.make_async_copy(attn_g.at[own], attn_in.at[own], own_sems.at[0])
    own_copy.start()
    scatter.first()

    def onward(index):
        goal = index // per_layer
        piece = index % per_layer
        return remote(
            attn_in.at[index],
            attn_z.at[layer, piece],
            z_send.at[index],
            z_recv.at[layer, piece],
            {"tp": goal},
        )

    def forward(index):
        @pl.when(index // per_layer != layer)
        def _():
            onward(index).start()

    own_copy.wait()
    forward(own)
    for step in range(1, 8):
        attn_copies[step - 1].wait_recv()
        forward((own + 8 - step) % 8)
    ffn_own = pltpu.make_async_copy(ffn_g.at[own], ffn_out.at[own], own_sems.at[1])
    ffn_own.start()
    ffn_copies = []
    for step in range(1, 8):
        there = (own + step) % 8
        ffn_copies.append(
            remote(
                ffn_g.at[there],
                ffn_out.at[own],
                f_send.at[step - 1],
                f_recv.at[step - 1],
                {"wide": there},
            )
        )
    scatter.middle()
    for copy in ffn_copies:
        copy.start()
    scatter.own_sums()
    scatter.finish()
    for step in range(1, depth):
        source = (layer + step) % depth
        for piece in range(per_layer):
            remote(
                attn_in.at[piece],
                attn_z.at[source, piece],
                z_send.at[piece],
                z_recv.at[source, piece],
                {"tp": source},
            ).wait_recv()
    for piece in range(per_layer):
        for kind in range(4):
            total = attn_in[layer * per_layer + piece, kind].astype(F32)
            for step in range(1, depth):
                total = total + attn_z[(layer + step) % depth, piece, kind].astype(F32)
            attn_out[piece, kind] = total
    for copy in attn_copies:
        copy.wait_send()
    for index in range(8):
        @pl.when(index // per_layer != layer)
        def _(index=index):
            onward(index).wait_send()

    for copy in ffn_copies:
        copy.wait_recv()
    for copy in ffn_copies:
        copy.wait_send()
    ffn_own.wait()


def last_exchange(depth, shares, attn_g, ffn_g):
    width = shares.shape[-1]
    dma = pltpu.SemaphoreType.DMA
    per_layer = 8 // depth
    return pl.pallas_call(
        functools.partial(last_body, depth),
        out_shape=[
            jax.ShapeDtypeStruct((2, BLK, width), F32),
            jax.ShapeDtypeStruct((per_layer, 4, BLK, BLK), F32),
            jax.ShapeDtypeStruct((8, 2, BLK, BLK), BF),
        ],
        in_specs=[vmem()] * 3,
        out_specs=[vmem()] * 3,
        scratch_shapes=[
            pltpu.VMEM((8, 4, BLK, BLK), BF),
            pltpu.VMEM((depth, per_layer, 4, BLK, BLK), BF),
        ]
        + scatter_scratch(1, width)
        + [
            dma((7,)),
            dma((7,)),
            dma((8,)),
            dma((depth, per_layer)),
            dma((7,)),
            dma((7,)),
            dma((2,)),
        ],
        compiler_params=pltpu.CompilerParams(collective_id=11, has_side_effects=True),
        name="last_exchange",
    )(shares, attn_g, ffn_g)


def sums_body(depth, parts, gathered, send, recv, local):
    own = lax.axis_index("wide")
    layer = lax.axis_index("tp")
    others = []
    for up in range(depth):
        for step in range(8):
            if up or step:
                others.append(((own + step) % 8, (layer + up) % depth))
    greet([{"wide": wide, "tp": tp} for wide, tp in others])
    keep = pltpu.make_async_copy(parts.at[own], gathered.at[own, layer], local.at[0])
    keep.start()
    copies = [
        remote(
            parts.at[wide],
            gathered.at[own, layer],
            send.at[index],
            recv.at[index],
            {"wide": wide, "tp": tp},
        )
        for index, (wide, tp) in enumerate(others)
    ]
    for copy in copies:
        copy.start()
    for copy in copies:
        copy.wait_recv()
    for copy in copies:
        copy.wait_send()
    keep.wait()


def share_sums(depth, parts):
    dma = pltpu.SemaphoreType.DMA
    return pl.pallas_call(
        functools.partial(sums_body, depth),
        out_shape=jax.ShapeDtypeStruct((8, depth) + parts.shape[1:], F32),
        in_specs=[vmem()],
        out_specs=vmem(),
        scratch_shapes=[dma((8 * depth - 1,)), dma((8 * depth - 1,)), dma((1,))],
        compiler_params=pltpu.CompilerParams(collective_id=12, has_side_effects=True),
        name="share_sums",
    )(parts)


def head_bias(length, slope, rows):
    place = lax.broadcasted_iota(jnp.int32, (rows, QB), 0)
    bias = slope * place.astype(F32)
    return jnp.where(place < length, bias, NEG)


QB = 256


def dot_nt(first, second):
    return lax.dot_general(first, second, (((1,), (1,)), ((), ())), preferred_element_type=F32)


def dot_nn(first, second):
    return lax.dot_general(first, second, (((1,), (0,)), ((), ())), preferred_element_type=F32)


def later_key(size):
    key_place = lax.broadcasted_iota(jnp.int32, (size, size), 0)
    query_place = lax.broadcasted_iota(jnp.int32, (size, size), 1)
    return key_place > query_place


def attend_body(lengths, slopes, qkv, out, totals, bias):
    slot = pl.program_id(0)
    rows = qkv.shape[1]
    length = lengths[slot]
    scale = 0.125 * LOG2E
    for head in range(2):
        lanes = pl.ds(head * HEAD, HEAD)
        bias[...] = head_bias(length, slopes[head], rows)
        key = qkv[0, :, pl.ds(2 * HEAD + head * HEAD, HEAD)]
        value = qkv[0, :, pl.ds(4 * HEAD + head * HEAD, HEAD)]
        value_t = value.T
        for step in range(rows // QB):
            here = pl.ds(step * QB, QB)
            extent = (step + 1) * QB
            query = qkv[0, here, lanes]
            scores = dot_nt(key[:extent], query) * scale + bias[:extent]
            low_part = jnp.where(later_key(QB), NEG, scores[extent - QB :])
            scores = low_part if step == 0 else jnp.concatenate([scores[: extent - QB], low_part], 0)
            highest = jnp.max(scores, axis=0, keepdims=True)
            weights = jnp.exp2(scores - highest)
            total = jnp.sum(weights, axis=0, keepdims=True)
            mixed = dot_nn(value_t[:, :extent], weights.astype(BF)) / total
            out[0, here, lanes] = mixed.T.astype(BF)
            totals[0, pl.ds(head, 1), here] = highest + jnp.log2(total)


def attend(lengths, slopes, qkv):
    slots, rows, _width = qkv.shape
    return pl.pallas_call(
        attend_body,
        grid=(slots,),
        out_shape=[
            jax.ShapeDtypeStruct((slots, rows, 2 * HEAD), BF),
            jax.ShapeDtypeStruct((slots, 2, rows), F32),
        ],
        in_specs=[
            pl.BlockSpec(memory_space=pltpu.SMEM),
            pl.BlockSpec(memory_space=pltpu.SMEM),
            pl.BlockSpec((1, rows, 6 * HEAD), lambda s: (s, 0, 0)),
        ],
        out_specs=[
            pl.BlockSpec((1, rows, 2 * HEAD), lambda s: (s, 0, 0)),
            pl.BlockSpec((1, 2, rows), lambda s: (s, 0, 0)),
        ],
        scratch_shapes=[pltpu.VMEM((rows, QB), F32)],
        name="attend",
    )(lengths, slopes, qkv)


def attend_back_body(lengths, slopes, qkv, attention, grad, totals, out, bias, key_sum, value_sum):
    slot = pl.program_id(0)
    rows = qkv.shape[1]
    length = lengths[slot]
    scale = 0.125 * LOG2E
    for head in range(2):
        lanes = pl.ds(head * HEAD, HEAD)
        key_lanes = pl.ds(2 * HEAD + head * HEAD, HEAD)
        value_lanes = pl.ds(4 * HEAD + head * HEAD, HEAD)
        bias[...] = head_bias(length, slopes[head], rows)
        key = qkv[0, :, key_lanes]
        value = qkv[0, :, value_lanes]
        key_t = key.T
        key_sum[...] = jnp.zeros_like(key_sum)
        value_sum[...] = jnp.zeros_like(value_sum)
        for step in range(rows // QB):
            here = pl.ds(step * QB, QB)
            extent = (step + 1) * QB
            query = qkv[0, here, lanes]
            grad_rows = grad[0, here, lanes]
            product = grad_rows.astype(F32) * attention[0, here, lanes].astype(F32)
            delta = jnp.sum(product.T, axis=0, keepdims=True)
            scores = dot_nt(key[:extent], query) * scale + bias[:extent]
            low_part = jnp.where(later_key(QB), NEG, scores[extent - QB :])
            scores = low_part if step == 0 else jnp.concatenate([scores[: extent - QB], low_part], 0)
            probs = jnp.exp2(scores - totals[0, pl.ds(head, 1), here])
            grad_probs = dot_nt(value[:extent], grad_rows)
            grad_scores = (probs * (grad_probs - delta)).astype(BF)
            span = pl.ds(0, extent)
            value_sum[span] += dot_nn(probs.astype(BF), grad_rows)
            key_sum[span] += dot_nn(grad_scores, query)
            grad_query = dot_nn(key_t[:, :extent], grad_scores)
            out[0, here, lanes] = (grad_query.T * 0.125).astype(BF)
        out[0, :, key_lanes] = (key_sum[...] * 0.125).astype(BF)
        out[0, :, value_lanes] = value_sum[...].astype(BF)


def attend_back(lengths, slopes, qkv, attention, grad, totals):
    slots, rows, _width = qkv.shape
    return pl.pallas_call(
        attend_back_body,
        grid=(slots,),
        out_shape=jax.ShapeDtypeStruct((slots, rows, 6 * HEAD), BF),
        in_specs=[
            pl.BlockSpec(memory_space=pltpu.SMEM),
            pl.BlockSpec(memory_space=pltpu.SMEM),
            pl.BlockSpec((1, rows, 6 * HEAD), lambda s: (s, 0, 0)),
            pl.BlockSpec((1, rows, 2 * HEAD), lambda s: (s, 0, 0)),
            pl.BlockSpec((1, rows, 2 * HEAD), lambda s: (s, 0, 0)),
            pl.BlockSpec((1, 2, rows), lambda s: (s, 0, 0)),
        ],
        out_specs=pl.BlockSpec((1, rows, 6 * HEAD), lambda s: (s, 0, 0)),
        scratch_shapes=[
            pltpu.VMEM((rows, QB), F32),
            pltpu.VMEM((rows, HEAD), F32),
            pltpu.VMEM((rows, HEAD), F32),
        ],
        name="attend_back",
    )(lengths, slopes, qkv, attention, grad, totals)


def norm_stats(values):
    middle = jnp.mean(values, axis=-1, keepdims=True)
    centred = values - middle
    spread = jnp.mean(centred * centred, axis=-1, keepdims=True)
    inverse = lax.rsqrt(spread + 1e-05)
    return centred * inverse, inverse


def norm_back_rows(grad, hat, inverse, gain):
    scaled = grad * gain
    first = jnp.mean(scaled, axis=-1, keepdims=True)
    second = jnp.mean(scaled * hat, axis=-1, keepdims=True)
    return (scaled - first - hat * second) * inverse


def gelu_parts(values):
    root = math.sqrt(2 / math.pi)
    squared = values * values
    inner = jnp.tanh(root * values * (1.0 + 0.044715 * squared))
    half = 0.5 * (1.0 + inner)
    slope = half + 0.5 * values * (1.0 - inner * inner) * root * (1.0 + 3 * 0.044715 * squared)
    return values * half, slope


def square_device(
    hidden_in,
    lengths,
    pre_gain,
    pre_shift,
    w_query,
    w_key,
    w_value,
    b_query,
    b_value,
    w_dense,
    b_dense,
    mid_gain,
    mid_shift,
    w_up,
    b_up,
    w_down,
    b_down,
    cotangent,
):
    depth = lax.axis_size("tp")
    own = lax.axis_index("wide")
    layer = lax.axis_index("tp")
    width = hidden_in.shape[-1]
    rows = 8 * BLK
    per_layer = 8 // depth
    heads_dev = b_query.shape[0]
    own_lengths = lax.dynamic_slice_in_dim(lengths, layer * 2, 2, 0)
    head_index = 2 * own + jnp.arange(2, dtype=jnp.int32)
    slopes = jnp.exp2(-0.5 * (head_index.astype(F32) + 1.0)) * LOG2E

    def halves(weight):
        return weight.reshape(BLK, per_layer, BLK).transpose(1, 0, 2)

    attn_w = jnp.stack(
        [halves(w_query), halves(w_key), halves(w_value), w_dense.reshape(per_layer, BLK, BLK)], 1
    )
    ffn_w = jnp.stack(
        [w_up.reshape(BLK, 8, BLK).transpose(1, 0, 2), w_down.reshape(8, BLK, BLK)], 1
    )
    head_row = jnp.concatenate(
        [b_query.reshape(-1), b_value.reshape(-1), jnp.zeros((BLK - 16 * heads_dev,), BF)]
    )
    vec = jnp.stack(
        [pre_gain, pre_shift, mid_gain, mid_shift, b_dense, b_down, b_up.reshape(-1), head_row]
    ).astype(F32)
    hidden_all, attn_all, ffn_all, vec_all = first_exchange(depth, hidden_in, attn_w, ffn_w, vec)
    ffn_z = lax.all_gather(ffn_all, "tp", axis=0, tiled=False)

    def wide_vector(index):
        return vec_all[:, 0, index].reshape(width)

    gain_one, shift_one, gain_two, shift_two, dense_b, down_b = [wide_vector(i) for i in range(6)]
    up_b = vec_all[:, :, 6].reshape(8, depth, heads_dev, 4 * 8).transpose(1, 2, 0, 3)
    up_b = lax.dynamic_index_in_dim(up_b.reshape(depth, 8, BLK), own, 1, False).reshape(-1)
    span = heads_dev * 8

    def head_vector(index):
        full = vec_all[:, :, 7, index * span : (index + 1) * span]
        full = full.reshape(8, depth, heads_dev, 8).transpose(1, 2, 0, 3).reshape(8, 2 * HEAD)
        return lax.dynamic_index_in_dim(full, own, 0, False)

    qkv_b = jnp.concatenate([head_vector(0), jnp.zeros((2 * HEAD,), F32), head_vector(1)])
    qkv_w = attn_all[:3].reshape(3, width, BLK).transpose(1, 0, 2).reshape(width, 3 * BLK)
    dense_w = attn_all[3].transpose(1, 0, 2).reshape(BLK, width)
    normed = norm_stats(hidden_all.astype(F32))[0] * gain_one + shift_one
    normed = normed.astype(BF)
    qkv = (row_product(normed, qkv_w) + qkv_b).astype(BF)
    attention, totals = attend(own_lengths, slopes, qkv)
    branch = square_scatter(row_product(attention, dense_w).astype(BF))[0]

    hidden = hidden_in.astype(F32)
    residual = hidden + branch + dense_b
    hat_two, inverse_two = norm_stats(residual)
    second = (hat_two * gain_two + shift_two).astype(BF)
    places = own * BLK + jnp.arange(BLK, dtype=jnp.int32)
    validity = (places[None, :] < own_lengths[:, None]).astype(F32)[:, :, None]
    grad_output = validity * cotangent.astype(F32)
    second_all, down_all = square_gather(second, grad_output.astype(BF))

    up_w = ffn_z[:, 0].reshape(depth, width, BLK).transpose(1, 0, 2).reshape(width, depth * BLK)
    down_w = ffn_z[:, 1].transpose(0, 2, 1, 3).reshape(depth * BLK, width)
    pre_act = row_product(second_all, up_w) + up_b
    act_value, act_slope = gelu_parts(pre_act)
    activated = act_value.astype(BF)
    grad_pre = (times_transposed(down_all, down_w) * act_slope).astype(BF)
    down_share = row_product(activated, down_w).astype(BF)
    second_share = times_transposed(grad_pre, up_w).astype(BF)
    grad_up = inner_rows(second_all, grad_pre).astype(BF)
    grad_down = inner_rows(activated, down_all).astype(BF)
    grad_up_b = jnp.sum(flatten_rows(grad_pre), axis=0, dtype=F32)
    ffn_g = jnp.stack(
        [
            grad_up.reshape(8, BLK, depth, BLK).transpose(2, 0, 1, 3),
            grad_down.reshape(depth, BLK, 8, BLK).transpose(0, 2, 1, 3),
        ],
        2,
    )
    ffn_g = lax.psum_scatter(ffn_g, "tp", scatter_dimension=0, tiled=False)
    down_out, grad_second = square_scatter(down_share, second_share)

    output = (validity * (residual + down_out + down_b)).astype(BF)
    grad_resid = grad_output + norm_back_rows(grad_second, hat_two, inverse_two, gain_two)
    branch_all = square_gather(grad_resid.astype(BF))[0]
    grad_attention = times_transposed(branch_all, dense_w).astype(BF)
    grad_dense = inner_rows(attention, branch_all).astype(BF)
    grad_qkv = attend_back(own_lengths, slopes, qkv, attention, grad_attention, totals)
    normed_share = times_transposed(grad_qkv, qkv_w).astype(BF)
    grad_qkv_w = inner_rows(normed, grad_qkv).astype(BF)
    grad_qkv_b = jnp.sum(flatten_rows(grad_qkv), axis=0, dtype=F32)
    attn_g = jnp.concatenate(
        [
            grad_qkv_w.reshape(8, BLK, 3, BLK).transpose(0, 2, 1, 3),
            grad_dense.reshape(BLK, 8, BLK).transpose(1, 0, 2)[:, None],
        ],
        1,
    )
    grad_normed, attn_sum, ffn_sum = last_exchange(depth, normed_share, attn_g, ffn_g)

    hat_one, inverse_one = norm_stats(hidden)
    grad_in = (grad_resid + norm_back_rows(grad_normed, hat_one, inverse_one, gain_one)).astype(BF)

    def token_sum(values):
        return jnp.sum(values, axis=(0, 1))

    parts = jnp.stack(
        [
            token_sum(grad_normed * hat_one),
            token_sum(grad_normed),
            token_sum(grad_resid),
            token_sum(grad_second * hat_two),
            token_sum(grad_second),
            token_sum(grad_output),
        ]
    )
    parts = parts.reshape(6, 8, BLK).transpose(1, 0, 2)
    own_sums = jnp.concatenate([grad_up_b, grad_qkv_b[: 2 * HEAD], grad_qkv_b[4 * HEAD :]])
    own_sums = jnp.broadcast_to(own_sums.reshape(1, -1, BLK), (8, depth + 2, BLK))
    pad = jnp.zeros((8, 16 - 8 - depth, BLK), F32)
    sums = share_sums(depth, jnp.concatenate([parts, own_sums, pad], 1))
    vec_sums = jnp.sum(sums[:, :, :6], axis=(0, 1))
    unit_sums = jnp.sum(sums[:, :, 6 : 8 + depth], axis=1)
    up_sum = unit_sums[:, :depth].transpose(1, 0, 2).reshape(2 * HEAD // 8, 8 * depth * BLK // 16)
    head_sums = unit_sums[:, depth:].transpose(1, 0, 2).reshape(2, 16, HEAD)

    def own_block(tensor, size):
        return lax.dynamic_slice(tensor, (layer * heads_dev, own * size), (heads_dev, size))

    def side_by_side(blocks):
        return blocks.transpose(1, 0, 2).reshape(BLK, -1)

    ffn_sum = ffn_sum.astype(F32)
    return (
        output,
        grad_in,
        vec_sums[0],
        vec_sums[1],
        side_by_side(attn_sum[:, 0]),
        side_by_side(attn_sum[:, 1]),
        side_by_side(attn_sum[:, 2]),
        own_block(head_sums[0], 8),
        own_block(head_sums[1], 8),
        attn_sum[:, 3].reshape(per_layer * BLK, BLK),
        vec_sums[2],
        vec_sums[3],
        vec_sums[4],
        side_by_side(ffn_sum[:, 0]),
        own_block(up_sum, 4 * 8),
        ffn_sum[:, 1].reshape(8 * BLK, BLK),
        vec_sums[5],
    )


def solution(mesh):
    square = mesh.shape["wide"] == 8 and mesh.shape["tp"] == 4
    return jax.shard_map(
        square_device if square else per_device,
        mesh=mesh,
        in_specs=(
            P("tp", "wide", None),
            P(),
            P("wide"),
            P("wide"),
            P("wide", "tp"),
            P("wide", "tp"),
            P("wide", "tp"),
            P("tp", "wide"),
            P("tp", "wide"),
            P("tp", "wide"),
            P("wide"),
            P("wide"),
            P("wide"),
            P("wide", "tp"),
            P("tp", "wide"),
            P("tp", "wide"),
            P("wide"),
            P("tp", "wide", None),
        ),
        out_specs=(
            P("tp", "wide", None),
            P("tp", "wide", None),
            P("wide"),
            P("wide"),
            P("wide", "tp"),
            P("wide", "tp"),
            P("wide", "tp"),
            P("tp", "wide"),
            P("tp", "wide"),
            P("tp", "wide"),
            P("wide"),
            P("wide"),
            P("wide"),
            P("wide", "tp"),
            P("tp", "wide"),
            P("tp", "wide"),
            P("wide"),
        ),
        check_vma=False,
    )
```

```python
import functools
import math

import jax
import jax.numpy as jnp
from jax import lax
from jax.experimental import pallas as pl
from jax.experimental.pallas import tpu as pltpu
from jax.sharding import PartitionSpec as P

HEAD = 64
MESH = pl.DeviceIdType.MESH


def norm_rows(values, gain_vec, shift_vec):
    middle = jnp.mean(values, axis=-1, keepdims=True)
    centred = values - middle
    spread = jnp.mean(centred * centred, axis=-1, keepdims=True)
    return centred * lax.rsqrt(spread + 1e-05) * gain_vec + shift_vec


def flatten_rows(tensor):
    return tensor.reshape(-1, tensor.shape[-1])


def row_product(first_op, second_op):
    return jnp.dot(first_op, second_op, preferred_element_type=jnp.float32)


def inner_rows(first_op, second_op):
    return lax.dot_general(
        flatten_rows(first_op),
        flatten_rows(second_op),
        (((0,), (0,)), ((), ())),
        preferred_element_type=jnp.float32,
    )


def times_transposed(first_op, second_op):
    return lax.dot_general(
        first_op,
        second_op,
        (((first_op.ndim - 1,), (1,)), ((), ())),
        preferred_element_type=jnp.float32,
    )


def activate(values):
    return jax.nn.gelu(values, approximate=True)


def masked_scores(query_blk, key_blk, lengths_blk, slopes, distance, causal_mask, key_places):
    raw_scores = (
        jnp.einsum("gihd,gjhd->ghij", query_blk, key_blk, preferred_element_type=jnp.float32)
        * 0.125
    )
    raw_scores = raw_scores - slopes[None, :, None, None] * distance[None, None]
    allowed = causal_mask[None] & (key_places[None, None, :] < lengths_blk[:, None, None])
    return jnp.where(allowed[:, None], raw_scores, -jnp.inf)


def per_device(
    hidden_in,
    lengths,
    pre_gain,
    pre_shift,
    w_query,
    w_key,
    w_value,
    b_query,
    b_value,
    w_dense,
    b_dense,
    mid_gain,
    mid_shift,
    w_up,
    b_up,
    w_down,
    b_down,
    cotangent,
):
    local_slots, block_len, _unused = hidden_in.shape
    heads_dev = b_query.shape[0]
    head_width = heads_dev * HEAD
    slot_total = local_slots * lax.axis_size("tp")
    slot_len = block_len * lax.axis_size("wide")
    wide_at = lax.axis_index("wide")
    tp_at = lax.axis_index("tp")
    vec_part = pre_gain.shape[0]
    (
        gain_one,
        shift_one,
        query_w,
        key_w,
        value_w,
        query_b,
        value_b,
        dense_w,
        dense_b,
        gain_two,
        shift_two,
        up_w,
        up_b,
        down_w,
        down_b,
    ) = (
        lax.all_gather(pre_gain, "wide", axis=0, tiled=True),
        lax.all_gather(pre_shift, "wide", axis=0, tiled=True),
        lax.all_gather(w_query, "wide", axis=0, tiled=True),
        lax.all_gather(w_key, "wide", axis=0, tiled=True),
        lax.all_gather(w_value, "wide", axis=0, tiled=True),
        lax.all_gather(b_query, "wide", axis=1, tiled=True),
        lax.all_gather(b_value, "wide", axis=1, tiled=True),
        lax.all_gather(w_dense, "wide", axis=1, tiled=True),
        lax.all_gather(b_dense, "wide", axis=0, tiled=True),
        lax.all_gather(mid_gain, "wide", axis=0, tiled=True),
        lax.all_gather(mid_shift, "wide", axis=0, tiled=True),
        lax.all_gather(w_up, "wide", axis=0, tiled=True),
        lax.all_gather(b_up, "wide", axis=1, tiled=True),
        lax.all_gather(w_down, "wide", axis=1, tiled=True),
        lax.all_gather(b_down, "wide", axis=0, tiled=True),
    )
    gain_one = gain_one.astype(jnp.float32)
    shift_one = shift_one.astype(jnp.float32)
    gain_two = gain_two.astype(jnp.float32)
    shift_two = shift_two.astype(jnp.float32)
    query_places = wide_at * block_len + jnp.arange(block_len, dtype=jnp.int32)
    key_places = jnp.arange(slot_len, dtype=jnp.int32)
    distance = (query_places[:, None] - key_places[None, :]).astype(jnp.float32)
    causal_mask = key_places[None, :] <= query_places[:, None]
    head_index = tp_at * heads_dev + jnp.arange(heads_dev, dtype=jnp.int32)
    slopes = jnp.exp2(-0.5 * (head_index.astype(jnp.float32) + 1.0))
    own_lengths = lax.dynamic_slice_in_dim(lengths, tp_at * local_slots, local_slots, 0)
    validity = (query_places[None, :] < own_lengths[:, None]).astype(jnp.float32)
    group_size = math.gcd(slot_total, max(1, 512 // block_len))
    group_count = slot_total // group_size
    grouped_lengths = lengths.reshape(group_count, group_size)
    hidden = hidden_in.astype(jnp.float32)

    def query_view(tensor):
        return tensor.reshape(group_count, group_size, block_len, heads_dev, HEAD)

    def pair_view(tensor):
        return tensor.reshape(group_count, group_size, slot_len, 2, heads_dev, HEAD)

    def forward_group(inputs):
        query_blk, pair_blk, lengths_blk = inputs
        masked = masked_scores(
            query_blk, pair_blk[:, :, 0], lengths_blk, slopes, distance, causal_mask, key_places
        )
        highest = jnp.max(masked, axis=-1, keepdims=True)
        totals = highest + jnp.log(jnp.sum(jnp.exp(masked - highest), axis=-1, keepdims=True))
        probabilities = jnp.exp(masked - totals).astype(jnp.bfloat16)
        summed = jnp.einsum(
            "ghij,gjhd->gihd", probabilities, pair_blk[:, :, 1], preferred_element_type=jnp.float32
        )
        return (totals[..., 0], summed)

    def attention_forward(hidden_rows):
        normed_f, norm_back = jax.vjp(norm_rows, hidden_rows, gain_one, shift_one)
        normed = normed_f.astype(jnp.bfloat16)
        normed_all = lax.all_gather(normed, "tp", axis=0, tiled=True)
        queries = (
            row_product(normed_all, query_w) + query_b.reshape(head_width).astype(jnp.float32)
        ).astype(jnp.bfloat16)
        keys_now = row_product(normed_all, key_w).astype(jnp.bfloat16)
        values_now = (
            row_product(normed_all, value_w) + value_b.reshape(head_width).astype(jnp.float32)
        ).astype(jnp.bfloat16)
        pairs = jnp.concatenate([keys_now, values_now], axis=-1)
        pairs_all = lax.all_gather(pairs, "wide", axis=1, tiled=True)
        totals, summed = lax.map(
            forward_group, (query_view(queries), pair_view(pairs_all), grouped_lengths)
        )
        return (
            normed_all,
            queries,
            pairs_all,
            totals,
            summed.reshape(slot_total, block_len, head_width),
            norm_back,
        )

    forward_parts = attention_forward(hidden)
    attention = forward_parts[4].astype(jnp.bfloat16)
    branch = lax.psum_scatter(
        row_product(attention, dense_w).astype(jnp.bfloat16), "tp", scatter_dimension=0, tiled=True
    ).astype(jnp.float32)
    residual = hidden + branch + dense_b.astype(jnp.float32)
    second_f, second_back = jax.vjp(norm_rows, residual, gain_two, shift_two)
    second = second_f.astype(jnp.bfloat16)
    grad_output = validity[:, :, None] * cotangent.astype(jnp.float32)
    grad_down = grad_output.astype(jnp.bfloat16)
    second_all, grad_down_all = (
        lax.all_gather(second, "tp", axis=0, tiled=True),
        lax.all_gather(grad_down, "tp", axis=0, tiled=True),
    )
    pre_act = row_product(second_all, up_w) + up_b.reshape(-1).astype(jnp.float32)
    act_value, act_back = jax.vjp(activate, pre_act)
    activated = act_value.astype(jnp.bfloat16)
    down_out = lax.psum_scatter(
        row_product(activated, down_w).astype(jnp.bfloat16), "tp", scatter_dimension=0, tiled=True
    ).astype(jnp.float32)
    grad_act = times_transposed(grad_down_all, down_w)
    grad_pre = act_back(grad_act)[0].astype(jnp.bfloat16)
    grad_up = inner_rows(second_all, grad_pre)
    grad_up_b = jnp.sum(flatten_rows(grad_pre), axis=0, dtype=jnp.float32).reshape(up_b.shape)
    grad_down_w = inner_rows(activated, grad_down_all)
    grad_second = lax.psum_scatter(
        times_transposed(grad_pre, up_w), "tp", scatter_dimension=0, tiled=True
    )
    output = (validity[:, :, None] * (residual + down_out + down_b.astype(jnp.float32))).astype(
        jnp.bfloat16
    )
    grad_resid_norm, grad_gain_two, grad_shift_two = second_back(grad_second)
    grad_resid = grad_output + grad_resid_norm
    grad_branch = grad_resid.astype(jnp.bfloat16)
    hidden_again, grad_branch = lax.optimization_barrier((hidden, grad_branch))
    forward_parts = attention_forward(hidden_again)
    normed_all, queries, pairs_all, totals, summed, norm_back = forward_parts
    attention_back = summed.astype(jnp.bfloat16)
    branch_all = lax.all_gather(grad_branch, "tp", axis=0, tiled=True)
    grad_dense_w = inner_rows(attention_back, branch_all)
    grad_attention = times_transposed(branch_all, dense_w).astype(jnp.bfloat16)

    def backward_group(inputs):
        query_blk, pair_blk, lengths_blk, totals_blk, grad_blk = inputs
        masked = masked_scores(
            query_blk, pair_blk[:, :, 0], lengths_blk, slopes, distance, causal_mask, key_places
        )
        probabilities = jnp.exp(masked - totals_blk[..., None])
        grad_probs = jnp.einsum(
            "gihd,gjhd->ghij", grad_blk, pair_blk[:, :, 1], preferred_element_type=jnp.float32
        )
        row_delta = jnp.sum(probabilities * grad_probs, axis=-1, keepdims=True)
        grad_scores = (probabilities * (grad_probs - row_delta)).astype(jnp.bfloat16)
        grad_query = (
            jnp.einsum(
                "ghij,gjhd->gihd",
                grad_scores,
                pair_blk[:, :, 0],
                preferred_element_type=jnp.float32,
            )
            * 0.125
        )
        grad_key = (
            jnp.einsum(
                "ghij,gihd->gjhd", grad_scores, query_blk, preferred_element_type=jnp.float32
            )
            * 0.125
        )
        grad_value = jnp.einsum(
            "ghij,gihd->gjhd",
            probabilities.astype(jnp.bfloat16),
            grad_blk,
            preferred_element_type=jnp.float32,
        )
        return (grad_query, jnp.stack([grad_key, grad_value], axis=2))

    grad_query_all, grad_pairs = lax.map(
        backward_group,
        (
            query_view(queries),
            pair_view(pairs_all),
            grouped_lengths,
            totals,
            query_view(grad_attention),
        ),
    )
    grad_pairs_local = lax.psum_scatter(
        grad_pairs.reshape(slot_total, slot_len, 2 * head_width).astype(jnp.bfloat16),
        "wide",
        scatter_dimension=1,
        tiled=True,
    ).astype(jnp.float32)
    grad_queries = grad_query_all.reshape(slot_total, block_len, head_width).astype(jnp.bfloat16)
    grad_keys = grad_pairs_local[:, :, :head_width].astype(jnp.bfloat16)
    grad_values = grad_pairs_local[:, :, head_width:].astype(jnp.bfloat16)
    grad_query_w = inner_rows(normed_all, grad_queries)
    grad_key_w = inner_rows(normed_all, grad_keys)
    grad_value_w = inner_rows(normed_all, grad_values)
    grad_query_b = jnp.sum(flatten_rows(grad_queries), axis=0, dtype=jnp.float32).reshape(
        heads_dev, HEAD
    )
    grad_value_b = jnp.sum(flatten_rows(grad_values), axis=0, dtype=jnp.float32).reshape(
        heads_dev, HEAD
    )
    grad_normed = lax.psum_scatter(
        (
            times_transposed(grad_queries, query_w)
            + times_transposed(grad_keys, key_w)
            + times_transposed(grad_values, value_w)
        ).astype(jnp.bfloat16),
        "tp",
        scatter_dimension=0,
        tiled=True,
    ).astype(jnp.float32)
    grad_hidden_norm, grad_gain_one, grad_shift_one = norm_back(grad_normed)
    grad_in = (grad_resid + grad_hidden_norm).astype(jnp.bfloat16)
    (
        sum_query_w,
        sum_key_w,
        sum_value_w,
        sum_query_b,
        sum_value_b,
        sum_dense_w,
        sum_up_w,
        sum_up_b,
        sum_down_w,
    ) = (
        lax.psum_scatter(
            grad_query_w.astype(jnp.bfloat16), "wide", scatter_dimension=0, tiled=True
        ).astype(jnp.float32),
        lax.psum_scatter(
            grad_key_w.astype(jnp.bfloat16), "wide", scatter_dimension=0, tiled=True
        ).astype(jnp.float32),
        lax.psum_scatter(
            grad_value_w.astype(jnp.bfloat16), "wide", scatter_dimension=0, tiled=True
        ).astype(jnp.float32),
        lax.psum_scatter(
            grad_query_b.astype(jnp.bfloat16), "wide", scatter_dimension=1, tiled=True
        ).astype(jnp.float32),
        lax.psum_scatter(
            grad_value_b.astype(jnp.bfloat16), "wide", scatter_dimension=1, tiled=True
        ).astype(jnp.float32),
        lax.psum_scatter(
            grad_dense_w.astype(jnp.bfloat16), "wide", scatter_dimension=1, tiled=True
        ).astype(jnp.float32),
        lax.psum_scatter(
            grad_up.astype(jnp.bfloat16), "wide", scatter_dimension=0, tiled=True
        ).astype(jnp.float32),
        lax.psum_scatter(
            grad_up_b.astype(jnp.bfloat16), "wide", scatter_dimension=1, tiled=True
        ).astype(jnp.float32),
        lax.psum_scatter(
            grad_down_w.astype(jnp.bfloat16), "wide", scatter_dimension=1, tiled=True
        ).astype(jnp.float32),
    )
    grad_dense_b = jnp.sum(grad_resid, axis=(0, 1))
    grad_down_b = jnp.sum(grad_output, axis=(0, 1))
    sum_gain_one, sum_shift_one, sum_dense_b, sum_gain_two, sum_shift_two, sum_down_b = lax.psum(
        (grad_gain_one, grad_shift_one, grad_dense_b, grad_gain_two, grad_shift_two, grad_down_b),
        ("wide", "tp"),
    )

    def own_part(tensor):
        return lax.dynamic_slice_in_dim(tensor, wide_at * vec_part, vec_part, 0)

    return (
        output,
        grad_in,
        own_part(sum_gain_one),
        own_part(sum_shift_one),
        sum_query_w,
        sum_key_w,
        sum_value_w,
        sum_query_b,
        sum_value_b,
        sum_dense_w,
        own_part(sum_dense_b),
        own_part(sum_gain_two),
        own_part(sum_shift_two),
        sum_up_w,
        sum_up_b,
        sum_down_w,
        own_part(sum_down_b),
    )


BF = jnp.bfloat16
F32 = jnp.float32
LOG2E = 1.4426950408889634
NEG = -1e30
BLK = 128


def hbm():
    return pl.BlockSpec(memory_space=pl.ANY)


def vmem():
    return pl.BlockSpec(memory_space=pltpu.VMEM)


def square_places():
    own = lax.axis_index("wide")
    core = own % 2
    col = (own // 2) % 2
    row = own // 4
    pair = own + 1 - 2 * core
    along_x = own + 2 - 4 * col
    along_y = own + 4 - 8 * row
    return own, pair, along_x, along_y, along_x + along_y - own


def greet(targets):
    barrier = pltpu.get_barrier_semaphore()
    for target in targets:
        pl.semaphore_signal(barrier, inc=1, device_id=target, device_id_type=MESH)
    pl.semaphore_wait(barrier, len(targets))


def remote(src, dst, send_sem, recv_sem, target):
    return pltpu.make_async_remote_copy(
        src_ref=src,
        dst_ref=dst,
        send_sem=send_sem,
        recv_sem=recv_sem,
        device_id=target,
        device_id_type=MESH,
    )


class SquareGather:
    SENDS = 13

    def __init__(self, src, dst, send, recv, local):
        own, pair, ax, ay, dg = square_places()

        def place(slot, dev):
            return dst.at[slot, pl.ds(pl.multiple_of(dev * BLK, BLK), BLK)]

        def both(dev):
            return dst.at[:, pl.ds(pl.multiple_of(dev * BLK, BLK), BLK)]

        to_x, to_y, to_p = {"wide": ax}, {"wide": ay}, {"wide": pair}
        self.local = pltpu.make_async_copy(src, both(own), local)
        copies = {}
        copies["x0"] = remote(src.at[0], place(0, own), send.at[0], recv.at[0], to_x)
        copies["x1"] = remote(src.at[1], place(1, own), send.at[1], recv.at[1], to_x)
        copies["y0"] = remote(src.at[0], place(0, own), send.at[2], recv.at[2], to_y)
        copies["y1"] = remote(src.at[1], place(1, own), send.at[3], recv.at[3], to_y)
        copies["d0"] = remote(place(0, ay), place(0, ay), send.at[4], recv.at[4], to_x)
        copies["d1"] = remote(place(1, ax), place(1, ax), send.at[5], recv.at[5], to_y)
        copies["p"] = remote(src, both(own), send.at[6], recv.at[6], to_p)
        for index, (name, slot, dev) in enumerate(
            (("x0", 0, ax), ("x1", 1, ax), ("y0", 0, ay), ("y1", 1, ay), ("d0", 0, dg), ("d1", 1, dg))
        ):
            copies["p" + name] = remote(
                place(slot, dev), place(slot, dev), send.at[7 + index], recv.at[7 + index], to_p
            )
        self.copies = copies

    def start(self):
        for name in ("y0", "x1", "x0", "y1", "p"):
            self.copies[name].start()
        self.local.start()

    def pass_on(self, arrived, sends):
        self.copies[arrived].wait_recv()
        for name in sends:
            self.copies[name].start()

    def first(self):
        self.pass_on("y0", ("d0", "py0"))
        self.pass_on("x1", ("d1", "px1"))

    def second(self):
        self.pass_on("x0", ("px0",))
        self.pass_on("y1", ("py1",))

    def third(self):
        self.pass_on("d0", ("pd0",))
        self.pass_on("d1", ("pd1",))

    def arrive(self, *names):
        for name in names:
            self.copies[name].wait_recv()

    def sent(self):
        for copy in self.copies.values():
            copy.wait_send()

    def finish(self):
        self.arrive("p", "px0", "px1", "py0", "py1", "pd0", "pd1")
        self.sent()
        self.local.wait()


def wide_square(own_places):
    _own, pair, ax, ay, _dg = own_places
    return [{"wide": pair}, {"wide": ax}, {"wide": ay}]


def gather_body(count, *refs):
    srcs, dsts = refs[:count], refs[count : 2 * count]
    send, recv, local = refs[2 * count :]
    greet(wide_square(square_places()))
    parts = [
        SquareGather(srcs[i], dsts[i], send.at[i], recv.at[i], local.at[i]) for i in range(count)
    ]
    for part in parts:
        part.start()
    for part in parts:
        part.first()
    for part in parts:
        part.second()
    for part in parts:
        part.third()
    for part in parts:
        part.finish()


def square_gather(*arrays):
    count = len(arrays)
    width = arrays[0].shape[-1]
    shape = jax.ShapeDtypeStruct((2, 8 * BLK, width), arrays[0].dtype)
    return pl.pallas_call(
        functools.partial(gather_body, count),
        out_shape=[shape] * count,
        in_specs=[vmem()] * count,
        out_specs=[hbm()] * count,
        scratch_shapes=[
            pltpu.SemaphoreType.DMA((count, SquareGather.SENDS)),
            pltpu.SemaphoreType.DMA((count, SquareGather.SENDS)),
            pltpu.SemaphoreType.DMA((count,)),
        ],
        compiler_params=pltpu.CompilerParams(collective_id=count, has_side_effects=True),
        name="square_gather" + str(count),
    )(*arrays)


def add_rows(dst, first, second, third=None):
    step = 16

    def body(index, carry):
        rows = pl.ds(pl.multiple_of(index * step, step), step)
        total = first[rows].astype(F32) + second[rows].astype(F32)
        if third is not None:
            total = total + third[rows].astype(F32)
        dst[rows] = total.astype(dst.dtype)
        return carry

    lax.fori_loop(0, BLK // step, body, 0)


class SquareScatter:
    SENDS = 10

    def __init__(self, src, out, from_pair, summed, from_x, from_y, send, recv):
        own, pair, ax, ay, dg = square_places()
        shift = pair - own
        to_x, to_y, to_p = {"wide": ax}, {"wide": ay}, {"wide": pair}
        self.src, self.out = src, out
        self.from_pair, self.summed, self.from_x, self.from_y = from_pair, summed, from_x, from_y
        self.dests = (dg, ax, ay, own)
        self.pairs = []
        for chip in range(4):
            rows = pl.ds(pl.multiple_of((self.dests[chip] + shift) * BLK, BLK), BLK)
            self.pairs.append(
                remote(src.at[:, rows], from_pair.at[chip], send.at[chip], recv.at[chip], to_p)
            )
        self.dx = remote(summed.at[0, 0], from_x.at[0], send.at[4], recv.at[4], to_x)
        self.dy = remote(summed.at[0, 1], from_y.at[0], send.at[5], recv.at[5], to_y)
        self.xx = remote(summed.at[1, 0], from_x.at[1], send.at[6], recv.at[6], to_x)
        self.yy = remote(summed.at[2, 1], from_y.at[1], send.at[7], recv.at[7], to_y)
        self.ty = remote(summed.at[2, 0], from_y.at[2], send.at[8], recv.at[8], to_y)
        self.tx = remote(summed.at[1, 1], from_x.at[2], send.at[9], recv.at[9], to_x)

    def block(self, slot, chip):
        rows = pl.ds(pl.multiple_of(self.dests[chip] * BLK, BLK), BLK)
        return self.src.at[slot, rows]

    def pair_sum(self, chip, slot, third=None):
        add_rows(
            self.summed.at[chip, slot],
            self.block(slot, chip),
            self.from_pair.at[chip, slot],
            third,
        )

    def near(self, chip):
        self.pairs[chip].wait_recv()
        if chip == 0:
            self.pair_sum(0, 0)
            self.dx.start()
            self.pair_sum(0, 1)
            self.dy.start()
        elif chip == 1:
            self.pair_sum(1, 0)
            self.xx.start()
        elif chip == 2:
            self.pair_sum(2, 1)
            self.yy.start()
        else:
            self.pair_sum(3, 0)
            self.pair_sum(3, 1)

    def middle(self):
        self.dx.wait_recv()
        self.pair_sum(2, 0, self.from_x.at[0])
        self.ty.start()
        self.dy.wait_recv()
        self.pair_sum(1, 1, self.from_y.at[0])
        self.tx.start()

    def start(self):
        for chip in range(4):
            self.pairs[chip].start()

    def first(self):
        for chip in range(3):
            self.near(chip)

    def own_sums(self):
        self.near(3)

    def finish(self):
        self.xx.wait_recv()
        self.ty.wait_recv()
        add_rows(self.out.at[0], self.summed.at[3, 0], self.from_x.at[1], self.from_y.at[2])
        self.yy.wait_recv()
        self.tx.wait_recv()
        add_rows(self.out.at[1], self.summed.at[3, 1], self.from_y.at[1], self.from_x.at[2])
        for copy in self.pairs:
            copy.wait_send()
        for copy in (self.dx, self.dy, self.xx, self.yy, self.ty, self.tx):
            copy.wait_send()


def scatter_scratch(count, width):
    return [
        pltpu.VMEM((count, 4, 2, BLK, width), BF),
        pltpu.VMEM((count, 4, 2, BLK, width), BF),
        pltpu.VMEM((count, 3, BLK, width), BF),
        pltpu.VMEM((count, 3, BLK, width), BF),
        pltpu.SemaphoreType.DMA((count, SquareScatter.SENDS)),
        pltpu.SemaphoreType.DMA((count, SquareScatter.SENDS)),
    ]


def scatter_parts(srcs, outs, scratch):
    return [
        SquareScatter(srcs[i], outs[i], *[buffer.at[i] for buffer in scratch])
        for i in range(len(srcs))
    ]


def scatter_body(count, *refs):
    srcs, outs = refs[:count], refs[count : 2 * count]
    greet(wide_square(square_places()))
    parts = scatter_parts(srcs, outs, refs[2 * count :])
    for part in parts:
        part.start()
    for part in parts:
        part.first()
    for part in parts:
        part.middle()
    for part in parts:
        part.own_sums()
    for part in parts:
        part.finish()


def square_scatter(*arrays):
    count = len(arrays)
    width = arrays[0].shape[-1]
    shape = jax.ShapeDtypeStruct((2, BLK, width), F32)
    return pl.pallas_call(
        functools.partial(scatter_body, count),
        out_shape=[shape] * count,
        in_specs=[vmem()] * count,
        out_specs=[vmem()] * count,
        scratch_shapes=scatter_scratch(count, width),
        compiler_params=pltpu.CompilerParams(collective_id=4 + count, has_side_effects=True),
        name="square_scatter" + str(count),
    )(*arrays)


def wide_others(own):
    return [{"wide": (own + step) % 8} for step in range(1, 8)]


def first_body(
    depth,
    hidden,
    attn_w,
    ffn_w,
    vec,
    hidden_all,
    attn_all,
    ffn_all,
    vec_all,
    attn_z,
    vec_z,
    send,
    recv,
    local,
    z_send,
    z_recv,
    a_send,
    a_recv,
    f_send,
    f_recv,
    v_send,
    v_recv,
    own_sems,
):
    own, pair, ax, ay, dg = square_places()
    layer = lax.axis_index("tp")
    greet(wide_others(own) + [{"tp": (layer + step) % depth} for step in range(1, depth)])
    gather = SquareGather(hidden, hidden_all, send, recv, local.at[0])
    gather.start()

    def up_copies(step):
        index = layer - step + 1
        sem = step - 1
        src_w = attn_w if step == 1 else attn_z.at[index]
        src_v = vec if step == 1 else vec_z.at[index]
        up = {"tp": layer + 1}
        return (
            remote(src_w, attn_z.at[index], z_send.at[0, sem], z_recv.at[0, sem], up),
            remote(src_v, vec_z.at[index], z_send.at[1, sem], z_recv.at[1, sem], up),
        )

    def down_copies(step):
        index = layer + step - 1
        sem = step - 1
        src_w = attn_w if step == 1 else attn_z.at[index]
        src_v = vec if step == 1 else vec_z.at[index]
        down = {"tp": layer - 1}
        return (
            remote(src_w, attn_z.at[index], z_send.at[2, sem], z_recv.at[2, sem], down),
            remote(src_v, vec_z.at[index], z_send.at[3, sem], z_recv.at[3, sem], down),
        )

    def z_start(step):
        @pl.when((layer < depth - 1) & (layer - step + 1 >= 0))
        def _():
            for copy in up_copies(step):
                copy.start()

        @pl.when((layer > 0) & (layer + step - 1 < depth))
        def _():
            for copy in down_copies(step):
                copy.start()

    def z_arrive(step):
        @pl.when(layer - step >= 0)
        def _():
            for copy in up_copies(step):
                copy.wait_recv()

        @pl.when(layer + step < depth)
        def _():
            for copy in down_copies(step):
                copy.wait_recv()

    def z_sent(step):
        @pl.when((layer < depth - 1) & (layer - step + 1 >= 0))
        def _():
            for copy in up_copies(step):
                copy.wait_send()

        @pl.when((layer > 0) & (layer + step - 1 < depth))
        def _():
            for copy in down_copies(step):
                copy.wait_send()

    z_start(1)
    own_z = [
        pltpu.make_async_copy(attn_w, attn_z.at[layer], own_sems.at[0]),
        pltpu.make_async_copy(vec, vec_z.at[layer], own_sems.at[1]),
    ]
    for copy in own_z:
        copy.start()
    gather.first()
    ffn_own = pltpu.make_async_copy(ffn_w.at[own], ffn_all.at[:, own], own_sems.at[2])
    ffn_own.start()
    ffn_copies = []
    for step in range(1, 8):
        there = (own + step) % 8
        ffn_copies.append(
            remote(
                ffn_w.at[there],
                ffn_all.at[:, own],
                f_send.at[step - 1],
                f_recv.at[step - 1],
                {"wide": there},
            )
        )
    for copy in ffn_copies:
        copy.start()
    z_arrive(1)
    if depth > 2:
        z_start(2)
    gather.second()
    if depth > 2:
        z_arrive(2)
    if depth > 3:
        z_start(3)
    gather.third()
    if depth > 3:
        z_arrive(3)
    for copy in own_z:
        copy.wait()
    per_layer = 8 // depth
    attn_own = pltpu.make_async_copy(
        attn_z.at[own // per_layer, own % per_layer], attn_all.at[:, own], own_sems.at[3]
    )
    attn_own.start()
    vec_own = pltpu.make_async_copy(vec_z, vec_all.at[own], own_sems.at[4])
    vec_own.start()
    late = []
    for step in range(1, 8):
        there = (own + step) % 8
        late.append(
            remote(vec_z, vec_all.at[own], v_send.at[step - 1], v_recv.at[step - 1], {"wide": there})
        )
        late.append(
            remote(
                attn_z.at[there // per_layer, there % per_layer],
                attn_all.at[:, own],
                a_send.at[step - 1],
                a_recv.at[step - 1],
                {"wide": there},
            )
        )
    for copy in late:
        copy.start()
    gather.finish()
    for copy in ffn_copies + late:
        copy.wait_recv()
    for copy in ffn_copies + late:
        copy.wait_send()
    ffn_own.wait()
    attn_own.wait()
    vec_own.wait()
    for step in range(1, depth):
        z_sent(step)


def first_exchange(depth, hidden, attn_w, ffn_w, vec):
    width = hidden.shape[-1]
    dma = pltpu.SemaphoreType.DMA
    return pl.pallas_call(
        functools.partial(first_body, depth),
        out_shape=[
            jax.ShapeDtypeStruct((2, 8 * BLK, width), BF),
            jax.ShapeDtypeStruct((4, 8, BLK, BLK), BF),
            jax.ShapeDtypeStruct((2, 8, BLK, BLK), BF),
            jax.ShapeDtypeStruct((8, depth) + vec.shape, F32),
        ],
        in_specs=[vmem()] * 4,
        out_specs=[hbm(), hbm(), hbm(), vmem()],
        scratch_shapes=[
            pltpu.VMEM((depth,) + attn_w.shape, BF),
            pltpu.VMEM((depth,) + vec.shape, F32),
            dma((SquareGather.SENDS,)),
            dma((SquareGather.SENDS,)),
            dma((1,)),
            dma((4, depth - 1)),
            dma((4, depth - 1)),
            dma((7,)),
            dma((7,)),
            dma((7,)),
            dma((7,)),
            dma((7,)),
            dma((7,)),
            dma((5,)),
        ],
        compiler_params=pltpu.CompilerParams(collective_id=10, has_side_effects=True),
        name="first_exchange",
    )(hidden, attn_w, ffn_w, vec)


def last_body(
    depth,
    shares,
    attn_g,
    ffn_g,
    rows_out,
    attn_out,
    ffn_out,
    attn_in,
    attn_z,
    from_pair,
    summed,
    from_x,
    from_y,
    s_send,
    s_recv,
    a_send,
    a_recv,
    z_send,
    z_recv,
    f_send,
    f_recv,
    own_sems,
):
    own, pair, ax, ay, dg = square_places()
    layer = lax.axis_index("tp")
    per_layer = 8 // depth
    greet(wide_others(own) + [{"tp": (layer + step) % depth} for step in range(1, depth)])
    scatter = scatter_parts(
        [shares], [rows_out], (from_pair, summed, from_x, from_y, s_send, s_recv)
    )[0]
    scatter.start()
    attn_copies = []
    for step in range(1, 8):
        there = (own + step) % 8
        attn_copies.append(
            remote(
                attn_g.at[there],
                attn_in.at[own],
                a_send.at[step - 1],
                a_recv.at[step - 1],
                {"wide": there},
            )
        )
    for copy in attn_copies:
        copy.start()
    own_copy = pltpu.make_async_copy(attn_g.at[own], attn_in.at[own], own_sems.at[0])
    own_copy.start()
    scatter.first()

    def onward(index):
        goal = index // per_layer
        piece = index % per_layer
        return remote(
            attn_in.at[index],
            attn_z.at[layer, piece],
            z_send.at[index],
            z_recv.at[layer, piece],
            {"tp": goal},
        )

    def forward(index):
        @pl.when(index // per_layer != layer)
        def _():
            onward(index).start()

    own_copy.wait()
    forward(own)
    for step in range(1, 8):
        attn_copies[step - 1].wait_recv()
        forward((own + 8 - step) % 8)
    ffn_own = pltpu.make_async_copy(ffn_g.at[own], ffn_out.at[own], own_sems.at[1])
    ffn_own.start()
    ffn_copies = []
    for step in range(1, 8):
        there = (own + step) % 8
        ffn_copies.append(
            remote(
                ffn_g.at[there],
                ffn_out.at[own],
                f_send.at[step - 1],
                f_recv.at[step - 1],
                {"wide": there},
            )
        )
    scatter.middle()
    for copy in ffn_copies:
        copy.start()
    scatter.own_sums()
    scatter.finish()
    for step in range(1, depth):
        source = (layer + step) % depth
        for piece in range(per_layer):
            remote(
                attn_in.at[piece],
                attn_z.at[source, piece],
                z_send.at[piece],
                z_recv.at[source, piece],
                {"tp": source},
            ).wait_recv()
    for piece in range(per_layer):
        for kind in range(4):
            total = attn_in[layer * per_layer + piece, kind].astype(F32)
            for step in range(1, depth):
                total = total + attn_z[(layer + step) % depth, piece, kind].astype(F32)
            attn_out[piece, kind] = total
    for copy in attn_copies:
        copy.wait_send()
    for index in range(8):
        @pl.when(index // per_layer != layer)
        def _(index=index):
            onward(index).wait_send()

    for copy in ffn_copies:
        copy.wait_recv()
    for copy in ffn_copies:
        copy.wait_send()
    ffn_own.wait()


def last_exchange(depth, shares, attn_g, ffn_g):
    width = shares.shape[-1]
    dma = pltpu.SemaphoreType.DMA
    per_layer = 8 // depth
    return pl.pallas_call(
        functools.partial(last_body, depth),
        out_shape=[
            jax.ShapeDtypeStruct((2, BLK, width), F32),
            jax.ShapeDtypeStruct((per_layer, 4, BLK, BLK), F32),
            jax.ShapeDtypeStruct((8, 2, BLK, BLK), BF),
        ],
        in_specs=[vmem()] * 3,
        out_specs=[vmem()] * 3,
        scratch_shapes=[
            pltpu.VMEM((8, 4, BLK, BLK), BF),
            pltpu.VMEM((depth, per_layer, 4, BLK, BLK), BF),
        ]
        + scatter_scratch(1, width)
        + [
            dma((7,)),
            dma((7,)),
            dma((8,)),
            dma((depth, per_layer)),
            dma((7,)),
            dma((7,)),
            dma((2,)),
        ],
        compiler_params=pltpu.CompilerParams(collective_id=11, has_side_effects=True),
        name="last_exchange",
    )(shares, attn_g, ffn_g)


def sums_body(depth, parts, gathered, send, recv, local):
    own = lax.axis_index("wide")
    layer = lax.axis_index("tp")
    others = []
    for up in range(depth):
        for step in range(8):
            if up or step:
                others.append(((own + step) % 8, (layer + up) % depth))
    greet([{"wide": wide, "tp": tp} for wide, tp in others])
    keep = pltpu.make_async_copy(parts.at[own], gathered.at[own, layer], local.at[0])
    keep.start()
    copies = [
        remote(
            parts.at[wide],
            gathered.at[own, layer],
            send.at[index],
            recv.at[index],
            {"wide": wide, "tp": tp},
        )
        for index, (wide, tp) in enumerate(others)
    ]
    for copy in copies:
        copy.start()
    for copy in copies:
        copy.wait_recv()
    for copy in copies:
        copy.wait_send()
    keep.wait()


def share_sums(depth, parts):
    dma = pltpu.SemaphoreType.DMA
    return pl.pallas_call(
        functools.partial(sums_body, depth),
        out_shape=jax.ShapeDtypeStruct((8, depth) + parts.shape[1:], F32),
        in_specs=[vmem()],
        out_specs=vmem(),
        scratch_shapes=[dma((8 * depth - 1,)), dma((8 * depth - 1,)), dma((1,))],
        compiler_params=pltpu.CompilerParams(collective_id=12, has_side_effects=True),
        name="share_sums",
    )(parts)


def head_bias(length, slope, rows):
    place = lax.broadcasted_iota(jnp.int32, (rows, QB), 0)
    bias = slope * place.astype(F32)
    return jnp.where(place < length, bias, NEG)


QB = 256


def dot_nt(first, second):
    return lax.dot_general(first, second, (((1,), (1,)), ((), ())), preferred_element_type=F32)


def dot_nn(first, second):
    return lax.dot_general(first, second, (((1,), (0,)), ((), ())), preferred_element_type=F32)


def later_key(size):
    key_place = lax.broadcasted_iota(jnp.int32, (size, size), 0)
    query_place = lax.broadcasted_iota(jnp.int32, (size, size), 1)
    return key_place > query_place


def attend_body(lengths, slopes, qkv, out, totals, bias):
    slot = pl.program_id(0)
    rows = qkv.shape[1]
    length = lengths[slot]
    scale = 0.125 * LOG2E
    for head in range(2):
        lanes = pl.ds(head * HEAD, HEAD)
        bias[...] = head_bias(length, slopes[head], rows)
        key = qkv[0, :, pl.ds(2 * HEAD + head * HEAD, HEAD)]
        value = qkv[0, :, pl.ds(4 * HEAD + head * HEAD, HEAD)]
        value_t = value.T
        for step in range(rows // QB):
            here = pl.ds(step * QB, QB)
            extent = (step + 1) * QB
            query = qkv[0, here, lanes]
            scores = dot_nt(key[:extent], query) * scale + bias[:extent]
            low_part = jnp.where(later_key(QB), NEG, scores[extent - QB :])
            scores = low_part if step == 0 else jnp.concatenate([scores[: extent - QB], low_part], 0)
            highest = jnp.max(scores, axis=0, keepdims=True)
            weights = jnp.exp2(scores - highest)
            total = jnp.sum(weights, axis=0, keepdims=True)
            mixed = dot_nn(value_t[:, :extent], weights.astype(BF)) / total
            out[0, here, lanes] = mixed.T.astype(BF)
            totals[0, pl.ds(head, 1), here] = highest + jnp.log2(total)


def attend(lengths, slopes, qkv):
    slots, rows, _width = qkv.shape
    return pl.pallas_call(
        attend_body,
        grid=(slots,),
        out_shape=[
            jax.ShapeDtypeStruct((slots, rows, 2 * HEAD), BF),
            jax.ShapeDtypeStruct((slots, 2, rows), F32),
        ],
        in_specs=[
            pl.BlockSpec(memory_space=pltpu.SMEM),
            pl.BlockSpec(memory_space=pltpu.SMEM),
            pl.BlockSpec((1, rows, 6 * HEAD), lambda s: (s, 0, 0)),
        ],
        out_specs=[
            pl.BlockSpec((1, rows, 2 * HEAD), lambda s: (s, 0, 0)),
            pl.BlockSpec((1, 2, rows), lambda s: (s, 0, 0)),
        ],
        scratch_shapes=[pltpu.VMEM((rows, QB), F32)],
        name="attend",
    )(lengths, slopes, qkv)


def attend_back_body(lengths, slopes, qkv, attention, grad, totals, out, bias, key_sum, value_sum):
    slot = pl.program_id(0)
    rows = qkv.shape[1]
    length = lengths[slot]
    scale = 0.125 * LOG2E
    for head in range(2):
        lanes = pl.ds(head * HEAD, HEAD)
        key_lanes = pl.ds(2 * HEAD + head * HEAD, HEAD)
        value_lanes = pl.ds(4 * HEAD + head * HEAD, HEAD)
        bias[...] = head_bias(length, slopes[head], rows)
        key = qkv[0, :, key_lanes]
        value = qkv[0, :, value_lanes]
        key_t = key.T
        key_sum[...] = jnp.zeros_like(key_sum)
        value_sum[...] = jnp.zeros_like(value_sum)
        for step in range(rows // QB):
            here = pl.ds(step * QB, QB)
            extent = (step + 1) * QB
            query = qkv[0, here, lanes]
            grad_rows = grad[0, here, lanes]
            product = grad_rows.astype(F32) * attention[0, here, lanes].astype(F32)
            delta = jnp.sum(product.T, axis=0, keepdims=True)
            scores = dot_nt(key[:extent], query) * scale + bias[:extent]
            low_part = jnp.where(later_key(QB), NEG, scores[extent - QB :])
            scores = low_part if step == 0 else jnp.concatenate([scores[: extent - QB], low_part], 0)
            probs = jnp.exp2(scores - totals[0, pl.ds(head, 1), here])
            grad_probs = dot_nt(value[:extent], grad_rows)
            grad_scores = (probs * (grad_probs - delta)).astype(BF)
            span = pl.ds(0, extent)
            value_sum[span] += dot_nn(probs.astype(BF), grad_rows)
            key_sum[span] += dot_nn(grad_scores, query)
            grad_query = dot_nn(key_t[:, :extent], grad_scores)
            out[0, here, lanes] = (grad_query.T * 0.125).astype(BF)
        out[0, :, key_lanes] = (key_sum[...] * 0.125).astype(BF)
        out[0, :, value_lanes] = value_sum[...].astype(BF)


def attend_back(lengths, slopes, qkv, attention, grad, totals):
    slots, rows, _width = qkv.shape
    return pl.pallas_call(
        attend_back_body,
        grid=(slots,),
        out_shape=jax.ShapeDtypeStruct((slots, rows, 6 * HEAD), BF),
        in_specs=[
            pl.BlockSpec(memory_space=pltpu.SMEM),
            pl.BlockSpec(memory_space=pltpu.SMEM),
            pl.BlockSpec((1, rows, 6 * HEAD), lambda s: (s, 0, 0)),
            pl.BlockSpec((1, rows, 2 * HEAD), lambda s: (s, 0, 0)),
            pl.BlockSpec((1, rows, 2 * HEAD), lambda s: (s, 0, 0)),
            pl.BlockSpec((1, 2, rows), lambda s: (s, 0, 0)),
        ],
        out_specs=pl.BlockSpec((1, rows, 6 * HEAD), lambda s: (s, 0, 0)),
        scratch_shapes=[
            pltpu.VMEM((rows, QB), F32),
            pltpu.VMEM((rows, HEAD), F32),
            pltpu.VMEM((rows, HEAD), F32),
        ],
        name="attend_back",
    )(lengths, slopes, qkv, attention, grad, totals)


def norm_stats(values):
    middle = jnp.mean(values, axis=-1, keepdims=True)
    centred = values - middle
    spread = jnp.mean(centred * centred, axis=-1, keepdims=True)
    inverse = lax.rsqrt(spread + 1e-05)
    return centred * inverse, inverse


def norm_back_rows(grad, hat, inverse, gain):
    scaled = grad * gain
    first = jnp.mean(scaled, axis=-1, keepdims=True)
    second = jnp.mean(scaled * hat, axis=-1, keepdims=True)
    return (scaled - first - hat * second) * inverse


def gelu_parts(values):
    root = math.sqrt(2 / math.pi)
    squared = values * values
    inner = jnp.tanh(root * values * (1.0 + 0.044715 * squared))
    half = 0.5 * (1.0 + inner)
    slope = half + 0.5 * values * (1.0 - inner * inner) * root * (1.0 + 3 * 0.044715 * squared)
    return values * half, slope


def relation(index):
    own = lax.axis_index("wide")
    core = (own + index) % 2
    col = (own // 2 + index // 2) % 2
    row = (own // 4 + index // 4) % 2
    return row * 4 + col * 2 + core


def middle_body(
    depth,
    hidden,
    branch,
    vectors,
    up_b,
    cotangent,
    valid,
    down_all,
    ffn_z,
    branch_all,
    down_share,
    residual,
    grad_resid,
    sums,
    ffn_g,
    grad_up_b,
    second_all,
    second_share,
    up_w,
    down_w,
    act_t,
    pre_t,
    own_rows,
    grad_second,
    from_pair,
    summed,
    from_x,
    from_y,
    s_send,
    s_recv,
    g_send,
    g_recv,
    h_send,
    h_recv,
    local,
    w_sems,
):
    width = hidden.shape[-1]
    units = depth * BLK
    loads = []
    for up in range(depth):
        lanes = pl.ds(up * BLK, BLK)
        for blk in range(8):
            rows = pl.ds(blk * BLK, BLK)
            loads.append(
                pltpu.make_async_copy(ffn_z.at[up, 0, blk], up_w.at[rows, lanes], w_sems.at[0, up * 8 + blk])
            )
            loads.append(
                pltpu.make_async_copy(ffn_z.at[up, 1, blk], down_w.at[lanes, rows], w_sems.at[1, up * 8 + blk])
            )
    for load in loads:
        load.start()
    greet(wide_square(square_places()))
    step = 32

    def norm_part(index, carry):
        rows = pl.ds(pl.multiple_of(index * step, step), step)
        for slot in range(2):
            values = hidden[slot, rows].astype(F32) + branch[slot, rows] + vectors[4:5]
            residual[slot, rows] = values
            hat, _inverse = norm_stats(values)
            own_rows[slot, rows] = (hat * vectors[2:3] + vectors[3:4]).astype(BF)
        return carry

    lax.fori_loop(0, BLK // step, norm_part, 0)
    gather = SquareGather(own_rows, second_all, g_send, g_recv, local.at[0])
    gather.start()
    scatter = SquareScatter(
        second_share, grad_second, from_pair, summed, from_x, from_y, s_send, s_recv
    )
    for load in loads:
        load.wait()

    def compute(index, carry):
        source = relation(index)
        rows = pl.ds(pl.multiple_of(source * BLK, BLK), BLK)
        values = second_all[:, rows].reshape(2 * BLK, width)
        pre_act = dot_nn(values, up_w[...]) + up_b[...]
        act_value, act_slope = gelu_parts(pre_act)
        activated = act_value.astype(BF)
        grad_rows = down_all[:, rows].reshape(2 * BLK, width)
        grad_pre = (dot_nt(grad_rows, down_w[...]) * act_slope).astype(BF)
        down_share[:, rows] = dot_nn(activated, down_w[...]).astype(BF).reshape(2, BLK, width)
        second_share[:, rows] = dot_nt(grad_pre, up_w[...]).astype(BF).reshape(2, BLK, width)
        grad_up_b[...] += jnp.sum(grad_pre.astype(F32), axis=0, keepdims=True)
        for slot in range(2):
            lanes = pl.ds(pl.multiple_of(slot * 8 * BLK + source * BLK, BLK), BLK)
            part = slice(slot * BLK, (slot + 1) * BLK)
            act_t[:, lanes] = activated[part].T
            pre_t[:, lanes] = grad_pre[part].T
        return carry

    grad_up_b[...] = jnp.zeros_like(grad_up_b)
    gather.arrive("p")
    gather.local.wait()
    lax.fori_loop(0, 2, compute, 0)
    scatter.pairs[3].start()
    gather.first()
    gather.second()
    gather.arrive("px0", "px1", "py0", "py1")
    lax.fori_loop(2, 4, compute, 0)
    scatter.pairs[1].start()
    scatter.near(3)
    lax.fori_loop(4, 6, compute, 0)
    scatter.pairs[2].start()
    gather.third()
    scatter.near(1)
    gather.arrive("pd0", "pd1")
    lax.fori_loop(6, 8, compute, 0)
    scatter.pairs[0].start()
    scatter.near(2)
    scatter.near(0)

    def weight_grads(left, right, kind):
        def one(up, carry):
            rows = pl.ds(pl.multiple_of(up * BLK, BLK), BLK)
            total = dot_nn(left[rows, pl.ds(0, 8 * BLK)], right[0])
            total = total + dot_nn(left[rows, pl.ds(8 * BLK, 8 * BLK)], right[1])
            total = total.astype(BF)
            for blk in range(8):
                ffn_g[up, blk, kind] = total[:, blk * BLK : (blk + 1) * BLK]
            return carry

        lax.fori_loop(0, depth, one, 0)

    weight_grads(pre_t, second_all, 0)
    scatter.middle()
    weight_grads(act_t, down_all, 1)
    scatter.finish()
    gather.sent()

    sums[...] = jnp.zeros_like(sums)

    def back_part(index, carry):
        rows = pl.ds(pl.multiple_of(index * step, step), step)
        for slot in range(2):
            hat, inverse = norm_stats(residual[slot, rows])
            grad = grad_second[slot, rows]
            mask = valid[slot, rows][:, :1]
            grad_out = mask * cotangent[slot, rows].astype(F32)
            total = grad_out + norm_back_rows(grad, hat, inverse, vectors[2:3])
            grad_resid[slot, rows] = total
            own_rows[slot, rows] = total.astype(BF)
            for place, value in enumerate((total, grad * hat, grad, grad_out)):
                sums[pl.ds(place, 1)] += jnp.sum(value, axis=0, keepdims=True)
        return carry

    lax.fori_loop(0, BLK // step, back_part, 0)
    again = SquareGather(own_rows, branch_all, h_send, h_recv, local.at[1])
    again.start()
    again.first()
    again.second()
    again.third()
    again.finish()


def middle(depth, hidden, branch, vectors, up_b, cotangent, valid, down_all, ffn_z):
    width = hidden.shape[-1]
    units = depth * BLK
    dma = pltpu.SemaphoreType.DMA
    tokens = jax.ShapeDtypeStruct((2, 8 * BLK, width), BF)
    rows = jax.ShapeDtypeStruct((2, BLK, width), F32)
    return pl.pallas_call(
        functools.partial(middle_body, depth),
        out_shape=[
            tokens,
            tokens,
            rows,
            rows,
            jax.ShapeDtypeStruct((8, width), F32),
            jax.ShapeDtypeStruct((depth, 8, 2, BLK, BLK), BF),
            jax.ShapeDtypeStruct((1, units), F32),
        ],
        in_specs=[vmem()] * 7 + [hbm()],
        out_specs=[hbm()] + [vmem()] * 6,
        scratch_shapes=[
            pltpu.VMEM((2, 8 * BLK, width), BF),
            pltpu.VMEM((2, 8 * BLK, width), BF),
            pltpu.VMEM((width, units), BF),
            pltpu.VMEM((units, width), BF),
            pltpu.VMEM((units, 16 * BLK), BF),
            pltpu.VMEM((units, 16 * BLK), BF),
            pltpu.VMEM((2, BLK, width), BF),
            pltpu.VMEM((2, BLK, width), F32),
        ]
        + single_scratch(width)
        + [
            dma((SquareGather.SENDS,)),
            dma((SquareGather.SENDS,)),
            dma((SquareGather.SENDS,)),
            dma((SquareGather.SENDS,)),
            dma((2,)),
            dma((2, 8 * depth)),
        ],
        compiler_params=pltpu.CompilerParams(
            collective_id=13, has_side_effects=True, vmem_limit_bytes=62 * 1024 * 1024
        ),
        name="middle",
    )(hidden, branch, vectors, up_b, cotangent, valid, down_all, ffn_z)


def single_scratch(width):
    return [
        pltpu.VMEM((4, 2, BLK, width), BF),
        pltpu.VMEM((4, 2, BLK, width), BF),
        pltpu.VMEM((3, BLK, width), BF),
        pltpu.VMEM((3, BLK, width), BF),
        pltpu.SemaphoreType.DMA((SquareScatter.SENDS,)),
        pltpu.SemaphoreType.DMA((SquareScatter.SENDS,)),
    ]


def square_device(
    hidden_in,
    lengths,
    pre_gain,
    pre_shift,
    w_query,
    w_key,
    w_value,
    b_query,
    b_value,
    w_dense,
    b_dense,
    mid_gain,
    mid_shift,
    w_up,
    b_up,
    w_down,
    b_down,
    cotangent,
):
    depth = lax.axis_size("tp")
    own = lax.axis_index("wide")
    layer = lax.axis_index("tp")
    width = hidden_in.shape[-1]
    rows = 8 * BLK
    per_layer = 8 // depth
    heads_dev = b_query.shape[0]
    own_lengths = lax.dynamic_slice_in_dim(lengths, layer * 2, 2, 0)
    head_index = 2 * own + jnp.arange(2, dtype=jnp.int32)
    slopes = jnp.exp2(-0.5 * (head_index.astype(F32) + 1.0)) * LOG2E

    def halves(weight):
        return weight.reshape(BLK, per_layer, BLK).transpose(1, 0, 2)

    attn_w = jnp.stack(
        [halves(w_query), halves(w_key), halves(w_value), w_dense.reshape(per_layer, BLK, BLK)], 1
    )
    ffn_w = jnp.stack(
        [w_up.reshape(BLK, 8, BLK).transpose(1, 0, 2), w_down.reshape(8, BLK, BLK)], 1
    )
    head_row = jnp.concatenate(
        [b_query.reshape(-1), b_value.reshape(-1), jnp.zeros((BLK - 16 * heads_dev,), BF)]
    )
    vec = jnp.stack(
        [pre_gain, pre_shift, mid_gain, mid_shift, b_dense, b_down, b_up.reshape(-1), head_row]
    ).astype(F32)
    hidden_all, attn_all, ffn_all, vec_all = first_exchange(depth, hidden_in, attn_w, ffn_w, vec)
    ffn_z = lax.all_gather(ffn_all, "tp", axis=0, tiled=False)

    vectors = vec_all[:, 0].transpose(1, 0, 2).reshape(8, width)
    gain_one, shift_one = vectors[0], vectors[1]
    up_b = vec_all[:, :, 6].reshape(8, depth, heads_dev, 4 * 8).transpose(1, 2, 0, 3)
    up_b = lax.dynamic_index_in_dim(up_b.reshape(depth, 8, BLK), own, 1, False).reshape(-1)
    span = heads_dev * 8

    def head_vector(index):
        full = vec_all[:, :, 7, index * span : (index + 1) * span]
        full = full.reshape(8, depth, heads_dev, 8).transpose(1, 2, 0, 3).reshape(8, 2 * HEAD)
        return lax.dynamic_index_in_dim(full, own, 0, False)

    qkv_b = jnp.concatenate([head_vector(0), jnp.zeros((2 * HEAD,), F32), head_vector(1)])
    qkv_w = attn_all[:3].reshape(3, width, BLK).transpose(1, 0, 2).reshape(width, 3 * BLK)
    dense_w = attn_all[3].transpose(1, 0, 2).reshape(BLK, width)
    normed = norm_stats(hidden_all.astype(F32))[0] * gain_one + shift_one
    normed = normed.astype(BF)
    qkv = (row_product(normed, qkv_w) + qkv_b).astype(BF)
    attention, totals = attend(own_lengths, slopes, qkv)
    branch = square_scatter(row_product(attention, dense_w).astype(BF))[0]

    hidden = hidden_in.astype(F32)
    places = own * BLK + jnp.arange(BLK, dtype=jnp.int32)
    validity = (places[None, :] < own_lengths[:, None]).astype(F32)[:, :, None]
    grad_output = validity * cotangent.astype(F32)
    down_all = square_gather(grad_output.astype(BF))[0]
    branch_all, down_share, residual, grad_resid, mid_sums, ffn_g, grad_up_b = middle(
        depth,
        hidden_in,
        branch,
        vectors,
        up_b.reshape(1, -1),
        cotangent,
        jnp.broadcast_to(validity, (2, BLK, BLK)),
        down_all,
        ffn_z,
    )
    grad_up_b = grad_up_b[0]
    ffn_g = lax.psum_scatter(ffn_g, "tp", scatter_dimension=0, tiled=False)
    down_out = square_scatter(down_share)[0]
    output = (validity * (residual + down_out + vectors[5])).astype(BF)
    grad_attention = times_transposed(branch_all, dense_w).astype(BF)
    grad_dense = inner_rows(attention, branch_all).astype(BF)
    grad_qkv = attend_back(own_lengths, slopes, qkv, attention, grad_attention, totals)
    normed_share = times_transposed(grad_qkv, qkv_w).astype(BF)
    grad_qkv_w = inner_rows(normed, grad_qkv).astype(BF)
    grad_qkv_b = jnp.sum(flatten_rows(grad_qkv), axis=0, dtype=F32)
    attn_g = jnp.concatenate(
        [
            grad_qkv_w.reshape(8, BLK, 3, BLK).transpose(0, 2, 1, 3),
            grad_dense.reshape(BLK, 8, BLK).transpose(1, 0, 2)[:, None],
        ],
        1,
    )
    grad_normed, attn_sum, ffn_sum = last_exchange(depth, normed_share, attn_g, ffn_g)

    hat_one, inverse_one = norm_stats(hidden)
    grad_in = (grad_resid + norm_back_rows(grad_normed, hat_one, inverse_one, gain_one)).astype(BF)

    def token_sum(values):
        return jnp.sum(values, axis=(0, 1))

    parts = jnp.concatenate(
        [jnp.stack([token_sum(grad_normed * hat_one), token_sum(grad_normed)]), mid_sums[:4]]
    )
    parts = parts.reshape(6, 8, BLK).transpose(1, 0, 2)
    own_sums = jnp.concatenate([grad_up_b, grad_qkv_b[: 2 * HEAD], grad_qkv_b[4 * HEAD :]])
    own_sums = jnp.broadcast_to(own_sums.reshape(1, -1, BLK), (8, depth + 2, BLK))
    pad = jnp.zeros((8, 16 - 8 - depth, BLK), F32)
    sums = share_sums(depth, jnp.concatenate([parts, own_sums, pad], 1))
    vec_sums = jnp.sum(sums[:, :, :6], axis=(0, 1))
    unit_sums = jnp.sum(sums[:, :, 6 : 8 + depth], axis=1)
    up_sum = unit_sums[:, :depth].transpose(1, 0, 2).reshape(2 * HEAD // 8, 8 * depth * BLK // 16)
    head_sums = unit_sums[:, depth:].transpose(1, 0, 2).reshape(2, 16, HEAD)

    def own_block(tensor, size):
        return lax.dynamic_slice(tensor, (layer * heads_dev, own * size), (heads_dev, size))

    def side_by_side(blocks):
        return blocks.transpose(1, 0, 2).reshape(BLK, -1)

    ffn_sum = ffn_sum.astype(F32)
    return (
        output,
        grad_in,
        vec_sums[0],
        vec_sums[1],
        side_by_side(attn_sum[:, 0]),
        side_by_side(attn_sum[:, 1]),
        side_by_side(attn_sum[:, 2]),
        own_block(head_sums[0], 8),
        own_block(head_sums[1], 8),
        attn_sum[:, 3].reshape(per_layer * BLK, BLK),
        vec_sums[2],
        vec_sums[3],
        vec_sums[4],
        ffn_sum[:, 0].reshape(8 * BLK, BLK).T,
        own_block(up_sum, 4 * 8),
        ffn_sum[:, 1].reshape(8 * BLK, BLK),
        vec_sums[5],
    )


def solution(mesh):
    square = mesh.shape["wide"] == 8 and mesh.shape["tp"] == 4
    return jax.shard_map(
        square_device if square else per_device,
        mesh=mesh,
        in_specs=(
            P("tp", "wide", None),
            P(),
            P("wide"),
            P("wide"),
            P("wide", "tp"),
            P("wide", "tp"),
            P("wide", "tp"),
            P("tp", "wide"),
            P("tp", "wide"),
            P("tp", "wide"),
            P("wide"),
            P("wide"),
            P("wide"),
            P("wide", "tp"),
            P("tp", "wide"),
            P("tp", "wide"),
            P("wide"),
            P("tp", "wide", None),
        ),
        out_specs=(
            P("tp", "wide", None),
            P("tp", "wide", None),
            P("wide"),
            P("wide"),
            P("wide", "tp"),
            P("wide", "tp"),
            P("wide", "tp"),
            P("tp", "wide"),
            P("tp", "wide"),
            P("tp", "wide"),
            P("wide"),
            P("wide"),
            P("wide"),
            P("wide", "tp"),
            P("tp", "wide"),
            P("tp", "wide"),
            P("wide"),
        ),
        check_vma=False,
    )
```

```python
import functools
import math

import jax
import jax.numpy as jnp
from jax import lax
from jax.experimental import pallas as pl
from jax.experimental.pallas import tpu as pltpu
from jax.sharding import PartitionSpec as P

HEAD = 64
MESH = pl.DeviceIdType.MESH


def norm_rows(values, gain_vec, shift_vec):
    middle = jnp.mean(values, axis=-1, keepdims=True)
    centred = values - middle
    spread = jnp.mean(centred * centred, axis=-1, keepdims=True)
    return centred * lax.rsqrt(spread + 1e-05) * gain_vec + shift_vec


def flatten_rows(tensor):
    return tensor.reshape(-1, tensor.shape[-1])


def row_product(first_op, second_op):
    return jnp.dot(first_op, second_op, preferred_element_type=jnp.float32)


def inner_rows(first_op, second_op):
    return lax.dot_general(
        flatten_rows(first_op),
        flatten_rows(second_op),
        (((0,), (0,)), ((), ())),
        preferred_element_type=jnp.float32,
    )


def times_transposed(first_op, second_op):
    return lax.dot_general(
        first_op,
        second_op,
        (((first_op.ndim - 1,), (1,)), ((), ())),
        preferred_element_type=jnp.float32,
    )


def activate(values):
    return jax.nn.gelu(values, approximate=True)


def masked_scores(query_blk, key_blk, lengths_blk, slopes, distance, causal_mask, key_places):
    raw_scores = (
        jnp.einsum("gihd,gjhd->ghij", query_blk, key_blk, preferred_element_type=jnp.float32)
        * 0.125
    )
    raw_scores = raw_scores - slopes[None, :, None, None] * distance[None, None]
    allowed = causal_mask[None] & (key_places[None, None, :] < lengths_blk[:, None, None])
    return jnp.where(allowed[:, None], raw_scores, -jnp.inf)


def per_device(
    hidden_in,
    lengths,
    pre_gain,
    pre_shift,
    w_query,
    w_key,
    w_value,
    b_query,
    b_value,
    w_dense,
    b_dense,
    mid_gain,
    mid_shift,
    w_up,
    b_up,
    w_down,
    b_down,
    cotangent,
):
    local_slots, block_len, _unused = hidden_in.shape
    heads_dev = b_query.shape[0]
    head_width = heads_dev * HEAD
    slot_total = local_slots * lax.axis_size("tp")
    slot_len = block_len * lax.axis_size("wide")
    wide_at = lax.axis_index("wide")
    tp_at = lax.axis_index("tp")
    vec_part = pre_gain.shape[0]
    (
        gain_one,
        shift_one,
        query_w,
        key_w,
        value_w,
        query_b,
        value_b,
        dense_w,
        dense_b,
        gain_two,
        shift_two,
        up_w,
        up_b,
        down_w,
        down_b,
    ) = (
        lax.all_gather(pre_gain, "wide", axis=0, tiled=True),
        lax.all_gather(pre_shift, "wide", axis=0, tiled=True),
        lax.all_gather(w_query, "wide", axis=0, tiled=True),
        lax.all_gather(w_key, "wide", axis=0, tiled=True),
        lax.all_gather(w_value, "wide", axis=0, tiled=True),
        lax.all_gather(b_query, "wide", axis=1, tiled=True),
        lax.all_gather(b_value, "wide", axis=1, tiled=True),
        lax.all_gather(w_dense, "wide", axis=1, tiled=True),
        lax.all_gather(b_dense, "wide", axis=0, tiled=True),
        lax.all_gather(mid_gain, "wide", axis=0, tiled=True),
        lax.all_gather(mid_shift, "wide", axis=0, tiled=True),
        lax.all_gather(w_up, "wide", axis=0, tiled=True),
        lax.all_gather(b_up, "wide", axis=1, tiled=True),
        lax.all_gather(w_down, "wide", axis=1, tiled=True),
        lax.all_gather(b_down, "wide", axis=0, tiled=True),
    )
    gain_one = gain_one.astype(jnp.float32)
    shift_one = shift_one.astype(jnp.float32)
    gain_two = gain_two.astype(jnp.float32)
    shift_two = shift_two.astype(jnp.float32)
    query_places = wide_at * block_len + jnp.arange(block_len, dtype=jnp.int32)
    key_places = jnp.arange(slot_len, dtype=jnp.int32)
    distance = (query_places[:, None] - key_places[None, :]).astype(jnp.float32)
    causal_mask = key_places[None, :] <= query_places[:, None]
    head_index = tp_at * heads_dev + jnp.arange(heads_dev, dtype=jnp.int32)
    slopes = jnp.exp2(-0.5 * (head_index.astype(jnp.float32) + 1.0))
    own_lengths = lax.dynamic_slice_in_dim(lengths, tp_at * local_slots, local_slots, 0)
    validity = (query_places[None, :] < own_lengths[:, None]).astype(jnp.float32)
    group_size = math.gcd(slot_total, max(1, 512 // block_len))
    group_count = slot_total // group_size
    grouped_lengths = lengths.reshape(group_count, group_size)
    hidden = hidden_in.astype(jnp.float32)

    def query_view(tensor):
        return tensor.reshape(group_count, group_size, block_len, heads_dev, HEAD)

    def pair_view(tensor):
        return tensor.reshape(group_count, group_size, slot_len, 2, heads_dev, HEAD)

    def forward_group(inputs):
        query_blk, pair_blk, lengths_blk = inputs
        masked = masked_scores(
            query_blk, pair_blk[:, :, 0], lengths_blk, slopes, distance, causal_mask, key_places
        )
        highest = jnp.max(masked, axis=-1, keepdims=True)
        totals = highest + jnp.log(jnp.sum(jnp.exp(masked - highest), axis=-1, keepdims=True))
        probabilities = jnp.exp(masked - totals).astype(jnp.bfloat16)
        summed = jnp.einsum(
            "ghij,gjhd->gihd", probabilities, pair_blk[:, :, 1], preferred_element_type=jnp.float32
        )
        return (totals[..., 0], summed)

    def attention_forward(hidden_rows):
        normed_f, norm_back = jax.vjp(norm_rows, hidden_rows, gain_one, shift_one)
        normed = normed_f.astype(jnp.bfloat16)
        normed_all = lax.all_gather(normed, "tp", axis=0, tiled=True)
        queries = (
            row_product(normed_all, query_w) + query_b.reshape(head_width).astype(jnp.float32)
        ).astype(jnp.bfloat16)
        keys_now = row_product(normed_all, key_w).astype(jnp.bfloat16)
        values_now = (
            row_product(normed_all, value_w) + value_b.reshape(head_width).astype(jnp.float32)
        ).astype(jnp.bfloat16)
        pairs = jnp.concatenate([keys_now, values_now], axis=-1)
        pairs_all = lax.all_gather(pairs, "wide", axis=1, tiled=True)
        totals, summed = lax.map(
            forward_group, (query_view(queries), pair_view(pairs_all), grouped_lengths)
        )
        return (
            normed_all,
            queries,
            pairs_all,
            totals,
            summed.reshape(slot_total, block_len, head_width),
            norm_back,
        )

    forward_parts = attention_forward(hidden)
    attention = forward_parts[4].astype(jnp.bfloat16)
    branch = lax.psum_scatter(
        row_product(attention, dense_w).astype(jnp.bfloat16), "tp", scatter_dimension=0, tiled=True
    ).astype(jnp.float32)
    residual = hidden + branch + dense_b.astype(jnp.float32)
    second_f, second_back = jax.vjp(norm_rows, residual, gain_two, shift_two)
    second = second_f.astype(jnp.bfloat16)
    grad_output = validity[:, :, None] * cotangent.astype(jnp.float32)
    grad_down = grad_output.astype(jnp.bfloat16)
    second_all, grad_down_all = (
        lax.all_gather(second, "tp", axis=0, tiled=True),
        lax.all_gather(grad_down, "tp", axis=0, tiled=True),
    )
    pre_act = row_product(second_all, up_w) + up_b.reshape(-1).astype(jnp.float32)
    act_value, act_back = jax.vjp(activate, pre_act)
    activated = act_value.astype(jnp.bfloat16)
    down_out = lax.psum_scatter(
        row_product(activated, down_w).astype(jnp.bfloat16), "tp", scatter_dimension=0, tiled=True
    ).astype(jnp.float32)
    grad_act = times_transposed(grad_down_all, down_w)
    grad_pre = act_back(grad_act)[0].astype(jnp.bfloat16)
    grad_up = inner_rows(second_all, grad_pre)
    grad_up_b = jnp.sum(flatten_rows(grad_pre), axis=0, dtype=jnp.float32).reshape(up_b.shape)
    grad_down_w = inner_rows(activated, grad_down_all)
    grad_second = lax.psum_scatter(
        times_transposed(grad_pre, up_w), "tp", scatter_dimension=0, tiled=True
    )
    output = (validity[:, :, None] * (residual + down_out + down_b.astype(jnp.float32))).astype(
        jnp.bfloat16
    )
    grad_resid_norm, grad_gain_two, grad_shift_two = second_back(grad_second)
    grad_resid = grad_output + grad_resid_norm
    grad_branch = grad_resid.astype(jnp.bfloat16)
    hidden_again, grad_branch = lax.optimization_barrier((hidden, grad_branch))
    forward_parts = attention_forward(hidden_again)
    normed_all, queries, pairs_all, totals, summed, norm_back = forward_parts
    attention_back = summed.astype(jnp.bfloat16)
    branch_all = lax.all_gather(grad_branch, "tp", axis=0, tiled=True)
    grad_dense_w = inner_rows(attention_back, branch_all)
    grad_attention = times_transposed(branch_all, dense_w).astype(jnp.bfloat16)

    def backward_group(inputs):
        query_blk, pair_blk, lengths_blk, totals_blk, grad_blk = inputs
        masked = masked_scores(
            query_blk, pair_blk[:, :, 0], lengths_blk, slopes, distance, causal_mask, key_places
        )
        probabilities = jnp.exp(masked - totals_blk[..., None])
        grad_probs = jnp.einsum(
            "gihd,gjhd->ghij", grad_blk, pair_blk[:, :, 1], preferred_element_type=jnp.float32
        )
        row_delta = jnp.sum(probabilities * grad_probs, axis=-1, keepdims=True)
        grad_scores = (probabilities * (grad_probs - row_delta)).astype(jnp.bfloat16)
        grad_query = (
            jnp.einsum(
                "ghij,gjhd->gihd",
                grad_scores,
                pair_blk[:, :, 0],
                preferred_element_type=jnp.float32,
            )
            * 0.125
        )
        grad_key = (
            jnp.einsum(
                "ghij,gihd->gjhd", grad_scores, query_blk, preferred_element_type=jnp.float32
            )
            * 0.125
        )
        grad_value = jnp.einsum(
            "ghij,gihd->gjhd",
            probabilities.astype(jnp.bfloat16),
            grad_blk,
            preferred_element_type=jnp.float32,
        )
        return (grad_query, jnp.stack([grad_key, grad_value], axis=2))

    grad_query_all, grad_pairs = lax.map(
        backward_group,
        (
            query_view(queries),
            pair_view(pairs_all),
            grouped_lengths,
            totals,
            query_view(grad_attention),
        ),
    )
    grad_pairs_local = lax.psum_scatter(
        grad_pairs.reshape(slot_total, slot_len, 2 * head_width).astype(jnp.bfloat16),
        "wide",
        scatter_dimension=1,
        tiled=True,
    ).astype(jnp.float32)
    grad_queries = grad_query_all.reshape(slot_total, block_len, head_width).astype(jnp.bfloat16)
    grad_keys = grad_pairs_local[:, :, :head_width].astype(jnp.bfloat16)
    grad_values = grad_pairs_local[:, :, head_width:].astype(jnp.bfloat16)
    grad_query_w = inner_rows(normed_all, grad_queries)
    grad_key_w = inner_rows(normed_all, grad_keys)
    grad_value_w = inner_rows(normed_all, grad_values)
    grad_query_b = jnp.sum(flatten_rows(grad_queries), axis=0, dtype=jnp.float32).reshape(
        heads_dev, HEAD
    )
    grad_value_b = jnp.sum(flatten_rows(grad_values), axis=0, dtype=jnp.float32).reshape(
        heads_dev, HEAD
    )
    grad_normed = lax.psum_scatter(
        (
            times_transposed(grad_queries, query_w)
            + times_transposed(grad_keys, key_w)
            + times_transposed(grad_values, value_w)
        ).astype(jnp.bfloat16),
        "tp",
        scatter_dimension=0,
        tiled=True,
    ).astype(jnp.float32)
    grad_hidden_norm, grad_gain_one, grad_shift_one = norm_back(grad_normed)
    grad_in = (grad_resid + grad_hidden_norm).astype(jnp.bfloat16)
    (
        sum_query_w,
        sum_key_w,
        sum_value_w,
        sum_query_b,
        sum_value_b,
        sum_dense_w,
        sum_up_w,
        sum_up_b,
        sum_down_w,
    ) = (
        lax.psum_scatter(
            grad_query_w.astype(jnp.bfloat16), "wide", scatter_dimension=0, tiled=True
        ).astype(jnp.float32),
        lax.psum_scatter(
            grad_key_w.astype(jnp.bfloat16), "wide", scatter_dimension=0, tiled=True
        ).astype(jnp.float32),
        lax.psum_scatter(
            grad_value_w.astype(jnp.bfloat16), "wide", scatter_dimension=0, tiled=True
        ).astype(jnp.float32),
        lax.psum_scatter(
            grad_query_b.astype(jnp.bfloat16), "wide", scatter_dimension=1, tiled=True
        ).astype(jnp.float32),
        lax.psum_scatter(
            grad_value_b.astype(jnp.bfloat16), "wide", scatter_dimension=1, tiled=True
        ).astype(jnp.float32),
        lax.psum_scatter(
            grad_dense_w.astype(jnp.bfloat16), "wide", scatter_dimension=1, tiled=True
        ).astype(jnp.float32),
        lax.psum_scatter(
            grad_up.astype(jnp.bfloat16), "wide", scatter_dimension=0, tiled=True
        ).astype(jnp.float32),
        lax.psum_scatter(
            grad_up_b.astype(jnp.bfloat16), "wide", scatter_dimension=1, tiled=True
        ).astype(jnp.float32),
        lax.psum_scatter(
            grad_down_w.astype(jnp.bfloat16), "wide", scatter_dimension=1, tiled=True
        ).astype(jnp.float32),
    )
    grad_dense_b = jnp.sum(grad_resid, axis=(0, 1))
    grad_down_b = jnp.sum(grad_output, axis=(0, 1))
    sum_gain_one, sum_shift_one, sum_dense_b, sum_gain_two, sum_shift_two, sum_down_b = lax.psum(
        (grad_gain_one, grad_shift_one, grad_dense_b, grad_gain_two, grad_shift_two, grad_down_b),
        ("wide", "tp"),
    )

    def own_part(tensor):
        return lax.dynamic_slice_in_dim(tensor, wide_at * vec_part, vec_part, 0)

    return (
        output,
        grad_in,
        own_part(sum_gain_one),
        own_part(sum_shift_one),
        sum_query_w,
        sum_key_w,
        sum_value_w,
        sum_query_b,
        sum_value_b,
        sum_dense_w,
        own_part(sum_dense_b),
        own_part(sum_gain_two),
        own_part(sum_shift_two),
        sum_up_w,
        sum_up_b,
        sum_down_w,
        own_part(sum_down_b),
    )


BF = jnp.bfloat16
F32 = jnp.float32
LOG2E = 1.4426950408889634
NEG = -1e30
BLK = 128


def hbm():
    return pl.BlockSpec(memory_space=pl.ANY)


def vmem():
    return pl.BlockSpec(memory_space=pltpu.VMEM)


def square_places():
    own = lax.axis_index("wide")
    core = own % 2
    col = (own // 2) % 2
    row = own // 4
    pair = own + 1 - 2 * core
    along_x = own + 2 - 4 * col
    along_y = own + 4 - 8 * row
    return own, pair, along_x, along_y, along_x + along_y - own


def greet(targets):
    barrier = pltpu.get_barrier_semaphore()
    for target in targets:
        pl.semaphore_signal(barrier, inc=1, device_id=target, device_id_type=MESH)
    pl.semaphore_wait(barrier, len(targets))


def remote(src, dst, send_sem, recv_sem, target):
    return pltpu.make_async_remote_copy(
        src_ref=src,
        dst_ref=dst,
        send_sem=send_sem,
        recv_sem=recv_sem,
        device_id=target,
        device_id_type=MESH,
    )


class SquareGather:
    SENDS = 13

    def __init__(self, src, dst, send, recv, local):
        own, pair, ax, ay, dg = square_places()

        def place(slot, dev):
            return dst.at[slot, pl.ds(pl.multiple_of(dev * BLK, BLK), BLK)]

        def both(dev):
            return dst.at[:, pl.ds(pl.multiple_of(dev * BLK, BLK), BLK)]

        to_x, to_y, to_p = {"wide": ax}, {"wide": ay}, {"wide": pair}
        self.local = pltpu.make_async_copy(src, both(own), local)
        copies = {}
        copies["x0"] = remote(src.at[0], place(0, own), send.at[0], recv.at[0], to_x)
        copies["x1"] = remote(src.at[1], place(1, own), send.at[1], recv.at[1], to_x)
        copies["y0"] = remote(src.at[0], place(0, own), send.at[2], recv.at[2], to_y)
        copies["y1"] = remote(src.at[1], place(1, own), send.at[3], recv.at[3], to_y)
        copies["d0"] = remote(place(0, ay), place(0, ay), send.at[4], recv.at[4], to_x)
        copies["d1"] = remote(place(1, ax), place(1, ax), send.at[5], recv.at[5], to_y)
        copies["p"] = remote(src, both(own), send.at[6], recv.at[6], to_p)
        for index, (name, slot, dev) in enumerate(
            (("x0", 0, ax), ("x1", 1, ax), ("y0", 0, ay), ("y1", 1, ay), ("d0", 0, dg), ("d1", 1, dg))
        ):
            copies["p" + name] = remote(
                place(slot, dev), place(slot, dev), send.at[7 + index], recv.at[7 + index], to_p
            )
        self.copies = copies

    def start(self):
        for name in ("y0", "x1", "x0", "y1", "p"):
            self.copies[name].start()
        self.local.start()

    def pass_on(self, arrived, sends):
        self.copies[arrived].wait_recv()
        for name in sends:
            self.copies[name].start()

    def first(self):
        self.pass_on("y0", ("d0", "py0"))
        self.pass_on("x1", ("d1", "px1"))

    def second(self):
        self.pass_on("x0", ("px0",))
        self.pass_on("y1", ("py1",))

    def third(self):
        self.pass_on("d0", ("pd0",))
        self.pass_on("d1", ("pd1",))

    def arrive(self, *names):
        for name in names:
            self.copies[name].wait_recv()

    def sent(self):
        for copy in self.copies.values():
            copy.wait_send()

    def finish(self):
        self.arrive("p", "px0", "px1", "py0", "py1", "pd0", "pd1")
        self.sent()
        self.local.wait()


def wide_square(own_places):
    _own, pair, ax, ay, _dg = own_places
    return [{"wide": pair}, {"wide": ax}, {"wide": ay}]


def add_rows(dst, first, second, third=None):
    step = 16

    def body(index, carry):
        rows = pl.ds(pl.multiple_of(index * step, step), step)
        total = first[rows].astype(F32) + second[rows].astype(F32)
        if third is not None:
            total = total + third[rows].astype(F32)
        dst[rows] = total.astype(dst.dtype)
        return carry

    lax.fori_loop(0, BLK // step, body, 0)


class SquareScatter:
    SENDS = 10

    def __init__(self, src, out, from_pair, summed, from_x, from_y, send, recv):
        own, pair, ax, ay, dg = square_places()
        shift = pair - own
        to_x, to_y, to_p = {"wide": ax}, {"wide": ay}, {"wide": pair}
        self.src, self.out = src, out
        self.from_pair, self.summed, self.from_x, self.from_y = from_pair, summed, from_x, from_y
        self.dests = (dg, ax, ay, own)
        self.pairs = []
        for chip in range(4):
            rows = pl.ds(pl.multiple_of((self.dests[chip] + shift) * BLK, BLK), BLK)
            self.pairs.append(
                remote(src.at[:, rows], from_pair.at[chip], send.at[chip], recv.at[chip], to_p)
            )
        self.dx = remote(summed.at[0, 0], from_x.at[0], send.at[4], recv.at[4], to_x)
        self.dy = remote(summed.at[0, 1], from_y.at[0], send.at[5], recv.at[5], to_y)
        self.xx = remote(summed.at[1, 0], from_x.at[1], send.at[6], recv.at[6], to_x)
        self.yy = remote(summed.at[2, 1], from_y.at[1], send.at[7], recv.at[7], to_y)
        self.ty = remote(summed.at[2, 0], from_y.at[2], send.at[8], recv.at[8], to_y)
        self.tx = remote(summed.at[1, 1], from_x.at[2], send.at[9], recv.at[9], to_x)

    def block(self, slot, chip):
        rows = pl.ds(pl.multiple_of(self.dests[chip] * BLK, BLK), BLK)
        return self.src.at[slot, rows]

    def pair_sum(self, chip, slot, third=None):
        add_rows(
            self.summed.at[chip, slot],
            self.block(slot, chip),
            self.from_pair.at[chip, slot],
            third,
        )

    def near(self, chip):
        self.pairs[chip].wait_recv()
        if chip == 0:
            self.pair_sum(0, 0)
            self.dx.start()
            self.pair_sum(0, 1)
            self.dy.start()
        elif chip == 1:
            self.pair_sum(1, 0)
            self.xx.start()
        elif chip == 2:
            self.pair_sum(2, 1)
            self.yy.start()
        else:
            self.pair_sum(3, 0)
            self.pair_sum(3, 1)

    def middle(self):
        self.dx.wait_recv()
        self.pair_sum(2, 0, self.from_x.at[0])
        self.ty.start()
        self.dy.wait_recv()
        self.pair_sum(1, 1, self.from_y.at[0])
        self.tx.start()

    def start(self):
        for chip in range(4):
            self.pairs[chip].start()

    def first(self):
        for chip in range(3):
            self.near(chip)

    def own_sums(self):
        self.near(3)

    def finish(self):
        self.xx.wait_recv()
        self.ty.wait_recv()
        add_rows(self.out.at[0], self.summed.at[3, 0], self.from_x.at[1], self.from_y.at[2])
        self.yy.wait_recv()
        self.tx.wait_recv()
        add_rows(self.out.at[1], self.summed.at[3, 1], self.from_y.at[1], self.from_x.at[2])
        for copy in self.pairs:
            copy.wait_send()
        for copy in (self.dx, self.dy, self.xx, self.yy, self.ty, self.tx):
            copy.wait_send()


class LineGather:
    def __init__(self, depth, pieces, send, recv):
        self.depth, self.pieces, self.send, self.recv = depth, pieces, send, recv
        self.layer = lax.axis_index("tp")

    def copies(self, step, up):
        index = self.layer - step + 1 if up else self.layer + step - 1
        goal = {"tp": self.layer + 1 if up else self.layer - 1}
        side = 0 if up else 1
        made = []
        for number, (own, buffer) in enumerate(self.pieces):
            source = own if step == 1 else buffer.at[index]
            made.append(
                remote(
                    source,
                    buffer.at[index],
                    self.send.at[side, number, step - 1],
                    self.recv.at[side, number, step - 1],
                    goal,
                )
            )
        return made

    def each(self, step, act):
        layer = self.layer

        @pl.when((layer < self.depth - 1) & (layer - step + 1 >= 0))
        def _():
            for copy in self.copies(step, True):
                act(copy)

        @pl.when((layer > 0) & (layer + step - 1 < self.depth))
        def _():
            for copy in self.copies(step, False):
                act(copy)

    def start(self, step):
        self.each(step, lambda copy: copy.start())

    def sent(self, step):
        self.each(step, lambda copy: copy.wait_send())

    def arrive(self, step):
        layer = self.layer

        @pl.when(layer - step >= 0)
        def _():
            for copy in self.copies(step, True):
                copy.wait_recv()

        @pl.when(layer + step < self.depth)
        def _():
            for copy in self.copies(step, False):
                copy.wait_recv()


def wide_others(own):
    return [{"wide": (own + step) % 8} for step in range(1, 8)]


def first_body(
    depth,
    hidden,
    attn_w,
    ffn_w,
    vec,
    hidden_all,
    attn_all,
    ffn_all,
    vec_all,
    attn_z,
    vec_z,
    send,
    recv,
    local,
    z_send,
    z_recv,
    a_send,
    a_recv,
    f_send,
    f_recv,
    v_send,
    v_recv,
    own_sems,
):
    own, pair, ax, ay, dg = square_places()
    layer = lax.axis_index("tp")
    greet(wide_others(own) + [{"tp": (layer + step) % depth} for step in range(1, depth)])
    gather = SquareGather(hidden, hidden_all, send, recv, local.at[0])
    gather.start()

    line = LineGather(depth, [(attn_w, attn_z), (vec, vec_z)], z_send, z_recv)
    line.start(1)
    own_z = [
        pltpu.make_async_copy(attn_w, attn_z.at[layer], own_sems.at[0]),
        pltpu.make_async_copy(vec, vec_z.at[layer], own_sems.at[1]),
    ]
    for copy in own_z:
        copy.start()
    gather.first()
    ffn_own = pltpu.make_async_copy(ffn_w.at[own], ffn_all.at[:, own], own_sems.at[2])
    ffn_own.start()
    ffn_copies = []
    for step in range(1, 8):
        there = (own + step) % 8
        ffn_copies.append(
            remote(
                ffn_w.at[there],
                ffn_all.at[:, own],
                f_send.at[step - 1],
                f_recv.at[step - 1],
                {"wide": there},
            )
        )
    for copy in ffn_copies:
        copy.start()
    line.arrive(1)
    if depth > 2:
        line.start(2)
    gather.second()
    if depth > 2:
        line.arrive(2)
    if depth > 3:
        line.start(3)
    gather.third()
    if depth > 3:
        line.arrive(3)
    for copy in own_z:
        copy.wait()
    per_layer = 8 // depth
    attn_own = pltpu.make_async_copy(
        attn_z.at[own // per_layer, own % per_layer], attn_all.at[:, own], own_sems.at[3]
    )
    attn_own.start()
    vec_own = pltpu.make_async_copy(vec_z, vec_all.at[own], own_sems.at[4])
    vec_own.start()
    late = []
    for step in range(1, 8):
        there = (own + step) % 8
        late.append(
            remote(vec_z, vec_all.at[own], v_send.at[step - 1], v_recv.at[step - 1], {"wide": there})
        )
        late.append(
            remote(
                attn_z.at[there // per_layer, there % per_layer],
                attn_all.at[:, own],
                a_send.at[step - 1],
                a_recv.at[step - 1],
                {"wide": there},
            )
        )
    for copy in late:
        copy.start()
    gather.finish()
    for copy in ffn_copies + late:
        copy.wait_recv()
    for copy in ffn_copies + late:
        copy.wait_send()
    ffn_own.wait()
    attn_own.wait()
    vec_own.wait()
    for step in range(1, depth):
        line.sent(step)


def first_exchange(depth, hidden, attn_w, ffn_w, vec):
    width = hidden.shape[-1]
    dma = pltpu.SemaphoreType.DMA
    return pl.pallas_call(
        functools.partial(first_body, depth),
        out_shape=[
            jax.ShapeDtypeStruct((2, 8 * BLK, width), BF),
            jax.ShapeDtypeStruct((4, 8, BLK, BLK), BF),
            jax.ShapeDtypeStruct((2, 8, BLK, BLK), BF),
            jax.ShapeDtypeStruct((8, depth) + vec.shape, F32),
        ],
        in_specs=[vmem()] * 4,
        out_specs=[hbm(), hbm(), hbm(), vmem()],
        scratch_shapes=[
            pltpu.VMEM((depth,) + attn_w.shape, BF),
            pltpu.VMEM((depth,) + vec.shape, F32),
            dma((SquareGather.SENDS,)),
            dma((SquareGather.SENDS,)),
            dma((1,)),
            dma((2, 2, depth - 1)),
            dma((2, 2, depth - 1)),
            dma((7,)),
            dma((7,)),
            dma((7,)),
            dma((7,)),
            dma((7,)),
            dma((7,)),
            dma((5,)),
        ],
        compiler_params=pltpu.CompilerParams(collective_id=10, has_side_effects=True),
        name="first_exchange",
    )(hidden, attn_w, ffn_w, vec)


def head_bias(length, slope, rows):
    place = lax.broadcasted_iota(jnp.int32, (rows, QB), 0)
    bias = slope * place.astype(F32)
    return jnp.where(place < length, bias, NEG)


QB = 256


def dot_nt(first, second):
    return lax.dot_general(first, second, (((1,), (1,)), ((), ())), preferred_element_type=F32)


def dot_nn(first, second):
    return lax.dot_general(first, second, (((1,), (0,)), ((), ())), preferred_element_type=F32)


def later_key(size):
    key_place = lax.broadcasted_iota(jnp.int32, (size, size), 0)
    query_place = lax.broadcasted_iota(jnp.int32, (size, size), 1)
    return key_place > query_place


def slot_scores(key, query, bias, step):
    extent = (step + 1) * QB
    scores = dot_nt(key[:extent], query) * (0.125 * LOG2E) + bias[:extent]
    edge = jnp.where(later_key(QB), NEG, scores[extent - QB :])
    return edge if step == 0 else jnp.concatenate([scores[: extent - QB], edge], 0)


def attend_slot(slot, length, slopes, qkv, out, totals, bias):
    rows = qkv.shape[1]
    for head in range(2):
        lanes = pl.ds(head * HEAD, HEAD)
        bias[...] = head_bias(length, slopes[head], rows)
        key = qkv[slot, :, pl.ds(2 * HEAD + head * HEAD, HEAD)]
        value_t = qkv[slot, :, pl.ds(4 * HEAD + head * HEAD, HEAD)].T
        for step in range(rows // QB):
            here = pl.ds(step * QB, QB)
            scores = slot_scores(key, qkv[slot, here, lanes], bias, step)
            highest = jnp.max(scores, axis=0, keepdims=True)
            weights = jnp.exp2(scores - highest)
            total = jnp.sum(weights, axis=0, keepdims=True)
            mixed = dot_nn(value_t[:, : (step + 1) * QB], weights.astype(BF)) / total
            out[slot, here, lanes] = mixed.T.astype(BF)
            totals[slot, pl.ds(head, 1), here] = highest + jnp.log2(total)


def attend_slot_back(
    slot, length, slopes, qkv, attention, grad, totals, out, bias, key_sum, value_sum
):
    rows = qkv.shape[1]
    for head in range(2):
        lanes = pl.ds(head * HEAD, HEAD)
        key_lanes = pl.ds(2 * HEAD + head * HEAD, HEAD)
        value_lanes = pl.ds(4 * HEAD + head * HEAD, HEAD)
        bias[...] = head_bias(length, slopes[head], rows)
        key = qkv[slot, :, key_lanes]
        value = qkv[slot, :, value_lanes]
        key_t = key.T
        key_sum[...] = jnp.zeros_like(key_sum)
        value_sum[...] = jnp.zeros_like(value_sum)
        for step in range(rows // QB):
            here = pl.ds(step * QB, QB)
            extent = (step + 1) * QB
            query = qkv[slot, here, lanes]
            grad_rows = grad[slot, here, lanes]
            product = grad_rows.astype(F32) * attention[slot, here, lanes].astype(F32)
            delta = jnp.sum(product.T, axis=0, keepdims=True)
            scores = slot_scores(key, query, bias, step)
            probs = jnp.exp2(scores - totals[slot, pl.ds(head, 1), here])
            grad_probs = dot_nt(value[:extent], grad_rows)
            grad_scores = (probs * (grad_probs - delta)).astype(BF)
            span = pl.ds(0, extent)
            value_sum[span] += dot_nn(probs.astype(BF), grad_rows)
            key_sum[span] += dot_nn(grad_scores, query)
            grad_query = dot_nn(key_t[:, :extent], grad_scores)
            out[slot, here, lanes] = (grad_query.T * 0.125).astype(BF)
        out[slot, :, key_lanes] = (key_sum[...] * 0.125).astype(BF)
        out[slot, :, value_lanes] = value_sum[...].astype(BF)


def weight_loads(attn_all, qkv_w, dense_w, sems):
    loads = []
    for blk in range(8):
        rows = pl.ds(blk * BLK, BLK)
        for kind in range(3):
            lanes = pl.ds(kind * BLK, BLK)
            loads.append(
                pltpu.make_async_copy(attn_all.at[kind, blk], qkv_w.at[rows, lanes], sems.at[kind, blk])
            )
        loads.append(pltpu.make_async_copy(attn_all.at[3, blk], dense_w.at[:, rows], sems.at[3, blk]))
    return loads


def front_body(
    depth,
    lengths,
    slopes,
    hidden_all,
    attn_all,
    ffn_all,
    vectors,
    qkv_b,
    down_own,
    normed,
    qkv,
    attention,
    totals,
    branch,
    down_all,
    ffn_z,
    share,
    qkv_w,
    dense_w,
    bias,
    from_pair,
    summed,
    from_x,
    from_y,
    s_send,
    s_recv,
    g_send,
    g_recv,
    l_send,
    l_recv,
    local,
    w_sems,
):
    width = hidden_all.shape[-1]
    layer = lax.axis_index("tp")
    loads = weight_loads(attn_all, qkv_w, dense_w, w_sems)
    for load in loads:
        load.start()
    greet(wide_square(square_places()) + line_others(depth))
    gather = SquareGather(down_own, down_all, g_send, g_recv, local.at[0])
    gather.start()
    line = LineGather(depth, [(ffn_all, ffn_z)], l_send, l_recv)
    line.start(1)
    own_z = pltpu.make_async_copy(ffn_all, ffn_z.at[layer], local.at[1])
    own_z.start()
    scatter = SquareScatter(share, branch, from_pair, summed, from_x, from_y, s_send, s_recv)
    for load in loads:
        load.wait()
    step = 32

    def one_slot(slot, carry):
        def block(index, carry):
            def norm_part(part, carry):
                rows = pl.ds(pl.multiple_of(index * QB + part * step, step), step)
                hat, _inverse = norm_stats(hidden_all[slot, rows].astype(F32))
                normed[slot, rows] = (hat * vectors[0:1] + vectors[1:2]).astype(BF)
                return carry

            lax.fori_loop(0, QB // step, norm_part, 0)
            rows = pl.ds(pl.multiple_of(index * QB, QB), QB)
            qkv[slot, rows] = (dot_nn(normed[slot, rows], qkv_w[...]) + qkv_b[...]).astype(BF)
            return carry

        lax.fori_loop(0, 8 * BLK // QB, block, 0)
        attend_slot(slot, lengths[slot], slopes, qkv, attention, totals, bias)

        @pl.when(slot == 0)
        def _():
            gather.first()

        return carry

    lax.fori_loop(0, 2, one_slot, 0)

    def compute(index, carry):
        rows = pl.ds(pl.multiple_of(relation(index) * BLK, BLK), BLK)
        values = attention[:, rows].reshape(2 * BLK, 2 * HEAD)
        share[:, rows] = dot_nn(values, dense_w[...]).astype(BF).reshape(2, BLK, width)
        return carry

    for number, chip in enumerate((0, 1, 2, 3)):
        start = (6, 2, 4, 0)[number]
        lax.fori_loop(start, start + 2, compute, 0)
        scatter.pairs[chip].start()
    gather.second()
    scatter.near(0)
    scatter.near(1)
    scatter.near(2)
    line.arrive(1)
    line.start(2)
    gather.third()
    scatter.near(3)
    line.arrive(2)
    line.start(3)
    scatter.middle()
    gather.finish()
    scatter.finish()
    own_z.wait()
    line.arrive(3)
    for number in range(1, depth):
        line.sent(number)


def line_others(depth):
    layer = lax.axis_index("tp")
    return [{"tp": (layer + step) % depth} for step in range(1, depth)]


def front(depth, lengths, slopes, hidden_all, attn_all, ffn_all, vectors, qkv_b, down_own):
    width = hidden_all.shape[-1]
    dma = pltpu.SemaphoreType.DMA
    smem = pl.BlockSpec(memory_space=pltpu.SMEM)
    tokens = jax.ShapeDtypeStruct((2, 8 * BLK, width), BF)
    return pl.pallas_call(
        functools.partial(front_body, depth),
        out_shape=[
            tokens,
            jax.ShapeDtypeStruct((2, 8 * BLK, 6 * HEAD), BF),
            jax.ShapeDtypeStruct((2, 8 * BLK, 2 * HEAD), BF),
            jax.ShapeDtypeStruct((2, 2, 8 * BLK), F32),
            jax.ShapeDtypeStruct((2, BLK, width), F32),
            tokens,
            jax.ShapeDtypeStruct((depth,) + ffn_all.shape, BF),
        ],
        in_specs=[smem, smem, vmem(), hbm()] + [vmem()] * 4,
        out_specs=[vmem()] * 5 + [hbm()] * 2,
        scratch_shapes=[
            pltpu.VMEM((2, 8 * BLK, width), BF),
            pltpu.VMEM((width, 6 * HEAD), BF),
            pltpu.VMEM((2 * HEAD, width), BF),
            pltpu.VMEM((8 * BLK, QB), F32),
        ]
        + single_scratch(width)
        + [
            dma((SquareGather.SENDS,)),
            dma((SquareGather.SENDS,)),
            dma((2, 1, depth - 1)),
            dma((2, 1, depth - 1)),
            dma((2,)),
            dma((4, 8)),
        ],
        compiler_params=pltpu.CompilerParams(
            collective_id=11, has_side_effects=True, vmem_limit_bytes=VMEM_MAX
        ),
        name="front",
    )(lengths, slopes, hidden_all, attn_all, ffn_all, vectors, qkv_b, down_own)


VMEM_MAX = 62 * 1024 * 1024


def norm_stats(values):
    middle = jnp.mean(values, axis=-1, keepdims=True)
    centred = values - middle
    spread = jnp.mean(centred * centred, axis=-1, keepdims=True)
    inverse = lax.rsqrt(spread + 1e-05)
    return centred * inverse, inverse


def norm_back_rows(grad, hat, inverse, gain):
    scaled = grad * gain
    first = jnp.mean(scaled, axis=-1, keepdims=True)
    second = jnp.mean(scaled * hat, axis=-1, keepdims=True)
    return (scaled - first - hat * second) * inverse


def gelu_parts(values):
    root = math.sqrt(2 / math.pi)
    squared = values * values
    inner = jnp.tanh(root * values * (1.0 + 0.044715 * squared))
    half = 0.5 * (1.0 + inner)
    slope = half + 0.5 * values * (1.0 - inner * inner) * root * (1.0 + 3 * 0.044715 * squared)
    return values * half, slope


def relation(index):
    own = lax.axis_index("wide")
    core = (own + index) % 2
    col = (own // 2 + index // 2) % 2
    row = (own // 4 + index // 4) % 2
    return row * 4 + col * 2 + core


def middle_body(
    depth,
    hidden,
    branch,
    vectors,
    up_b,
    cotangent,
    valid,
    down_all,
    ffn_z,
    branch_all,
    down_share,
    residual,
    grad_resid,
    sums,
    ffn_sum,
    grad_up_b,
    second_all,
    second_share,
    up_w,
    down_w,
    act_t,
    pre_t,
    own_rows,
    grad_second,
    ffn_g,
    ffn_in,
    from_pair,
    summed,
    from_x,
    from_y,
    s_send,
    s_recv,
    g_send,
    g_recv,
    h_send,
    h_recv,
    local,
    w_sems,
    z_send,
    z_recv,
):
    width = hidden.shape[-1]
    layer = lax.axis_index("tp")
    units = depth * BLK
    loads = []
    for up in range(depth):
        lanes = pl.ds(up * BLK, BLK)
        for blk in range(8):
            rows = pl.ds(blk * BLK, BLK)
            loads.append(
                pltpu.make_async_copy(ffn_z.at[up, 0, blk], up_w.at[rows, lanes], w_sems.at[0, up * 8 + blk])
            )
            loads.append(
                pltpu.make_async_copy(ffn_z.at[up, 1, blk], down_w.at[lanes, rows], w_sems.at[1, up * 8 + blk])
            )
    for load in loads:
        load.start()
    greet(wide_square(square_places()) + line_others(depth))
    step = 32

    def norm_part(index, carry):
        rows = pl.ds(pl.multiple_of(index * step, step), step)
        for slot in range(2):
            values = hidden[slot, rows].astype(F32) + branch[slot, rows] + vectors[4:5]
            residual[slot, rows] = values
            hat, _inverse = norm_stats(values)
            own_rows[slot, rows] = (hat * vectors[2:3] + vectors[3:4]).astype(BF)
        return carry

    lax.fori_loop(0, BLK // step, norm_part, 0)
    gather = SquareGather(own_rows, second_all, g_send, g_recv, local.at[0])
    gather.start()
    scatter = SquareScatter(
        second_share, grad_second, from_pair, summed, from_x, from_y, s_send, s_recv
    )
    for load in loads:
        load.wait()

    def compute(index, carry):
        source = relation(index)
        rows = pl.ds(pl.multiple_of(source * BLK, BLK), BLK)
        values = second_all[:, rows].reshape(2 * BLK, width)
        pre_act = dot_nn(values, up_w[...]) + up_b[...]
        act_value, act_slope = gelu_parts(pre_act)
        activated = act_value.astype(BF)
        grad_rows = down_all[:, rows].reshape(2 * BLK, width)
        grad_pre = (dot_nt(grad_rows, down_w[...]) * act_slope).astype(BF)
        down_share[:, rows] = dot_nn(activated, down_w[...]).astype(BF).reshape(2, BLK, width)
        second_share[:, rows] = dot_nt(grad_pre, up_w[...]).astype(BF).reshape(2, BLK, width)
        grad_up_b[...] += jnp.sum(grad_pre.astype(F32), axis=0, keepdims=True)
        for slot in range(2):
            lanes = pl.ds(pl.multiple_of(slot * 8 * BLK + source * BLK, BLK), BLK)
            part = slice(slot * BLK, (slot + 1) * BLK)
            act_t[:, lanes] = activated[part].T
            pre_t[:, lanes] = grad_pre[part].T
        return carry

    grad_up_b[...] = jnp.zeros_like(grad_up_b)
    gather.arrive("p")
    gather.local.wait()
    lax.fori_loop(0, 2, compute, 0)
    scatter.pairs[3].start()
    gather.first()
    gather.second()
    gather.arrive("px0", "px1", "py0", "py1")
    lax.fori_loop(2, 4, compute, 0)
    scatter.pairs[1].start()
    scatter.near(3)
    lax.fori_loop(4, 6, compute, 0)
    scatter.pairs[2].start()
    gather.third()
    scatter.near(1)
    gather.arrive("pd0", "pd1")
    lax.fori_loop(6, 8, compute, 0)
    scatter.pairs[0].start()
    scatter.near(2)
    scatter.near(0)

    def weight_grads(left, right, kind):
        def one(up, carry):
            rows = pl.ds(pl.multiple_of(up * BLK, BLK), BLK)
            total = dot_nn(left[rows, pl.ds(0, 8 * BLK)], right[0])
            total = total + dot_nn(left[rows, pl.ds(8 * BLK, 8 * BLK)], right[1])
            total = total.astype(BF)
            for blk in range(8):
                ffn_g[kind, up, blk] = total[:, blk * BLK : (blk + 1) * BLK]
            return carry

        lax.fori_loop(0, depth, one, 0)

    def line_copies(kind):
        made = []
        for up in range(1, depth):
            goal = (layer + up) % depth
            made.append(
                remote(
                    ffn_g.at[kind, goal],
                    ffn_in.at[kind, up - 1],
                    z_send.at[kind, up - 1],
                    z_recv.at[kind, up - 1],
                    {"tp": goal},
                )
            )
        return made

    weight_grads(pre_t, second_all, 0)
    for copy in line_copies(0):
        copy.start()
    scatter.middle()
    weight_grads(act_t, down_all, 1)
    for copy in line_copies(1):
        copy.start()
    scatter.finish()
    gather.sent()

    sums[...] = jnp.zeros_like(sums)

    def back_part(index, carry):
        rows = pl.ds(pl.multiple_of(index * step, step), step)
        for slot in range(2):
            hat, inverse = norm_stats(residual[slot, rows])
            grad = grad_second[slot, rows]
            mask = valid[slot, rows][:, :1]
            grad_out = mask * cotangent[slot, rows].astype(F32)
            total = grad_out + norm_back_rows(grad, hat, inverse, vectors[2:3])
            grad_resid[slot, rows] = total
            own_rows[slot, rows] = total.astype(BF)
            for place, value in enumerate((total, grad * hat, grad, grad_out)):
                sums[pl.ds(place, 1)] += jnp.sum(value, axis=0, keepdims=True)
        return carry

    lax.fori_loop(0, BLK // step, back_part, 0)
    again = SquareGather(own_rows, branch_all, h_send, h_recv, local.at[1])
    again.start()
    again.first()
    again.second()
    again.third()
    for kind in range(2):
        for copy in line_copies(kind):
            copy.wait_recv()

        def add_block(blk, carry, kind=kind):
            total = ffn_g[kind, layer, blk].astype(F32)
            for up in range(depth - 1):
                total = total + ffn_in[kind, up, blk].astype(F32)
            ffn_sum[blk, kind] = total.astype(BF)
            return carry

        lax.fori_loop(0, 8, add_block, 0)
        for copy in line_copies(kind):
            copy.wait_send()
    again.finish()


def middle(depth, hidden, branch, vectors, up_b, cotangent, valid, down_all, ffn_z):
    width = hidden.shape[-1]
    units = depth * BLK
    dma = pltpu.SemaphoreType.DMA
    tokens = jax.ShapeDtypeStruct((2, 8 * BLK, width), BF)
    rows = jax.ShapeDtypeStruct((2, BLK, width), F32)
    return pl.pallas_call(
        functools.partial(middle_body, depth),
        out_shape=[
            tokens,
            tokens,
            rows,
            rows,
            jax.ShapeDtypeStruct((8, width), F32),
            jax.ShapeDtypeStruct((8, 2, BLK, BLK), BF),
            jax.ShapeDtypeStruct((1, units), F32),
        ],
        in_specs=[vmem()] * 7 + [hbm()],
        out_specs=[hbm()] + [vmem()] * 6,
        scratch_shapes=[
            pltpu.VMEM((2, 8 * BLK, width), BF),
            pltpu.VMEM((2, 8 * BLK, width), BF),
            pltpu.VMEM((width, units), BF),
            pltpu.VMEM((units, width), BF),
            pltpu.VMEM((units, 16 * BLK), BF),
            pltpu.VMEM((units, 16 * BLK), BF),
            pltpu.VMEM((2, BLK, width), BF),
            pltpu.VMEM((2, BLK, width), F32),
            pltpu.VMEM((2, depth, 8, BLK, BLK), BF),
            pltpu.VMEM((2, depth - 1, 8, BLK, BLK), BF),
        ]
        + single_scratch(width)
        + [
            dma((SquareGather.SENDS,)),
            dma((SquareGather.SENDS,)),
            dma((SquareGather.SENDS,)),
            dma((SquareGather.SENDS,)),
            dma((2,)),
            dma((2, 8 * depth)),
            dma((2, depth - 1)),
            dma((2, depth - 1)),
        ],
        compiler_params=pltpu.CompilerParams(
            collective_id=13, has_side_effects=True, vmem_limit_bytes=VMEM_MAX
        ),
        name="middle",
    )(hidden, branch, vectors, up_b, cotangent, valid, down_all, ffn_z)


def single_scratch(width):
    return [
        pltpu.VMEM((4, 2, BLK, width), BF),
        pltpu.VMEM((4, 2, BLK, width), BF),
        pltpu.VMEM((3, BLK, width), BF),
        pltpu.VMEM((3, BLK, width), BF),
        pltpu.SemaphoreType.DMA((SquareScatter.SENDS,)),
        pltpu.SemaphoreType.DMA((SquareScatter.SENDS,)),
    ]


class WideExchange:
    def __init__(self, source, target, send, recv):
        own = lax.axis_index("wide")
        self.copies = [
            remote(
                source((own + step) % 8),
                target(own),
                send.at[step - 1],
                recv.at[step - 1],
                {"wide": (own + step) % 8},
            )
            for step in range(1, 8)
        ]

    def start(self):
        for copy in self.copies:
            copy.start()

    def arrive(self):
        for copy in self.copies:
            copy.wait_recv()

    def sent(self):
        for copy in self.copies:
            copy.wait_send()


def back_body(
    depth,
    lengths,
    slopes,
    hidden,
    residual,
    grad_resid,
    valid,
    vectors,
    branch_all,
    attn_all,
    qkv,
    attention,
    totals,
    normed,
    down_share,
    mid_sums,
    grad_up_b,
    ffn_sum,
    output,
    grad_in,
    vec_sums,
    unit_sums,
    grad_q,
    grad_k,
    grad_v,
    grad_d,
    grad_up,
    grad_down,
    grad_att,
    grad_qkv,
    share,
    qkv_w,
    dense_w,
    bias,
    key_sum,
    value_sum,
    down_out,
    grad_normed,
    attn_g,
    attn_in,
    attn_z,
    ffn_in,
    parts,
    gathered,
    d_pair,
    d_summed,
    d_x,
    d_y,
    d_send,
    d_recv,
    n_pair,
    n_summed,
    n_x,
    n_y,
    n_send,
    n_recv,
    w_sems,
    f_send,
    f_recv,
    a_send,
    a_recv,
    z_send,
    z_recv,
    v_send,
    v_recv,
):
    own = lax.axis_index("wide")
    layer = lax.axis_index("tp")
    per_layer = 8 // depth
    width = hidden.shape[-1]
    step = 32
    others = [
        ((own + side) % 8, (layer + up) % depth)
        for up in range(depth)
        for side in range(8)
        if up or side
    ]
    loads = weight_loads(attn_all, qkv_w, dense_w, w_sems)
    for load in loads:
        load.start()
    greet([{"wide": wide, "tp": tp} for wide, tp in others])
    down = SquareScatter(down_share, down_out, d_pair, d_summed, d_x, d_y, d_send, d_recv)
    down.start()
    ffn = WideExchange(lambda dev: ffn_sum.at[dev], lambda dev: ffn_in.at[dev], f_send, f_recv)
    ffn.start()
    for load in loads:
        load.wait()

    def att_block(index, carry):
        slot = index // 4
        rows = pl.ds(pl.multiple_of((index % 4) * QB, QB), QB)
        grad_att[slot, rows] = dot_nt(branch_all[slot, rows], dense_w[...]).astype(BF)
        return carry

    lax.fori_loop(0, 8, att_block, 0)
    for chip in range(3):
        down.near(chip)
    dense_part = dot_nn(attention[0].T, branch_all[0]) + dot_nn(attention[1].T, branch_all[1])
    dense_part = dense_part.astype(BF)
    for blk in range(8):
        attn_g[blk, 3] = dense_part[:, blk * BLK : (blk + 1) * BLK]
    kinds = (pl.ds(3, 1), pl.ds(0, 3))
    exchanges = [
        WideExchange(
            lambda dev, kind=kind: attn_g.at[dev, kind],
            lambda dev, kind=kind: attn_in.at[dev, kind],
            a_send.at[group],
            a_recv.at[group],
        )
        for group, kind in enumerate(kinds)
    ]

    def onward(group, index, source):
        return remote(
            source.at[index, kinds[group]],
            attn_z.at[layer, index % per_layer, kinds[group]],
            z_send.at[group, index],
            z_recv.at[group, layer, index % per_layer],
            {"tp": index // per_layer},
        )

    def forward(group, index, source):
        @pl.when(index // per_layer != layer)
        def _():
            onward(group, index, source).start()

    def forward_all(group):
        for number in range(1, 8):
            exchanges[group].copies[number - 1].wait_recv()
            forward(group, (own + 8 - number) % 8, attn_in)

    exchanges[0].start()
    forward(0, own, attn_g)

    def slot_back(slot, carry):
        attend_slot_back(
            slot,
            lengths[slot],
            slopes,
            qkv,
            attention,
            grad_att,
            totals,
            grad_qkv,
            bias,
            key_sum,
            value_sum,
        )

        @pl.when(slot == 0)
        def _():
            forward_all(0)
            down.middle()

        return carry

    lax.fori_loop(0, 2, slot_back, 0)

    weight_part = dot_nn(grad_qkv[0].T, normed[0]) + dot_nn(grad_qkv[1].T, normed[1])
    weight_part = weight_part.astype(BF)
    for kind in range(3):
        for blk in range(8):
            attn_g[blk, kind] = weight_part[
                kind * BLK : (kind + 1) * BLK, blk * BLK : (blk + 1) * BLK
            ]
    exchanges[1].start()
    forward(1, own, attn_g)
    scatter = SquareScatter(share, grad_normed, n_pair, n_summed, n_x, n_y, n_send, n_recv)

    def compute(index, carry):
        rows = pl.ds(pl.multiple_of(relation(index) * BLK, BLK), BLK)
        values = grad_qkv[:, rows].reshape(2 * BLK, 6 * HEAD)
        share[:, rows] = dot_nt(values, qkv_w[...]).astype(BF).reshape(2, BLK, width)
        return carry

    for chip in range(4):
        start = (6, 2, 4, 0)[chip]
        lax.fori_loop(start, start + 2, compute, 0)
        scatter.pairs[chip].start()
        if chip:
            scatter.near(chip - 1)
    head_sum = jnp.sum(grad_qkv[0].astype(F32), axis=0, keepdims=True)
    head_sum = head_sum + jnp.sum(grad_qkv[1].astype(F32), axis=0, keepdims=True)
    down.near(3)
    down.finish()

    def out_part(index, carry):
        rows = pl.ds(pl.multiple_of(index * step, step), step)
        for slot in range(2):
            total = residual[slot, rows] + down_out[slot, rows] + vectors[5:6]
            output[slot, rows] = (valid[slot, rows][:, :1] * total).astype(BF)
        return carry

    lax.fori_loop(0, BLK // step, out_part, 0)
    forward_all(1)
    scatter.near(3)
    ffn.arrive()
    ffn_in[own] = ffn_sum[own]
    for blk in range(8):
        lanes = slice(blk * BLK, (blk + 1) * BLK)
        grad_up[:, lanes] = ffn_in[blk, 0].astype(F32).T
        grad_down[lanes] = ffn_in[blk, 1].astype(F32)
    scatter.middle()
    for blk in range(8):
        lanes = slice(blk * BLK, (blk + 1) * BLK)
        for place in range(4):
            parts[blk, pl.ds(2 + place, 1)] = mid_sums[place : place + 1, lanes]
        for place in range(depth):
            parts[blk, pl.ds(6 + place, 1)] = grad_up_b[:, place * BLK : (place + 1) * BLK]
        parts[blk, pl.ds(6 + depth, 1)] = head_sum[:, : 2 * HEAD]
        parts[blk, pl.ds(7 + depth, 1)] = head_sum[:, 4 * HEAD :]
    scatter.finish()

    def back_part(index, carry):
        gain_sum, shift_sum = carry
        rows = pl.ds(pl.multiple_of(index * step, step), step)
        for slot in range(2):
            hat, inverse = norm_stats(hidden[slot, rows].astype(F32))
            grad = grad_normed[slot, rows]
            total = grad_resid[slot, rows] + norm_back_rows(grad, hat, inverse, vectors[0:1])
            grad_in[slot, rows] = total.astype(BF)
            gain_sum = gain_sum + jnp.sum(grad * hat, axis=0, keepdims=True)
            shift_sum = shift_sum + jnp.sum(grad, axis=0, keepdims=True)
        return gain_sum, shift_sum

    zero = jnp.zeros((1, width), F32)
    gain_sum, shift_sum = lax.fori_loop(0, BLK // step, back_part, (zero, zero))
    for blk in range(8):
        lanes = slice(blk * BLK, (blk + 1) * BLK)
        parts[blk, pl.ds(0, 1)] = gain_sum[:, lanes]
        parts[blk, pl.ds(1, 1)] = shift_sum[:, lanes]
    sum_copies = [
        remote(
            parts.at[wide],
            gathered.at[own, layer],
            v_send.at[index],
            v_recv.at[index],
            {"wide": wide, "tp": tp},
        )
        for index, (wide, tp) in enumerate(others)
    ]
    for copy in sum_copies:
        copy.start()
    gathered[own, layer] = parts[own]

    for group in range(2):
        for up in range(1, depth):
            source = (layer + up) % depth
            for piece in range(per_layer):
                remote(
                    attn_in.at[piece, kinds[group]],
                    attn_z.at[source, piece, kinds[group]],
                    z_send.at[group, piece],
                    z_recv.at[group, source, piece],
                    {"tp": source},
                ).wait_recv()
    attn_in[own] = attn_g[own]
    for piece in range(per_layer):
        for kind, target in enumerate((grad_q, grad_k, grad_v, grad_d)):
            total = attn_in[layer * per_layer + piece, kind].astype(F32)
            for up in range(1, depth):
                total = total + attn_z[(layer + up) % depth, piece, kind].astype(F32)
            lanes = slice(piece * BLK, (piece + 1) * BLK)
            if kind < 3:
                target[:, lanes] = total.T
            else:
                target[lanes] = total
    for copy in sum_copies:
        copy.wait_recv()

    def unit_part(dev, carry):
        total = gathered[dev, 0]
        for up in range(1, depth):
            total = total + gathered[dev, up]
        unit_sums[dev] = total
        return carry + total

    vec_sums[...] = lax.fori_loop(0, 8, unit_part, jnp.zeros((16, BLK), F32))
    for copy in sum_copies:
        copy.wait_send()
    ffn.sent()
    for group in range(2):
        exchanges[group].sent()
        for index in range(8):

            @pl.when(index // per_layer != layer)
            def _(index=index, group=group):
                onward(group, index, attn_in).wait_send()


def back(depth, *operands):
    width = operands[2].shape[-1]
    dma = pltpu.SemaphoreType.DMA
    smem = pl.BlockSpec(memory_space=pltpu.SMEM)
    per_layer = 8 // depth
    rows = jax.ShapeDtypeStruct((2, BLK, width), BF)
    square = jax.ShapeDtypeStruct((BLK, per_layer * BLK), F32)
    peers = 8 * depth - 1
    return pl.pallas_call(
        functools.partial(back_body, depth),
        out_shape=[
            rows,
            rows,
            jax.ShapeDtypeStruct((16, BLK), F32),
            jax.ShapeDtypeStruct((8, 16, BLK), F32),
            square,
            square,
            square,
            jax.ShapeDtypeStruct((per_layer * BLK, BLK), F32),
            jax.ShapeDtypeStruct((BLK, 8 * BLK), F32),
            jax.ShapeDtypeStruct((8 * BLK, BLK), F32),
        ],
        in_specs=[smem, smem] + [vmem()] * 6 + [hbm()] + [vmem()] * 8,
        out_specs=[vmem()] * 10,
        scratch_shapes=[
            pltpu.VMEM((2, 8 * BLK, 2 * HEAD), BF),
            pltpu.VMEM((2, 8 * BLK, 6 * HEAD), BF),
            pltpu.VMEM((2, 8 * BLK, width), BF),
            pltpu.VMEM((width, 6 * HEAD), BF),
            pltpu.VMEM((2 * HEAD, width), BF),
            pltpu.VMEM((8 * BLK, QB), F32),
            pltpu.VMEM((8 * BLK, HEAD), F32),
            pltpu.VMEM((8 * BLK, HEAD), F32),
            pltpu.VMEM((2, BLK, width), F32),
            pltpu.VMEM((2, BLK, width), F32),
            pltpu.VMEM((8, 4, BLK, BLK), BF),
            pltpu.VMEM((8, 4, BLK, BLK), BF),
            pltpu.VMEM((depth, per_layer, 4, BLK, BLK), BF),
            pltpu.VMEM((8, 2, BLK, BLK), BF),
            pltpu.VMEM((8, 16, BLK), F32),
            pltpu.VMEM((8, depth, 16, BLK), F32),
        ]
        + single_scratch(width)
        + single_scratch(width)
        + [
            dma((4, 8)),
            dma((7,)),
            dma((7,)),
            dma((2, 7)),
            dma((2, 7)),
            dma((2, 8)),
            dma((2, depth, per_layer)),
            dma((peers,)),
            dma((peers,)),
        ],
        compiler_params=pltpu.CompilerParams(
            collective_id=12, has_side_effects=True, vmem_limit_bytes=VMEM_MAX
        ),
        name="back",
    )(*operands)


def square_device(
    hidden_in,
    lengths,
    pre_gain,
    pre_shift,
    w_query,
    w_key,
    w_value,
    b_query,
    b_value,
    w_dense,
    b_dense,
    mid_gain,
    mid_shift,
    w_up,
    b_up,
    w_down,
    b_down,
    cotangent,
):
    depth = lax.axis_size("tp")
    own = lax.axis_index("wide")
    layer = lax.axis_index("tp")
    width = hidden_in.shape[-1]
    rows = 8 * BLK
    per_layer = 8 // depth
    heads_dev = b_query.shape[0]
    own_lengths = lax.dynamic_slice_in_dim(lengths, layer * 2, 2, 0)
    head_index = 2 * own + jnp.arange(2, dtype=jnp.int32)
    slopes = jnp.exp2(-0.5 * (head_index.astype(F32) + 1.0)) * LOG2E

    def halves(weight):
        return weight.reshape(BLK, per_layer, BLK).transpose(1, 0, 2)

    attn_w = jnp.stack(
        [halves(w_query), halves(w_key), halves(w_value), w_dense.reshape(per_layer, BLK, BLK)], 1
    )
    ffn_w = jnp.stack(
        [w_up.reshape(BLK, 8, BLK).transpose(1, 0, 2), w_down.reshape(8, BLK, BLK)], 1
    )
    head_row = jnp.concatenate(
        [b_query.reshape(-1), b_value.reshape(-1), jnp.zeros((BLK - 16 * heads_dev,), BF)]
    )
    vec = jnp.stack(
        [pre_gain, pre_shift, mid_gain, mid_shift, b_dense, b_down, b_up.reshape(-1), head_row]
    ).astype(F32)
    hidden_all, attn_all, ffn_all, vec_all = first_exchange(depth, hidden_in, attn_w, ffn_w, vec)
    vectors = vec_all[:, 0].transpose(1, 0, 2).reshape(8, width)
    up_b = vec_all[:, :, 6].reshape(8, depth, heads_dev, 4 * 8).transpose(1, 2, 0, 3)
    up_b = lax.dynamic_index_in_dim(up_b.reshape(depth, 8, BLK), own, 1, False).reshape(-1)
    span = heads_dev * 8

    def head_vector(index):
        full = vec_all[:, :, 7, index * span : (index + 1) * span]
        full = full.reshape(8, depth, heads_dev, 8).transpose(1, 2, 0, 3).reshape(8, 2 * HEAD)
        return lax.dynamic_index_in_dim(full, own, 0, False)

    qkv_b = jnp.concatenate([head_vector(0), jnp.zeros((2 * HEAD,), F32), head_vector(1)])
    places = own * BLK + jnp.arange(BLK, dtype=jnp.int32)
    validity = (places[None, :] < own_lengths[:, None]).astype(F32)[:, :, None]
    down_own = (validity * cotangent.astype(F32)).astype(BF)
    valid = jnp.broadcast_to(validity, (2, BLK, BLK))
    normed, qkv, attention, totals, branch, down_all, ffn_z = front(
        depth,
        own_lengths,
        slopes,
        hidden_all,
        attn_all,
        ffn_all,
        vectors,
        qkv_b.reshape(1, -1),
        down_own,
    )
    branch_all, down_share, residual, grad_resid, mid_sums, ffn_sum, grad_up_b = middle(
        depth,
        hidden_in,
        branch,
        vectors,
        up_b.reshape(1, -1),
        cotangent,
        valid,
        down_all,
        ffn_z,
    )
    (
        output,
        grad_in,
        vec_sums,
        unit_sums,
        grad_q,
        grad_k,
        grad_v,
        grad_d,
        grad_up,
        grad_down,
    ) = back(
        depth,
        own_lengths,
        slopes,
        hidden_in,
        residual,
        grad_resid,
        valid,
        vectors,
        branch_all,
        attn_all,
        qkv,
        attention,
        totals,
        normed,
        down_share,
        mid_sums,
        grad_up_b,
        ffn_sum,
    )
    up_sum = unit_sums[:, 6 : 6 + depth].transpose(1, 0, 2).reshape(16, 2 * depth * HEAD // 2)
    head_sums = unit_sums[:, 6 + depth : 8 + depth].transpose(1, 0, 2).reshape(2, 16, HEAD)

    def own_block(tensor, size):
        return lax.dynamic_slice(tensor, (layer * heads_dev, own * size), (heads_dev, size))

    return (
        output,
        grad_in,
        vec_sums[0],
        vec_sums[1],
        grad_q,
        grad_k,
        grad_v,
        own_block(head_sums[0], 8),
        own_block(head_sums[1], 8),
        grad_d,
        vec_sums[2],
        vec_sums[3],
        vec_sums[4],
        grad_up,
        own_block(up_sum, 4 * 8),
        grad_down,
        vec_sums[5],
    )


def solution(mesh):
    square = mesh.shape["wide"] == 8 and mesh.shape["tp"] == 4
    return jax.shard_map(
        square_device if square else per_device,
        mesh=mesh,
        in_specs=(
            P("tp", "wide", None),
            P(),
            P("wide"),
            P("wide"),
            P("wide", "tp"),
            P("wide", "tp"),
            P("wide", "tp"),
            P("tp", "wide"),
            P("tp", "wide"),
            P("tp", "wide"),
            P("wide"),
            P("wide"),
            P("wide"),
            P("wide", "tp"),
            P("tp", "wide"),
            P("tp", "wide"),
            P("wide"),
            P("tp", "wide", None),
        ),
        out_specs=(
            P("tp", "wide", None),
            P("tp", "wide", None),
            P("wide"),
            P("wide"),
            P("wide", "tp"),
            P("wide", "tp"),
            P("wide", "tp"),
            P("tp", "wide"),
            P("tp", "wide"),
            P("tp", "wide"),
            P("wide"),
            P("wide"),
            P("wide"),
            P("wide", "tp"),
            P("tp", "wide"),
            P("tp", "wide"),
            P("wide"),
        ),
        check_vma=False,
    )
```

```python
import functools
import math

import jax
import jax.numpy as jnp
from jax import lax
from jax.experimental import pallas as pl
from jax.experimental.pallas import tpu as pltpu
from jax.sharding import PartitionSpec as P

HEAD = 64
MESH = pl.DeviceIdType.MESH


def norm_rows(values, gain_vec, shift_vec):
    middle = jnp.mean(values, axis=-1, keepdims=True)
    centred = values - middle
    spread = jnp.mean(centred * centred, axis=-1, keepdims=True)
    return centred * lax.rsqrt(spread + 1e-05) * gain_vec + shift_vec


def flatten_rows(tensor):
    return tensor.reshape(-1, tensor.shape[-1])


def row_product(first_op, second_op):
    return jnp.dot(first_op, second_op, preferred_element_type=jnp.float32)


def inner_rows(first_op, second_op):
    return lax.dot_general(
        flatten_rows(first_op),
        flatten_rows(second_op),
        (((0,), (0,)), ((), ())),
        preferred_element_type=jnp.float32,
    )


def times_transposed(first_op, second_op):
    return lax.dot_general(
        first_op,
        second_op,
        (((first_op.ndim - 1,), (1,)), ((), ())),
        preferred_element_type=jnp.float32,
    )


def activate(values):
    return jax.nn.gelu(values, approximate=True)


def masked_scores(query_blk, key_blk, lengths_blk, slopes, distance, causal_mask, key_places):
    raw_scores = (
        jnp.einsum("gihd,gjhd->ghij", query_blk, key_blk, preferred_element_type=jnp.float32)
        * 0.125
    )
    raw_scores = raw_scores - slopes[None, :, None, None] * distance[None, None]
    allowed = causal_mask[None] & (key_places[None, None, :] < lengths_blk[:, None, None])
    return jnp.where(allowed[:, None], raw_scores, -jnp.inf)


def per_device(
    hidden_in,
    lengths,
    pre_gain,
    pre_shift,
    w_query,
    w_key,
    w_value,
    b_query,
    b_value,
    w_dense,
    b_dense,
    mid_gain,
    mid_shift,
    w_up,
    b_up,
    w_down,
    b_down,
    cotangent,
):
    local_slots, block_len, _unused = hidden_in.shape
    heads_dev = b_query.shape[0]
    head_width = heads_dev * HEAD
    slot_total = local_slots * lax.axis_size("tp")
    slot_len = block_len * lax.axis_size("wide")
    wide_at = lax.axis_index("wide")
    tp_at = lax.axis_index("tp")
    vec_part = pre_gain.shape[0]
    (
        gain_one,
        shift_one,
        query_w,
        key_w,
        value_w,
        query_b,
        value_b,
        dense_w,
        dense_b,
        gain_two,
        shift_two,
        up_w,
        up_b,
        down_w,
        down_b,
    ) = (
        lax.all_gather(pre_gain, "wide", axis=0, tiled=True),
        lax.all_gather(pre_shift, "wide", axis=0, tiled=True),
        lax.all_gather(w_query, "wide", axis=0, tiled=True),
        lax.all_gather(w_key, "wide", axis=0, tiled=True),
        lax.all_gather(w_value, "wide", axis=0, tiled=True),
        lax.all_gather(b_query, "wide", axis=1, tiled=True),
        lax.all_gather(b_value, "wide", axis=1, tiled=True),
        lax.all_gather(w_dense, "wide", axis=1, tiled=True),
        lax.all_gather(b_dense, "wide", axis=0, tiled=True),
        lax.all_gather(mid_gain, "wide", axis=0, tiled=True),
        lax.all_gather(mid_shift, "wide", axis=0, tiled=True),
        lax.all_gather(w_up, "wide", axis=0, tiled=True),
        lax.all_gather(b_up, "wide", axis=1, tiled=True),
        lax.all_gather(w_down, "wide", axis=1, tiled=True),
        lax.all_gather(b_down, "wide", axis=0, tiled=True),
    )
    gain_one = gain_one.astype(jnp.float32)
    shift_one = shift_one.astype(jnp.float32)
    gain_two = gain_two.astype(jnp.float32)
    shift_two = shift_two.astype(jnp.float32)
    query_places = wide_at * block_len + jnp.arange(block_len, dtype=jnp.int32)
    key_places = jnp.arange(slot_len, dtype=jnp.int32)
    distance = (query_places[:, None] - key_places[None, :]).astype(jnp.float32)
    causal_mask = key_places[None, :] <= query_places[:, None]
    head_index = tp_at * heads_dev + jnp.arange(heads_dev, dtype=jnp.int32)
    slopes = jnp.exp2(-0.5 * (head_index.astype(jnp.float32) + 1.0))
    own_lengths = lax.dynamic_slice_in_dim(lengths, tp_at * local_slots, local_slots, 0)
    validity = (query_places[None, :] < own_lengths[:, None]).astype(jnp.float32)
    group_size = math.gcd(slot_total, max(1, 512 // block_len))
    group_count = slot_total // group_size
    grouped_lengths = lengths.reshape(group_count, group_size)
    hidden = hidden_in.astype(jnp.float32)

    def query_view(tensor):
        return tensor.reshape(group_count, group_size, block_len, heads_dev, HEAD)

    def pair_view(tensor):
        return tensor.reshape(group_count, group_size, slot_len, 2, heads_dev, HEAD)

    def forward_group(inputs):
        query_blk, pair_blk, lengths_blk = inputs
        masked = masked_scores(
            query_blk, pair_blk[:, :, 0], lengths_blk, slopes, distance, causal_mask, key_places
        )
        highest = jnp.max(masked, axis=-1, keepdims=True)
        totals = highest + jnp.log(jnp.sum(jnp.exp(masked - highest), axis=-1, keepdims=True))
        probabilities = jnp.exp(masked - totals).astype(jnp.bfloat16)
        summed = jnp.einsum(
            "ghij,gjhd->gihd", probabilities, pair_blk[:, :, 1], preferred_element_type=jnp.float32
        )
        return (totals[..., 0], summed)

    def attention_forward(hidden_rows):
        normed_f, norm_back = jax.vjp(norm_rows, hidden_rows, gain_one, shift_one)
        normed = normed_f.astype(jnp.bfloat16)
        normed_all = lax.all_gather(normed, "tp", axis=0, tiled=True)
        queries = (
            row_product(normed_all, query_w) + query_b.reshape(head_width).astype(jnp.float32)
        ).astype(jnp.bfloat16)
        keys_now = row_product(normed_all, key_w).astype(jnp.bfloat16)
        values_now = (
            row_product(normed_all, value_w) + value_b.reshape(head_width).astype(jnp.float32)
        ).astype(jnp.bfloat16)
        pairs = jnp.concatenate([keys_now, values_now], axis=-1)
        pairs_all = lax.all_gather(pairs, "wide", axis=1, tiled=True)
        totals, summed = lax.map(
            forward_group, (query_view(queries), pair_view(pairs_all), grouped_lengths)
        )
        return (
            normed_all,
            queries,
            pairs_all,
            totals,
            summed.reshape(slot_total, block_len, head_width),
            norm_back,
        )

    forward_parts = attention_forward(hidden)
    attention = forward_parts[4].astype(jnp.bfloat16)
    branch = lax.psum_scatter(
        row_product(attention, dense_w).astype(jnp.bfloat16), "tp", scatter_dimension=0, tiled=True
    ).astype(jnp.float32)
    residual = hidden + branch + dense_b.astype(jnp.float32)
    second_f, second_back = jax.vjp(norm_rows, residual, gain_two, shift_two)
    second = second_f.astype(jnp.bfloat16)
    grad_output = validity[:, :, None] * cotangent.astype(jnp.float32)
    grad_down = grad_output.astype(jnp.bfloat16)
    second_all, grad_down_all = (
        lax.all_gather(second, "tp", axis=0, tiled=True),
        lax.all_gather(grad_down, "tp", axis=0, tiled=True),
    )
    pre_act = row_product(second_all, up_w) + up_b.reshape(-1).astype(jnp.float32)
    act_value, act_back = jax.vjp(activate, pre_act)
    activated = act_value.astype(jnp.bfloat16)
    down_out = lax.psum_scatter(
        row_product(activated, down_w).astype(jnp.bfloat16), "tp", scatter_dimension=0, tiled=True
    ).astype(jnp.float32)
    grad_act = times_transposed(grad_down_all, down_w)
    grad_pre = act_back(grad_act)[0].astype(jnp.bfloat16)
    grad_up = inner_rows(second_all, grad_pre)
    grad_up_b = jnp.sum(flatten_rows(grad_pre), axis=0, dtype=jnp.float32).reshape(up_b.shape)
    grad_down_w = inner_rows(activated, grad_down_all)
    grad_second = lax.psum_scatter(
        times_transposed(grad_pre, up_w), "tp", scatter_dimension=0, tiled=True
    )
    output = (validity[:, :, None] * (residual + down_out + down_b.astype(jnp.float32))).astype(
        jnp.bfloat16
    )
    grad_resid_norm, grad_gain_two, grad_shift_two = second_back(grad_second)
    grad_resid = grad_output + grad_resid_norm
    grad_branch = grad_resid.astype(jnp.bfloat16)
    hidden_again, grad_branch = lax.optimization_barrier((hidden, grad_branch))
    forward_parts = attention_forward(hidden_again)
    normed_all, queries, pairs_all, totals, summed, norm_back = forward_parts
    attention_back = summed.astype(jnp.bfloat16)
    branch_all = lax.all_gather(grad_branch, "tp", axis=0, tiled=True)
    grad_dense_w = inner_rows(attention_back, branch_all)
    grad_attention = times_transposed(branch_all, dense_w).astype(jnp.bfloat16)

    def backward_group(inputs):
        query_blk, pair_blk, lengths_blk, totals_blk, grad_blk = inputs
        masked = masked_scores(
            query_blk, pair_blk[:, :, 0], lengths_blk, slopes, distance, causal_mask, key_places
        )
        probabilities = jnp.exp(masked - totals_blk[..., None])
        grad_probs = jnp.einsum(
            "gihd,gjhd->ghij", grad_blk, pair_blk[:, :, 1], preferred_element_type=jnp.float32
        )
        row_delta = jnp.sum(probabilities * grad_probs, axis=-1, keepdims=True)
        grad_scores = (probabilities * (grad_probs - row_delta)).astype(jnp.bfloat16)
        grad_query = (
            jnp.einsum(
                "ghij,gjhd->gihd",
                grad_scores,
                pair_blk[:, :, 0],
                preferred_element_type=jnp.float32,
            )
            * 0.125
        )
        grad_key = (
            jnp.einsum(
                "ghij,gihd->gjhd", grad_scores, query_blk, preferred_element_type=jnp.float32
            )
            * 0.125
        )
        grad_value = jnp.einsum(
            "ghij,gihd->gjhd",
            probabilities.astype(jnp.bfloat16),
            grad_blk,
            preferred_element_type=jnp.float32,
        )
        return (grad_query, jnp.stack([grad_key, grad_value], axis=2))

    grad_query_all, grad_pairs = lax.map(
        backward_group,
        (
            query_view(queries),
            pair_view(pairs_all),
            grouped_lengths,
            totals,
            query_view(grad_attention),
        ),
    )
    grad_pairs_local = lax.psum_scatter(
        grad_pairs.reshape(slot_total, slot_len, 2 * head_width).astype(jnp.bfloat16),
        "wide",
        scatter_dimension=1,
        tiled=True,
    ).astype(jnp.float32)
    grad_queries = grad_query_all.reshape(slot_total, block_len, head_width).astype(jnp.bfloat16)
    grad_keys = grad_pairs_local[:, :, :head_width].astype(jnp.bfloat16)
    grad_values = grad_pairs_local[:, :, head_width:].astype(jnp.bfloat16)
    grad_query_w = inner_rows(normed_all, grad_queries)
    grad_key_w = inner_rows(normed_all, grad_keys)
    grad_value_w = inner_rows(normed_all, grad_values)
    grad_query_b = jnp.sum(flatten_rows(grad_queries), axis=0, dtype=jnp.float32).reshape(
        heads_dev, HEAD
    )
    grad_value_b = jnp.sum(flatten_rows(grad_values), axis=0, dtype=jnp.float32).reshape(
        heads_dev, HEAD
    )
    grad_normed = lax.psum_scatter(
        (
            times_transposed(grad_queries, query_w)
            + times_transposed(grad_keys, key_w)
            + times_transposed(grad_values, value_w)
        ).astype(jnp.bfloat16),
        "tp",
        scatter_dimension=0,
        tiled=True,
    ).astype(jnp.float32)
    grad_hidden_norm, grad_gain_one, grad_shift_one = norm_back(grad_normed)
    grad_in = (grad_resid + grad_hidden_norm).astype(jnp.bfloat16)
    (
        sum_query_w,
        sum_key_w,
        sum_value_w,
        sum_query_b,
        sum_value_b,
        sum_dense_w,
        sum_up_w,
        sum_up_b,
        sum_down_w,
    ) = (
        lax.psum_scatter(
            grad_query_w.astype(jnp.bfloat16), "wide", scatter_dimension=0, tiled=True
        ).astype(jnp.float32),
        lax.psum_scatter(
            grad_key_w.astype(jnp.bfloat16), "wide", scatter_dimension=0, tiled=True
        ).astype(jnp.float32),
        lax.psum_scatter(
            grad_value_w.astype(jnp.bfloat16), "wide", scatter_dimension=0, tiled=True
        ).astype(jnp.float32),
        lax.psum_scatter(
            grad_query_b.astype(jnp.bfloat16), "wide", scatter_dimension=1, tiled=True
        ).astype(jnp.float32),
        lax.psum_scatter(
            grad_value_b.astype(jnp.bfloat16), "wide", scatter_dimension=1, tiled=True
        ).astype(jnp.float32),
        lax.psum_scatter(
            grad_dense_w.astype(jnp.bfloat16), "wide", scatter_dimension=1, tiled=True
        ).astype(jnp.float32),
        lax.psum_scatter(
            grad_up.astype(jnp.bfloat16), "wide", scatter_dimension=0, tiled=True
        ).astype(jnp.float32),
        lax.psum_scatter(
            grad_up_b.astype(jnp.bfloat16), "wide", scatter_dimension=1, tiled=True
        ).astype(jnp.float32),
        lax.psum_scatter(
            grad_down_w.astype(jnp.bfloat16), "wide", scatter_dimension=1, tiled=True
        ).astype(jnp.float32),
    )
    grad_dense_b = jnp.sum(grad_resid, axis=(0, 1))
    grad_down_b = jnp.sum(grad_output, axis=(0, 1))
    sum_gain_one, sum_shift_one, sum_dense_b, sum_gain_two, sum_shift_two, sum_down_b = lax.psum(
        (grad_gain_one, grad_shift_one, grad_dense_b, grad_gain_two, grad_shift_two, grad_down_b),
        ("wide", "tp"),
    )

    def own_part(tensor):
        return lax.dynamic_slice_in_dim(tensor, wide_at * vec_part, vec_part, 0)

    return (
        output,
        grad_in,
        own_part(sum_gain_one),
        own_part(sum_shift_one),
        sum_query_w,
        sum_key_w,
        sum_value_w,
        sum_query_b,
        sum_value_b,
        sum_dense_w,
        own_part(sum_dense_b),
        own_part(sum_gain_two),
        own_part(sum_shift_two),
        sum_up_w,
        sum_up_b,
        sum_down_w,
        own_part(sum_down_b),
    )


BF = jnp.bfloat16
F32 = jnp.float32
LOG2E = 1.4426950408889634
NEG = -1e30
BLK = 128


def hbm():
    return pl.BlockSpec(memory_space=pl.ANY)


def vmem():
    return pl.BlockSpec(memory_space=pltpu.VMEM)


def square_places():
    own = lax.axis_index("wide")
    core = own % 2
    col = (own // 2) % 2
    row = own // 4
    pair = own + 1 - 2 * core
    along_x = own + 2 - 4 * col
    along_y = own + 4 - 8 * row
    return own, pair, along_x, along_y, along_x + along_y - own


def greet(targets):
    barrier = pltpu.get_barrier_semaphore()
    for target in targets:
        pl.semaphore_signal(barrier, inc=1, device_id=target, device_id_type=MESH)
    pl.semaphore_wait(barrier, len(targets))


def remote(src, dst, send_sem, recv_sem, target):
    return pltpu.make_async_remote_copy(
        src_ref=src,
        dst_ref=dst,
        send_sem=send_sem,
        recv_sem=recv_sem,
        device_id=target,
        device_id_type=MESH,
    )


class SquareGather:
    SENDS = 13

    def __init__(self, src, dst, send, recv, local):
        own, pair, ax, ay, dg = square_places()

        def place(slot, dev):
            return dst.at[slot, pl.ds(pl.multiple_of(dev * BLK, BLK), BLK)]

        def both(dev):
            return dst.at[:, pl.ds(pl.multiple_of(dev * BLK, BLK), BLK)]

        to_x, to_y, to_p = {"wide": ax}, {"wide": ay}, {"wide": pair}
        self.local = pltpu.make_async_copy(src, both(own), local)
        copies = {}
        copies["x0"] = remote(src.at[0], place(0, own), send.at[0], recv.at[0], to_x)
        copies["x1"] = remote(src.at[1], place(1, own), send.at[1], recv.at[1], to_x)
        copies["y0"] = remote(src.at[0], place(0, own), send.at[2], recv.at[2], to_y)
        copies["y1"] = remote(src.at[1], place(1, own), send.at[3], recv.at[3], to_y)
        copies["d0"] = remote(place(0, ay), place(0, ay), send.at[4], recv.at[4], to_x)
        copies["d1"] = remote(place(1, ax), place(1, ax), send.at[5], recv.at[5], to_y)
        copies["p"] = remote(src, both(own), send.at[6], recv.at[6], to_p)
        for index, (name, slot, dev) in enumerate(
            (("x0", 0, ax), ("x1", 1, ax), ("y0", 0, ay), ("y1", 1, ay), ("d0", 0, dg), ("d1", 1, dg))
        ):
            copies["p" + name] = remote(
                place(slot, dev), place(slot, dev), send.at[7 + index], recv.at[7 + index], to_p
            )
        self.copies = copies

    def start(self):
        for name in ("y0", "x1", "x0", "y1", "p"):
            self.copies[name].start()
        self.local.start()

    def pass_on(self, arrived, sends):
        self.copies[arrived].wait_recv()
        for name in sends:
            self.copies[name].start()

    def first(self):
        self.pass_on("y0", ("d0", "py0"))
        self.pass_on("x1", ("d1", "px1"))

    def second(self):
        self.pass_on("x0", ("px0",))
        self.pass_on("y1", ("py1",))

    def third(self):
        self.pass_on("d0", ("pd0",))
        self.pass_on("d1", ("pd1",))

    def arrive(self, *names):
        for name in names:
            self.copies[name].wait_recv()

    def sent(self):
        for copy in self.copies.values():
            copy.wait_send()

    def finish(self):
        self.arrive("p", "px0", "px1", "py0", "py1", "pd0", "pd1")
        self.sent()
        self.local.wait()


def wide_square(own_places):
    _own, pair, ax, ay, _dg = own_places
    return [{"wide": pair}, {"wide": ax}, {"wide": ay}]


def add_rows(dst, first, second, third=None):
    step = 16

    def body(index, carry):
        rows = pl.ds(pl.multiple_of(index * step, step), step)
        total = first[rows].astype(F32) + second[rows].astype(F32)
        if third is not None:
            total = total + third[rows].astype(F32)
        dst[rows] = total.astype(dst.dtype)
        return carry

    lax.fori_loop(0, BLK // step, body, 0)


class SquareScatter:
    SENDS = 10

    def __init__(self, src, out, summed, from_x, from_y, send, recv):
        own, pair, ax, ay, dg = square_places()
        shift = pair - own
        to_x, to_y, to_p = {"wide": ax}, {"wide": ay}, {"wide": pair}
        self.src, self.out = src, out
        self.summed, self.from_x, self.from_y = summed, from_x, from_y
        self.dests = (dg, ax, ay, own)
        self.pairs = []
        for chip in range(4):
            rows = pl.ds(pl.multiple_of((self.dests[chip] + shift) * BLK, BLK), BLK)
            self.pairs.append(
                remote(src.at[:, rows], summed.at[chip], send.at[chip], recv.at[chip], to_p)
            )
        self.dx = remote(summed.at[0, 0], from_x.at[0], send.at[4], recv.at[4], to_x)
        self.dy = remote(summed.at[0, 1], from_y.at[0], send.at[5], recv.at[5], to_y)
        self.xx = remote(summed.at[1, 0], from_x.at[1], send.at[6], recv.at[6], to_x)
        self.yy = remote(summed.at[2, 1], from_y.at[1], send.at[7], recv.at[7], to_y)
        self.ty = remote(summed.at[2, 0], from_y.at[2], send.at[8], recv.at[8], to_y)
        self.tx = remote(summed.at[1, 1], from_x.at[2], send.at[9], recv.at[9], to_x)

    def block(self, slot, chip):
        rows = pl.ds(pl.multiple_of(self.dests[chip] * BLK, BLK), BLK)
        return self.src.at[slot, rows]

    def pair_sum(self, chip, slot, third=None):
        add_rows(
            self.summed.at[chip, slot],
            self.block(slot, chip),
            self.summed.at[chip, slot],
            third,
        )

    def near(self, chip):
        self.pairs[chip].wait_recv()
        if chip == 0:
            self.pair_sum(0, 0)
            self.dx.start()
            self.pair_sum(0, 1)
            self.dy.start()
        elif chip == 1:
            self.pair_sum(1, 0)
            self.xx.start()
        elif chip == 2:
            self.pair_sum(2, 1)
            self.yy.start()
        else:
            self.pair_sum(3, 0)
            self.pair_sum(3, 1)

    def middle(self):
        self.dx.wait_recv()
        self.pair_sum(2, 0, self.from_x.at[0])
        self.ty.start()
        self.dy.wait_recv()
        self.pair_sum(1, 1, self.from_y.at[0])
        self.tx.start()

    def start(self):
        for chip in range(4):
            self.pairs[chip].start()

    def first(self):
        for chip in range(3):
            self.near(chip)

    def own_sums(self):
        self.near(3)

    def finish(self):
        self.xx.wait_recv()
        self.ty.wait_recv()
        add_rows(self.out.at[0], self.summed.at[3, 0], self.from_x.at[1], self.from_y.at[2])
        self.yy.wait_recv()
        self.tx.wait_recv()
        add_rows(self.out.at[1], self.summed.at[3, 1], self.from_y.at[1], self.from_x.at[2])
        for copy in self.pairs:
            copy.wait_send()
        for copy in (self.dx, self.dy, self.xx, self.yy, self.ty, self.tx):
            copy.wait_send()


class LineGather:
    def __init__(self, depth, pieces, send, recv):
        self.depth, self.pieces, self.send, self.recv = depth, pieces, send, recv
        self.layer = lax.axis_index("tp")

    def copies(self, step, up):
        index = self.layer - step + 1 if up else self.layer + step - 1
        goal = {"tp": self.layer + 1 if up else self.layer - 1}
        side = 0 if up else 1
        made = []
        for number, (own, place) in enumerate(self.pieces):
            source = own if step == 1 else place(index)
            made.append(
                remote(
                    source,
                    place(index),
                    self.send.at[side, number, step - 1],
                    self.recv.at[side, number, step - 1],
                    goal,
                )
            )
        return made

    def each(self, step, act):
        layer = self.layer

        @pl.when((layer < self.depth - 1) & (layer - step + 1 >= 0))
        def _():
            for copy in self.copies(step, True):
                act(copy)

        @pl.when((layer > 0) & (layer + step - 1 < self.depth))
        def _():
            for copy in self.copies(step, False):
                act(copy)

    def start(self, step):
        self.each(step, lambda copy: copy.start())

    def sent(self, step):
        self.each(step, lambda copy: copy.wait_send())

    def arrive(self, step):
        layer = self.layer

        @pl.when(layer - step >= 0)
        def _():
            for copy in self.copies(step, True):
                copy.wait_recv()

        @pl.when(layer + step < self.depth)
        def _():
            for copy in self.copies(step, False):
                copy.wait_recv()


def wide_others(own):
    return [{"wide": (own + step) % 8} for step in range(1, 8)]


def head_bias(length, slope, rows):
    place = lax.broadcasted_iota(jnp.int32, (rows, QB), 0)
    return jnp.where(place < length, slope * place.astype(F32), NEG)


QB = 256


def dot_nt(first, second):
    return lax.dot_general(first, second, (((1,), (1,)), ((), ())), preferred_element_type=F32)


def dot_nn(first, second):
    return lax.dot_general(first, second, (((1,), (0,)), ((), ())), preferred_element_type=F32)


def later_key(size):
    key_place = lax.broadcasted_iota(jnp.int32, (size, size), 0)
    query_place = lax.broadcasted_iota(jnp.int32, (size, size), 1)
    return key_place > query_place


def slot_scores(key, query, bias, step):
    extent = (step + 1) * QB
    scores = dot_nt(key[:extent], query) * (0.125 * LOG2E) + bias[:extent]
    edge = jnp.where(later_key(QB), NEG, scores[extent - QB :])
    return edge if step == 0 else jnp.concatenate([scores[: extent - QB], edge], 0)


def attend_slot(slot, length, slopes, qkv, out, totals, bias):
    rows = qkv.shape[1]
    for head in range(2):
        lanes = pl.ds(head * HEAD, HEAD)
        bias[...] = head_bias(length, slopes[head], rows)
        key = qkv[slot, :, pl.ds(2 * HEAD + head * HEAD, HEAD)]
        value_t = qkv[slot, :, pl.ds(4 * HEAD + head * HEAD, HEAD)].T
        for step in range(rows // QB):
            here = pl.ds(step * QB, QB)
            scores = slot_scores(key, qkv[slot, here, lanes], bias, step)
            highest = jnp.max(scores, axis=0, keepdims=True)
            weights = jnp.exp2(scores - highest)
            total = jnp.sum(weights, axis=0, keepdims=True)
            mixed = dot_nn(value_t[:, : (step + 1) * QB], weights.astype(BF)) / total
            out[slot, here, lanes] = mixed.T.astype(BF)
            totals[slot, pl.ds(head, 1), here] = highest + jnp.log2(total)


def attend_slot_back(
    slot, length, slopes, qkv, attention, grad, totals, out, bias, key_sum, value_sum
):
    rows = qkv.shape[1]
    for head in range(2):
        lanes = pl.ds(head * HEAD, HEAD)
        key_lanes = pl.ds(2 * HEAD + head * HEAD, HEAD)
        value_lanes = pl.ds(4 * HEAD + head * HEAD, HEAD)
        bias[...] = head_bias(length, slopes[head], rows)
        key = qkv[slot, :, key_lanes]
        value = qkv[slot, :, value_lanes]
        key_t = key.T
        key_sum[...] = jnp.zeros_like(key_sum)
        value_sum[...] = jnp.zeros_like(value_sum)
        for step in range(rows // QB):
            here = pl.ds(step * QB, QB)
            extent = (step + 1) * QB
            query = qkv[slot, here, lanes]
            grad_rows = grad[slot, here, lanes]
            product = grad_rows.astype(F32) * attention[slot, here, lanes].astype(F32)
            delta = jnp.sum(product.T, axis=0, keepdims=True)
            scores = slot_scores(key, query, bias, step)
            probs = jnp.exp2(scores - totals[slot, pl.ds(head, 1), here])
            grad_probs = dot_nt(value[:extent], grad_rows)
            grad_scores = (probs * (grad_probs - delta)).astype(BF)
            span = pl.ds(0, extent)
            value_sum[span] += dot_nn(probs.astype(BF), grad_rows)
            key_sum[span] += dot_nn(grad_scores, query)
            grad_query = dot_nn(key_t[:, :extent], grad_scores)
            out[slot, here, lanes] = (grad_query.T * 0.125).astype(BF)
        out[slot, :, key_lanes] = (key_sum[...] * 0.125).astype(BF)
        out[slot, :, value_lanes] = value_sum[...].astype(BF)


def line_others(depth):
    layer = lax.axis_index("tp")
    return [{"tp": (layer + step) % depth} for step in range(1, depth)]


VMEM_MAX = 67043328


def norm_stats(values):
    middle = jnp.mean(values, axis=-1, keepdims=True)
    centred = values - middle
    spread = jnp.mean(centred * centred, axis=-1, keepdims=True)
    inverse = lax.rsqrt(spread + 1e-05)
    return centred * inverse, inverse


def norm_back_rows(grad, hat, inverse, gain):
    scaled = grad * gain
    first = jnp.mean(scaled, axis=-1, keepdims=True)
    second = jnp.mean(scaled * hat, axis=-1, keepdims=True)
    return (scaled - first - hat * second) * inverse


def gelu_parts(values):
    root = math.sqrt(2 / math.pi)
    squared = values * values
    inner = jnp.tanh(root * values * (1.0 + 0.044715 * squared))
    half = 0.5 * (1.0 + inner)
    slope = half + 0.5 * values * (1.0 - inner * inner) * root * (1.0 + 3 * 0.044715 * squared)
    return values * half, slope


def relation(index):
    own = lax.axis_index("wide")
    core = (own + index) % 2
    col = (own // 2 + index // 2) % 2
    row = (own // 4 + index // 4) % 2
    return row * 4 + col * 2 + core


class WideExchange:
    def __init__(self, source, target, send, recv):
        own = lax.axis_index("wide")
        self.copies = [
            remote(
                source((own + step) % 8),
                target(own),
                send.at[step - 1],
                recv.at[step - 1],
                {"wide": (own + step) % 8},
            )
            for step in range(1, 8)
        ]

    def start(self):
        for copy in self.copies:
            copy.start()

    def arrive(self):
        for copy in self.copies:
            copy.wait_recv()

    def sent(self):
        for copy in self.copies:
            copy.wait_send()


def layer_body(
    depth,
    lengths,
    hidden,
    cotangent,
    w_query,
    w_key,
    w_value,
    w_dense,
    w_up,
    w_down,
    pre_gain,
    pre_shift,
    mid_gain,
    mid_shift,
    b_dense,
    b_down,
    b_up,
    b_query,
    b_value,
    output,
    grad_in,
    attn_sum,
    ffn_x,
    vec_sums,
    unit_sums,
    hidden_all,
    normed,
    down_all,
    branch_all,
    second_share,
    down_share,
    qkv,
    attention,
    grad_att,
    act_t,
    pre_t,
    totals,
    bias,
    key_sum,
    value_sum,
    qkv_w,
    dense_w,
    up_t,
    down_t,
    up_w,
    down_w,
    z_qkv,
    z_dense,
    z_vec,
    vec_wide,
    vec_line,
    vec_wide_all,
    vec_line_all,
    vectors,
    up_bias,
    qkv_bias,
    own_rows,
    down_own,
    residual,
    grad_second,
    grad_resid,
    down_out,
    sums,
    up_sum,
    ffn_g,
    ffn_in,
    ffn_sum,
    attn_g,
    attn_in,
    attn_z,
    parts,
    gathered,
    a_summed,
    a_x,
    a_y,
    b_summed,
    b_x,
    b_y,
    gather_send,
    gather_recv,
    gather_local,
    scatter_send,
    scatter_recv,
    line_send,
    line_recv,
    ffn_line_send,
    ffn_line_recv,
    wide_send,
    wide_recv,
    grad_line_send,
    grad_line_recv,
    onward_send,
    onward_recv,
    sum_send,
    sum_recv,
    own_sems,
):
    own = lax.axis_index("wide")
    layer = lax.axis_index("tp")
    per_layer = 8 // depth
    width = hidden.shape[-1]
    step = 32
    steps = BLK // step
    others = [
        ((own + side) % 8, (layer + up) % depth)
        for up in range(depth)
        for side in range(8)
        if up or side
    ]
    own_lanes = pl.ds(pl.multiple_of(own * BLK, BLK), BLK)

    for place, ref in enumerate((pre_gain, pre_shift, mid_gain, mid_shift, b_dense, b_down)):
        vec_wide[pl.ds(place, 1)] = ref[...].astype(F32)
    vec_line[...] = jnp.zeros_like(vec_line)
    vec_line[0 : b_up.shape[0], 0 : b_up.shape[1]] = b_up[...].astype(F32)
    vec_line[b_up.shape[0] :, 0:8] = b_query[...].astype(F32)
    vec_line[b_up.shape[0] :, 8:16] = b_value[...].astype(F32)
    first_row = own * BLK

    def token_mask(slot, rows, count):
        place = first_row + rows * count + lax.broadcasted_iota(jnp.int32, (count, BLK), 0)
        inside = place < lengths[layer * 2 + slot]
        return jnp.where(inside, 1.0, 0.0).astype(F32)[:, :1]

    def down_part(index, carry):
        rows = pl.ds(pl.multiple_of(index * step, step), step)
        for slot in range(2):
            values = token_mask(slot, index, step) * cotangent[slot, rows].astype(F32)
            down_own[slot, rows] = values.astype(BF)
        return carry

    lax.fori_loop(0, steps, down_part, 0)
    greet([{"wide": wide, "tp": tp} for wide, tp in others])

    def gather_of(number, src, dst):
        return SquareGather(
            src, dst, gather_send.at[number], gather_recv.at[number], gather_local.at[number]
        )

    def wide_of(number, source, target):
        return WideExchange(source, target, wide_send.at[number], wide_recv.at[number])

    gains = wide_of(0, lambda dev: vec_wide, lambda dev: vec_wide_all.at[dev])
    gains.start()
    hid = gather_of(0, hidden, hidden_all)
    hid.start()
    line = LineGather(
        depth,
        [
            (w_query, lambda at: z_qkv.at[at, 0]),
            (w_key, lambda at: z_qkv.at[at, 1]),
            (w_value, lambda at: z_qkv.at[at, 2]),
            (w_dense, lambda at: z_dense.at[at]),
            (vec_line, lambda at: z_vec.at[at]),
        ],
        line_send,
        line_recv,
    )
    line.start(1)
    own_copies = [
        pltpu.make_async_copy(ref, place(layer), own_sems.at[number])
        for number, (ref, place) in enumerate(line.pieces)
    ]
    for copy in own_copies:
        copy.start()
    vec_wide_all[own] = vec_wide[...]
    gains.arrive()
    for dev in range(8):
        vectors[:, dev * BLK : (dev + 1) * BLK] = vec_wide_all[dev]

    def norm_block(index, carry):
        base = relation(index) * BLK

        def norm_part(part, carry):
            rows = pl.ds(pl.multiple_of(base + part * step, step), step)
            for slot in range(2):
                hat, _inverse = norm_stats(hidden_all[slot, rows].astype(F32))
                normed[slot, rows] = (hat * vectors[0:1] + vectors[1:2]).astype(BF)
            return carry

        return lax.fori_loop(0, steps, norm_part, carry)

    hid.arrive("p")
    hid.local.wait()
    lax.fori_loop(0, 2, norm_block, 0)
    hid.first()
    line.arrive(1)
    line.start(2)
    hid.second()
    line.arrive(2)
    line.start(3)
    hid.arrive("px0", "px1", "py0", "py1")
    lax.fori_loop(2, 6, norm_block, 0)
    hid.third()
    line.arrive(3)
    for copy in own_copies:
        copy.wait()

    def goal_lanes(dev):
        return pl.ds(pl.multiple_of((dev % per_layer) * BLK, BLK), BLK)

    heads = wide_of(
        1,
        lambda dev: z_qkv.at[dev // per_layer, :, :, goal_lanes(dev)],
        lambda dev: attn_in.at[dev, pl.ds(0, 3)],
    )
    dense = wide_of(
        2,
        lambda dev: z_dense.at[dev // per_layer, goal_lanes(dev)],
        lambda dev: dense_w.at[:, own_lanes],
    )
    biases = wide_of(3, lambda dev: z_vec, lambda dev: vec_line_all.at[dev])
    ups = wide_of(
        4,
        lambda dev: w_up.at[:, pl.ds(pl.multiple_of(dev * BLK, BLK), BLK)],
        lambda dev: up_t.at[own_lanes],
    )
    downs = wide_of(
        5,
        lambda dev: w_down.at[pl.ds(pl.multiple_of(dev * BLK, BLK), BLK)],
        lambda dev: down_t.at[:, own_lanes],
    )
    arrivals = (biases, heads, dense, ups, downs)
    for exchange in arrivals:
        exchange.start()
    gd = gather_of(1, down_own, down_all)
    gd.start()
    own_copies = [
        pltpu.make_async_copy(z_qkv.at[own // per_layer, :, :, goal_lanes(own)], attn_in.at[own, pl.ds(0, 3)], own_sems.at[5]),
        pltpu.make_async_copy(z_dense.at[own // per_layer, goal_lanes(own)], dense_w.at[:, own_lanes], own_sems.at[6]),
        pltpu.make_async_copy(w_up.at[:, own_lanes], up_t.at[own_lanes], own_sems.at[7]),
        pltpu.make_async_copy(w_down.at[own_lanes], down_t.at[:, own_lanes], own_sems.at[8]),
    ]
    for copy in own_copies:
        copy.start()
    vec_line_all[own] = z_vec[...]
    hid.arrive("pd0", "pd1")
    lax.fori_loop(6, 8, norm_block, 0)
    biases.arrive()
    head_layer = own // per_layer
    piece = own % per_layer
    unit_row = own // 2
    for dev in range(8):
        for head in range(2):
            lanes = slice(head * HEAD + dev * 8, head * HEAD + dev * 8 + 8)
            row = pl.ds(b_up.shape[0] + 2 * piece + head, 1)
            values = vec_line_all[dev, head_layer, row]
            qkv_bias[:, lanes] = values[:, 0:8]
            lanes = slice(4 * HEAD + lanes.start, 4 * HEAD + lanes.stop)
            qkv_bias[:, lanes] = values[:, 8:16]
    qkv_bias[:, 2 * HEAD : 4 * HEAD] = jnp.zeros((1, 2 * HEAD), F32)
    for up in range(depth):
        for part in range(4):
            values = vec_line_all[4 * (own % 2) + part, up, pl.ds(unit_row, 1)]
            up_bias[:, up * BLK + part * 32 : up * BLK + part * 32 + 32] = values[:, 0:32]
    heads.arrive()
    for copy in own_copies:
        copy.wait()
    for dev in range(8):
        for kind in range(3):
            qkv_w[dev * BLK : (dev + 1) * BLK, kind * BLK : (kind + 1) * BLK] = attn_in[dev, kind]

    ffn_line = LineGather(
        depth,
        [
            (up_t, lambda at: up_w.at[:, pl.ds(pl.multiple_of(at * BLK, BLK), BLK)]),
            (down_t, lambda at: down_w.at[pl.ds(pl.multiple_of(at * BLK, BLK), BLK)]),
        ],
        ffn_line_send,
        ffn_line_recv,
    )
    slopes = [
        jnp.exp2(-0.5 * (jnp.full((1, 1), 2 * own + head, jnp.int32).astype(F32) + 1.0)) * LOG2E
        for head in range(2)
    ]

    def one_slot(slot, carry):
        def block(index, carry):
            rows = pl.ds(pl.multiple_of(index * QB, QB), QB)
            qkv[slot, rows] = (dot_nn(normed[slot, rows], qkv_w[...]) + qkv_bias[...]).astype(BF)
            return carry

        lax.fori_loop(0, 8 * BLK // QB, block, 0)
        attend_slot(slot, lengths[layer * 2 + slot], slopes, qkv, attention, totals, bias)

        @pl.when(slot == 0)
        def _():
            ups.arrive()
            downs.arrive()
            ffn_line.start(1)

        return carry

    lax.fori_loop(0, 2, one_slot, 0)
    own_copies = [
        pltpu.make_async_copy(ref, place(layer), own_sems.at[9 + number])
        for number, (ref, place) in enumerate(ffn_line.pieces)
    ]
    for copy in own_copies:
        copy.start()
    hid.sent()
    dense.arrive()
    share = branch_all

    def dense_block(index, carry):
        rows = pl.ds(pl.multiple_of(relation(index) * BLK, BLK), BLK)
        values = attention[:, rows].reshape(2 * BLK, 2 * HEAD)
        share[:, rows] = dot_nn(values, dense_w[...]).astype(BF).reshape(2, BLK, width)
        return carry

    def scatter_of(number, src, out, buffers):
        return SquareScatter(src, out, *buffers, scatter_send.at[number], scatter_recv.at[number])

    scatter = scatter_of(0, share, residual, (a_summed, a_x, a_y))
    for chip in range(4):
        start = (6, 2, 4, 0)[chip]
        lax.fori_loop(start, start + 2, dense_block, 0)
        scatter.pairs[chip].start()
        if chip:
            scatter.near(chip - 1)
    gd.first()
    ffn_line.arrive(1)
    ffn_line.start(2)
    scatter.near(3)
    gd.second()
    scatter.middle()
    gd.third()
    ffn_line.arrive(2)
    ffn_line.start(3)
    scatter.finish()

    def second_part(index, carry):
        rows = pl.ds(pl.multiple_of(index * step, step), step)
        for slot in range(2):
            values = hidden[slot, rows].astype(F32) + residual[slot, rows] + vectors[4:5]
            residual[slot, rows] = values
            hat, _inverse = norm_stats(values)
            own_rows[slot, rows] = (hat * vectors[2:3] + vectors[3:4]).astype(BF)
        return carry

    lax.fori_loop(0, steps, second_part, 0)
    second_all = hidden_all
    gather = gather_of(2, own_rows, second_all)
    gather.start()
    scatter = scatter_of(1, second_share, grad_second, (a_summed, a_x, a_y))
    gd.arrive("p", "px0", "px1", "py0", "py1", "pd0", "pd1")
    gd.local.wait()
    for copy in own_copies:
        copy.wait()
    ffn_line.arrive(3)

    def compute(index, carry):
        source = relation(index)
        rows = pl.ds(pl.multiple_of(source * BLK, BLK), BLK)
        values = second_all[:, rows].reshape(2 * BLK, width)
        act_value, act_slope = gelu_parts(dot_nn(values, up_w[...]) + up_bias[...])
        activated = act_value.astype(BF)
        grad_rows = down_all[:, rows].reshape(2 * BLK, width)
        grad_pre = (dot_nt(grad_rows, down_w[...]) * act_slope).astype(BF)
        second_share[:, rows] = dot_nt(grad_pre, up_w[...]).astype(BF).reshape(2, BLK, width)
        down_share[:, rows] = dot_nn(activated, down_w[...]).astype(BF).reshape(2, BLK, width)
        up_sum[...] += jnp.sum(grad_pre.astype(F32), axis=0, keepdims=True)
        for slot in range(2):
            lanes = pl.ds(pl.multiple_of(slot * 8 * BLK + source * BLK, BLK), BLK)
            part = slice(slot * BLK, (slot + 1) * BLK)
            act_t[:, lanes] = activated[part].T
            pre_t[:, lanes] = grad_pre[part].T
        return carry

    up_sum[...] = jnp.zeros_like(up_sum)
    gather.arrive("p")
    gather.local.wait()
    lax.fori_loop(0, 2, compute, 0)
    scatter.pairs[3].start()
    gather.first()
    gather.second()
    gather.arrive("px0", "px1", "py0", "py1")
    lax.fori_loop(2, 4, compute, 0)
    scatter.pairs[1].start()
    scatter.near(3)
    lax.fori_loop(4, 6, compute, 0)
    scatter.pairs[2].start()
    gather.third()
    scatter.near(1)
    gather.arrive("pd0", "pd1")
    lax.fori_loop(6, 8, compute, 0)
    scatter.pairs[0].start()
    scatter.near(2)
    scatter.near(0)

    def weight_grads(left, right, kind):
        def one(up, carry):
            rows = pl.ds(pl.multiple_of(up * BLK, BLK), BLK)
            total = dot_nn(left[rows, pl.ds(0, 8 * BLK)], right[0])
            total = total + dot_nn(left[rows, pl.ds(8 * BLK, 8 * BLK)], right[1])
            total = total.astype(BF)
            for blk in range(8):
                ffn_g[kind, up, blk] = total[:, blk * BLK : (blk + 1) * BLK]
            return carry

        lax.fori_loop(0, depth, one, 0)

    def line_copies(kind):
        return [
            remote(
                ffn_g.at[kind, (layer + up) % depth],
                ffn_in.at[kind, up - 1],
                grad_line_send.at[kind, up - 1],
                grad_line_recv.at[kind, up - 1],
                {"tp": (layer + up) % depth},
            )
            for up in range(1, depth)
        ]

    def line_sums(kind):
        for copy in line_copies(kind):
            copy.wait_recv()

        def add_block(blk, carry):
            total = ffn_g[kind, layer, blk].astype(F32)
            for up in range(depth - 1):
                total = total + ffn_in[kind, up, blk].astype(F32)
            ffn_sum[blk, kind] = total.astype(BF)
            return carry

        lax.fori_loop(0, 8, add_block, 0)

    weight_grads(pre_t, second_all, 0)
    for copy in line_copies(0):
        copy.start()
    scatter.middle()
    weight_grads(act_t, down_all, 1)
    for copy in line_copies(1):
        copy.start()
    scatter.finish()
    gather.sent()
    sums[...] = jnp.zeros_like(sums)

    def back_part(index, carry):
        rows = pl.ds(pl.multiple_of(index * step, step), step)
        for slot in range(2):
            hat, inverse = norm_stats(residual[slot, rows])
            grad = grad_second[slot, rows]
            grad_out = token_mask(slot, index, step) * cotangent[slot, rows].astype(F32)
            total = grad_out + norm_back_rows(grad, hat, inverse, vectors[2:3])
            grad_resid[slot, rows] = total
            own_rows[slot, rows] = total.astype(BF)
            for place, value in enumerate((total, grad * hat, grad, grad_out)):
                sums[pl.ds(place, 1)] += jnp.sum(value, axis=0, keepdims=True)
        return carry

    lax.fori_loop(0, steps, back_part, 0)
    again = gather_of(3, own_rows, branch_all)
    again.start()
    down = scatter_of(2, down_share, down_out, (b_summed, b_x, b_y))
    down.start()

    def att_block(index, carry):
        rows = pl.ds(pl.multiple_of(relation(index) * BLK, BLK), BLK)
        values = branch_all[:, rows].reshape(2 * BLK, width)
        grad_att[:, rows] = dot_nt(values, dense_w[...]).astype(BF).reshape(2, BLK, 2 * HEAD)
        return carry

    again.arrive("p")
    again.local.wait()
    lax.fori_loop(0, 2, att_block, 0)
    again.first()
    down.near(0)
    again.second()
    again.arrive("px0", "px1", "py0", "py1")
    down.near(1)
    down.near(2)
    lax.fori_loop(2, 6, att_block, 0)
    again.third()
    again.arrive("pd0", "pd1")
    lax.fori_loop(6, 8, att_block, 0)

    dense_part = dot_nn(attention[0].T, branch_all[0]) + dot_nn(attention[1].T, branch_all[1])
    dense_part = dense_part.astype(BF)
    for blk in range(8):
        attn_g[blk, 3] = dense_part[:, blk * BLK : (blk + 1) * BLK]
    kinds = (pl.ds(3, 1), pl.ds(0, 3))
    exchanges = [
        wide_of(
            6 + group,
            lambda dev, kind=kind: attn_g.at[dev, kind],
            lambda dev, kind=kind: attn_in.at[dev, kind],
        )
        for group, kind in enumerate(kinds)
    ]

    def onward(group, index, source):
        return remote(
            source.at[index, kinds[group]],
            attn_z.at[layer, index % per_layer, kinds[group]],
            onward_send.at[group, index],
            onward_recv.at[group, layer, index % per_layer],
            {"tp": index // per_layer},
        )

    def forward(group, index, source):
        @pl.when(index // per_layer != layer)
        def _():
            onward(group, index, source).start()

    def forward_all(group):
        for number in range(1, 8):
            exchanges[group].copies[number - 1].wait_recv()
            forward(group, (own + 8 - number) % 8, attn_in)

    exchanges[0].start()
    forward(0, own, attn_g)
    ffn = wide_of(8, lambda dev: ffn_sum.at[dev], lambda dev: ffn_x.at[dev])

    def slot_back(slot, carry):
        attend_slot_back(
            slot,
            lengths[layer * 2 + slot],
            slopes,
            qkv,
            attention,
            grad_att,
            totals,
            qkv,
            bias,
            key_sum,
            value_sum,
        )

        @pl.when(slot == 0)
        def _():
            forward_all(0)
            down.middle()
            line_sums(0)

        return carry

    lax.fori_loop(0, 2, slot_back, 0)
    grad_qkv = qkv
    weight_part = dot_nn(grad_qkv[0].T, normed[0]) + dot_nn(grad_qkv[1].T, normed[1])
    weight_part = weight_part.astype(BF)
    for kind in range(3):
        for blk in range(8):
            attn_g[blk, kind] = weight_part[
                kind * BLK : (kind + 1) * BLK, blk * BLK : (blk + 1) * BLK
            ]
    exchanges[1].start()
    forward(1, own, attn_g)
    share = second_share
    grad_normed = grad_second
    scatter = scatter_of(3, share, grad_normed, (a_summed, a_x, a_y))

    def normed_block(index, carry):
        rows = pl.ds(pl.multiple_of(relation(index) * BLK, BLK), BLK)
        values = grad_qkv[:, rows].reshape(2 * BLK, 6 * HEAD)
        share[:, rows] = dot_nt(values, qkv_w[...]).astype(BF).reshape(2, BLK, width)
        return carry

    for chip in range(4):
        start = (6, 2, 4, 0)[chip]
        lax.fori_loop(start, start + 2, normed_block, 0)
        scatter.pairs[chip].start()
        if chip:
            scatter.near(chip - 1)
    line_sums(1)
    ffn.start()
    head_sum = jnp.sum(grad_qkv[0].astype(F32), axis=0, keepdims=True)
    head_sum = head_sum + jnp.sum(grad_qkv[1].astype(F32), axis=0, keepdims=True)
    down.near(3)
    down.finish()

    def out_part(index, carry):
        rows = pl.ds(pl.multiple_of(index * step, step), step)
        for slot in range(2):
            total = residual[slot, rows] + down_out[slot, rows] + vectors[5:6]
            output[slot, rows] = (token_mask(slot, index, step) * total).astype(BF)
        return carry

    lax.fori_loop(0, steps, out_part, 0)
    forward_all(1)
    scatter.near(3)
    scatter.middle()
    for blk in range(8):
        lanes = slice(blk * BLK, (blk + 1) * BLK)
        for place in range(4):
            parts[blk, pl.ds(2 + place, 1)] = sums[place : place + 1, lanes]
        for place in range(depth):
            parts[blk, pl.ds(6 + place, 1)] = up_sum[:, place * BLK : (place + 1) * BLK]
        parts[blk, pl.ds(6 + depth, 1)] = head_sum[:, : 2 * HEAD]
        parts[blk, pl.ds(7 + depth, 1)] = head_sum[:, 4 * HEAD :]
    scatter.finish()

    def last_part(index, carry):
        gain_sum, shift_sum = carry
        rows = pl.ds(pl.multiple_of(index * step, step), step)
        for slot in range(2):
            hat, inverse = norm_stats(hidden[slot, rows].astype(F32))
            grad = grad_normed[slot, rows]
            total = grad_resid[slot, rows] + norm_back_rows(grad, hat, inverse, vectors[0:1])
            grad_in[slot, rows] = total.astype(BF)
            gain_sum = gain_sum + jnp.sum(grad * hat, axis=0, keepdims=True)
            shift_sum = shift_sum + jnp.sum(grad, axis=0, keepdims=True)
        return gain_sum, shift_sum

    zero = jnp.zeros((1, width), F32)
    gain_sum, shift_sum = lax.fori_loop(0, steps, last_part, (zero, zero))
    for blk in range(8):
        lanes = slice(blk * BLK, (blk + 1) * BLK)
        parts[blk, pl.ds(0, 1)] = gain_sum[:, lanes]
        parts[blk, pl.ds(1, 1)] = shift_sum[:, lanes]
    sum_copies = [
        remote(
            parts.at[wide],
            gathered.at[own, layer],
            sum_send.at[index],
            sum_recv.at[index],
            {"wide": wide, "tp": tp},
        )
        for index, (wide, tp) in enumerate(others)
    ]
    for copy in sum_copies:
        copy.start()
    gathered[own, layer] = parts[own]
    for group in range(2):
        for up in range(1, depth):
            source = (layer + up) % depth
            for number in range(per_layer):
                remote(
                    attn_in.at[number, kinds[group]],
                    attn_z.at[source, number, kinds[group]],
                    onward_send.at[group, number],
                    onward_recv.at[group, source, number],
                    {"tp": source},
                ).wait_recv()
    attn_in[own] = attn_g[own]
    for number in range(per_layer):
        for kind in range(4):
            total = attn_in[layer * per_layer + number, kind].astype(F32)
            for up in range(1, depth):
                total = total + attn_z[(layer + up) % depth, number, kind].astype(F32)
            attn_sum[number, kind] = total
    ffn_x[own] = ffn_sum[own]
    ffn.arrive()
    for copy in sum_copies:
        copy.wait_recv()

    def unit_part(dev, carry):
        total = gathered[dev, 0]
        for up in range(1, depth):
            total = total + gathered[dev, up]
        unit_sums[dev] = total
        return carry + total

    vec_sums[...] = lax.fori_loop(0, 8, unit_part, jnp.zeros((16, BLK), F32))

    for copy in sum_copies:
        copy.wait_send()
    for exchange in (gains, ffn) + arrivals + tuple(exchanges):
        exchange.sent()
    for number in range(1, depth):
        line.sent(number)
        ffn_line.sent(number)
    for kind in range(2):
        for copy in line_copies(kind):
            copy.wait_send()
    gd.sent()
    again.sent()
    for group in range(2):
        for index in range(8):

            @pl.when(index // per_layer != layer)
            def _(index=index, group=group):
                onward(group, index, attn_in).wait_send()


def layer_pass(depth, lengths, hidden, cotangent, *weights):
    width = hidden.shape[-1]
    units = depth * BLK
    per_layer = 8 // depth
    dma = pltpu.SemaphoreType.DMA
    rows = jax.ShapeDtypeStruct((2, BLK, width), BF)
    tokens = pltpu.VMEM((2, 8 * BLK, width), BF)
    own_f32 = pltpu.VMEM((2, BLK, width), F32)
    own_bf = pltpu.VMEM((2, BLK, width), BF)
    line_vec = (8, BLK)
    peers = 8 * depth - 1
    vectors = [part.reshape(1, BLK) for part in weights[6:12]]
    operands = (hidden, cotangent) + weights[:6] + tuple(vectors) + weights[12:]
    return pl.pallas_call(
        functools.partial(layer_body, depth),
        out_shape=[
            rows,
            rows,
            jax.ShapeDtypeStruct((per_layer, 4, BLK, BLK), F32),
            jax.ShapeDtypeStruct((8, 2, BLK, BLK), BF),
            jax.ShapeDtypeStruct((16, BLK), F32),
            jax.ShapeDtypeStruct((8, 16, BLK), F32),
        ],
        in_specs=[pl.BlockSpec(memory_space=pltpu.SMEM)] + [vmem()] * len(operands),
        out_specs=[vmem()] * 6,
        scratch_shapes=[tokens] * 6
        + [
            pltpu.VMEM((2, 8 * BLK, 6 * HEAD), BF),
            pltpu.VMEM((2, 8 * BLK, 2 * HEAD), BF),
            pltpu.VMEM((2, 8 * BLK, 2 * HEAD), BF),
            pltpu.VMEM((units, 16 * BLK), BF),
            pltpu.VMEM((units, 16 * BLK), BF),
            pltpu.VMEM((2, 2, 8 * BLK), F32),
            pltpu.VMEM((8 * BLK, QB), F32),
            pltpu.VMEM((8 * BLK, HEAD), F32),
            pltpu.VMEM((8 * BLK, HEAD), F32),
            pltpu.VMEM((width, 6 * HEAD), BF),
            pltpu.VMEM((2 * HEAD, width), BF),
            pltpu.VMEM((width, BLK), BF),
            pltpu.VMEM((BLK, width), BF),
            pltpu.VMEM((width, units), BF),
            pltpu.VMEM((units, width), BF),
            pltpu.VMEM((depth, 3, BLK, per_layer * BLK), BF),
            pltpu.VMEM((depth, per_layer * BLK, BLK), BF),
            pltpu.VMEM((depth,) + line_vec, F32),
            pltpu.VMEM((8, BLK), F32),
            pltpu.VMEM(line_vec, F32),
            pltpu.VMEM((8, 8, BLK), F32),
            pltpu.VMEM((8, depth) + line_vec, F32),
            pltpu.VMEM((8, width), F32),
            pltpu.VMEM((1, units), F32),
            pltpu.VMEM((1, 6 * HEAD), F32),
            own_bf,
            own_bf,
            own_f32,
            own_f32,
            own_f32,
            own_f32,
            pltpu.VMEM((8, width), F32),
            pltpu.VMEM((1, units), F32),
            pltpu.VMEM((2, depth, 8, BLK, BLK), BF),
            pltpu.VMEM((2, depth - 1, 8, BLK, BLK), BF),
            pltpu.VMEM((8, 2, BLK, BLK), BF),
            pltpu.VMEM((8, 4, BLK, BLK), BF),
            pltpu.VMEM((8, 4, BLK, BLK), BF),
            pltpu.VMEM((depth, per_layer, 4, BLK, BLK), BF),
            pltpu.VMEM((8, 16, BLK), F32),
            pltpu.VMEM((8, depth, 16, BLK), F32),
        ]
        + [
            pltpu.VMEM((4, 2, BLK, width), BF),
            pltpu.VMEM((3, BLK, width), BF),
            pltpu.VMEM((3, BLK, width), BF),
        ]
        * 2
        + [
            dma((4, SquareGather.SENDS)),
            dma((4, SquareGather.SENDS)),
            dma((4,)),
            dma((4, SquareScatter.SENDS)),
            dma((4, SquareScatter.SENDS)),
            dma((2, 5, depth - 1)),
            dma((2, 5, depth - 1)),
            dma((2, 2, depth - 1)),
            dma((2, 2, depth - 1)),
            dma((9, 7)),
            dma((9, 7)),
            dma((2, depth - 1)),
            dma((2, depth - 1)),
            dma((2, 8)),
            dma((2, depth, per_layer)),
            dma((peers,)),
            dma((peers,)),
            dma((11,)),
        ],
        compiler_params=pltpu.CompilerParams(
            collective_id=1, has_side_effects=True, vmem_limit_bytes=VMEM_MAX
        ),
        name="layer",
    )(lengths, *operands)


def write_body(
    depth,
    output_in,
    grad_in_in,
    attn_sum,
    ffn_x,
    vec_in,
    unit_sums,
    output,
    grad_in,
    grad_q,
    grad_k,
    grad_v,
    grad_d,
    grad_up,
    grad_down,
    up_b,
    query_b,
    value_b,
    vec_sums,
):
    own = lax.axis_index("wide")
    layer = lax.axis_index("tp")
    per_layer = 8 // depth
    output[...] = output_in[...]
    grad_in[...] = grad_in_in[...]
    for number in range(per_layer):
        lanes = slice(number * BLK, (number + 1) * BLK)
        for kind, target in enumerate((grad_q, grad_k, grad_v)):
            target[:, lanes] = attn_sum[number, kind].T
        grad_d[lanes] = attn_sum[number, 3]
    for blk in range(8):
        lanes = slice(blk * BLK, (blk + 1) * BLK)
        grad_up[:, lanes] = ffn_x[blk, 0].astype(F32).T
        grad_down[lanes] = ffn_x[blk, 1].astype(F32)
    for row in range(up_b.shape[0]):
        unit = unit_sums[2 * row + own // 4, pl.ds(6 + layer, 1)]
        moved = pltpu.roll(unit, (BLK - 32 * (own % 4)) % BLK, 1)
        up_b[row : row + 1] = moved[:, :32]
        shift = (BLK - ((row % 2) * HEAD + 8 * own)) % BLK
        for place, target in enumerate((query_b, value_b)):
            unit = unit_sums[per_layer * layer + row // 2, pl.ds(6 + depth + place, 1)]
            target[row : row + 1] = pltpu.roll(unit, shift, 1)[:, :8]
    vec_sums[...] = vec_in[...]


def write_out(depth, *pieces):
    per_layer = 8 // depth
    width = pieces[0].shape[-1]
    rows = jax.ShapeDtypeStruct(pieces[0].shape, BF)
    square = jax.ShapeDtypeStruct((BLK, per_layer * BLK), F32)
    head = jax.ShapeDtypeStruct((4, 8), F32)
    return pl.pallas_call(
        functools.partial(write_body, depth),
        out_shape=[
            rows,
            rows,
            square,
            square,
            square,
            jax.ShapeDtypeStruct((per_layer * BLK, BLK), F32),
            jax.ShapeDtypeStruct((BLK, width), F32),
            jax.ShapeDtypeStruct((width, BLK), F32),
            jax.ShapeDtypeStruct((4, 32), F32),
            head,
            head,
            jax.ShapeDtypeStruct((16, BLK), F32),
        ],
        in_specs=[vmem()] * 6,
        out_specs=[vmem()] * 12,
        name="write_out",
    )(*pieces)


def square_device(
    hidden_in,
    lengths,
    pre_gain,
    pre_shift,
    w_query,
    w_key,
    w_value,
    b_query,
    b_value,
    w_dense,
    b_dense,
    mid_gain,
    mid_shift,
    w_up,
    b_up,
    w_down,
    b_down,
    cotangent,
):
    depth = lax.axis_size("tp")
    pieces = layer_pass(
        depth,
        lengths,
        hidden_in,
        cotangent,
        w_query,
        w_key,
        w_value,
        w_dense,
        w_up,
        w_down,
        pre_gain,
        pre_shift,
        mid_gain,
        mid_shift,
        b_dense,
        b_down,
        b_up,
        b_query,
        b_value,
    )
    (
        output,
        grad_in,
        grad_q,
        grad_k,
        grad_v,
        grad_d,
        grad_up,
        grad_down,
        up_b,
        query_b,
        value_b,
        vec_sums,
    ) = write_out(depth, *pieces)
    return (
        output,
        grad_in,
        vec_sums[0],
        vec_sums[1],
        grad_q,
        grad_k,
        grad_v,
        query_b,
        value_b,
        grad_d,
        vec_sums[2],
        vec_sums[3],
        vec_sums[4],
        grad_up,
        up_b,
        grad_down,
        vec_sums[5],
    )


def solution(mesh):
    square = mesh.shape["wide"] == 8 and mesh.shape["tp"] == 4
    return jax.shard_map(
        square_device if square else per_device,
        mesh=mesh,
        in_specs=(
            P("tp", "wide", None),
            P(),
            P("wide"),
            P("wide"),
            P("wide", "tp"),
            P("wide", "tp"),
            P("wide", "tp"),
            P("tp", "wide"),
            P("tp", "wide"),
            P("tp", "wide"),
            P("wide"),
            P("wide"),
            P("wide"),
            P("wide", "tp"),
            P("tp", "wide"),
            P("tp", "wide"),
            P("wide"),
            P("tp", "wide", None),
        ),
        out_specs=(
            P("tp", "wide", None),
            P("tp", "wide", None),
            P("wide"),
            P("wide"),
            P("wide", "tp"),
            P("wide", "tp"),
            P("wide", "tp"),
            P("tp", "wide"),
            P("tp", "wide"),
            P("tp", "wide"),
            P("wide"),
            P("wide"),
            P("wide"),
            P("wide", "tp"),
            P("tp", "wide"),
            P("tp", "wide"),
            P("wide"),
        ),
        check_vma=False,
    )
```

```python
import functools
import math

import jax
import jax.numpy as jnp
from jax import lax
from jax.experimental import pallas as pl
from jax.experimental.pallas import tpu as pltpu
from jax.sharding import PartitionSpec as P

HEAD = 64
MESH = pl.DeviceIdType.MESH


def norm_rows(values, gain_vec, shift_vec):
    middle = jnp.mean(values, axis=-1, keepdims=True)
    centred = values - middle
    spread = jnp.mean(centred * centred, axis=-1, keepdims=True)
    return centred * lax.rsqrt(spread + 1e-05) * gain_vec + shift_vec


def flatten_rows(tensor):
    return tensor.reshape(-1, tensor.shape[-1])


def row_product(first_op, second_op):
    return jnp.dot(first_op, second_op, preferred_element_type=jnp.float32)


def inner_rows(first_op, second_op):
    return lax.dot_general(
        flatten_rows(first_op),
        flatten_rows(second_op),
        (((0,), (0,)), ((), ())),
        preferred_element_type=jnp.float32,
    )


def times_transposed(first_op, second_op):
    return lax.dot_general(
        first_op,
        second_op,
        (((first_op.ndim - 1,), (1,)), ((), ())),
        preferred_element_type=jnp.float32,
    )


def activate(values):
    return jax.nn.gelu(values, approximate=True)


def masked_scores(query_blk, key_blk, lengths_blk, slopes, distance, causal_mask, key_places):
    raw_scores = (
        jnp.einsum("gihd,gjhd->ghij", query_blk, key_blk, preferred_element_type=jnp.float32)
        * 0.125
    )
    raw_scores = raw_scores - slopes[None, :, None, None] * distance[None, None]
    allowed = causal_mask[None] & (key_places[None, None, :] < lengths_blk[:, None, None])
    return jnp.where(allowed[:, None], raw_scores, -jnp.inf)


def per_device(
    hidden_in,
    lengths,
    pre_gain,
    pre_shift,
    w_query,
    w_key,
    w_value,
    b_query,
    b_value,
    w_dense,
    b_dense,
    mid_gain,
    mid_shift,
    w_up,
    b_up,
    w_down,
    b_down,
    cotangent,
):
    local_slots, block_len, _unused = hidden_in.shape
    heads_dev = b_query.shape[0]
    head_width = heads_dev * HEAD
    slot_total = local_slots * lax.axis_size("tp")
    slot_len = block_len * lax.axis_size("wide")
    wide_at = lax.axis_index("wide")
    tp_at = lax.axis_index("tp")
    vec_part = pre_gain.shape[0]
    (
        gain_one,
        shift_one,
        query_w,
        key_w,
        value_w,
        query_b,
        value_b,
        dense_w,
        dense_b,
        gain_two,
        shift_two,
        up_w,
        up_b,
        down_w,
        down_b,
    ) = (
        lax.all_gather(pre_gain, "wide", axis=0, tiled=True),
        lax.all_gather(pre_shift, "wide", axis=0, tiled=True),
        lax.all_gather(w_query, "wide", axis=0, tiled=True),
        lax.all_gather(w_key, "wide", axis=0, tiled=True),
        lax.all_gather(w_value, "wide", axis=0, tiled=True),
        lax.all_gather(b_query, "wide", axis=1, tiled=True),
        lax.all_gather(b_value, "wide", axis=1, tiled=True),
        lax.all_gather(w_dense, "wide", axis=1, tiled=True),
        lax.all_gather(b_dense, "wide", axis=0, tiled=True),
        lax.all_gather(mid_gain, "wide", axis=0, tiled=True),
        lax.all_gather(mid_shift, "wide", axis=0, tiled=True),
        lax.all_gather(w_up, "wide", axis=0, tiled=True),
        lax.all_gather(b_up, "wide", axis=1, tiled=True),
        lax.all_gather(w_down, "wide", axis=1, tiled=True),
        lax.all_gather(b_down, "wide", axis=0, tiled=True),
    )
    gain_one = gain_one.astype(jnp.float32)
    shift_one = shift_one.astype(jnp.float32)
    gain_two = gain_two.astype(jnp.float32)
    shift_two = shift_two.astype(jnp.float32)
    query_places = wide_at * block_len + jnp.arange(block_len, dtype=jnp.int32)
    key_places = jnp.arange(slot_len, dtype=jnp.int32)
    distance = (query_places[:, None] - key_places[None, :]).astype(jnp.float32)
    causal_mask = key_places[None, :] <= query_places[:, None]
    head_index = tp_at * heads_dev + jnp.arange(heads_dev, dtype=jnp.int32)
    slopes = jnp.exp2(-0.5 * (head_index.astype(jnp.float32) + 1.0))
    own_lengths = lax.dynamic_slice_in_dim(lengths, tp_at * local_slots, local_slots, 0)
    validity = (query_places[None, :] < own_lengths[:, None]).astype(jnp.float32)
    group_size = math.gcd(slot_total, max(1, 512 // block_len))
    group_count = slot_total // group_size
    grouped_lengths = lengths.reshape(group_count, group_size)
    hidden = hidden_in.astype(jnp.float32)

    def query_view(tensor):
        return tensor.reshape(group_count, group_size, block_len, heads_dev, HEAD)

    def pair_view(tensor):
        return tensor.reshape(group_count, group_size, slot_len, 2, heads_dev, HEAD)

    def forward_group(inputs):
        query_blk, pair_blk, lengths_blk = inputs
        masked = masked_scores(
            query_blk, pair_blk[:, :, 0], lengths_blk, slopes, distance, causal_mask, key_places
        )
        highest = jnp.max(masked, axis=-1, keepdims=True)
        totals = highest + jnp.log(jnp.sum(jnp.exp(masked - highest), axis=-1, keepdims=True))
        probabilities = jnp.exp(masked - totals).astype(jnp.bfloat16)
        summed = jnp.einsum(
            "ghij,gjhd->gihd", probabilities, pair_blk[:, :, 1], preferred_element_type=jnp.float32
        )
        return (totals[..., 0], summed)

    def attention_forward(hidden_rows):
        normed_f, norm_back = jax.vjp(norm_rows, hidden_rows, gain_one, shift_one)
        normed = normed_f.astype(jnp.bfloat16)
        normed_all = lax.all_gather(normed, "tp", axis=0, tiled=True)
        queries = (
            row_product(normed_all, query_w) + query_b.reshape(head_width).astype(jnp.float32)
        ).astype(jnp.bfloat16)
        keys_now = row_product(normed_all, key_w).astype(jnp.bfloat16)
        values_now = (
            row_product(normed_all, value_w) + value_b.reshape(head_width).astype(jnp.float32)
        ).astype(jnp.bfloat16)
        pairs = jnp.concatenate([keys_now, values_now], axis=-1)
        pairs_all = lax.all_gather(pairs, "wide", axis=1, tiled=True)
        totals, summed = lax.map(
            forward_group, (query_view(queries), pair_view(pairs_all), grouped_lengths)
        )
        return (
            normed_all,
            queries,
            pairs_all,
            totals,
            summed.reshape(slot_total, block_len, head_width),
            norm_back,
        )

    forward_parts = attention_forward(hidden)
    attention = forward_parts[4].astype(jnp.bfloat16)
    branch = lax.psum_scatter(
        row_product(attention, dense_w).astype(jnp.bfloat16), "tp", scatter_dimension=0, tiled=True
    ).astype(jnp.float32)
    residual = hidden + branch + dense_b.astype(jnp.float32)
    second_f, second_back = jax.vjp(norm_rows, residual, gain_two, shift_two)
    second = second_f.astype(jnp.bfloat16)
    grad_output = validity[:, :, None] * cotangent.astype(jnp.float32)
    grad_down = grad_output.astype(jnp.bfloat16)
    second_all, grad_down_all = (
        lax.all_gather(second, "tp", axis=0, tiled=True),
        lax.all_gather(grad_down, "tp", axis=0, tiled=True),
    )
    pre_act = row_product(second_all, up_w) + up_b.reshape(-1).astype(jnp.float32)
    act_value, act_back = jax.vjp(activate, pre_act)
    activated = act_value.astype(jnp.bfloat16)
    down_out = lax.psum_scatter(
        row_product(activated, down_w).astype(jnp.bfloat16), "tp", scatter_dimension=0, tiled=True
    ).astype(jnp.float32)
    grad_act = times_transposed(grad_down_all, down_w)
    grad_pre = act_back(grad_act)[0].astype(jnp.bfloat16)
    grad_up = inner_rows(second_all, grad_pre)
    grad_up_b = jnp.sum(flatten_rows(grad_pre), axis=0, dtype=jnp.float32).reshape(up_b.shape)
    grad_down_w = inner_rows(activated, grad_down_all)
    grad_second = lax.psum_scatter(
        times_transposed(grad_pre, up_w), "tp", scatter_dimension=0, tiled=True
    )
    output = (validity[:, :, None] * (residual + down_out + down_b.astype(jnp.float32))).astype(
        jnp.bfloat16
    )
    grad_resid_norm, grad_gain_two, grad_shift_two = second_back(grad_second)
    grad_resid = grad_output + grad_resid_norm
    grad_branch = grad_resid.astype(jnp.bfloat16)
    hidden_again, grad_branch = lax.optimization_barrier((hidden, grad_branch))
    forward_parts = attention_forward(hidden_again)
    normed_all, queries, pairs_all, totals, summed, norm_back = forward_parts
    attention_back = summed.astype(jnp.bfloat16)
    branch_all = lax.all_gather(grad_branch, "tp", axis=0, tiled=True)
    grad_dense_w = inner_rows(attention_back, branch_all)
    grad_attention = times_transposed(branch_all, dense_w).astype(jnp.bfloat16)

    def backward_group(inputs):
        query_blk, pair_blk, lengths_blk, totals_blk, grad_blk = inputs
        masked = masked_scores(
            query_blk, pair_blk[:, :, 0], lengths_blk, slopes, distance, causal_mask, key_places
        )
        probabilities = jnp.exp(masked - totals_blk[..., None])
        grad_probs = jnp.einsum(
            "gihd,gjhd->ghij", grad_blk, pair_blk[:, :, 1], preferred_element_type=jnp.float32
        )
        row_delta = jnp.sum(probabilities * grad_probs, axis=-1, keepdims=True)
        grad_scores = (probabilities * (grad_probs - row_delta)).astype(jnp.bfloat16)
        grad_query = (
            jnp.einsum(
                "ghij,gjhd->gihd",
                grad_scores,
                pair_blk[:, :, 0],
                preferred_element_type=jnp.float32,
            )
            * 0.125
        )
        grad_key = (
            jnp.einsum(
                "ghij,gihd->gjhd", grad_scores, query_blk, preferred_element_type=jnp.float32
            )
            * 0.125
        )
        grad_value = jnp.einsum(
            "ghij,gihd->gjhd",
            probabilities.astype(jnp.bfloat16),
            grad_blk,
            preferred_element_type=jnp.float32,
        )
        return (grad_query, jnp.stack([grad_key, grad_value], axis=2))

    grad_query_all, grad_pairs = lax.map(
        backward_group,
        (
            query_view(queries),
            pair_view(pairs_all),
            grouped_lengths,
            totals,
            query_view(grad_attention),
        ),
    )
    grad_pairs_local = lax.psum_scatter(
        grad_pairs.reshape(slot_total, slot_len, 2 * head_width).astype(jnp.bfloat16),
        "wide",
        scatter_dimension=1,
        tiled=True,
    ).astype(jnp.float32)
    grad_queries = grad_query_all.reshape(slot_total, block_len, head_width).astype(jnp.bfloat16)
    grad_keys = grad_pairs_local[:, :, :head_width].astype(jnp.bfloat16)
    grad_values = grad_pairs_local[:, :, head_width:].astype(jnp.bfloat16)
    grad_query_w = inner_rows(normed_all, grad_queries)
    grad_key_w = inner_rows(normed_all, grad_keys)
    grad_value_w = inner_rows(normed_all, grad_values)
    grad_query_b = jnp.sum(flatten_rows(grad_queries), axis=0, dtype=jnp.float32).reshape(
        heads_dev, HEAD
    )
    grad_value_b = jnp.sum(flatten_rows(grad_values), axis=0, dtype=jnp.float32).reshape(
        heads_dev, HEAD
    )
    grad_normed = lax.psum_scatter(
        (
            times_transposed(grad_queries, query_w)
            + times_transposed(grad_keys, key_w)
            + times_transposed(grad_values, value_w)
        ).astype(jnp.bfloat16),
        "tp",
        scatter_dimension=0,
        tiled=True,
    ).astype(jnp.float32)
    grad_hidden_norm, grad_gain_one, grad_shift_one = norm_back(grad_normed)
    grad_in = (grad_resid + grad_hidden_norm).astype(jnp.bfloat16)
    (
        sum_query_w,
        sum_key_w,
        sum_value_w,
        sum_query_b,
        sum_value_b,
        sum_dense_w,
        sum_up_w,
        sum_up_b,
        sum_down_w,
    ) = (
        lax.psum_scatter(
            grad_query_w.astype(jnp.bfloat16), "wide", scatter_dimension=0, tiled=True
        ).astype(jnp.float32),
        lax.psum_scatter(
            grad_key_w.astype(jnp.bfloat16), "wide", scatter_dimension=0, tiled=True
        ).astype(jnp.float32),
        lax.psum_scatter(
            grad_value_w.astype(jnp.bfloat16), "wide", scatter_dimension=0, tiled=True
        ).astype(jnp.float32),
        lax.psum_scatter(
            grad_query_b.astype(jnp.bfloat16), "wide", scatter_dimension=1, tiled=True
        ).astype(jnp.float32),
        lax.psum_scatter(
            grad_value_b.astype(jnp.bfloat16), "wide", scatter_dimension=1, tiled=True
        ).astype(jnp.float32),
        lax.psum_scatter(
            grad_dense_w.astype(jnp.bfloat16), "wide", scatter_dimension=1, tiled=True
        ).astype(jnp.float32),
        lax.psum_scatter(
            grad_up.astype(jnp.bfloat16), "wide", scatter_dimension=0, tiled=True
        ).astype(jnp.float32),
        lax.psum_scatter(
            grad_up_b.astype(jnp.bfloat16), "wide", scatter_dimension=1, tiled=True
        ).astype(jnp.float32),
        lax.psum_scatter(
            grad_down_w.astype(jnp.bfloat16), "wide", scatter_dimension=1, tiled=True
        ).astype(jnp.float32),
    )
    grad_dense_b = jnp.sum(grad_resid, axis=(0, 1))
    grad_down_b = jnp.sum(grad_output, axis=(0, 1))
    sum_gain_one, sum_shift_one, sum_dense_b, sum_gain_two, sum_shift_two, sum_down_b = lax.psum(
        (grad_gain_one, grad_shift_one, grad_dense_b, grad_gain_two, grad_shift_two, grad_down_b),
        ("wide", "tp"),
    )

    def own_part(tensor):
        return lax.dynamic_slice_in_dim(tensor, wide_at * vec_part, vec_part, 0)

    return (
        output,
        grad_in,
        own_part(sum_gain_one),
        own_part(sum_shift_one),
        sum_query_w,
        sum_key_w,
        sum_value_w,
        sum_query_b,
        sum_value_b,
        sum_dense_w,
        own_part(sum_dense_b),
        own_part(sum_gain_two),
        own_part(sum_shift_two),
        sum_up_w,
        sum_up_b,
        sum_down_w,
        own_part(sum_down_b),
    )


BF = jnp.bfloat16
F32 = jnp.float32
LOG2E = 1.4426950408889634
NEG = -1e30
BLK = 128


def hbm():
    return pl.BlockSpec(memory_space=pl.ANY)


def vmem():
    return pl.BlockSpec(memory_space=pltpu.VMEM)


def square_places():
    own = lax.axis_index("wide")
    core = own % 2
    col = (own // 2) % 2
    row = own // 4
    pair = own + 1 - 2 * core
    along_x = own + 2 - 4 * col
    along_y = own + 4 - 8 * row
    return own, pair, along_x, along_y, along_x + along_y - own


def greet(targets):
    barrier = pltpu.get_barrier_semaphore()
    for target in targets:
        pl.semaphore_signal(barrier, inc=1, device_id=target, device_id_type=MESH)
    pl.semaphore_wait(barrier, len(targets))


def remote(src, dst, send_sem, recv_sem, target):
    return pltpu.make_async_remote_copy(
        src_ref=src,
        dst_ref=dst,
        send_sem=send_sem,
        recv_sem=recv_sem,
        device_id=target,
        device_id_type=MESH,
    )


class SquareGather:
    SENDS = 13

    def __init__(self, src, place, both, send, recv, local=None):
        own, pair, ax, ay, dg = square_places()
        first, second, whole = src
        to_x, to_y, to_p = {"wide": ax}, {"wide": ay}, {"wide": pair}
        self.local = None if local is None else pltpu.make_async_copy(whole, both(own), local)
        copies = {}
        copies["x0"] = remote(first, place(0, own), send.at[0], recv.at[0], to_x)
        copies["x1"] = remote(second, place(1, own), send.at[1], recv.at[1], to_x)
        copies["y0"] = remote(first, place(0, own), send.at[2], recv.at[2], to_y)
        copies["y1"] = remote(second, place(1, own), send.at[3], recv.at[3], to_y)
        copies["d0"] = remote(place(0, ay), place(0, ay), send.at[4], recv.at[4], to_x)
        copies["d1"] = remote(place(1, ax), place(1, ax), send.at[5], recv.at[5], to_y)
        copies["p"] = remote(whole, both(own), send.at[6], recv.at[6], to_p)
        for index, (name, slot, dev) in enumerate(
            (("x0", 0, ax), ("x1", 1, ax), ("y0", 0, ay), ("y1", 1, ay), ("d0", 0, dg), ("d1", 1, dg))
        ):
            copies["p" + name] = remote(
                place(slot, dev), place(slot, dev), send.at[7 + index], recv.at[7 + index], to_p
            )
        self.copies = copies

    def start(self):
        for name in ("y0", "x1", "x0", "y1", "p"):
            self.copies[name].start()
        if self.local is not None:
            self.local.start()

    def pass_on(self, arrived, sends):
        self.copies[arrived].wait_recv()
        for name in sends:
            self.copies[name].start()

    def first(self):
        self.pass_on("y0", ("d0", "py0"))
        self.pass_on("x1", ("d1", "px1"))

    def second(self):
        self.pass_on("x0", ("px0",))
        self.pass_on("y1", ("py1",))

    def third(self):
        self.pass_on("d0", ("pd0",))
        self.pass_on("d1", ("pd1",))

    def arrive(self, *names):
        for name in names:
            self.copies[name].wait_recv()

    def sent(self):
        for copy in self.copies.values():
            copy.wait_send()


def wide_square(own_places):
    _own, pair, ax, ay, _dg = own_places
    return [{"wide": pair}, {"wide": ax}, {"wide": ay}]


def add_rows(dst, first, second, third=None):
    step = 16

    def body(index, carry):
        rows = pl.ds(pl.multiple_of(index * step, step), step)
        total = first[rows].astype(F32) + second[rows].astype(F32)
        if third is not None:
            total = total + third[rows].astype(F32)
        dst[rows] = total.astype(dst.dtype)
        return carry

    lax.fori_loop(0, BLK // step, body, 0)


class SquareScatter:
    SENDS = 10

    def __init__(self, both, half, out, summed_both, summed, from_x, from_y, send, recv):
        own, pair, ax, ay, dg = square_places()
        shift = pair - own
        to_x, to_y, to_p = {"wide": ax}, {"wide": ay}, {"wide": pair}
        self.half, self.out = half, out
        self.summed, self.from_x, self.from_y = summed, from_x, from_y
        self.dests = (dg, ax, ay, own)
        self.pairs = [
            remote(
                both(self.dests[chip] + shift), summed_both(chip), send.at[chip], recv.at[chip], to_p
            )
            for chip in range(4)
        ]
        self.dx = remote(summed(0, 0), from_x(0), send.at[4], recv.at[4], to_x)
        self.dy = remote(summed(0, 1), from_y(0), send.at[5], recv.at[5], to_y)
        self.xx = remote(summed(1, 0), from_x(1), send.at[6], recv.at[6], to_x)
        self.yy = remote(summed(2, 1), from_y(1), send.at[7], recv.at[7], to_y)
        self.ty = remote(summed(2, 0), from_y(2), send.at[8], recv.at[8], to_y)
        self.tx = remote(summed(1, 1), from_x(2), send.at[9], recv.at[9], to_x)

    def pair_sum(self, chip, slot, third=None):
        place = self.summed(chip, slot)
        add_rows(place, self.half(slot, self.dests[chip]), place, third)

    def near(self, chip):
        self.pairs[chip].wait_recv()
        if chip == 0:
            self.pair_sum(0, 0)
            self.dx.start()
            self.pair_sum(0, 1)
            self.dy.start()
        elif chip == 1:
            self.pair_sum(1, 0)
            self.xx.start()
        elif chip == 2:
            self.pair_sum(2, 1)
            self.yy.start()
        else:
            self.pair_sum(3, 0)
            self.pair_sum(3, 1)

    def middle(self):
        self.dx.wait_recv()
        self.pair_sum(2, 0, self.from_x(0))
        self.ty.start()
        self.dy.wait_recv()
        self.pair_sum(1, 1, self.from_y(0))
        self.tx.start()

    def start(self):
        for chip in range(4):
            self.pairs[chip].start()

    def finish(self):
        self.xx.wait_recv()
        self.ty.wait_recv()
        add_rows(self.out.at[0], self.summed(3, 0), self.from_x(1), self.from_y(2))
        self.yy.wait_recv()
        self.tx.wait_recv()
        add_rows(self.out.at[1], self.summed(3, 1), self.from_y(1), self.from_x(2))
        for copy in self.pairs:
            copy.wait_send()
        for copy in (self.dx, self.dy, self.xx, self.yy, self.ty, self.tx):
            copy.wait_send()


class LineGather:
    def __init__(self, depth, pieces, send, recv):
        self.depth, self.pieces, self.send, self.recv = depth, pieces, send, recv
        self.layer = lax.axis_index("tp")

    def copies(self, step, up):
        index = self.layer - step + 1 if up else self.layer + step - 1
        goal = {"tp": self.layer + 1 if up else self.layer - 1}
        side = 0 if up else 1
        made = []
        for number, (own, place) in enumerate(self.pieces):
            source = own if step == 1 else place(index)
            made.append(
                remote(
                    source,
                    place(index),
                    self.send.at[side, number, step - 1],
                    self.recv.at[side, number, step - 1],
                    goal,
                )
            )
        return made

    def each(self, step, act):
        layer = self.layer

        @pl.when((layer < self.depth - 1) & (layer - step + 1 >= 0))
        def _():
            for copy in self.copies(step, True):
                act(copy)

        @pl.when((layer > 0) & (layer + step - 1 < self.depth))
        def _():
            for copy in self.copies(step, False):
                act(copy)

    def start(self, step):
        self.each(step, lambda copy: copy.start())

    def sent(self, step):
        self.each(step, lambda copy: copy.wait_send())

    def arrive(self, step):
        layer = self.layer

        @pl.when(layer - step >= 0)
        def _():
            for copy in self.copies(step, True):
                copy.wait_recv()

        @pl.when(layer + step < self.depth)
        def _():
            for copy in self.copies(step, False):
                copy.wait_recv()


def wide_others(own):
    return [{"wide": (own + step) % 8} for step in range(1, 8)]


def head_bias(length, slope, rows):
    place = lax.broadcasted_iota(jnp.int32, (rows, QB), 0)
    return jnp.where(place < length, slope * place.astype(F32), NEG)


QB = 256


def dot_nt(first, second):
    return lax.dot_general(first, second, (((1,), (1,)), ((), ())), preferred_element_type=F32)


def dot_nn(first, second):
    return lax.dot_general(first, second, (((1,), (0,)), ((), ())), preferred_element_type=F32)


def later_key(size):
    key_place = lax.broadcasted_iota(jnp.int32, (size, size), 0)
    query_place = lax.broadcasted_iota(jnp.int32, (size, size), 1)
    return key_place > query_place


def slot_scores(key, query, bias, step):
    extent = (step + 1) * QB
    scores = dot_nt(key[:extent], query) * (0.125 * LOG2E) + bias[:extent]
    edge = jnp.where(later_key(QB), NEG, scores[extent - QB :])
    return edge if step == 0 else jnp.concatenate([scores[: extent - QB], edge], 0)


def attend_head(slot, head, length, slopes, qkv, out, totals, bias):
    rows = qkv.shape[1]
    lanes = pl.ds(head * HEAD, HEAD)
    bias[...] = head_bias(length, slopes[head], rows)
    key = qkv[slot, :, pl.ds(2 * HEAD + head * HEAD, HEAD)]
    value_t = qkv[slot, :, pl.ds(4 * HEAD + head * HEAD, HEAD)].T
    for step in range(rows // QB):
        here = pl.ds(step * QB, QB)
        scores = slot_scores(key, qkv[slot, here, lanes], bias, step)
        highest = jnp.max(scores, axis=0, keepdims=True)
        weights = jnp.exp2(scores - highest)
        total = jnp.sum(weights, axis=0, keepdims=True)
        mixed = dot_nn(value_t[:, : (step + 1) * QB], weights.astype(BF)) / total
        out[slot, here, lanes] = mixed.T.astype(BF)
        totals[slot, pl.ds(head, 1), here] = highest + jnp.log2(total)


def attend_head_back(
    slot, head, length, slopes, qkv, attention, grad, totals, out, bias, key_sum, value_sum
):
    rows = qkv.shape[1]
    lanes = pl.ds(head * HEAD, HEAD)
    key_lanes = pl.ds(2 * HEAD + head * HEAD, HEAD)
    value_lanes = pl.ds(4 * HEAD + head * HEAD, HEAD)
    bias[...] = head_bias(length, slopes[head], rows)
    key = qkv[slot, :, key_lanes]
    value = qkv[slot, :, value_lanes]
    key_t = key.T
    key_sum[...] = jnp.zeros_like(key_sum)
    value_sum[...] = jnp.zeros_like(value_sum)
    for step in range(rows // QB):
        here = pl.ds(step * QB, QB)
        extent = (step + 1) * QB
        query = qkv[slot, here, lanes]
        grad_rows = grad[slot, here, lanes]
        product = grad_rows.astype(F32) * attention[slot, here, lanes].astype(F32)
        delta = jnp.sum(product.T, axis=0, keepdims=True)
        scores = slot_scores(key, query, bias, step)
        probs = jnp.exp2(scores - totals[slot, pl.ds(head, 1), here])
        grad_probs = dot_nt(value[:extent], grad_rows)
        grad_scores = (probs * (grad_probs - delta)).astype(BF)
        span = pl.ds(0, extent)
        value_sum[span] += dot_nn(probs.astype(BF), grad_rows)
        key_sum[span] += dot_nn(grad_scores, query)
        grad_query = dot_nn(key_t[:, :extent], grad_scores)
        out[slot, here, lanes] = (grad_query.T * 0.125).astype(BF)
    out[slot, :, key_lanes] = (key_sum[...] * 0.125).astype(BF)
    out[slot, :, value_lanes] = value_sum[...].astype(BF)


def line_others(depth):
    layer = lax.axis_index("tp")
    return [{"tp": (layer + step) % depth} for step in range(1, depth)]


VMEM_MAX = 67043328


def norm_stats(values):
    middle = jnp.mean(values, axis=-1, keepdims=True)
    centred = values - middle
    spread = jnp.mean(centred * centred, axis=-1, keepdims=True)
    inverse = lax.rsqrt(spread + 1e-05)
    return centred * inverse, inverse


def norm_back_rows(grad, hat, inverse, gain):
    scaled = grad * gain
    first = jnp.mean(scaled, axis=-1, keepdims=True)
    second = jnp.mean(scaled * hat, axis=-1, keepdims=True)
    return (scaled - first - hat * second) * inverse


def gelu_parts(values):
    root = math.sqrt(2 / math.pi)
    squared = values * values
    inner = jnp.tanh(root * values * (1.0 + 0.044715 * squared))
    half = 0.5 * (1.0 + inner)
    slope = half + 0.5 * values * (1.0 - inner * inner) * root * (1.0 + 3 * 0.044715 * squared)
    return values * half, slope


def relation(index):
    own = lax.axis_index("wide")
    core = (own + index) % 2
    col = (own // 2 + index // 2) % 2
    row = (own // 4 + index // 4) % 2
    return row * 4 + col * 2 + core


class WideExchange:
    def __init__(self, source, target, send, recv):
        own = lax.axis_index("wide")
        self.copies = [
            remote(
                source((own + step) % 8),
                target(own),
                send.at[step - 1],
                recv.at[step - 1],
                {"wide": (own + step) % 8},
            )
            for step in range(1, 8)
        ]

    def start(self):
        for copy in self.copies:
            copy.start()

    def arrive(self):
        for copy in self.copies:
            copy.wait_recv()

    def sent(self):
        for copy in self.copies:
            copy.wait_send()


def layer_body(
    depth,
    lengths,
    hidden,
    cotangent,
    w_query,
    w_key,
    w_value,
    w_dense,
    w_up,
    w_down,
    pre_gain,
    pre_shift,
    mid_gain,
    mid_shift,
    b_dense,
    b_down,
    b_up,
    b_query,
    b_value,
    output,
    grad_in,
    attn_sum,
    dense_sum,
    ffn_x,
    vec_sums,
    unit_sums,
    hidden_all,
    normed,
    down_all,
    second_share,
    down_share,
    qkv,
    attention,
    grad_att,
    act_t,
    pre_t,
    totals,
    bias,
    key_sum,
    value_sum,
    qkv_w,
    dense_all,
    att_own,
    att_grad_own,
    up_t,
    down_t,
    up_w,
    down_w,
    z_qkv,
    z_vec,
    vec_wide,
    vec_line,
    vec_wide_all,
    vec_line_all,
    vectors,
    up_bias,
    qkv_bias,
    own_rows,
    down_own,
    residual,
    grad_second,
    grad_resid,
    down_out,
    sums,
    up_sum,
    ffn_g,
    ffn_in,
    ffn_sum,
    attn_g,
    attn_in,
    attn_z,
    dense_out,
    dense_in,
    parts,
    gathered,
    a_summed,
    a_x,
    a_y,
    b_summed,
    b_x,
    b_y,
    gather_send,
    gather_recv,
    gather_local,
    scatter_send,
    scatter_recv,
    line_send,
    line_recv,
    ffn_line_send,
    ffn_line_recv,
    wide_send,
    wide_recv,
    grad_line_send,
    grad_line_recv,
    onward_send,
    onward_recv,
    dense_send,
    dense_recv,
    sum_send,
    sum_recv,
    own_sems,
):
    own = lax.axis_index("wide")
    layer = lax.axis_index("tp")
    per_layer = 8 // depth
    width = hidden.shape[-1]
    step = 32
    steps = BLK // step
    others = [
        ((own + side) % 8, (layer + up) % depth)
        for up in range(depth)
        for side in range(8)
        if up or side
    ]
    own_lanes = pl.ds(pl.multiple_of(own * BLK, BLK), BLK)

    for place, ref in enumerate((pre_gain, pre_shift, mid_gain, mid_shift, b_dense, b_down)):
        vec_wide[pl.ds(place, 1)] = ref[...].astype(F32)
    vec_line[...] = jnp.zeros_like(vec_line)
    vec_line[0 : b_up.shape[0], 0 : b_up.shape[1]] = b_up[...].astype(F32)
    vec_line[b_up.shape[0] :, 0:8] = b_query[...].astype(F32)
    vec_line[b_up.shape[0] :, 8:16] = b_value[...].astype(F32)
    first_row = own * BLK

    def token_mask(slot, rows, count):
        place = first_row + rows * count + lax.broadcasted_iota(jnp.int32, (count, BLK), 0)
        inside = place < lengths[layer * 2 + slot]
        return jnp.where(inside, 1.0, 0.0).astype(F32)[:, :1]

    def down_part(index, carry):
        rows = pl.ds(pl.multiple_of(index * step, step), step)
        for slot in range(2):
            values = token_mask(slot, index, step) * cotangent[slot, rows].astype(F32)
            down_own[slot, rows] = values.astype(BF)
        return carry

    lax.fori_loop(0, steps, down_part, 0)
    greet(wide_others(own) + line_others(depth))

    def block_rows(dev):
        return pl.ds(pl.multiple_of(dev * BLK, BLK), BLK)

    def gather_of(number, src, dst):
        return SquareGather(
            (src.at[0], src.at[1], src),
            lambda slot, dev: dst.at[slot, block_rows(dev)],
            lambda dev: dst.at[:, block_rows(dev)],
            gather_send.at[number],
            gather_recv.at[number],
            gather_local.at[number],
        )

    def wide_of(number, source, target):
        return WideExchange(source, target, wide_send.at[number], wide_recv.at[number])

    gains = wide_of(0, lambda dev: vec_wide, lambda dev: vec_wide_all.at[dev])
    gains.start()
    hid = gather_of(0, hidden, hidden_all)
    hid.start()
    line = LineGather(
        depth,
        [
            (w_query, lambda at: z_qkv.at[at, 0]),
            (w_key, lambda at: z_qkv.at[at, 1]),
            (w_value, lambda at: z_qkv.at[at, 2]),
            (w_dense, lambda at: dense_all.at[own, at]),
            (vec_line, lambda at: z_vec.at[at]),
        ],
        line_send,
        line_recv,
    )
    line.start(1)
    own_copies = [
        pltpu.make_async_copy(ref, place(layer), own_sems.at[number])
        for number, (ref, place) in enumerate(line.pieces)
    ]
    for copy in own_copies:
        copy.start()
    vec_wide_all[own] = vec_wide[...]
    gains.arrive()
    for dev in range(8):
        vectors[:, dev * BLK : (dev + 1) * BLK] = vec_wide_all[dev]

    def norm_block(index, carry):
        base = relation(index) * BLK

        def norm_part(part, carry):
            rows = pl.ds(pl.multiple_of(base + part * step, step), step)
            for slot in range(2):
                hat, _inverse = norm_stats(hidden_all[slot, rows].astype(F32))
                normed[slot, rows] = (hat * vectors[0:1] + vectors[1:2]).astype(BF)
            return carry

        return lax.fori_loop(0, steps, norm_part, carry)

    hid.arrive("p")
    hid.local.wait()
    lax.fori_loop(0, 2, norm_block, 0)
    hid.first()
    line.arrive(1)
    line.start(2)
    hid.second()
    ups = wide_of(
        3, lambda dev: w_up.at[:, block_rows(dev)], lambda dev: up_t.at[block_rows(dev)]
    )
    downs = wide_of(
        4, lambda dev: w_down.at[block_rows(dev)], lambda dev: down_t.at[:, block_rows(dev)]
    )
    unit_copies = [
        pltpu.make_async_copy(w_up.at[:, own_lanes], up_t.at[own_lanes], own_sems.at[6]),
        pltpu.make_async_copy(w_down.at[own_lanes], down_t.at[:, own_lanes], own_sems.at[7]),
    ]
    ups.start()
    downs.start()
    for copy in unit_copies:
        copy.start()
    line.arrive(2)
    line.start(3)
    hid.arrive("px0", "px1", "py0", "py1")
    lax.fori_loop(2, 6, norm_block, 0)
    hid.third()
    line.arrive(3)
    for copy in own_copies:
        copy.wait()

    def goal_lanes(dev):
        return pl.ds(pl.multiple_of((dev % per_layer) * BLK, BLK), BLK)

    heads = wide_of(
        1,
        lambda dev: z_qkv.at[dev // per_layer, :, :, goal_lanes(dev)],
        lambda dev: attn_in.at[dev],
    )
    biases = wide_of(2, lambda dev: z_vec, lambda dev: vec_line_all.at[dev])
    dense = SquareGather(
        (dense_all.at[own, pl.ds(0, 2)], dense_all.at[own, pl.ds(2, 2)], dense_all.at[own]),
        lambda half, dev: dense_all.at[dev, pl.ds(2 * half, 2)],
        lambda dev: dense_all.at[dev],
        gather_send.at[3],
        gather_recv.at[3],
    )
    biases.start()
    heads.start()
    dense.start()
    gd = gather_of(1, down_own, down_all)
    own_copies = [
        pltpu.make_async_copy(z_qkv.at[own // per_layer, :, :, goal_lanes(own)], attn_in.at[own], own_sems.at[5]),
    ]
    for copy in own_copies:
        copy.start()
    vec_line_all[own] = z_vec[...]
    hid.arrive("pd0", "pd1")
    lax.fori_loop(6, 8, norm_block, 0)
    biases.arrive()
    head_layer = own // per_layer
    piece = own % per_layer
    unit_row = own // 2
    for dev in range(8):
        for head in range(2):
            lanes = slice(head * HEAD + dev * 8, head * HEAD + dev * 8 + 8)
            row = pl.ds(b_up.shape[0] + 2 * piece + head, 1)
            values = vec_line_all[dev, head_layer, row]
            qkv_bias[:, lanes] = values[:, 0:8]
            lanes = slice(4 * HEAD + lanes.start, 4 * HEAD + lanes.stop)
            qkv_bias[:, lanes] = values[:, 8:16]
    qkv_bias[:, 2 * HEAD : 4 * HEAD] = jnp.zeros((1, 2 * HEAD), F32)
    for up in range(depth):
        for part in range(4):
            values = vec_line_all[4 * (own % 2) + part, up, pl.ds(unit_row, 1)]
            up_bias[:, up * BLK + part * 32 : up * BLK + part * 32 + 32] = values[:, 0:32]
    heads.arrive()
    hid.sent()
    for copy in own_copies + unit_copies:
        copy.wait()
    ups.arrive()
    downs.arrive()
    for dev in range(8):
        for kind in range(3):
            qkv_w[dev * BLK : (dev + 1) * BLK, kind * BLK : (kind + 1) * BLK] = attn_in[dev, kind]

    ffn_line = LineGather(
        depth,
        [
            (up_t, lambda at: up_w.at[:, pl.ds(pl.multiple_of(at * BLK, BLK), BLK)]),
            (down_t, lambda at: down_w.at[pl.ds(pl.multiple_of(at * BLK, BLK), BLK)]),
        ],
        ffn_line_send,
        ffn_line_recv,
    )
    ffn_line.start(1)
    unit_copies = [
        pltpu.make_async_copy(ref, place(layer), own_sems.at[8 + number])
        for number, (ref, place) in enumerate(ffn_line.pieces)
    ]
    for copy in unit_copies:
        copy.start()
    slopes = [
        jnp.exp2(-0.5 * (jnp.full((1, 1), 2 * own + head, jnp.int32).astype(F32) + 1.0)) * LOG2E
        for head in range(2)
    ]

    def att_exchange(slot):
        return wide_of(
            7 + slot,
            lambda dev: attention.at[slot, block_rows(dev)],
            lambda dev: att_own.at[slot, :, block_rows(dev)],
        )

    def att_local(slot):
        return pltpu.make_async_copy(
            attention.at[slot, block_rows(own)], att_own.at[slot, :, block_rows(own)], own_sems.at[10 + slot]
        )

    def one_slot(slot, carry):
        def block(index, carry):
            rows = pl.ds(pl.multiple_of(index * QB, QB), QB)
            qkv[slot, rows] = (dot_nn(normed[slot, rows], qkv_w[...]) + qkv_bias[...]).astype(BF)
            return carry

        lax.fori_loop(0, 8 * BLK // QB, block, 0)
        length = lengths[layer * 2 + slot]
        attend_head(slot, 0, length, slopes, qkv, attention, totals, bias)

        @pl.when(slot == 0)
        def _():
            dense.first()
            dense.second()

        attend_head(slot, 1, length, slopes, qkv, attention, totals, bias)
        att_exchange(slot).start()
        att_local(slot).start()

        @pl.when(slot == 0)
        def _():
            ffn_line.arrive(1)
            ffn_line.start(2)
            dense.third()
            gd.start()

        return carry

    lax.fori_loop(0, 2, one_slot, 0)
    gd.first()
    gd.second()
    ffn_line.arrive(2)
    ffn_line.start(3)
    dense.arrive("p", "px0", "px1", "py0", "py1", "pd0", "pd1")
    for slot in range(2):
        att_exchange(slot).arrive()
        att_local(slot).wait()

    for part in range(4):
        columns = [dense_all[2 * part + side].reshape(width, BLK) for side in range(2)]
        product = dot_nn(att_own[...].reshape(2 * BLK, width), jnp.concatenate(columns, 1))
        residual[:, :, part * QB : (part + 1) * QB] = product.reshape(2, BLK, QB)

    def scatter_of(number, share, out, buffers):
        summed, from_x, from_y = buffers
        return SquareScatter(
            lambda dev: share.at[:, block_rows(dev)],
            lambda slot, dev: share.at[slot, block_rows(dev)],
            out,
            lambda chip: summed.at[chip],
            lambda chip, slot: summed.at[chip, slot],
            lambda place: from_x.at[place],
            lambda place: from_y.at[place],
            scatter_send.at[number],
            scatter_recv.at[number],
        )

    def second_part(index, carry):
        rows = pl.ds(pl.multiple_of(index * step, step), step)
        for slot in range(2):
            values = hidden[slot, rows].astype(F32) + residual[slot, rows] + vectors[4:5]
            residual[slot, rows] = values
            hat, _inverse = norm_stats(values)
            own_rows[slot, rows] = (hat * vectors[2:3] + vectors[3:4]).astype(BF)
        return carry

    lax.fori_loop(0, steps, second_part, 0)
    second_all = hidden_all
    gather = gather_of(2, own_rows, second_all)
    gather.start()
    scatter = scatter_of(0, second_share, grad_second, (a_summed, a_x, a_y))
    gd.arrive("p")
    gd.local.wait()
    for copy in unit_copies:
        copy.wait()
    ffn_line.arrive(3)

    def compute(index, carry):
        source = relation(index)
        rows = pl.ds(pl.multiple_of(source * BLK, BLK), BLK)
        values = second_all[:, rows].reshape(2 * BLK, width)
        act_value, act_slope = gelu_parts(dot_nn(values, up_w[...]) + up_bias[...])
        activated = act_value.astype(BF)
        grad_rows = down_all[:, rows].reshape(2 * BLK, width)
        grad_pre = (dot_nt(grad_rows, down_w[...]) * act_slope).astype(BF)
        second_share[:, rows] = dot_nt(grad_pre, up_w[...]).astype(BF).reshape(2, BLK, width)
        down_share[:, rows] = dot_nn(activated, down_w[...]).astype(BF).reshape(2, BLK, width)
        up_sum[...] += jnp.sum(grad_pre.astype(F32), axis=0, keepdims=True)
        for slot in range(2):
            lanes = pl.ds(pl.multiple_of(slot * 8 * BLK + source * BLK, BLK), BLK)
            part = slice(slot * BLK, (slot + 1) * BLK)
            act_t[:, lanes] = activated[part].T
            pre_t[:, lanes] = grad_pre[part].T
        return carry

    up_sum[...] = jnp.zeros_like(up_sum)
    gather.arrive("p")
    gather.local.wait()
    lax.fori_loop(0, 2, compute, 0)
    scatter.pairs[3].start()
    gather.first()
    gd.third()
    gather.second()
    gd.arrive("px0", "px1", "py0", "py1")
    gather.arrive("px0", "px1", "py0", "py1")
    lax.fori_loop(2, 4, compute, 0)
    scatter.pairs[1].start()
    scatter.near(3)
    lax.fori_loop(4, 6, compute, 0)
    scatter.pairs[2].start()
    gather.third()
    scatter.near(1)
    gd.arrive("pd0", "pd1")
    gather.arrive("pd0", "pd1")
    lax.fori_loop(6, 8, compute, 0)
    scatter.pairs[0].start()
    scatter.near(2)
    scatter.near(0)

    def weight_grads(left, right, kind):
        def one(up, carry):
            rows = pl.ds(pl.multiple_of(up * BLK, BLK), BLK)
            total = dot_nn(left[rows, pl.ds(0, 8 * BLK)], right[0])
            total = total + dot_nn(left[rows, pl.ds(8 * BLK, 8 * BLK)], right[1])
            total = total.astype(BF)
            for blk in range(8):
                ffn_g[kind, up, blk] = total[:, blk * BLK : (blk + 1) * BLK]
            return carry

        lax.fori_loop(0, depth, one, 0)

    def line_copies(kind):
        return [
            remote(
                ffn_g.at[kind, (layer + up) % depth],
                ffn_in.at[kind, up - 1],
                grad_line_send.at[kind, up - 1],
                grad_line_recv.at[kind, up - 1],
                {"tp": (layer + up) % depth},
            )
            for up in range(1, depth)
        ]

    def line_sums(kind):
        for copy in line_copies(kind):
            copy.wait_recv()

        def add_block(blk, carry):
            total = ffn_g[kind, layer, blk].astype(F32)
            for up in range(depth - 1):
                total = total + ffn_in[kind, up, blk].astype(F32)
            ffn_sum[blk, kind] = total.astype(BF)
            return carry

        lax.fori_loop(0, 8, add_block, 0)

    weight_grads(pre_t, second_all, 0)
    for copy in line_copies(0):
        copy.start()
    scatter.middle()
    weight_grads(act_t, down_all, 1)
    for copy in line_copies(1):
        copy.start()
    scatter.finish()
    gather.sent()
    sums[...] = jnp.zeros_like(sums)

    def back_part(index, carry):
        rows = pl.ds(pl.multiple_of(index * step, step), step)
        for slot in range(2):
            hat, inverse = norm_stats(residual[slot, rows])
            grad = grad_second[slot, rows]
            grad_out = token_mask(slot, index, step) * cotangent[slot, rows].astype(F32)
            total = grad_out + norm_back_rows(grad, hat, inverse, vectors[2:3])
            grad_resid[slot, rows] = total
            own_rows[slot, rows] = total.astype(BF)
            for place, value in enumerate((total, grad * hat, grad, grad_out)):
                sums[pl.ds(place, 1)] += jnp.sum(value, axis=0, keepdims=True)
        return carry

    lax.fori_loop(0, steps, back_part, 0)
    for at in range(depth):
        columns = jnp.concatenate([dense_all[dev, at] for dev in range(8)], 1)
        product = dot_nt(own_rows[...].reshape(2 * BLK, width), columns).astype(BF)
        att_grad_own[:, :, at * QB : (at + 1) * QB] = product.reshape(2, BLK, QB)

    def att_back(slot):
        return wide_of(
            9 + slot,
            lambda dev: att_grad_own.at[slot, :, block_rows(dev)],
            lambda dev: grad_att.at[slot, block_rows(dev)],
        )

    def att_back_local(slot):
        return pltpu.make_async_copy(
            att_grad_own.at[slot, :, block_rows(own)], grad_att.at[slot, block_rows(own)], own_sems.at[12 + slot]
        )

    for slot in range(2):
        att_back(slot).start()
        att_back_local(slot).start()
    down = scatter_of(1, down_share, down_out, (b_summed, b_x, b_y))
    down.start()

    half_lanes = pl.ds(0, width // 2)
    sum_lanes = pl.ds(width // 2, width // 2)
    for part in range(4):
        rows = slice(part * QB, (part + 1) * QB)
        left = own_rows[:, :, rows].reshape(2 * BLK, QB).T
        for half in range(2):
            lanes = slice(half * width // 2, (half + 1) * width // 2)
            product = dot_nn(left, att_own[:, :, lanes].reshape(2 * BLK, width // 2))
            second_all[half, rows, half_lanes] = product.astype(BF)
    dense_back = SquareScatter(
        lambda dev: second_all.at[:, block_rows(dev), half_lanes],
        lambda half, dev: second_all.at[half, block_rows(dev), half_lanes],
        dense_out,
        lambda chip: second_all.at[:, pl.ds(chip * BLK, BLK), sum_lanes],
        lambda chip, half: second_all.at[half, pl.ds(chip * BLK, BLK), sum_lanes],
        lambda place: second_all.at[0, pl.ds((4 + place) * BLK, BLK), sum_lanes],
        lambda place: second_all.at[1, pl.ds((4 + place) * BLK, BLK), sum_lanes],
        scatter_send.at[3],
        scatter_recv.at[3],
    )

    def dense_piece(at):
        return dense_out.at[at // 2, :, pl.ds(pl.multiple_of((at % 2) * QB, QB), QB)]

    def dense_copies():
        return [
            remote(
                dense_piece((layer + up) % depth),
                dense_in.at[up - 1],
                dense_send.at[up - 1],
                dense_recv.at[up - 1],
                {"tp": (layer + up) % depth},
            )
            for up in range(1, depth)
        ]

    att_back(0).arrive()
    att_back_local(0).wait()
    dense_back.start()
    for chip in range(3):
        down.near(chip)
    for chip in range(3):
        dense_back.near(chip)

    def ffn_exchange(kind):
        return wide_of(5 + kind, lambda dev: ffn_sum.at[dev, kind], lambda dev: ffn_x.at[dev, kind])

    def slot_back(slot, carry):
        def one_head(head):
            attend_head_back(
                slot,
                head,
                lengths[layer * 2 + slot],
                slopes,
                qkv,
                attention,
                grad_att,
                totals,
                qkv,
                bias,
                key_sum,
                value_sum,
            )

        one_head(0)

        @pl.when(slot == 0)
        def _():
            down.near(3)
            down.middle()
            dense_back.near(3)

        @pl.when(slot == 1)
        def _():
            dense_back.finish()
            for copy in dense_copies():
                copy.start()
            line_sums(0)
            ffn_exchange(0).start()

        one_head(1)

        @pl.when(slot == 0)
        def _():
            dense_back.middle()
            att_back(1).arrive()
            att_back_local(1).wait()

        return carry

    lax.fori_loop(0, 2, slot_back, 0)
    grad_qkv = qkv
    weight_part = dot_nn(grad_qkv[0].T, normed[0]) + dot_nn(grad_qkv[1].T, normed[1])
    weight_part = weight_part.astype(BF)
    for kind in range(3):
        for blk in range(8):
            attn_g[blk, kind] = weight_part[
                kind * BLK : (kind + 1) * BLK, blk * BLK : (blk + 1) * BLK
            ]
    exchange = wide_of(11, lambda dev: attn_g.at[dev], lambda dev: attn_in.at[dev])

    def onward(index, source):
        return remote(
            source.at[index],
            attn_z.at[layer, index % per_layer],
            onward_send.at[index],
            onward_recv.at[layer, index % per_layer],
            {"tp": index // per_layer},
        )

    def forward(index, source):
        @pl.when(index // per_layer != layer)
        def _():
            onward(index, source).start()

    exchange.start()
    forward(own, attn_g)
    share = second_share
    grad_normed = grad_second
    scatter = scatter_of(2, share, grad_normed, (a_summed, a_x, a_y))

    def normed_block(index, carry):
        rows = pl.ds(pl.multiple_of(relation(index) * BLK, BLK), BLK)
        values = grad_qkv[:, rows].reshape(2 * BLK, 6 * HEAD)
        share[:, rows] = dot_nt(values, qkv_w[...]).astype(BF).reshape(2, BLK, width)
        return carry

    for chip in range(4):
        start = (6, 2, 4, 0)[chip]
        lax.fori_loop(start, start + 2, normed_block, 0)
        scatter.pairs[chip].start()
        if chip:
            scatter.near(chip - 1)
    line_sums(1)
    ffn_exchange(1).start()
    head_sum = jnp.sum(grad_qkv[0].astype(F32), axis=0, keepdims=True)
    head_sum = head_sum + jnp.sum(grad_qkv[1].astype(F32), axis=0, keepdims=True)
    down.finish()

    def out_part(index, carry):
        rows = pl.ds(pl.multiple_of(index * step, step), step)
        for slot in range(2):
            total = residual[slot, rows] + down_out[slot, rows] + vectors[5:6]
            output[slot, rows] = (token_mask(slot, index, step) * total).astype(BF)
        return carry

    lax.fori_loop(0, steps, out_part, 0)
    for number in range(1, 8):
        exchange.copies[number - 1].wait_recv()
        forward((own + 8 - number) % 8, attn_in)
    scatter.near(3)
    scatter.middle()
    for blk in range(8):
        lanes = slice(blk * BLK, (blk + 1) * BLK)
        for place in range(4):
            parts[blk, pl.ds(2 + place, 1)] = sums[place : place + 1, lanes]
        for place in range(depth):
            parts[blk, pl.ds(6 + place, 1)] = up_sum[:, place * BLK : (place + 1) * BLK]
        parts[blk, pl.ds(6 + depth, 1)] = head_sum[:, : 2 * HEAD]
        parts[blk, pl.ds(7 + depth, 1)] = head_sum[:, 4 * HEAD :]
    scatter.finish()

    def last_part(index, carry):
        gain_sum, shift_sum = carry
        rows = pl.ds(pl.multiple_of(index * step, step), step)
        for slot in range(2):
            hat, inverse = norm_stats(hidden[slot, rows].astype(F32))
            grad = grad_normed[slot, rows]
            total = grad_resid[slot, rows] + norm_back_rows(grad, hat, inverse, vectors[0:1])
            grad_in[slot, rows] = total.astype(BF)
            gain_sum = gain_sum + jnp.sum(grad * hat, axis=0, keepdims=True)
            shift_sum = shift_sum + jnp.sum(grad, axis=0, keepdims=True)
        return gain_sum, shift_sum

    zero = jnp.zeros((1, width), F32)
    gain_sum, shift_sum = lax.fori_loop(0, steps, last_part, (zero, zero))
    for blk in range(8):
        lanes = slice(blk * BLK, (blk + 1) * BLK)
        parts[blk, pl.ds(0, 1)] = gain_sum[:, lanes]
        parts[blk, pl.ds(1, 1)] = shift_sum[:, lanes]
    sum_copies = [
        remote(
            parts.at[wide],
            gathered.at[own, layer],
            sum_send.at[index],
            sum_recv.at[index],
            {"wide": wide, "tp": tp},
        )
        for index, (wide, tp) in enumerate(others)
    ]
    for copy in sum_copies:
        copy.start()
    gathered[own, layer] = parts[own]
    for up in range(1, depth):
        source = (layer + up) % depth
        for number in range(per_layer):
            remote(
                attn_in.at[number],
                attn_z.at[source, number],
                onward_send.at[number],
                onward_recv.at[source, number],
                {"tp": source},
            ).wait_recv()
    attn_in[own] = attn_g[own]
    for number in range(per_layer):
        for kind in range(3):
            total = attn_in[layer * per_layer + number, kind].astype(F32)
            for up in range(1, depth):
                total = total + attn_z[(layer + up) % depth, number, kind].astype(F32)
            attn_sum[number, kind] = total
    for copy in dense_copies():
        copy.wait_recv()
    total = dense_out[layer // 2, :, pl.ds(pl.multiple_of((layer % 2) * QB, QB), QB)].astype(F32)
    for up in range(1, depth):
        total = total + dense_in[up - 1].astype(F32)
    dense_sum[...] = total
    ffn_x[own] = ffn_sum[own]
    for kind in range(2):
        ffn_exchange(kind).arrive()
    for copy in sum_copies:
        copy.wait_recv()

    def unit_part(dev, carry):
        total = gathered[dev, 0]
        for up in range(1, depth):
            total = total + gathered[dev, up]
        unit_sums[dev] = total
        return carry + total

    vec_sums[...] = lax.fori_loop(0, 8, unit_part, jnp.zeros((16, BLK), F32))

    for copy in sum_copies:
        copy.wait_send()
    for slot in range(2):
        att_exchange(slot).sent()
        att_back(slot).sent()
        ffn_exchange(slot).sent()
    for sends in (gains, biases, heads, ups, downs, exchange):
        sends.sent()
    for number in range(1, depth):
        line.sent(number)
        ffn_line.sent(number)
    for kind in range(2):
        for copy in line_copies(kind):
            copy.wait_send()
    for copy in dense_copies():
        copy.wait_send()
    gd.sent()
    dense.sent()
    for index in range(8):

        @pl.when(index // per_layer != layer)
        def _(index=index):
            onward(index, attn_in).wait_send()


def layer_pass(depth, lengths, hidden, cotangent, *weights):
    width = hidden.shape[-1]
    units = depth * BLK
    per_layer = 8 // depth
    dma = pltpu.SemaphoreType.DMA
    rows = jax.ShapeDtypeStruct((2, BLK, width), BF)
    tokens = pltpu.VMEM((2, 8 * BLK, width), BF)
    own_f32 = pltpu.VMEM((2, BLK, width), F32)
    own_bf = pltpu.VMEM((2, BLK, width), BF)
    line_vec = (8, BLK)
    peers = 8 * depth - 1
    vectors = [part.reshape(1, BLK) for part in weights[6:12]]
    operands = (hidden, cotangent) + weights[:6] + tuple(vectors) + weights[12:]
    return pl.pallas_call(
        functools.partial(layer_body, depth),
        out_shape=[
            rows,
            rows,
            jax.ShapeDtypeStruct((per_layer, 3, BLK, BLK), F32),
            jax.ShapeDtypeStruct((BLK, per_layer * BLK), F32),
            jax.ShapeDtypeStruct((8, 2, BLK, BLK), BF),
            jax.ShapeDtypeStruct((16, BLK), F32),
            jax.ShapeDtypeStruct((8, 16, BLK), F32),
        ],
        in_specs=[pl.BlockSpec(memory_space=pltpu.SMEM)] + [vmem()] * len(operands),
        out_specs=[vmem()] * 7,
        scratch_shapes=[tokens] * 5
        + [
            pltpu.VMEM((2, 8 * BLK, 6 * HEAD), BF),
            pltpu.VMEM((2, 8 * BLK, 2 * HEAD), BF),
            pltpu.VMEM((2, 8 * BLK, 2 * HEAD), BF),
            pltpu.VMEM((units, 16 * BLK), BF),
            pltpu.VMEM((units, 16 * BLK), BF),
            pltpu.VMEM((2, 2, 8 * BLK), F32),
            pltpu.VMEM((8 * BLK, QB), F32),
            pltpu.VMEM((8 * BLK, HEAD), F32),
            pltpu.VMEM((8 * BLK, HEAD), F32),
            pltpu.VMEM((width, 6 * HEAD), BF),
            pltpu.VMEM((8, depth, per_layer * BLK, BLK), BF),
            own_bf,
            own_bf,
            pltpu.VMEM((width, BLK), BF),
            pltpu.VMEM((BLK, width), BF),
            pltpu.VMEM((width, units), BF),
            pltpu.VMEM((units, width), BF),
            pltpu.VMEM((depth, 3, BLK, per_layer * BLK), BF),
            pltpu.VMEM((depth,) + line_vec, F32),
            pltpu.VMEM((8, BLK), F32),
            pltpu.VMEM(line_vec, F32),
            pltpu.VMEM((8, 8, BLK), F32),
            pltpu.VMEM((8, depth) + line_vec, F32),
            pltpu.VMEM((8, width), F32),
            pltpu.VMEM((1, units), F32),
            pltpu.VMEM((1, 6 * HEAD), F32),
            own_bf,
            own_bf,
            own_f32,
            own_f32,
            own_f32,
            own_f32,
            pltpu.VMEM((8, width), F32),
            pltpu.VMEM((1, units), F32),
            pltpu.VMEM((2, depth, 8, BLK, BLK), BF),
            pltpu.VMEM((2, depth - 1, 8, BLK, BLK), BF),
            pltpu.VMEM((8, 2, BLK, BLK), BF),
            pltpu.VMEM((8, 3, BLK, BLK), BF),
            pltpu.VMEM((8, 3, BLK, BLK), BF),
            pltpu.VMEM((depth, per_layer, 3, BLK, BLK), BF),
            pltpu.VMEM((2, BLK, width // 2), BF),
            pltpu.VMEM((depth - 1, BLK, per_layer * BLK), BF),
            pltpu.VMEM((8, 16, BLK), F32),
            pltpu.VMEM((8, depth, 16, BLK), F32),
        ]
        + [
            pltpu.VMEM((4, 2, BLK, width), BF),
            pltpu.VMEM((3, BLK, width), BF),
            pltpu.VMEM((3, BLK, width), BF),
        ]
        * 2
        + [
            dma((4, SquareGather.SENDS)),
            dma((4, SquareGather.SENDS)),
            dma((4,)),
            dma((4, SquareScatter.SENDS)),
            dma((4, SquareScatter.SENDS)),
            dma((2, 5, depth - 1)),
            dma((2, 5, depth - 1)),
            dma((2, 2, depth - 1)),
            dma((2, 2, depth - 1)),
            dma((12, 7)),
            dma((12, 7)),
            dma((2, depth - 1)),
            dma((2, depth - 1)),
            dma((8,)),
            dma((depth, per_layer)),
            dma((depth - 1,)),
            dma((depth - 1,)),
            dma((peers,)),
            dma((peers,)),
            dma((14,)),
        ],
        compiler_params=pltpu.CompilerParams(
            collective_id=1, has_side_effects=True, vmem_limit_bytes=VMEM_MAX
        ),
        name="layer",
    )(lengths, *operands)


def write_body(
    depth,
    output_in,
    grad_in_in,
    attn_sum,
    dense_sum,
    ffn_x,
    vec_in,
    unit_sums,
    output,
    grad_in,
    grad_q,
    grad_k,
    grad_v,
    grad_d,
    grad_up,
    grad_down,
    up_b,
    query_b,
    value_b,
    *vec_rows,
):
    own = lax.axis_index("wide")
    layer = lax.axis_index("tp")
    per_layer = 8 // depth
    output[...] = output_in[...]
    grad_in[...] = grad_in_in[...]
    for number in range(per_layer):
        lanes = slice(number * BLK, (number + 1) * BLK)
        for kind, target in enumerate((grad_q, grad_k, grad_v)):
            target[:, lanes] = attn_sum[number, kind].T
    grad_d[...] = dense_sum[...].T
    for blk in range(8):
        lanes = slice(blk * BLK, (blk + 1) * BLK)
        grad_up[:, lanes] = ffn_x[blk, 0].astype(F32).T
        grad_down[lanes] = ffn_x[blk, 1].astype(F32)
    for row in range(up_b.shape[0]):
        unit = unit_sums[2 * row + own // 4, pl.ds(6 + layer, 1)]
        moved = pltpu.roll(unit, (BLK - 32 * (own % 4)) % BLK, 1)
        up_b[row : row + 1] = moved[:, :32]
        shift = (BLK - ((row % 2) * HEAD + 8 * own)) % BLK
        for place, target in enumerate((query_b, value_b)):
            unit = unit_sums[per_layer * layer + row // 2, pl.ds(6 + depth + place, 1)]
            target[row : row + 1] = pltpu.roll(unit, shift, 1)[:, :8]
    for place, target in enumerate(vec_rows):
        target[...] = vec_in[pl.ds(place, 1)]


def write_out(depth, *pieces):
    per_layer = 8 // depth
    width = pieces[0].shape[-1]
    rows = jax.ShapeDtypeStruct(pieces[0].shape, BF)
    square = jax.ShapeDtypeStruct((BLK, per_layer * BLK), F32)
    head = jax.ShapeDtypeStruct((4, 8), F32)
    return pl.pallas_call(
        functools.partial(write_body, depth),
        out_shape=[
            rows,
            rows,
            square,
            square,
            square,
            jax.ShapeDtypeStruct((per_layer * BLK, BLK), F32),
            jax.ShapeDtypeStruct((BLK, width), F32),
            jax.ShapeDtypeStruct((width, BLK), F32),
            jax.ShapeDtypeStruct((4, 32), F32),
            head,
            head,
        ]
        + [jax.ShapeDtypeStruct((1, BLK), F32)] * 6,
        in_specs=[vmem()] * 7,
        out_specs=[vmem()] * 17,
        name="write_out",
    )(*pieces)


def square_device(
    hidden_in,
    lengths,
    pre_gain,
    pre_shift,
    w_query,
    w_key,
    w_value,
    b_query,
    b_value,
    w_dense,
    b_dense,
    mid_gain,
    mid_shift,
    w_up,
    b_up,
    w_down,
    b_down,
    cotangent,
):
    depth = lax.axis_size("tp")
    pieces = layer_pass(
        depth,
        lengths,
        hidden_in,
        cotangent,
        w_query,
        w_key,
        w_value,
        w_dense,
        w_up,
        w_down,
        pre_gain,
        pre_shift,
        mid_gain,
        mid_shift,
        b_dense,
        b_down,
        b_up,
        b_query,
        b_value,
    )
    (
        output,
        grad_in,
        grad_q,
        grad_k,
        grad_v,
        grad_d,
        grad_up,
        grad_down,
        up_b,
        query_b,
        value_b,
        *vec_rows,
    ) = write_out(depth, *pieces)
    vec_sums = [row.reshape(BLK) for row in vec_rows]
    return (
        output,
        grad_in,
        vec_sums[0],
        vec_sums[1],
        grad_q,
        grad_k,
        grad_v,
        query_b,
        value_b,
        grad_d,
        vec_sums[2],
        vec_sums[3],
        vec_sums[4],
        grad_up,
        up_b,
        grad_down,
        vec_sums[5],
    )


def solution(mesh):
    square = mesh.shape["wide"] == 8 and mesh.shape["tp"] == 4
    return jax.shard_map(
        square_device if square else per_device,
        mesh=mesh,
        in_specs=(
            P("tp", "wide", None),
            P(),
            P("wide"),
            P("wide"),
            P("wide", "tp"),
            P("wide", "tp"),
            P("wide", "tp"),
            P("tp", "wide"),
            P("tp", "wide"),
            P("tp", "wide"),
            P("wide"),
            P("wide"),
            P("wide"),
            P("wide", "tp"),
            P("tp", "wide"),
            P("tp", "wide"),
            P("wide"),
            P("tp", "wide", None),
        ),
        out_specs=(
            P("tp", "wide", None),
            P("tp", "wide", None),
            P("wide"),
            P("wide"),
            P("wide", "tp"),
            P("wide", "tp"),
            P("wide", "tp"),
            P("tp", "wide"),
            P("tp", "wide"),
            P("tp", "wide"),
            P("wide"),
            P("wide"),
            P("wide"),
            P("wide", "tp"),
            P("tp", "wide"),
            P("tp", "wide"),
            P("wide"),
        ),
        check_vma=False,
    )
```

```python
import functools
import math

import jax
import jax.numpy as jnp
from jax import lax
from jax.experimental import pallas as pl
from jax.experimental.pallas import tpu as pltpu
from jax.sharding import PartitionSpec as P

HEAD = 64
MESH = pl.DeviceIdType.MESH


def norm_rows(values, gain_vec, shift_vec):
    middle = jnp.mean(values, axis=-1, keepdims=True)
    centred = values - middle
    spread = jnp.mean(centred * centred, axis=-1, keepdims=True)
    return centred * lax.rsqrt(spread + 1e-05) * gain_vec + shift_vec


def flatten_rows(tensor):
    return tensor.reshape(-1, tensor.shape[-1])


def row_product(first_op, second_op):
    return jnp.dot(first_op, second_op, preferred_element_type=jnp.float32)


def inner_rows(first_op, second_op):
    return lax.dot_general(
        flatten_rows(first_op),
        flatten_rows(second_op),
        (((0,), (0,)), ((), ())),
        preferred_element_type=jnp.float32,
    )


def times_transposed(first_op, second_op):
    return lax.dot_general(
        first_op,
        second_op,
        (((first_op.ndim - 1,), (1,)), ((), ())),
        preferred_element_type=jnp.float32,
    )


def activate(values):
    return jax.nn.gelu(values, approximate=True)


def masked_scores(query_blk, key_blk, lengths_blk, slopes, distance, causal_mask, key_places):
    raw_scores = (
        jnp.einsum("gihd,gjhd->ghij", query_blk, key_blk, preferred_element_type=jnp.float32)
        * 0.125
    )
    raw_scores = raw_scores - slopes[None, :, None, None] * distance[None, None]
    allowed = causal_mask[None] & (key_places[None, None, :] < lengths_blk[:, None, None])
    return jnp.where(allowed[:, None], raw_scores, -jnp.inf)


def per_device(
    hidden_in,
    lengths,
    pre_gain,
    pre_shift,
    w_query,
    w_key,
    w_value,
    b_query,
    b_value,
    w_dense,
    b_dense,
    mid_gain,
    mid_shift,
    w_up,
    b_up,
    w_down,
    b_down,
    cotangent,
):
    local_slots, block_len, _unused = hidden_in.shape
    heads_dev = b_query.shape[0]
    head_width = heads_dev * HEAD
    slot_total = local_slots * lax.axis_size("tp")
    slot_len = block_len * lax.axis_size("wide")
    wide_at = lax.axis_index("wide")
    tp_at = lax.axis_index("tp")
    vec_part = pre_gain.shape[0]
    (
        gain_one,
        shift_one,
        query_w,
        key_w,
        value_w,
        query_b,
        value_b,
        dense_w,
        dense_b,
        gain_two,
        shift_two,
        up_w,
        up_b,
        down_w,
        down_b,
    ) = (
        lax.all_gather(pre_gain, "wide", axis=0, tiled=True),
        lax.all_gather(pre_shift, "wide", axis=0, tiled=True),
        lax.all_gather(w_query, "wide", axis=0, tiled=True),
        lax.all_gather(w_key, "wide", axis=0, tiled=True),
        lax.all_gather(w_value, "wide", axis=0, tiled=True),
        lax.all_gather(b_query, "wide", axis=1, tiled=True),
        lax.all_gather(b_value, "wide", axis=1, tiled=True),
        lax.all_gather(w_dense, "wide", axis=1, tiled=True),
        lax.all_gather(b_dense, "wide", axis=0, tiled=True),
        lax.all_gather(mid_gain, "wide", axis=0, tiled=True),
        lax.all_gather(mid_shift, "wide", axis=0, tiled=True),
        lax.all_gather(w_up, "wide", axis=0, tiled=True),
        lax.all_gather(b_up, "wide", axis=1, tiled=True),
        lax.all_gather(w_down, "wide", axis=1, tiled=True),
        lax.all_gather(b_down, "wide", axis=0, tiled=True),
    )
    gain_one = gain_one.astype(jnp.float32)
    shift_one = shift_one.astype(jnp.float32)
    gain_two = gain_two.astype(jnp.float32)
    shift_two = shift_two.astype(jnp.float32)
    query_places = wide_at * block_len + jnp.arange(block_len, dtype=jnp.int32)
    key_places = jnp.arange(slot_len, dtype=jnp.int32)
    distance = (query_places[:, None] - key_places[None, :]).astype(jnp.float32)
    causal_mask = key_places[None, :] <= query_places[:, None]
    head_index = tp_at * heads_dev + jnp.arange(heads_dev, dtype=jnp.int32)
    slopes = jnp.exp2(-0.5 * (head_index.astype(jnp.float32) + 1.0))
    own_lengths = lax.dynamic_slice_in_dim(lengths, tp_at * local_slots, local_slots, 0)
    validity = (query_places[None, :] < own_lengths[:, None]).astype(jnp.float32)
    group_size = math.gcd(slot_total, max(1, 512 // block_len))
    group_count = slot_total // group_size
    grouped_lengths = lengths.reshape(group_count, group_size)
    hidden = hidden_in.astype(jnp.float32)

    def query_view(tensor):
        return tensor.reshape(group_count, group_size, block_len, heads_dev, HEAD)

    def pair_view(tensor):
        return tensor.reshape(group_count, group_size, slot_len, 2, heads_dev, HEAD)

    def forward_group(inputs):
        query_blk, pair_blk, lengths_blk = inputs
        masked = masked_scores(
            query_blk, pair_blk[:, :, 0], lengths_blk, slopes, distance, causal_mask, key_places
        )
        highest = jnp.max(masked, axis=-1, keepdims=True)
        totals = highest + jnp.log(jnp.sum(jnp.exp(masked - highest), axis=-1, keepdims=True))
        probabilities = jnp.exp(masked - totals).astype(jnp.bfloat16)
        summed = jnp.einsum(
            "ghij,gjhd->gihd", probabilities, pair_blk[:, :, 1], preferred_element_type=jnp.float32
        )
        return (totals[..., 0], summed)

    def attention_forward(hidden_rows):
        normed_f, norm_back = jax.vjp(norm_rows, hidden_rows, gain_one, shift_one)
        normed = normed_f.astype(jnp.bfloat16)
        normed_all = lax.all_gather(normed, "tp", axis=0, tiled=True)
        queries = (
            row_product(normed_all, query_w) + query_b.reshape(head_width).astype(jnp.float32)
        ).astype(jnp.bfloat16)
        keys_now = row_product(normed_all, key_w).astype(jnp.bfloat16)
        values_now = (
            row_product(normed_all, value_w) + value_b.reshape(head_width).astype(jnp.float32)
        ).astype(jnp.bfloat16)
        pairs = jnp.concatenate([keys_now, values_now], axis=-1)
        pairs_all = lax.all_gather(pairs, "wide", axis=1, tiled=True)
        totals, summed = lax.map(
            forward_group, (query_view(queries), pair_view(pairs_all), grouped_lengths)
        )
        return (
            normed_all,
            queries,
            pairs_all,
            totals,
            summed.reshape(slot_total, block_len, head_width),
            norm_back,
        )

    forward_parts = attention_forward(hidden)
    attention = forward_parts[4].astype(jnp.bfloat16)
    branch = lax.psum_scatter(
        row_product(attention, dense_w).astype(jnp.bfloat16), "tp", scatter_dimension=0, tiled=True
    ).astype(jnp.float32)
    residual = hidden + branch + dense_b.astype(jnp.float32)
    second_f, second_back = jax.vjp(norm_rows, residual, gain_two, shift_two)
    second = second_f.astype(jnp.bfloat16)
    grad_output = validity[:, :, None] * cotangent.astype(jnp.float32)
    grad_down = grad_output.astype(jnp.bfloat16)
    second_all, grad_down_all = (
        lax.all_gather(second, "tp", axis=0, tiled=True),
        lax.all_gather(grad_down, "tp", axis=0, tiled=True),
    )
    pre_act = row_product(second_all, up_w) + up_b.reshape(-1).astype(jnp.float32)
    act_value, act_back = jax.vjp(activate, pre_act)
    activated = act_value.astype(jnp.bfloat16)
    down_out = lax.psum_scatter(
        row_product(activated, down_w).astype(jnp.bfloat16), "tp", scatter_dimension=0, tiled=True
    ).astype(jnp.float32)
    grad_act = times_transposed(grad_down_all, down_w)
    grad_pre = act_back(grad_act)[0].astype(jnp.bfloat16)
    grad_up = inner_rows(second_all, grad_pre)
    grad_up_b = jnp.sum(flatten_rows(grad_pre), axis=0, dtype=jnp.float32).reshape(up_b.shape)
    grad_down_w = inner_rows(activated, grad_down_all)
    grad_second = lax.psum_scatter(
        times_transposed(grad_pre, up_w), "tp", scatter_dimension=0, tiled=True
    )
    output = (validity[:, :, None] * (residual + down_out + down_b.astype(jnp.float32))).astype(
        jnp.bfloat16
    )
    grad_resid_norm, grad_gain_two, grad_shift_two = second_back(grad_second)
    grad_resid = grad_output + grad_resid_norm
    grad_branch = grad_resid.astype(jnp.bfloat16)
    hidden_again, grad_branch = lax.optimization_barrier((hidden, grad_branch))
    forward_parts = attention_forward(hidden_again)
    normed_all, queries, pairs_all, totals, summed, norm_back = forward_parts
    attention_back = summed.astype(jnp.bfloat16)
    branch_all = lax.all_gather(grad_branch, "tp", axis=0, tiled=True)
    grad_dense_w = inner_rows(attention_back, branch_all)
    grad_attention = times_transposed(branch_all, dense_w).astype(jnp.bfloat16)

    def backward_group(inputs):
        query_blk, pair_blk, lengths_blk, totals_blk, grad_blk = inputs
        masked = masked_scores(
            query_blk, pair_blk[:, :, 0], lengths_blk, slopes, distance, causal_mask, key_places
        )
        probabilities = jnp.exp(masked - totals_blk[..., None])
        grad_probs = jnp.einsum(
            "gihd,gjhd->ghij", grad_blk, pair_blk[:, :, 1], preferred_element_type=jnp.float32
        )
        row_delta = jnp.sum(probabilities * grad_probs, axis=-1, keepdims=True)
        grad_scores = (probabilities * (grad_probs - row_delta)).astype(jnp.bfloat16)
        grad_query = (
            jnp.einsum(
                "ghij,gjhd->gihd",
                grad_scores,
                pair_blk[:, :, 0],
                preferred_element_type=jnp.float32,
            )
            * 0.125
        )
        grad_key = (
            jnp.einsum(
                "ghij,gihd->gjhd", grad_scores, query_blk, preferred_element_type=jnp.float32
            )
            * 0.125
        )
        grad_value = jnp.einsum(
            "ghij,gihd->gjhd",
            probabilities.astype(jnp.bfloat16),
            grad_blk,
            preferred_element_type=jnp.float32,
        )
        return (grad_query, jnp.stack([grad_key, grad_value], axis=2))

    grad_query_all, grad_pairs = lax.map(
        backward_group,
        (
            query_view(queries),
            pair_view(pairs_all),
            grouped_lengths,
            totals,
            query_view(grad_attention),
        ),
    )
    grad_pairs_local = lax.psum_scatter(
        grad_pairs.reshape(slot_total, slot_len, 2 * head_width).astype(jnp.bfloat16),
        "wide",
        scatter_dimension=1,
        tiled=True,
    ).astype(jnp.float32)
    grad_queries = grad_query_all.reshape(slot_total, block_len, head_width).astype(jnp.bfloat16)
    grad_keys = grad_pairs_local[:, :, :head_width].astype(jnp.bfloat16)
    grad_values = grad_pairs_local[:, :, head_width:].astype(jnp.bfloat16)
    grad_query_w = inner_rows(normed_all, grad_queries)
    grad_key_w = inner_rows(normed_all, grad_keys)
    grad_value_w = inner_rows(normed_all, grad_values)
    grad_query_b = jnp.sum(flatten_rows(grad_queries), axis=0, dtype=jnp.float32).reshape(
        heads_dev, HEAD
    )
    grad_value_b = jnp.sum(flatten_rows(grad_values), axis=0, dtype=jnp.float32).reshape(
        heads_dev, HEAD
    )
    grad_normed = lax.psum_scatter(
        (
            times_transposed(grad_queries, query_w)
            + times_transposed(grad_keys, key_w)
            + times_transposed(grad_values, value_w)
        ).astype(jnp.bfloat16),
        "tp",
        scatter_dimension=0,
        tiled=True,
    ).astype(jnp.float32)
    grad_hidden_norm, grad_gain_one, grad_shift_one = norm_back(grad_normed)
    grad_in = (grad_resid + grad_hidden_norm).astype(jnp.bfloat16)
    (
        sum_query_w,
        sum_key_w,
        sum_value_w,
        sum_query_b,
        sum_value_b,
        sum_dense_w,
        sum_up_w,
        sum_up_b,
        sum_down_w,
    ) = (
        lax.psum_scatter(
            grad_query_w.astype(jnp.bfloat16), "wide", scatter_dimension=0, tiled=True
        ).astype(jnp.float32),
        lax.psum_scatter(
            grad_key_w.astype(jnp.bfloat16), "wide", scatter_dimension=0, tiled=True
        ).astype(jnp.float32),
        lax.psum_scatter(
            grad_value_w.astype(jnp.bfloat16), "wide", scatter_dimension=0, tiled=True
        ).astype(jnp.float32),
        lax.psum_scatter(
            grad_query_b.astype(jnp.bfloat16), "wide", scatter_dimension=1, tiled=True
        ).astype(jnp.float32),
        lax.psum_scatter(
            grad_value_b.astype(jnp.bfloat16), "wide", scatter_dimension=1, tiled=True
        ).astype(jnp.float32),
        lax.psum_scatter(
            grad_dense_w.astype(jnp.bfloat16), "wide", scatter_dimension=1, tiled=True
        ).astype(jnp.float32),
        lax.psum_scatter(
            grad_up.astype(jnp.bfloat16), "wide", scatter_dimension=0, tiled=True
        ).astype(jnp.float32),
        lax.psum_scatter(
            grad_up_b.astype(jnp.bfloat16), "wide", scatter_dimension=1, tiled=True
        ).astype(jnp.float32),
        lax.psum_scatter(
            grad_down_w.astype(jnp.bfloat16), "wide", scatter_dimension=1, tiled=True
        ).astype(jnp.float32),
    )
    grad_dense_b = jnp.sum(grad_resid, axis=(0, 1))
    grad_down_b = jnp.sum(grad_output, axis=(0, 1))
    sum_gain_one, sum_shift_one, sum_dense_b, sum_gain_two, sum_shift_two, sum_down_b = lax.psum(
        (grad_gain_one, grad_shift_one, grad_dense_b, grad_gain_two, grad_shift_two, grad_down_b),
        ("wide", "tp"),
    )

    def own_part(tensor):
        return lax.dynamic_slice_in_dim(tensor, wide_at * vec_part, vec_part, 0)

    return (
        output,
        grad_in,
        own_part(sum_gain_one),
        own_part(sum_shift_one),
        sum_query_w,
        sum_key_w,
        sum_value_w,
        sum_query_b,
        sum_value_b,
        sum_dense_w,
        own_part(sum_dense_b),
        own_part(sum_gain_two),
        own_part(sum_shift_two),
        sum_up_w,
        sum_up_b,
        sum_down_w,
        own_part(sum_down_b),
    )


BF = jnp.bfloat16
F32 = jnp.float32
LOG2E = 1.4426950408889634
NEG = -1e30
BLK = 128


def hbm():
    return pl.BlockSpec(memory_space=pl.ANY)


def vmem():
    return pl.BlockSpec(memory_space=pltpu.VMEM)


def square_places():
    own = lax.axis_index("wide")
    core = own % 2
    col = (own // 2) % 2
    row = own // 4
    pair = own + 1 - 2 * core
    along_x = own + 2 - 4 * col
    along_y = own + 4 - 8 * row
    return own, pair, along_x, along_y, along_x + along_y - own


def greet(targets):
    barrier = pltpu.get_barrier_semaphore()
    for target in targets:
        pl.semaphore_signal(barrier, inc=1, device_id=target, device_id_type=MESH)
    pl.semaphore_wait(barrier, len(targets))


def remote(src, dst, send_sem, recv_sem, target):
    return pltpu.make_async_remote_copy(
        src_ref=src,
        dst_ref=dst,
        send_sem=send_sem,
        recv_sem=recv_sem,
        device_id=target,
        device_id_type=MESH,
    )


class SquareGather:
    SENDS = 13

    def __init__(self, src, place, both, send, recv, local=None):
        own, pair, ax, ay, dg = square_places()
        first, second, whole = src
        to_x, to_y, to_p = {"wide": ax}, {"wide": ay}, {"wide": pair}
        self.local = None if local is None else pltpu.make_async_copy(whole, both(own), local)
        copies = {}
        copies["x0"] = remote(first, place(0, own), send.at[0], recv.at[0], to_x)
        copies["x1"] = remote(second, place(1, own), send.at[1], recv.at[1], to_x)
        copies["y0"] = remote(first, place(0, own), send.at[2], recv.at[2], to_y)
        copies["y1"] = remote(second, place(1, own), send.at[3], recv.at[3], to_y)
        copies["d0"] = remote(place(0, ay), place(0, ay), send.at[4], recv.at[4], to_x)
        copies["d1"] = remote(place(1, ax), place(1, ax), send.at[5], recv.at[5], to_y)
        copies["p"] = remote(whole, both(own), send.at[6], recv.at[6], to_p)
        for index, (name, slot, dev) in enumerate(
            (("x0", 0, ax), ("x1", 1, ax), ("y0", 0, ay), ("y1", 1, ay), ("d0", 0, dg), ("d1", 1, dg))
        ):
            copies["p" + name] = remote(
                place(slot, dev), place(slot, dev), send.at[7 + index], recv.at[7 + index], to_p
            )
        self.copies = copies

    def start_half(self):
        for name in ("y0", "x1"):
            self.copies[name].start()

    def start_rest(self):
        for name in ("x0", "y1", "p"):
            self.copies[name].start()
        if self.local is not None:
            self.local.start()

    def start(self):
        self.start_half()
        self.start_rest()

    def pass_on(self, arrived, sends):
        self.copies[arrived].wait_recv()
        for name in sends:
            self.copies[name].start()

    def first(self):
        self.pass_on("y0", ("d0", "py0"))
        self.pass_on("x1", ("d1", "px1"))

    def second(self):
        self.pass_on("x0", ("px0",))
        self.pass_on("y1", ("py1",))

    def third(self):
        self.pass_on("d0", ("pd0",))
        self.pass_on("d1", ("pd1",))

    def arrive(self, *names):
        for name in names:
            self.copies[name].wait_recv()

    def sent(self):
        for copy in self.copies.values():
            copy.wait_send()


def wide_square(own_places):
    _own, pair, ax, ay, _dg = own_places
    return [{"wide": pair}, {"wide": ax}, {"wide": ay}]


def add_rows(dst, first, second, third=None):
    step = 16

    def body(index, carry):
        rows = pl.ds(pl.multiple_of(index * step, step), step)
        total = first[rows].astype(F32) + second[rows].astype(F32)
        if third is not None:
            total = total + third[rows].astype(F32)
        dst[rows] = total.astype(dst.dtype)
        return carry

    lax.fori_loop(0, BLK // step, body, 0)


class SquareScatter:
    SENDS = 10

    def __init__(self, both, half, out, summed_both, summed, from_x, from_y, send, recv):
        own, pair, ax, ay, dg = square_places()
        shift = pair - own
        to_x, to_y, to_p = {"wide": ax}, {"wide": ay}, {"wide": pair}
        self.half, self.out = half, out
        self.summed, self.from_x, self.from_y = summed, from_x, from_y
        self.dests = (dg, ax, ay, own)
        self.pairs = [
            remote(
                both(self.dests[chip] + shift), summed_both(chip), send.at[chip], recv.at[chip], to_p
            )
            for chip in range(4)
        ]
        self.dx = remote(summed(0, 0), from_x(0), send.at[4], recv.at[4], to_x)
        self.dy = remote(summed(0, 1), from_y(0), send.at[5], recv.at[5], to_y)
        self.xx = remote(summed(1, 0), from_x(1), send.at[6], recv.at[6], to_x)
        self.yy = remote(summed(2, 1), from_y(1), send.at[7], recv.at[7], to_y)
        self.ty = remote(summed(2, 0), from_y(2), send.at[8], recv.at[8], to_y)
        self.tx = remote(summed(1, 1), from_x(2), send.at[9], recv.at[9], to_x)

    def pair_sum(self, chip, slot, third=None):
        place = self.summed(chip, slot)
        add_rows(place, self.half(slot, self.dests[chip]), place, third)

    def near(self, chip):
        self.pairs[chip].wait_recv()
        if chip == 0:
            self.pair_sum(0, 0)
            self.dx.start()
            self.pair_sum(0, 1)
            self.dy.start()
        elif chip == 1:
            self.pair_sum(1, 0)
            self.xx.start()
        elif chip == 2:
            self.pair_sum(2, 1)
            self.yy.start()
        else:
            self.pair_sum(3, 0)
            self.pair_sum(3, 1)

    def middle(self):
        self.dx.wait_recv()
        self.pair_sum(2, 0, self.from_x(0))
        self.ty.start()
        self.dy.wait_recv()
        self.pair_sum(1, 1, self.from_y(0))
        self.tx.start()

    def start(self):
        for chip in range(4):
            self.pairs[chip].start()

    def finish(self):
        self.xx.wait_recv()
        self.ty.wait_recv()
        add_rows(self.out.at[0], self.summed(3, 0), self.from_x(1), self.from_y(2))
        self.yy.wait_recv()
        self.tx.wait_recv()
        add_rows(self.out.at[1], self.summed(3, 1), self.from_y(1), self.from_x(2))
        for copy in self.pairs:
            copy.wait_send()
        for copy in (self.dx, self.dy, self.xx, self.yy, self.ty, self.tx):
            copy.wait_send()


class LineGather:
    def __init__(self, depth, pieces, send, recv):
        self.depth, self.pieces, self.send, self.recv = depth, pieces, send, recv
        self.layer = lax.axis_index("tp")

    def copies(self, step, up):
        index = self.layer - step + 1 if up else self.layer + step - 1
        goal = {"tp": self.layer + 1 if up else self.layer - 1}
        side = 0 if up else 1
        made = []
        for number, (own, place) in enumerate(self.pieces):
            source = own if step == 1 else place(index)
            made.append(
                remote(
                    source,
                    place(index),
                    self.send.at[side, number, step - 1],
                    self.recv.at[side, number, step - 1],
                    goal,
                )
            )
        return made

    def each(self, step, act):
        layer = self.layer

        @pl.when((layer < self.depth - 1) & (layer - step + 1 >= 0))
        def _():
            for copy in self.copies(step, True):
                act(copy)

        @pl.when((layer > 0) & (layer + step - 1 < self.depth))
        def _():
            for copy in self.copies(step, False):
                act(copy)

    def start(self, step):
        self.each(step, lambda copy: copy.start())

    def sent(self, step):
        self.each(step, lambda copy: copy.wait_send())

    def arrive(self, step):
        layer = self.layer

        @pl.when(layer - step >= 0)
        def _():
            for copy in self.copies(step, True):
                copy.wait_recv()

        @pl.when(layer + step < self.depth)
        def _():
            for copy in self.copies(step, False):
                copy.wait_recv()


def wide_others(own):
    return [{"wide": (own + step) % 8} for step in range(1, 8)]


def head_bias(length, slope, rows):
    place = lax.broadcasted_iota(jnp.int32, (rows, QB), 0)
    return jnp.where(place < length, slope * place.astype(F32), NEG)


QB = 256


def dot_nt(first, second):
    return lax.dot_general(first, second, (((1,), (1,)), ((), ())), preferred_element_type=F32)


def dot_nn(first, second):
    return lax.dot_general(first, second, (((1,), (0,)), ((), ())), preferred_element_type=F32)


def later_key(size):
    key_place = lax.broadcasted_iota(jnp.int32, (size, size), 0)
    query_place = lax.broadcasted_iota(jnp.int32, (size, size), 1)
    return key_place > query_place


def slot_scores(key, query, bias, step):
    extent = (step + 1) * QB
    scores = dot_nt(key[:extent], query) * (0.125 * LOG2E) + bias[:extent]
    edge = jnp.where(later_key(QB), NEG, scores[extent - QB :])
    return edge if step == 0 else jnp.concatenate([scores[: extent - QB], edge], 0)


def attend_head(slot, head, length, slopes, qkv, out, totals, bias):
    rows = qkv.shape[1]
    lanes = pl.ds(head * HEAD, HEAD)
    bias[...] = head_bias(length, slopes[head], rows)
    key = qkv[slot, :, pl.ds(2 * HEAD + head * HEAD, HEAD)]
    value_t = qkv[slot, :, pl.ds(4 * HEAD + head * HEAD, HEAD)].T
    for step in range(rows // QB):
        here = pl.ds(step * QB, QB)
        scores = slot_scores(key, qkv[slot, here, lanes], bias, step)
        highest = jnp.max(scores, axis=0, keepdims=True)
        weights = jnp.exp2(scores - highest)
        total = jnp.sum(weights, axis=0, keepdims=True)
        mixed = dot_nn(value_t[:, : (step + 1) * QB], weights.astype(BF)) / total
        out[slot, here, lanes] = mixed.T.astype(BF)
        totals[slot, pl.ds(head, 1), here] = highest + jnp.log2(total)


def attend_head_back(
    slot, head, length, slopes, qkv, attention, grad, totals, out, bias, key_sum, value_sum
):
    rows = qkv.shape[1]
    lanes = pl.ds(head * HEAD, HEAD)
    key_lanes = pl.ds(2 * HEAD + head * HEAD, HEAD)
    value_lanes = pl.ds(4 * HEAD + head * HEAD, HEAD)
    bias[...] = head_bias(length, slopes[head], rows)
    key = qkv[slot, :, key_lanes]
    value = qkv[slot, :, value_lanes]
    key_t = key.T
    key_sum[...] = jnp.zeros_like(key_sum)
    value_sum[...] = jnp.zeros_like(value_sum)
    for step in range(rows // QB):
        here = pl.ds(step * QB, QB)
        extent = (step + 1) * QB
        query = qkv[slot, here, lanes]
        grad_rows = grad[slot, here, lanes]
        product = grad_rows.astype(F32) * attention[slot, here, lanes].astype(F32)
        delta = jnp.sum(product.T, axis=0, keepdims=True)
        scores = slot_scores(key, query, bias, step)
        probs = jnp.exp2(scores - totals[slot, pl.ds(head, 1), here])
        grad_probs = dot_nt(value[:extent], grad_rows)
        grad_scores = (probs * (grad_probs - delta)).astype(BF)
        span = pl.ds(0, extent)
        value_sum[span] += dot_nn(probs.astype(BF), grad_rows)
        key_sum[span] += dot_nn(grad_scores, query)
        grad_query = dot_nn(key_t[:, :extent], grad_scores)
        out[slot, here, lanes] = (grad_query.T * 0.125).astype(BF)
    out[slot, :, key_lanes] = (key_sum[...] * 0.125).astype(BF)
    out[slot, :, value_lanes] = value_sum[...].astype(BF)


def line_others(depth):
    layer = lax.axis_index("tp")
    return [{"tp": (layer + step) % depth} for step in range(1, depth)]


VMEM_MAX = 67043328


def norm_stats(values):
    middle = jnp.mean(values, axis=-1, keepdims=True)
    centred = values - middle
    spread = jnp.mean(centred * centred, axis=-1, keepdims=True)
    inverse = lax.rsqrt(spread + 1e-05)
    return centred * inverse, inverse


def norm_back_rows(grad, hat, inverse, gain):
    scaled = grad * gain
    first = jnp.mean(scaled, axis=-1, keepdims=True)
    second = jnp.mean(scaled * hat, axis=-1, keepdims=True)
    return (scaled - first - hat * second) * inverse


def gelu_parts(values):
    root = math.sqrt(2 / math.pi)
    squared = values * values
    inner = jnp.tanh(root * values * (1.0 + 0.044715 * squared))
    half = 0.5 * (1.0 + inner)
    slope = half + 0.5 * values * (1.0 - inner * inner) * root * (1.0 + 3 * 0.044715 * squared)
    return values * half, slope


def relation(index):
    own = lax.axis_index("wide")
    core = (own + index) % 2
    col = (own // 2 + index // 2) % 2
    row = (own // 4 + index // 4) % 2
    return row * 4 + col * 2 + core


def pair_of(dev):
    col, row = (dev // 2) % 2, dev // 4
    return 2 * ((col + row) % 2 + 2 * (dev % 2)) + row


def dev_of(pair):
    at, row = pair // 2, pair % 2
    return 4 * row + 2 * ((at + row) % 2) + at // 2


class WideExchange:
    def __init__(self, source, target, send, recv):
        own = lax.axis_index("wide")
        self.copies = [
            remote(
                source((own + step) % 8),
                target(own),
                send.at[step - 1],
                recv.at[step - 1],
                {"wide": (own + step) % 8},
            )
            for step in range(1, 8)
        ]

    def start(self):
        for copy in self.copies:
            copy.start()

    def arrive(self):
        for copy in self.copies:
            copy.wait_recv()

    def sent(self):
        for copy in self.copies:
            copy.wait_send()


def layer_body(
    depth,
    lengths,
    hidden,
    cotangent,
    w_query,
    w_key,
    w_value,
    w_dense,
    w_up,
    w_down,
    pre_gain,
    pre_shift,
    mid_gain,
    mid_shift,
    b_dense,
    b_down,
    b_up,
    b_query,
    b_value,
    output,
    grad_in,
    attn_sum,
    dense_sum,
    ffn_x,
    vec_sums,
    unit_sums,
    hidden_all,
    normed,
    down_all,
    second_share,
    down_share,
    qkv,
    attention,
    grad_att,
    act_t,
    pre_t,
    totals,
    bias,
    key_sum,
    value_sum,
    qkv_w,
    dense_all,
    att_own,
    att_grad_own,
    up_t,
    down_t,
    up_w,
    down_w,
    qkv_all,
    z_vec,
    vec_wide,
    vec_line,
    vec_wide_all,
    vec_line_all,
    vectors,
    up_bias,
    qkv_bias,
    own_rows,
    down_own,
    residual,
    grad_second,
    grad_resid,
    down_out,
    sums,
    up_sum,
    ffn_g,
    ffn_in,
    ffn_sum,
    attn_g,
    attn_in,
    attn_z,
    dense_out,
    dense_in,
    parts,
    gathered,
    a_summed,
    a_x,
    a_y,
    b_summed,
    b_x,
    b_y,
    gather_send,
    gather_recv,
    gather_local,
    scatter_send,
    scatter_recv,
    line_send,
    line_recv,
    ffn_line_send,
    ffn_line_recv,
    wide_send,
    wide_recv,
    grad_line_send,
    grad_line_recv,
    onward_send,
    onward_recv,
    dense_send,
    dense_recv,
    head_send,
    head_recv,
    spread_send,
    spread_recv,
    sum_send,
    sum_recv,
    own_sems,
):
    own = lax.axis_index("wide")
    layer = lax.axis_index("tp")
    per_layer = 8 // depth
    width = hidden.shape[-1]
    step = 32
    steps = BLK // step
    others = [
        ((own + side) % 8, (layer + up) % depth)
        for up in range(depth)
        for side in range(8)
        if up or side
    ]
    own_lanes = pl.ds(pl.multiple_of(own * BLK, BLK), BLK)

    for place, ref in enumerate((pre_gain, pre_shift, mid_gain, mid_shift, b_dense, b_down)):
        vec_wide[pl.ds(place, 1)] = ref[...].astype(F32)
    vec_line[...] = jnp.zeros_like(vec_line)
    vec_line[0 : b_up.shape[0], 0 : b_up.shape[1]] = b_up[...].astype(F32)
    vec_line[b_up.shape[0] :, 0:8] = b_query[...].astype(F32)
    vec_line[b_up.shape[0] :, 8:16] = b_value[...].astype(F32)
    first_row = own * BLK

    def token_mask(slot, rows, count):
        place = first_row + rows * count + lax.broadcasted_iota(jnp.int32, (count, BLK), 0)
        inside = place < lengths[layer * 2 + slot]
        return jnp.where(inside, 1.0, 0.0).astype(F32)[:, :1]

    def down_part(index, carry):
        rows = pl.ds(pl.multiple_of(index * step, step), step)
        for slot in range(2):
            values = token_mask(slot, index, step) * cotangent[slot, rows].astype(F32)
            down_own[slot, rows] = values.astype(BF)
        return carry

    lax.fori_loop(0, steps, down_part, 0)
    greet(wide_others(own) + line_others(depth))

    def block_rows(dev):
        return pl.ds(pl.multiple_of(dev * BLK, BLK), BLK)

    def gather_of(number, src, dst):
        return SquareGather(
            (src.at[0], src.at[1], src),
            lambda slot, dev: dst.at[slot, block_rows(dev)],
            lambda dev: dst.at[:, block_rows(dev)],
            gather_send.at[number],
            gather_recv.at[number],
            gather_local.at[number],
        )

    def wide_of(number, source, target):
        return WideExchange(source, target, wide_send.at[number], wide_recv.at[number])

    gains = wide_of(0, lambda dev: vec_wide, lambda dev: vec_wide_all.at[dev])
    gains.start()

    mine = pair_of(own)
    origin, piece = mine // per_layer, mine % per_layer
    head_refs = (w_query, w_key, w_value)

    def head_copies(number):
        goal = dev_of(layer * per_layer + number)
        copies = [
            remote(
                ref.at[:, pl.ds(number * BLK, BLK)],
                qkv_all.at[kind, own],
                head_send.at[number, kind],
                head_recv.at[own, kind],
                {"wide": goal},
            )
            for kind, ref in enumerate(head_refs)
        ]
        return goal, copies

    def head_local(kind):
        return pltpu.make_async_copy(
            head_refs[kind].at[:, block_rows(piece)], qkv_all.at[kind, own], own_sems.at[2 + kind]
        )

    for number in range(per_layer):
        goal, copies = head_copies(number)

        @pl.when(goal != own)
        def _(copies=copies):
            for copy in copies:
                copy.start()

    @pl.when(layer == origin)
    def _():
        for kind in range(3):
            head_local(kind).start()

    def spread(kind, up):
        side = 0 if up else 1
        return remote(
            qkv_all.at[kind],
            qkv_all.at[kind],
            spread_send.at[side, kind],
            spread_recv.at[side, kind],
            {"tp": layer + 1 if up else layer - 1},
        )

    def spread_each(kind, act):
        @pl.when((layer >= origin) & (layer < depth - 1))
        def _():
            act(spread(kind, True))

        @pl.when((layer <= origin) & (layer > 0))
        def _():
            act(spread(kind, False))

    def head_pass(kind):
        @pl.when(layer == origin)
        def _():
            for side in range(1, 8):
                source = (own + side) % 8
                remote(
                    head_refs[kind].at[:, pl.ds(0, BLK)],
                    qkv_all.at[kind, source],
                    head_send.at[0, kind],
                    head_recv.at[source, kind],
                    {"wide": source},
                ).wait_recv()
            head_local(kind).wait()

        @pl.when(layer > origin)
        def _():
            spread(kind, True).wait_recv()

        @pl.when(layer < origin)
        def _():
            spread(kind, False).wait_recv()

        spread_each(kind, lambda copy: copy.start())

    hid = gather_of(0, hidden, hidden_all)
    hid.start()
    line = LineGather(
        depth,
        [
            (w_dense, lambda at: dense_all.at[own, at]),
            (vec_line, lambda at: z_vec.at[at]),
        ],
        line_send,
        line_recv,
    )
    line.start(1)
    own_copies = [
        pltpu.make_async_copy(ref, place(layer), own_sems.at[number])
        for number, (ref, place) in enumerate(line.pieces)
    ]
    for copy in own_copies:
        copy.start()
    vec_wide_all[own] = vec_wide[...]
    gains.arrive()
    for dev in range(8):
        vectors[:, dev * BLK : (dev + 1) * BLK] = vec_wide_all[dev]

    def norm_block(index, carry):
        base = relation(index) * BLK

        def norm_part(part, carry):
            rows = pl.ds(pl.multiple_of(base + part * step, step), step)
            for slot in range(2):
                hat, _inverse = norm_stats(hidden_all[slot, rows].astype(F32))
                normed[slot, rows] = (hat * vectors[0:1] + vectors[1:2]).astype(BF)
            return carry

        return lax.fori_loop(0, steps, norm_part, carry)

    head_pass(0)
    hid.first()
    line.arrive(1)
    line.start(2)
    head_pass(1)
    hid.second()
    ups = wide_of(
        3, lambda dev: w_up.at[:, block_rows(dev)], lambda dev: up_t.at[block_rows(dev)]
    )
    downs = wide_of(
        4, lambda dev: w_down.at[block_rows(dev)], lambda dev: down_t.at[:, block_rows(dev)]
    )
    unit_copies = [
        pltpu.make_async_copy(w_up.at[:, own_lanes], up_t.at[own_lanes], own_sems.at[6]),
        pltpu.make_async_copy(w_down.at[own_lanes], down_t.at[:, own_lanes], own_sems.at[7]),
    ]
    ups.start()
    downs.start()
    for copy in unit_copies:
        copy.start()
    head_pass(2)
    line.arrive(2)
    line.start(3)
    hid.arrive("p")
    hid.local.wait()
    lax.fori_loop(0, 2, norm_block, 0)
    hid.arrive("px0", "px1", "py0", "py1")
    lax.fori_loop(2, 6, norm_block, 0)
    hid.third()
    line.arrive(3)
    for copy in own_copies:
        copy.wait()

    biases = wide_of(2, lambda dev: z_vec, lambda dev: vec_line_all.at[dev])
    dense = SquareGather(
        (dense_all.at[own, pl.ds(0, 2)], dense_all.at[own, pl.ds(2, 2)], dense_all.at[own]),
        lambda half, dev: dense_all.at[dev, pl.ds(2 * half, 2)],
        lambda dev: dense_all.at[dev],
        gather_send.at[3],
        gather_recv.at[3],
    )
    biases.start()
    dense.start()
    gd = gather_of(1, down_own, down_all)
    vec_line_all[own] = z_vec[...]
    hid.arrive("pd0", "pd1")
    lax.fori_loop(6, 8, norm_block, 0)
    biases.arrive()
    unit_row = own // 2
    for dev in range(8):
        for head in range(2):
            lanes = slice(head * HEAD + dev * 8, head * HEAD + dev * 8 + 8)
            row = pl.ds(b_up.shape[0] + 2 * piece + head, 1)
            values = vec_line_all[dev, origin, row]
            qkv_bias[:, lanes] = values[:, 0:8]
            lanes = slice(4 * HEAD + lanes.start, 4 * HEAD + lanes.stop)
            qkv_bias[:, lanes] = values[:, 8:16]
    qkv_bias[:, 2 * HEAD : 4 * HEAD] = jnp.zeros((1, 2 * HEAD), F32)
    for up in range(depth):
        for part in range(4):
            values = vec_line_all[4 * (own % 2) + part, up, pl.ds(unit_row, 1)]
            up_bias[:, up * BLK + part * 32 : up * BLK + part * 32 + 32] = values[:, 0:32]
    hid.sent()
    for copy in unit_copies:
        copy.wait()
    ups.arrive()
    downs.arrive()
    for kind in range(3):
        qkv_w[:, kind * BLK : (kind + 1) * BLK] = qkv_all[kind].reshape(width, BLK)

    ffn_line = LineGather(
        depth,
        [
            (up_t, lambda at: up_w.at[:, pl.ds(pl.multiple_of(at * BLK, BLK), BLK)]),
            (down_t, lambda at: down_w.at[pl.ds(pl.multiple_of(at * BLK, BLK), BLK)]),
        ],
        ffn_line_send,
        ffn_line_recv,
    )
    ffn_line.start(1)
    unit_copies = [
        pltpu.make_async_copy(ref, place(layer), own_sems.at[8 + number])
        for number, (ref, place) in enumerate(ffn_line.pieces)
    ]
    for copy in unit_copies:
        copy.start()
    slopes = [
        jnp.exp2(-0.5 * (jnp.full((1, 1), 2 * mine + head, jnp.int32).astype(F32) + 1.0)) * LOG2E
        for head in range(2)
    ]

    def att_exchange(slot):
        return wide_of(
            7 + slot,
            lambda dev: attention.at[slot, block_rows(dev)],
            lambda dev: att_own.at[slot, :, block_rows(pair_of(dev))],
        )

    def att_local(slot):
        return pltpu.make_async_copy(
            attention.at[slot, block_rows(own)], att_own.at[slot, :, block_rows(mine)], own_sems.at[10 + slot]
        )

    def one_slot(slot, carry):
        def block(index, carry):
            rows = pl.ds(pl.multiple_of(index * QB, QB), QB)
            qkv[slot, rows] = (dot_nn(normed[slot, rows], qkv_w[...]) + qkv_bias[...]).astype(BF)
            return carry

        lax.fori_loop(0, 8 * BLK // QB, block, 0)
        length = lengths[layer * 2 + slot]
        attend_head(slot, 0, length, slopes, qkv, attention, totals, bias)

        @pl.when(slot == 0)
        def _():
            dense.first()
            dense.second()

        attend_head(slot, 1, length, slopes, qkv, attention, totals, bias)
        att_exchange(slot).start()
        att_local(slot).start()

        @pl.when(slot == 0)
        def _():
            ffn_line.arrive(1)
            ffn_line.start(2)
            dense.third()
            gd.start_half()

        return carry

    lax.fori_loop(0, 2, one_slot, 0)
    gd.start_rest()
    gd.first()
    ffn_line.arrive(2)
    ffn_line.start(3)
    dense.arrive("p", "px0", "px1", "py0", "py1", "pd0", "pd1")
    for slot in range(2):
        att_exchange(slot).arrive()
        att_local(slot).wait()

    for part in range(4):
        columns = [dense_all[2 * part + side].reshape(width, BLK) for side in range(2)]
        product = dot_nn(att_own[...].reshape(2 * BLK, width), jnp.concatenate(columns, 1))
        residual[:, :, part * QB : (part + 1) * QB] = product.reshape(2, BLK, QB)

    def scatter_of(number, share, out, buffers):
        summed, from_x, from_y = buffers
        return SquareScatter(
            lambda dev: share.at[:, block_rows(dev)],
            lambda slot, dev: share.at[slot, block_rows(dev)],
            out,
            lambda chip: summed.at[chip],
            lambda chip, slot: summed.at[chip, slot],
            lambda place: from_x.at[place],
            lambda place: from_y.at[place],
            scatter_send.at[number],
            scatter_recv.at[number],
        )

    def second_part(index, carry):
        rows = pl.ds(pl.multiple_of(index * step, step), step)
        for slot in range(2):
            values = hidden[slot, rows].astype(F32) + residual[slot, rows] + vectors[4:5]
            residual[slot, rows] = values
            hat, _inverse = norm_stats(values)
            own_rows[slot, rows] = (hat * vectors[2:3] + vectors[3:4]).astype(BF)
        return carry

    lax.fori_loop(0, steps, second_part, 0)
    second_all = hidden_all
    gather = gather_of(2, own_rows, second_all)
    gather.start()
    scatter = scatter_of(0, second_share, grad_second, (a_summed, a_x, a_y))
    gd.arrive("p")
    gd.local.wait()
    for copy in unit_copies:
        copy.wait()
    ffn_line.arrive(3)

    def compute(index, carry):
        source = relation(index)
        rows = pl.ds(pl.multiple_of(source * BLK, BLK), BLK)
        values = second_all[:, rows].reshape(2 * BLK, width)
        act_value, act_slope = gelu_parts(dot_nn(values, up_w[...]) + up_bias[...])
        activated = act_value.astype(BF)
        grad_rows = down_all[:, rows].reshape(2 * BLK, width)
        grad_pre = (dot_nt(grad_rows, down_w[...]) * act_slope).astype(BF)
        second_share[:, rows] = dot_nt(grad_pre, up_w[...]).astype(BF).reshape(2, BLK, width)
        down_share[:, rows] = dot_nn(activated, down_w[...]).astype(BF).reshape(2, BLK, width)
        up_sum[...] += jnp.sum(grad_pre.astype(F32), axis=0, keepdims=True)
        for slot in range(2):
            lanes = pl.ds(pl.multiple_of(slot * 8 * BLK + source * BLK, BLK), BLK)
            part = slice(slot * BLK, (slot + 1) * BLK)
            act_t[:, lanes] = activated[part].T
            pre_t[:, lanes] = grad_pre[part].T
        return carry

    up_sum[...] = jnp.zeros_like(up_sum)
    gather.arrive("p")
    gather.local.wait()
    lax.fori_loop(0, 2, compute, 0)
    scatter.pairs[3].start()
    gd.second()
    gather.first()
    gd.third()
    gather.second()
    gd.arrive("px0", "px1", "py0", "py1")
    gather.arrive("px0", "px1", "py0", "py1")
    lax.fori_loop(2, 4, compute, 0)
    scatter.pairs[1].start()
    scatter.near(3)
    lax.fori_loop(4, 6, compute, 0)
    scatter.pairs[2].start()
    gather.third()
    scatter.near(1)
    gd.arrive("pd0", "pd1")
    gather.arrive("pd0", "pd1")
    lax.fori_loop(6, 8, compute, 0)
    scatter.pairs[0].start()
    scatter.near(2)
    scatter.near(0)

    def weight_grads(left, right, kind):
        def one(up, carry):
            rows = pl.ds(pl.multiple_of(up * BLK, BLK), BLK)
            total = dot_nn(left[rows, pl.ds(0, 8 * BLK)], right[0])
            total = total + dot_nn(left[rows, pl.ds(8 * BLK, 8 * BLK)], right[1])
            total = total.astype(BF)
            for blk in range(8):
                ffn_g[kind, up, blk] = total[:, blk * BLK : (blk + 1) * BLK]
            return carry

        lax.fori_loop(0, depth, one, 0)

    def line_copies(kind):
        return [
            remote(
                ffn_g.at[kind, (layer + up) % depth],
                ffn_in.at[kind, up - 1],
                grad_line_send.at[kind, up - 1],
                grad_line_recv.at[kind, up - 1],
                {"tp": (layer + up) % depth},
            )
            for up in range(1, depth)
        ]

    def line_sums(kind):
        for copy in line_copies(kind):
            copy.wait_recv()

        def add_block(blk, carry):
            total = ffn_g[kind, layer, blk].astype(F32)
            for up in range(depth - 1):
                total = total + ffn_in[kind, up, blk].astype(F32)
            ffn_sum[blk, kind] = total.astype(BF)
            return carry

        lax.fori_loop(0, 8, add_block, 0)

    weight_grads(pre_t, second_all, 0)
    for copy in line_copies(0):
        copy.start()
    scatter.middle()
    weight_grads(act_t, down_all, 1)
    for copy in line_copies(1):
        copy.start()
    scatter.finish()
    gather.sent()
    sums[...] = jnp.zeros_like(sums)

    def back_part(index, carry):
        rows = pl.ds(pl.multiple_of(index * step, step), step)
        for slot in range(2):
            hat, inverse = norm_stats(residual[slot, rows])
            grad = grad_second[slot, rows]
            grad_out = token_mask(slot, index, step) * cotangent[slot, rows].astype(F32)
            total = grad_out + norm_back_rows(grad, hat, inverse, vectors[2:3])
            grad_resid[slot, rows] = total
            own_rows[slot, rows] = total.astype(BF)
            for place, value in enumerate((total, grad * hat, grad, grad_out)):
                sums[pl.ds(place, 1)] += jnp.sum(value, axis=0, keepdims=True)
        return carry

    lax.fori_loop(0, steps, back_part, 0)
    for at in range(depth):
        columns = jnp.concatenate([dense_all[dev, at] for dev in range(8)], 1)
        product = dot_nt(own_rows[...].reshape(2 * BLK, width), columns).astype(BF)
        att_grad_own[:, :, at * QB : (at + 1) * QB] = product.reshape(2, BLK, QB)

    def att_back(slot):
        return wide_of(
            9 + slot,
            lambda dev: att_grad_own.at[slot, :, block_rows(pair_of(dev))],
            lambda dev: grad_att.at[slot, block_rows(dev)],
        )

    def att_back_local(slot):
        return pltpu.make_async_copy(
            att_grad_own.at[slot, :, block_rows(mine)], grad_att.at[slot, block_rows(own)], own_sems.at[12 + slot]
        )

    for slot in range(2):
        att_back(slot).start()
        att_back_local(slot).start()
    down = scatter_of(1, down_share, down_out, (b_summed, b_x, b_y))
    down.start()

    half_lanes = pl.ds(0, width // 2)
    sum_lanes = pl.ds(width // 2, width // 2)
    for part in range(4):
        rows = slice(part * QB, (part + 1) * QB)
        left = own_rows[:, :, rows].reshape(2 * BLK, QB).T
        for half in range(2):
            lanes = slice(half * width // 2, (half + 1) * width // 2)
            product = dot_nn(left, att_own[:, :, lanes].reshape(2 * BLK, width // 2))
            second_all[half, rows, half_lanes] = product.astype(BF)
    dense_back = SquareScatter(
        lambda dev: second_all.at[:, block_rows(dev), half_lanes],
        lambda half, dev: second_all.at[half, block_rows(dev), half_lanes],
        dense_out,
        lambda chip: second_all.at[:, pl.ds(chip * BLK, BLK), sum_lanes],
        lambda chip, half: second_all.at[half, pl.ds(chip * BLK, BLK), sum_lanes],
        lambda place: second_all.at[0, pl.ds((4 + place) * BLK, BLK), sum_lanes],
        lambda place: second_all.at[1, pl.ds((4 + place) * BLK, BLK), sum_lanes],
        scatter_send.at[3],
        scatter_recv.at[3],
    )

    def dense_piece(at):
        return dense_out.at[at // 2, :, pl.ds(pl.multiple_of((at % 2) * QB, QB), QB)]

    def dense_copies():
        return [
            remote(
                dense_piece((layer + up) % depth),
                dense_in.at[up - 1],
                dense_send.at[up - 1],
                dense_recv.at[up - 1],
                {"tp": (layer + up) % depth},
            )
            for up in range(1, depth)
        ]

    att_back(0).arrive()
    att_back_local(0).wait()
    dense_back.start()
    for chip in range(3):
        down.near(chip)
    for chip in range(3):
        dense_back.near(chip)

    def ffn_exchange(kind):
        return wide_of(5 + kind, lambda dev: ffn_sum.at[dev, kind], lambda dev: ffn_x.at[dev, kind])

    def slot_back(slot, carry):
        def one_head(head):
            attend_head_back(
                slot,
                head,
                lengths[layer * 2 + slot],
                slopes,
                qkv,
                attention,
                grad_att,
                totals,
                qkv,
                bias,
                key_sum,
                value_sum,
            )

        one_head(0)

        @pl.when(slot == 0)
        def _():
            down.near(3)
            down.middle()
            dense_back.near(3)

        @pl.when(slot == 1)
        def _():
            dense_back.finish()
            for copy in dense_copies():
                copy.start()
            line_sums(0)
            ffn_exchange(0).start()

        one_head(1)

        @pl.when(slot == 0)
        def _():
            dense_back.middle()
            att_back(1).arrive()
            att_back_local(1).wait()

        return carry

    lax.fori_loop(0, 2, slot_back, 0)
    grad_qkv = qkv
    weight_part = dot_nn(grad_qkv[0].T, normed[0]) + dot_nn(grad_qkv[1].T, normed[1])
    weight_part = weight_part.astype(BF)
    for kind in range(3):
        for blk in range(8):
            attn_g[blk, kind] = weight_part[
                kind * BLK : (kind + 1) * BLK, blk * BLK : (blk + 1) * BLK
            ]
    kinds = (pl.ds(0, 2), pl.ds(2, 1))
    exchanges = [
        wide_of(
            (11, 1)[group],
            lambda dev, kind=kind: attn_g.at[dev, kind],
            lambda dev, kind=kind: attn_in.at[dev, kind],
        )
        for group, kind in enumerate(kinds)
    ]

    def onward(group, index, source):
        pair = pair_of(index)
        return remote(
            source.at[index, kinds[group]],
            attn_z.at[layer, pair % per_layer, kinds[group]],
            onward_send.at[group, index],
            onward_recv.at[group, layer, pair % per_layer],
            {"tp": pair // per_layer},
        )

    def forward(group, index, source):
        @pl.when(pair_of(index) // per_layer != layer)
        def _():
            onward(group, index, source).start()

    def forward_all(group):
        for number in range(1, 8):
            exchanges[group].copies[number - 1].wait_recv()
            forward(group, (own + 8 - number) % 8, attn_in)

    exchanges[0].start()
    for group in range(2):
        forward(group, own, attn_g)
    share = second_share
    grad_normed = grad_second
    scatter = scatter_of(2, share, grad_normed, (a_summed, a_x, a_y))

    def normed_block(index, carry):
        rows = pl.ds(pl.multiple_of(relation(index) * BLK, BLK), BLK)
        values = grad_qkv[:, rows].reshape(2 * BLK, 6 * HEAD)
        share[:, rows] = dot_nt(values, qkv_w[...]).astype(BF).reshape(2, BLK, width)
        return carry

    for chip in range(4):
        start = (6, 2, 4, 0)[chip]
        lax.fori_loop(start, start + 2, normed_block, 0)
        scatter.pairs[chip].start()
        if chip:
            scatter.near(chip - 1)
    exchanges[1].start()
    line_sums(1)
    head_sum = jnp.sum(grad_qkv[0].astype(F32), axis=0, keepdims=True)
    head_sum = head_sum + jnp.sum(grad_qkv[1].astype(F32), axis=0, keepdims=True)
    down.finish()

    def out_part(index, carry):
        rows = pl.ds(pl.multiple_of(index * step, step), step)
        for slot in range(2):
            total = residual[slot, rows] + down_out[slot, rows] + vectors[5:6]
            output[slot, rows] = (token_mask(slot, index, step) * total).astype(BF)
        return carry

    lax.fori_loop(0, steps, out_part, 0)
    forward_all(0)
    scatter.near(3)
    scatter.middle()
    ffn_exchange(1).start()
    forward_all(1)
    for blk in range(8):
        lanes = slice(blk * BLK, (blk + 1) * BLK)
        for place in range(4):
            parts[blk, pl.ds(2 + place, 1)] = sums[place : place + 1, lanes]
        for place in range(depth):
            parts[blk, pl.ds(6 + place, 1)] = up_sum[:, place * BLK : (place + 1) * BLK]
        parts[blk, pl.ds(6 + depth, 1)] = head_sum[:, : 2 * HEAD]
        parts[blk, pl.ds(7 + depth, 1)] = head_sum[:, 4 * HEAD :]
    scatter.finish()

    def last_part(index, carry):
        gain_sum, shift_sum = carry
        rows = pl.ds(pl.multiple_of(index * step, step), step)
        for slot in range(2):
            hat, inverse = norm_stats(hidden[slot, rows].astype(F32))
            grad = grad_normed[slot, rows]
            total = grad_resid[slot, rows] + norm_back_rows(grad, hat, inverse, vectors[0:1])
            grad_in[slot, rows] = total.astype(BF)
            gain_sum = gain_sum + jnp.sum(grad * hat, axis=0, keepdims=True)
            shift_sum = shift_sum + jnp.sum(grad, axis=0, keepdims=True)
        return gain_sum, shift_sum

    zero = jnp.zeros((1, width), F32)
    gain_sum, shift_sum = lax.fori_loop(0, steps, last_part, (zero, zero))
    for blk in range(8):
        lanes = slice(blk * BLK, (blk + 1) * BLK)
        parts[blk, pl.ds(0, 1)] = gain_sum[:, lanes]
        parts[blk, pl.ds(1, 1)] = shift_sum[:, lanes]
    sum_copies = [
        remote(
            parts.at[wide],
            gathered.at[own, layer],
            sum_send.at[index],
            sum_recv.at[index],
            {"wide": wide, "tp": tp},
        )
        for index, (wide, tp) in enumerate(others)
    ]
    for copy in sum_copies:
        copy.start()
    gathered[own, layer] = parts[own]
    for group in range(2):
        for up in range(1, depth):
            source = (layer + up) % depth
            for number in range(per_layer):
                remote(
                    attn_in.at[number, kinds[group]],
                    attn_z.at[source, number, kinds[group]],
                    onward_send.at[group, number],
                    onward_recv.at[group, source, number],
                    {"tp": source},
                ).wait_recv()
    attn_in[own] = attn_g[own]
    for number in range(per_layer):
        for kind in range(3):
            total = attn_in[dev_of(layer * per_layer + number), kind].astype(F32)
            for up in range(1, depth):
                total = total + attn_z[(layer + up) % depth, number, kind].astype(F32)
            attn_sum[number, kind] = total
    for copy in dense_copies():
        copy.wait_recv()
    total = dense_out[layer // 2, :, pl.ds(pl.multiple_of((layer % 2) * QB, QB), QB)].astype(F32)
    for up in range(1, depth):
        total = total + dense_in[up - 1].astype(F32)
    dense_sum[...] = total
    ffn_x[own] = ffn_sum[own]
    for kind in range(2):
        ffn_exchange(kind).arrive()
    for copy in sum_copies:
        copy.wait_recv()

    def unit_part(dev, carry):
        total = gathered[dev, 0]
        for up in range(1, depth):
            total = total + gathered[dev, up]
        unit_sums[dev] = total
        return carry + total

    vec_sums[...] = lax.fori_loop(0, 8, unit_part, jnp.zeros((16, BLK), F32))

    for copy in sum_copies:
        copy.wait_send()
    for slot in range(2):
        att_exchange(slot).sent()
        att_back(slot).sent()
        ffn_exchange(slot).sent()
    for sends in (gains, biases, ups, downs) + tuple(exchanges):
        sends.sent()
    for number in range(per_layer):
        goal, copies = head_copies(number)

        @pl.when(goal != own)
        def _(copies=copies):
            for copy in copies:
                copy.wait_send()

    for kind in range(3):
        spread_each(kind, lambda copy: copy.wait_send())
    for number in range(1, depth):
        line.sent(number)
        ffn_line.sent(number)
    for kind in range(2):
        for copy in line_copies(kind):
            copy.wait_send()
    for copy in dense_copies():
        copy.wait_send()
    gd.sent()
    dense.sent()
    for group in range(2):
        for index in range(8):

            @pl.when(pair_of(index) // per_layer != layer)
            def _(index=index, group=group):
                onward(group, index, attn_in).wait_send()


def layer_pass(depth, lengths, hidden, cotangent, *weights):
    width = hidden.shape[-1]
    units = depth * BLK
    per_layer = 8 // depth
    dma = pltpu.SemaphoreType.DMA
    rows = jax.ShapeDtypeStruct((2, BLK, width), BF)
    tokens = pltpu.VMEM((2, 8 * BLK, width), BF)
    own_f32 = pltpu.VMEM((2, BLK, width), F32)
    own_bf = pltpu.VMEM((2, BLK, width), BF)
    line_vec = (8, BLK)
    peers = 8 * depth - 1
    vectors = [part.reshape(1, BLK) for part in weights[6:12]]
    operands = (hidden, cotangent) + weights[:6] + tuple(vectors) + weights[12:]
    return pl.pallas_call(
        functools.partial(layer_body, depth),
        out_shape=[
            rows,
            rows,
            jax.ShapeDtypeStruct((per_layer, 3, BLK, BLK), F32),
            jax.ShapeDtypeStruct((BLK, per_layer * BLK), F32),
            jax.ShapeDtypeStruct((8, 2, BLK, BLK), BF),
            jax.ShapeDtypeStruct((16, BLK), F32),
            jax.ShapeDtypeStruct((8, 16, BLK), F32),
        ],
        in_specs=[pl.BlockSpec(memory_space=pltpu.SMEM)] + [vmem()] * len(operands),
        out_specs=[vmem()] * 7,
        scratch_shapes=[tokens] * 5
        + [
            pltpu.VMEM((2, 8 * BLK, 6 * HEAD), BF),
            pltpu.VMEM((2, 8 * BLK, 2 * HEAD), BF),
            pltpu.VMEM((2, 8 * BLK, 2 * HEAD), BF),
            pltpu.VMEM((units, 16 * BLK), BF),
            pltpu.VMEM((units, 16 * BLK), BF),
            pltpu.VMEM((2, 2, 8 * BLK), F32),
            pltpu.VMEM((8 * BLK, QB), F32),
            pltpu.VMEM((8 * BLK, HEAD), F32),
            pltpu.VMEM((8 * BLK, HEAD), F32),
            pltpu.VMEM((width, 6 * HEAD), BF),
            pltpu.VMEM((8, depth, per_layer * BLK, BLK), BF),
            own_bf,
            own_bf,
            pltpu.VMEM((width, BLK), BF),
            pltpu.VMEM((BLK, width), BF),
            pltpu.VMEM((width, units), BF),
            pltpu.VMEM((units, width), BF),
            pltpu.VMEM((3, 8, BLK, BLK), BF),
            pltpu.VMEM((depth,) + line_vec, F32),
            pltpu.VMEM((8, BLK), F32),
            pltpu.VMEM(line_vec, F32),
            pltpu.VMEM((8, 8, BLK), F32),
            pltpu.VMEM((8, depth) + line_vec, F32),
            pltpu.VMEM((8, width), F32),
            pltpu.VMEM((1, units), F32),
            pltpu.VMEM((1, 6 * HEAD), F32),
            own_bf,
            own_bf,
            own_f32,
            own_f32,
            own_f32,
            own_f32,
            pltpu.VMEM((8, width), F32),
            pltpu.VMEM((1, units), F32),
            pltpu.VMEM((2, depth, 8, BLK, BLK), BF),
            pltpu.VMEM((2, depth - 1, 8, BLK, BLK), BF),
            pltpu.VMEM((8, 2, BLK, BLK), BF),
            pltpu.VMEM((8, 3, BLK, BLK), BF),
            pltpu.VMEM((8, 3, BLK, BLK), BF),
            pltpu.VMEM((depth, per_layer, 3, BLK, BLK), BF),
            pltpu.VMEM((2, BLK, width // 2), BF),
            pltpu.VMEM((depth - 1, BLK, per_layer * BLK), BF),
            pltpu.VMEM((8, 16, BLK), F32),
            pltpu.VMEM((8, depth, 16, BLK), F32),
        ]
        + [
            pltpu.VMEM((4, 2, BLK, width), BF),
            pltpu.VMEM((3, BLK, width), BF),
            pltpu.VMEM((3, BLK, width), BF),
        ]
        * 2
        + [
            dma((4, SquareGather.SENDS)),
            dma((4, SquareGather.SENDS)),
            dma((4,)),
            dma((4, SquareScatter.SENDS)),
            dma((4, SquareScatter.SENDS)),
            dma((2, 2, depth - 1)),
            dma((2, 2, depth - 1)),
            dma((2, 2, depth - 1)),
            dma((2, 2, depth - 1)),
            dma((12, 7)),
            dma((12, 7)),
            dma((2, depth - 1)),
            dma((2, depth - 1)),
            dma((2, 8)),
            dma((2, depth, per_layer)),
            dma((depth - 1,)),
            dma((depth - 1,)),
            dma((per_layer, 3)),
            dma((8, 3)),
            dma((2, 3)),
            dma((2, 3)),
            dma((peers,)),
            dma((peers,)),
            dma((14,)),
        ],
        compiler_params=pltpu.CompilerParams(
            collective_id=1, has_side_effects=True, vmem_limit_bytes=VMEM_MAX
        ),
        name="layer",
    )(lengths, *operands)


def write_body(
    depth,
    output_in,
    grad_in_in,
    attn_sum,
    dense_sum,
    ffn_x,
    vec_in,
    unit_sums,
    output,
    grad_in,
    grad_q,
    grad_k,
    grad_v,
    grad_d,
    grad_up,
    grad_down,
    up_b,
    query_b,
    value_b,
    *vec_rows,
):
    own = lax.axis_index("wide")
    layer = lax.axis_index("tp")
    per_layer = 8 // depth
    output[...] = output_in[...]
    grad_in[...] = grad_in_in[...]
    for number in range(per_layer):
        lanes = slice(number * BLK, (number + 1) * BLK)
        for kind, target in enumerate((grad_q, grad_k, grad_v)):
            target[:, lanes] = attn_sum[number, kind].T
    grad_d[...] = dense_sum[...].T
    for blk in range(8):
        lanes = slice(blk * BLK, (blk + 1) * BLK)
        grad_up[:, lanes] = ffn_x[blk, 0].astype(F32).T
        grad_down[lanes] = ffn_x[blk, 1].astype(F32)
    for row in range(up_b.shape[0]):
        unit = unit_sums[2 * row + own // 4, pl.ds(6 + layer, 1)]
        moved = pltpu.roll(unit, (BLK - 32 * (own % 4)) % BLK, 1)
        up_b[row : row + 1] = moved[:, :32]
        shift = (BLK - ((row % 2) * HEAD + 8 * own)) % BLK
        for place, target in enumerate((query_b, value_b)):
            unit = unit_sums[dev_of(per_layer * layer + row // 2), pl.ds(6 + depth + place, 1)]
            target[row : row + 1] = pltpu.roll(unit, shift, 1)[:, :8]
    for place, target in enumerate(vec_rows):
        target[...] = vec_in[pl.ds(place, 1)]


def write_out(depth, *pieces):
    per_layer = 8 // depth
    width = pieces[0].shape[-1]
    rows = jax.ShapeDtypeStruct(pieces[0].shape, BF)
    square = jax.ShapeDtypeStruct((BLK, per_layer * BLK), F32)
    head = jax.ShapeDtypeStruct((4, 8), F32)
    return pl.pallas_call(
        functools.partial(write_body, depth),
        out_shape=[
            rows,
            rows,
            square,
            square,
            square,
            jax.ShapeDtypeStruct((per_layer * BLK, BLK), F32),
            jax.ShapeDtypeStruct((BLK, width), F32),
            jax.ShapeDtypeStruct((width, BLK), F32),
            jax.ShapeDtypeStruct((4, 32), F32),
            head,
            head,
        ]
        + [jax.ShapeDtypeStruct((1, BLK), F32)] * 6,
        in_specs=[vmem()] * 7,
        out_specs=[vmem()] * 17,
        name="write_out",
    )(*pieces)


def square_device(
    hidden_in,
    lengths,
    pre_gain,
    pre_shift,
    w_query,
    w_key,
    w_value,
    b_query,
    b_value,
    w_dense,
    b_dense,
    mid_gain,
    mid_shift,
    w_up,
    b_up,
    w_down,
    b_down,
    cotangent,
):
    depth = lax.axis_size("tp")
    pieces = layer_pass(
        depth,
        lengths,
        hidden_in,
        cotangent,
        w_query,
        w_key,
        w_value,
        w_dense,
        w_up,
        w_down,
        pre_gain,
        pre_shift,
        mid_gain,
        mid_shift,
        b_dense,
        b_down,
        b_up,
        b_query,
        b_value,
    )
    (
        output,
        grad_in,
        grad_q,
        grad_k,
        grad_v,
        grad_d,
        grad_up,
        grad_down,
        up_b,
        query_b,
        value_b,
        *vec_rows,
    ) = write_out(depth, *pieces)
    vec_sums = [row.reshape(BLK) for row in vec_rows]
    return (
        output,
        grad_in,
        vec_sums[0],
        vec_sums[1],
        grad_q,
        grad_k,
        grad_v,
        query_b,
        value_b,
        grad_d,
        vec_sums[2],
        vec_sums[3],
        vec_sums[4],
        grad_up,
        up_b,
        grad_down,
        vec_sums[5],
    )


def solution(mesh):
    square = mesh.shape["wide"] == 8 and mesh.shape["tp"] == 4
    return jax.shard_map(
        square_device if square else per_device,
        mesh=mesh,
        in_specs=(
            P("tp", "wide", None),
            P(),
            P("wide"),
            P("wide"),
            P("wide", "tp"),
            P("wide", "tp"),
            P("wide", "tp"),
            P("tp", "wide"),
            P("tp", "wide"),
            P("tp", "wide"),
            P("wide"),
            P("wide"),
            P("wide"),
            P("wide", "tp"),
            P("tp", "wide"),
            P("tp", "wide"),
            P("wide"),
            P("tp", "wide", None),
        ),
        out_specs=(
            P("tp", "wide", None),
            P("tp", "wide", None),
            P("wide"),
            P("wide"),
            P("wide", "tp"),
            P("wide", "tp"),
            P("wide", "tp"),
            P("tp", "wide"),
            P("tp", "wide"),
            P("tp", "wide"),
            P("wide"),
            P("wide"),
            P("wide"),
            P("wide", "tp"),
            P("tp", "wide"),
            P("tp", "wide"),
            P("wide"),
        ),
        check_vma=False,
    )
```

```python
import functools
import math

import jax
import jax.numpy as jnp
from jax import lax
from jax.experimental import pallas as pl
from jax.experimental.pallas import tpu as pltpu
from jax.sharding import PartitionSpec as P

HEAD = 64
MESH = pl.DeviceIdType.MESH


def norm_rows(values, gain_vec, shift_vec):
    middle = jnp.mean(values, axis=-1, keepdims=True)
    centred = values - middle
    spread = jnp.mean(centred * centred, axis=-1, keepdims=True)
    return centred * lax.rsqrt(spread + 1e-05) * gain_vec + shift_vec


def flatten_rows(tensor):
    return tensor.reshape(-1, tensor.shape[-1])


def row_product(first_op, second_op):
    return jnp.dot(first_op, second_op, preferred_element_type=jnp.float32)


def inner_rows(first_op, second_op):
    return lax.dot_general(
        flatten_rows(first_op),
        flatten_rows(second_op),
        (((0,), (0,)), ((), ())),
        preferred_element_type=jnp.float32,
    )


def times_transposed(first_op, second_op):
    return lax.dot_general(
        first_op,
        second_op,
        (((first_op.ndim - 1,), (1,)), ((), ())),
        preferred_element_type=jnp.float32,
    )


def activate(values):
    return jax.nn.gelu(values, approximate=True)


def masked_scores(query_blk, key_blk, lengths_blk, slopes, distance, causal_mask, key_places):
    raw_scores = (
        jnp.einsum("gihd,gjhd->ghij", query_blk, key_blk, preferred_element_type=jnp.float32)
        * 0.125
    )
    raw_scores = raw_scores - slopes[None, :, None, None] * distance[None, None]
    allowed = causal_mask[None] & (key_places[None, None, :] < lengths_blk[:, None, None])
    return jnp.where(allowed[:, None], raw_scores, -jnp.inf)


def per_device(
    hidden_in,
    lengths,
    pre_gain,
    pre_shift,
    w_query,
    w_key,
    w_value,
    b_query,
    b_value,
    w_dense,
    b_dense,
    mid_gain,
    mid_shift,
    w_up,
    b_up,
    w_down,
    b_down,
    cotangent,
):
    local_slots, block_len, _unused = hidden_in.shape
    heads_dev = b_query.shape[0]
    head_width = heads_dev * HEAD
    slot_total = local_slots * lax.axis_size("tp")
    slot_len = block_len * lax.axis_size("wide")
    wide_at = lax.axis_index("wide")
    tp_at = lax.axis_index("tp")
    vec_part = pre_gain.shape[0]
    (
        gain_one,
        shift_one,
        query_w,
        key_w,
        value_w,
        query_b,
        value_b,
        dense_w,
        dense_b,
        gain_two,
        shift_two,
        up_w,
        up_b,
        down_w,
        down_b,
    ) = (
        lax.all_gather(pre_gain, "wide", axis=0, tiled=True),
        lax.all_gather(pre_shift, "wide", axis=0, tiled=True),
        lax.all_gather(w_query, "wide", axis=0, tiled=True),
        lax.all_gather(w_key, "wide", axis=0, tiled=True),
        lax.all_gather(w_value, "wide", axis=0, tiled=True),
        lax.all_gather(b_query, "wide", axis=1, tiled=True),
        lax.all_gather(b_value, "wide", axis=1, tiled=True),
        lax.all_gather(w_dense, "wide", axis=1, tiled=True),
        lax.all_gather(b_dense, "wide", axis=0, tiled=True),
        lax.all_gather(mid_gain, "wide", axis=0, tiled=True),
        lax.all_gather(mid_shift, "wide", axis=0, tiled=True),
        lax.all_gather(w_up, "wide", axis=0, tiled=True),
        lax.all_gather(b_up, "wide", axis=1, tiled=True),
        lax.all_gather(w_down, "wide", axis=1, tiled=True),
        lax.all_gather(b_down, "wide", axis=0, tiled=True),
    )
    gain_one = gain_one.astype(jnp.float32)
    shift_one = shift_one.astype(jnp.float32)
    gain_two = gain_two.astype(jnp.float32)
    shift_two = shift_two.astype(jnp.float32)
    query_places = wide_at * block_len + jnp.arange(block_len, dtype=jnp.int32)
    key_places = jnp.arange(slot_len, dtype=jnp.int32)
    distance = (query_places[:, None] - key_places[None, :]).astype(jnp.float32)
    causal_mask = key_places[None, :] <= query_places[:, None]
    head_index = tp_at * heads_dev + jnp.arange(heads_dev, dtype=jnp.int32)
    slopes = jnp.exp2(-0.5 * (head_index.astype(jnp.float32) + 1.0))
    own_lengths = lax.dynamic_slice_in_dim(lengths, tp_at * local_slots, local_slots, 0)
    validity = (query_places[None, :] < own_lengths[:, None]).astype(jnp.float32)
    group_size = math.gcd(slot_total, max(1, 512 // block_len))
    group_count = slot_total // group_size
    grouped_lengths = lengths.reshape(group_count, group_size)
    hidden = hidden_in.astype(jnp.float32)

    def query_view(tensor):
        return tensor.reshape(group_count, group_size, block_len, heads_dev, HEAD)

    def pair_view(tensor):
        return tensor.reshape(group_count, group_size, slot_len, 2, heads_dev, HEAD)

    def forward_group(inputs):
        query_blk, pair_blk, lengths_blk = inputs
        masked = masked_scores(
            query_blk, pair_blk[:, :, 0], lengths_blk, slopes, distance, causal_mask, key_places
        )
        highest = jnp.max(masked, axis=-1, keepdims=True)
        totals = highest + jnp.log(jnp.sum(jnp.exp(masked - highest), axis=-1, keepdims=True))
        probabilities = jnp.exp(masked - totals).astype(jnp.bfloat16)
        summed = jnp.einsum(
            "ghij,gjhd->gihd", probabilities, pair_blk[:, :, 1], preferred_element_type=jnp.float32
        )
        return (totals[..., 0], summed)

    def attention_forward(hidden_rows):
        normed_f, norm_back = jax.vjp(norm_rows, hidden_rows, gain_one, shift_one)
        normed = normed_f.astype(jnp.bfloat16)
        normed_all = lax.all_gather(normed, "tp", axis=0, tiled=True)
        queries = (
            row_product(normed_all, query_w) + query_b.reshape(head_width).astype(jnp.float32)
        ).astype(jnp.bfloat16)
        keys_now = row_product(normed_all, key_w).astype(jnp.bfloat16)
        values_now = (
            row_product(normed_all, value_w) + value_b.reshape(head_width).astype(jnp.float32)
        ).astype(jnp.bfloat16)
        pairs = jnp.concatenate([keys_now, values_now], axis=-1)
        pairs_all = lax.all_gather(pairs, "wide", axis=1, tiled=True)
        totals, summed = lax.map(
            forward_group, (query_view(queries), pair_view(pairs_all), grouped_lengths)
        )
        return (
            normed_all,
            queries,
            pairs_all,
            totals,
            summed.reshape(slot_total, block_len, head_width),
            norm_back,
        )

    forward_parts = attention_forward(hidden)
    attention = forward_parts[4].astype(jnp.bfloat16)
    branch = lax.psum_scatter(
        row_product(attention, dense_w).astype(jnp.bfloat16), "tp", scatter_dimension=0, tiled=True
    ).astype(jnp.float32)
    residual = hidden + branch + dense_b.astype(jnp.float32)
    second_f, second_back = jax.vjp(norm_rows, residual, gain_two, shift_two)
    second = second_f.astype(jnp.bfloat16)
    grad_output = validity[:, :, None] * cotangent.astype(jnp.float32)
    grad_down = grad_output.astype(jnp.bfloat16)
    second_all, grad_down_all = (
        lax.all_gather(second, "tp", axis=0, tiled=True),
        lax.all_gather(grad_down, "tp", axis=0, tiled=True),
    )
    pre_act = row_product(second_all, up_w) + up_b.reshape(-1).astype(jnp.float32)
    act_value, act_back = jax.vjp(activate, pre_act)
    activated = act_value.astype(jnp.bfloat16)
    down_out = lax.psum_scatter(
        row_product(activated, down_w).astype(jnp.bfloat16), "tp", scatter_dimension=0, tiled=True
    ).astype(jnp.float32)
    grad_act = times_transposed(grad_down_all, down_w)
    grad_pre = act_back(grad_act)[0].astype(jnp.bfloat16)
    grad_up = inner_rows(second_all, grad_pre)
    grad_up_b = jnp.sum(flatten_rows(grad_pre), axis=0, dtype=jnp.float32).reshape(up_b.shape)
    grad_down_w = inner_rows(activated, grad_down_all)
    grad_second = lax.psum_scatter(
        times_transposed(grad_pre, up_w), "tp", scatter_dimension=0, tiled=True
    )
    output = (validity[:, :, None] * (residual + down_out + down_b.astype(jnp.float32))).astype(
        jnp.bfloat16
    )
    grad_resid_norm, grad_gain_two, grad_shift_two = second_back(grad_second)
    grad_resid = grad_output + grad_resid_norm
    grad_branch = grad_resid.astype(jnp.bfloat16)
    hidden_again, grad_branch = lax.optimization_barrier((hidden, grad_branch))
    forward_parts = attention_forward(hidden_again)
    normed_all, queries, pairs_all, totals, summed, norm_back = forward_parts
    attention_back = summed.astype(jnp.bfloat16)
    branch_all = lax.all_gather(grad_branch, "tp", axis=0, tiled=True)
    grad_dense_w = inner_rows(attention_back, branch_all)
    grad_attention = times_transposed(branch_all, dense_w).astype(jnp.bfloat16)

    def backward_group(inputs):
        query_blk, pair_blk, lengths_blk, totals_blk, grad_blk = inputs
        masked = masked_scores(
            query_blk, pair_blk[:, :, 0], lengths_blk, slopes, distance, causal_mask, key_places
        )
        probabilities = jnp.exp(masked - totals_blk[..., None])
        grad_probs = jnp.einsum(
            "gihd,gjhd->ghij", grad_blk, pair_blk[:, :, 1], preferred_element_type=jnp.float32
        )
        row_delta = jnp.sum(probabilities * grad_probs, axis=-1, keepdims=True)
        grad_scores = (probabilities * (grad_probs - row_delta)).astype(jnp.bfloat16)
        grad_query = (
            jnp.einsum(
                "ghij,gjhd->gihd",
                grad_scores,
                pair_blk[:, :, 0],
                preferred_element_type=jnp.float32,
            )
            * 0.125
        )
        grad_key = (
            jnp.einsum(
                "ghij,gihd->gjhd", grad_scores, query_blk, preferred_element_type=jnp.float32
            )
            * 0.125
        )
        grad_value = jnp.einsum(
            "ghij,gihd->gjhd",
            probabilities.astype(jnp.bfloat16),
            grad_blk,
            preferred_element_type=jnp.float32,
        )
        return (grad_query, jnp.stack([grad_key, grad_value], axis=2))

    grad_query_all, grad_pairs = lax.map(
        backward_group,
        (
            query_view(queries),
            pair_view(pairs_all),
            grouped_lengths,
            totals,
            query_view(grad_attention),
        ),
    )
    grad_pairs_local = lax.psum_scatter(
        grad_pairs.reshape(slot_total, slot_len, 2 * head_width).astype(jnp.bfloat16),
        "wide",
        scatter_dimension=1,
        tiled=True,
    ).astype(jnp.float32)
    grad_queries = grad_query_all.reshape(slot_total, block_len, head_width).astype(jnp.bfloat16)
    grad_keys = grad_pairs_local[:, :, :head_width].astype(jnp.bfloat16)
    grad_values = grad_pairs_local[:, :, head_width:].astype(jnp.bfloat16)
    grad_query_w = inner_rows(normed_all, grad_queries)
    grad_key_w = inner_rows(normed_all, grad_keys)
    grad_value_w = inner_rows(normed_all, grad_values)
    grad_query_b = jnp.sum(flatten_rows(grad_queries), axis=0, dtype=jnp.float32).reshape(
        heads_dev, HEAD
    )
    grad_value_b = jnp.sum(flatten_rows(grad_values), axis=0, dtype=jnp.float32).reshape(
        heads_dev, HEAD
    )
    grad_normed = lax.psum_scatter(
        (
            times_transposed(grad_queries, query_w)
            + times_transposed(grad_keys, key_w)
            + times_transposed(grad_values, value_w)
        ).astype(jnp.bfloat16),
        "tp",
        scatter_dimension=0,
        tiled=True,
    ).astype(jnp.float32)
    grad_hidden_norm, grad_gain_one, grad_shift_one = norm_back(grad_normed)
    grad_in = (grad_resid + grad_hidden_norm).astype(jnp.bfloat16)
    (
        sum_query_w,
        sum_key_w,
        sum_value_w,
        sum_query_b,
        sum_value_b,
        sum_dense_w,
        sum_up_w,
        sum_up_b,
        sum_down_w,
    ) = (
        lax.psum_scatter(
            grad_query_w.astype(jnp.bfloat16), "wide", scatter_dimension=0, tiled=True
        ).astype(jnp.float32),
        lax.psum_scatter(
            grad_key_w.astype(jnp.bfloat16), "wide", scatter_dimension=0, tiled=True
        ).astype(jnp.float32),
        lax.psum_scatter(
            grad_value_w.astype(jnp.bfloat16), "wide", scatter_dimension=0, tiled=True
        ).astype(jnp.float32),
        lax.psum_scatter(
            grad_query_b.astype(jnp.bfloat16), "wide", scatter_dimension=1, tiled=True
        ).astype(jnp.float32),
        lax.psum_scatter(
            grad_value_b.astype(jnp.bfloat16), "wide", scatter_dimension=1, tiled=True
        ).astype(jnp.float32),
        lax.psum_scatter(
            grad_dense_w.astype(jnp.bfloat16), "wide", scatter_dimension=1, tiled=True
        ).astype(jnp.float32),
        lax.psum_scatter(
            grad_up.astype(jnp.bfloat16), "wide", scatter_dimension=0, tiled=True
        ).astype(jnp.float32),
        lax.psum_scatter(
            grad_up_b.astype(jnp.bfloat16), "wide", scatter_dimension=1, tiled=True
        ).astype(jnp.float32),
        lax.psum_scatter(
            grad_down_w.astype(jnp.bfloat16), "wide", scatter_dimension=1, tiled=True
        ).astype(jnp.float32),
    )
    grad_dense_b = jnp.sum(grad_resid, axis=(0, 1))
    grad_down_b = jnp.sum(grad_output, axis=(0, 1))
    sum_gain_one, sum_shift_one, sum_dense_b, sum_gain_two, sum_shift_two, sum_down_b = lax.psum(
        (grad_gain_one, grad_shift_one, grad_dense_b, grad_gain_two, grad_shift_two, grad_down_b),
        ("wide", "tp"),
    )

    def own_part(tensor):
        return lax.dynamic_slice_in_dim(tensor, wide_at * vec_part, vec_part, 0)

    return (
        output,
        grad_in,
        own_part(sum_gain_one),
        own_part(sum_shift_one),
        sum_query_w,
        sum_key_w,
        sum_value_w,
        sum_query_b,
        sum_value_b,
        sum_dense_w,
        own_part(sum_dense_b),
        own_part(sum_gain_two),
        own_part(sum_shift_two),
        sum_up_w,
        sum_up_b,
        sum_down_w,
        own_part(sum_down_b),
    )


BF = jnp.bfloat16
F32 = jnp.float32
LOG2E = 1.4426950408889634
NEG = -1e30
BLK = 128


def hbm():
    return pl.BlockSpec(memory_space=pl.ANY)


def vmem():
    return pl.BlockSpec(memory_space=pltpu.VMEM)


def square_places():
    own = lax.axis_index("wide")
    core = own % 2
    col = (own // 2) % 2
    row = own // 4
    pair = own + 1 - 2 * core
    along_x = own + 2 - 4 * col
    along_y = own + 4 - 8 * row
    return own, pair, along_x, along_y, along_x + along_y - own


def greet(targets):
    barrier = pltpu.get_barrier_semaphore()
    for target in targets:
        pl.semaphore_signal(barrier, inc=1, device_id=target, device_id_type=MESH)
    pl.semaphore_wait(barrier, len(targets))


def remote(src, dst, send_sem, recv_sem, target):
    return pltpu.make_async_remote_copy(
        src_ref=src,
        dst_ref=dst,
        send_sem=send_sem,
        recv_sem=recv_sem,
        device_id=target,
        device_id_type=MESH,
    )


class SquareGather:
    SENDS = 13

    def __init__(self, src, place, both, send, recv, local=None):
        own, pair, ax, ay, dg = square_places()
        first, second, whole = src
        to_x, to_y, to_p = {"wide": ax}, {"wide": ay}, {"wide": pair}
        self.local = None if local is None else pltpu.make_async_copy(whole, both(own), local)
        copies = {}
        copies["x0"] = remote(first, place(0, own), send.at[0], recv.at[0], to_x)
        copies["x1"] = remote(second, place(1, own), send.at[1], recv.at[1], to_x)
        copies["y0"] = remote(first, place(0, own), send.at[2], recv.at[2], to_y)
        copies["y1"] = remote(second, place(1, own), send.at[3], recv.at[3], to_y)
        copies["d0"] = remote(place(0, ay), place(0, ay), send.at[4], recv.at[4], to_x)
        copies["d1"] = remote(place(1, ax), place(1, ax), send.at[5], recv.at[5], to_y)
        copies["p"] = remote(whole, both(own), send.at[6], recv.at[6], to_p)
        for index, (name, slot, dev) in enumerate(
            (("x0", 0, ax), ("x1", 1, ax), ("y0", 0, ay), ("y1", 1, ay), ("d0", 0, dg), ("d1", 1, dg))
        ):
            copies["p" + name] = remote(
                place(slot, dev), place(slot, dev), send.at[7 + index], recv.at[7 + index], to_p
            )
        self.copies = copies

    def start(self):
        for name in ("y0", "x1", "x0", "y1", "p"):
            self.copies[name].start()
        if self.local is not None:
            self.local.start()

    def pass_on(self, arrived, sends):
        self.copies[arrived].wait_recv()
        for name in sends:
            self.copies[name].start()

    def first(self):
        self.pass_on("y0", ("d0", "py0"))
        self.pass_on("x1", ("d1", "px1"))

    def second(self):
        self.pass_on("x0", ("px0",))
        self.pass_on("y1", ("py1",))

    def third(self):
        self.pass_on("d0", ("pd0",))
        self.pass_on("d1", ("pd1",))

    def arrive(self, *names):
        for name in names:
            self.copies[name].wait_recv()

    def sent(self):
        for copy in self.copies.values():
            copy.wait_send()


def wide_square(own_places):
    _own, pair, ax, ay, _dg = own_places
    return [{"wide": pair}, {"wide": ax}, {"wide": ay}]


def add_rows(dst, first, second, third=None):
    step = 16

    def body(index, carry):
        rows = pl.ds(pl.multiple_of(index * step, step), step)
        total = first[rows].astype(F32) + second[rows].astype(F32)
        if third is not None:
            total = total + third[rows].astype(F32)
        dst[rows] = total.astype(dst.dtype)
        return carry

    lax.fori_loop(0, BLK // step, body, 0)


class SquareScatter:
    SENDS = 10

    def __init__(self, both, half, out, summed_both, summed, from_x, from_y, send, recv):
        own, pair, ax, ay, dg = square_places()
        shift = pair - own
        to_x, to_y, to_p = {"wide": ax}, {"wide": ay}, {"wide": pair}
        self.half, self.out = half, out
        self.summed, self.from_x, self.from_y = summed, from_x, from_y
        self.dests = (dg, ax, ay, own)
        self.pairs = [
            remote(
                both(self.dests[chip] + shift), summed_both(chip), send.at[chip], recv.at[chip], to_p
            )
            for chip in range(4)
        ]
        self.dx = remote(summed(0, 0), from_x(0), send.at[4], recv.at[4], to_x)
        self.dy = remote(summed(0, 1), from_y(0), send.at[5], recv.at[5], to_y)
        self.xx = remote(summed(1, 0), from_x(1), send.at[6], recv.at[6], to_x)
        self.yy = remote(summed(2, 1), from_y(1), send.at[7], recv.at[7], to_y)
        self.ty = remote(summed(2, 0), from_y(2), send.at[8], recv.at[8], to_y)
        self.tx = remote(summed(1, 1), from_x(2), send.at[9], recv.at[9], to_x)

    def pair_sum(self, chip, slot, third=None):
        place = self.summed(chip, slot)
        add_rows(place, self.half(slot, self.dests[chip]), place, third)

    def near(self, chip):
        self.pairs[chip].wait_recv()
        if chip == 0:
            self.pair_sum(0, 0)
            self.dx.start()
            self.pair_sum(0, 1)
            self.dy.start()
        elif chip == 1:
            self.pair_sum(1, 0)
            self.xx.start()
        elif chip == 2:
            self.pair_sum(2, 1)
            self.yy.start()
        else:
            self.pair_sum(3, 0)
            self.pair_sum(3, 1)

    def middle(self):
        self.dx.wait_recv()
        self.pair_sum(2, 0, self.from_x(0))
        self.ty.start()
        self.dy.wait_recv()
        self.pair_sum(1, 1, self.from_y(0))
        self.tx.start()

    def start(self):
        for chip in range(4):
            self.pairs[chip].start()

    def finish(self):
        self.xx.wait_recv()
        self.ty.wait_recv()
        add_rows(self.out.at[0], self.summed(3, 0), self.from_x(1), self.from_y(2))
        self.yy.wait_recv()
        self.tx.wait_recv()
        add_rows(self.out.at[1], self.summed(3, 1), self.from_y(1), self.from_x(2))
        for copy in self.pairs:
            copy.wait_send()
        for copy in (self.dx, self.dy, self.xx, self.yy, self.ty, self.tx):
            copy.wait_send()


class LineGather:
    def __init__(self, depth, pieces, send, recv):
        self.depth, self.pieces, self.send, self.recv = depth, pieces, send, recv
        self.layer = lax.axis_index("tp")

    def copies(self, step, up):
        index = self.layer - step + 1 if up else self.layer + step - 1
        goal = {"tp": self.layer + 1 if up else self.layer - 1}
        side = 0 if up else 1
        made = []
        for number, (own, place) in enumerate(self.pieces):
            source = own if step == 1 else place(index)
            made.append(
                remote(
                    source,
                    place(index),
                    self.send.at[side, number, step - 1],
                    self.recv.at[side, number, step - 1],
                    goal,
                )
            )
        return made

    def each(self, step, act):
        layer = self.layer

        @pl.when((layer < self.depth - 1) & (layer - step + 1 >= 0))
        def _():
            for copy in self.copies(step, True):
                act(copy)

        @pl.when((layer > 0) & (layer + step - 1 < self.depth))
        def _():
            for copy in self.copies(step, False):
                act(copy)

    def start(self, step):
        self.each(step, lambda copy: copy.start())

    def sent(self, step):
        self.each(step, lambda copy: copy.wait_send())

    def arrive(self, step):
        layer = self.layer

        @pl.when(layer - step >= 0)
        def _():
            for copy in self.copies(step, True):
                copy.wait_recv()

        @pl.when(layer + step < self.depth)
        def _():
            for copy in self.copies(step, False):
                copy.wait_recv()


def wide_others(own):
    return [{"wide": (own + step) % 8} for step in range(1, 8)]


def head_bias(length, slope, rows):
    place = lax.broadcasted_iota(jnp.int32, (rows, QB), 0)
    return jnp.where(place < length, slope * place.astype(F32), NEG)


QB = 256


def dot_nt(first, second):
    return lax.dot_general(first, second, (((1,), (1,)), ((), ())), preferred_element_type=F32)


def dot_nn(first, second):
    return lax.dot_general(first, second, (((1,), (0,)), ((), ())), preferred_element_type=F32)


def later_key(size):
    key_place = lax.broadcasted_iota(jnp.int32, (size, size), 0)
    query_place = lax.broadcasted_iota(jnp.int32, (size, size), 1)
    return key_place > query_place


def slot_scores(key, query, bias, step):
    extent = (step + 1) * QB
    scores = dot_nt(key[:extent], query) * (0.125 * LOG2E) + bias[:extent]
    edge = jnp.where(later_key(QB), NEG, scores[extent - QB :])
    return edge if step == 0 else jnp.concatenate([scores[: extent - QB], edge], 0)


def attend_head(slot, head, length, slopes, qkv, out, totals, bias):
    rows = qkv.shape[1]
    lanes = pl.ds(head * HEAD, HEAD)
    bias[...] = head_bias(length, slopes[head], rows)
    key = qkv[slot, :, pl.ds(2 * HEAD + head * HEAD, HEAD)]
    value_t = qkv[slot, :, pl.ds(4 * HEAD + head * HEAD, HEAD)].T
    for step in range(rows // QB):
        here = pl.ds(step * QB, QB)
        scores = slot_scores(key, qkv[slot, here, lanes], bias, step)
        highest = jnp.max(scores, axis=0, keepdims=True)
        weights = jnp.exp2(scores - highest)
        total = jnp.sum(weights, axis=0, keepdims=True)
        mixed = dot_nn(value_t[:, : (step + 1) * QB], weights.astype(BF)) / total
        out[slot, here, lanes] = mixed.T.astype(BF)
        totals[slot, pl.ds(head, 1), here] = highest + jnp.log2(total)


def attend_head_back(
    slot, head, length, slopes, qkv, attention, grad, totals, out, bias, key_sum, value_sum
):
    rows = qkv.shape[1]
    lanes = pl.ds(head * HEAD, HEAD)
    key_lanes = pl.ds(2 * HEAD + head * HEAD, HEAD)
    value_lanes = pl.ds(4 * HEAD + head * HEAD, HEAD)
    bias[...] = head_bias(length, slopes[head], rows)
    key = qkv[slot, :, key_lanes]
    value = qkv[slot, :, value_lanes]
    key_t = key.T
    key_sum[...] = jnp.zeros_like(key_sum)
    value_sum[...] = jnp.zeros_like(value_sum)
    for step in range(rows // QB):
        here = pl.ds(step * QB, QB)
        extent = (step + 1) * QB
        query = qkv[slot, here, lanes]
        grad_rows = grad[slot, here, lanes]
        product = grad_rows.astype(F32) * attention[slot, here, lanes].astype(F32)
        delta = jnp.sum(product.T, axis=0, keepdims=True)
        scores = slot_scores(key, query, bias, step)
        probs = jnp.exp2(scores - totals[slot, pl.ds(head, 1), here])
        grad_probs = dot_nt(value[:extent], grad_rows)
        grad_scores = (probs * (grad_probs - delta)).astype(BF)
        span = pl.ds(0, extent)
        value_sum[span] += dot_nn(probs.astype(BF), grad_rows)
        key_sum[span] += dot_nn(grad_scores, query)
        grad_query = dot_nn(key_t[:, :extent], grad_scores)
        out[slot, here, lanes] = (grad_query.T * 0.125).astype(BF)
    out[slot, :, key_lanes] = (key_sum[...] * 0.125).astype(BF)
    out[slot, :, value_lanes] = value_sum[...].astype(BF)


def line_others(depth):
    layer = lax.axis_index("tp")
    return [{"tp": (layer + step) % depth} for step in range(1, depth)]


VMEM_MAX = 67043328


def norm_stats(values):
    middle = jnp.mean(values, axis=-1, keepdims=True)
    centred = values - middle
    spread = jnp.mean(centred * centred, axis=-1, keepdims=True)
    inverse = lax.rsqrt(spread + 1e-05)
    return centred * inverse, inverse


def norm_back_rows(grad, hat, inverse, gain):
    scaled = grad * gain
    first = jnp.mean(scaled, axis=-1, keepdims=True)
    second = jnp.mean(scaled * hat, axis=-1, keepdims=True)
    return (scaled - first - hat * second) * inverse


def gelu_parts(values):
    root = math.sqrt(2 / math.pi)
    squared = values * values
    inner = jnp.tanh(root * values * (1.0 + 0.044715 * squared))
    half = 0.5 * (1.0 + inner)
    slope = half + 0.5 * values * (1.0 - inner * inner) * root * (1.0 + 3 * 0.044715 * squared)
    return values * half, slope


def relation(index):
    own = lax.axis_index("wide")
    core = (own + index) % 2
    col = (own // 2 + index // 2) % 2
    row = (own // 4 + index // 4) % 2
    return row * 4 + col * 2 + core


class WideExchange:
    def __init__(self, source, target, send, recv):
        own = lax.axis_index("wide")
        self.copies = [
            remote(
                source((own + step) % 8),
                target(own),
                send.at[step - 1],
                recv.at[step - 1],
                {"wide": (own + step) % 8},
            )
            for step in range(1, 8)
        ]

    def start(self):
        for copy in self.copies:
            copy.start()

    def arrive(self):
        for copy in self.copies:
            copy.wait_recv()

    def sent(self):
        for copy in self.copies:
            copy.wait_send()


def layer_body(
    depth,
    lengths,
    hidden,
    cotangent,
    w_query,
    w_key,
    w_value,
    w_dense,
    w_up,
    w_down,
    pre_gain,
    pre_shift,
    mid_gain,
    mid_shift,
    b_dense,
    b_down,
    b_up,
    b_query,
    b_value,
    output,
    grad_in,
    attn_sum,
    dense_sum,
    ffn_x,
    vec_sums,
    unit_sums,
    hidden_all,
    normed,
    down_all,
    second_share,
    down_share,
    qkv,
    attention,
    grad_att,
    act_t,
    pre_t,
    totals,
    bias,
    key_sum,
    value_sum,
    qkv_w,
    dense_all,
    att_own,
    att_grad_own,
    up_t,
    down_t,
    up_w,
    down_w,
    z_qkv,
    z_vec,
    vec_wide,
    vec_line,
    vec_wide_all,
    vec_line_all,
    vectors,
    up_bias,
    qkv_bias,
    own_rows,
    down_own,
    residual,
    grad_second,
    grad_resid,
    down_out,
    sums,
    up_sum,
    ffn_g,
    ffn_in,
    ffn_sum,
    attn_g,
    attn_in,
    attn_z,
    dense_out,
    dense_in,
    parts,
    parts_bf,
    gathered,
    a_summed,
    a_x,
    a_y,
    b_summed,
    b_x,
    b_y,
    gather_send,
    gather_recv,
    gather_local,
    scatter_send,
    scatter_recv,
    line_send,
    line_recv,
    ffn_line_send,
    ffn_line_recv,
    wide_send,
    wide_recv,
    grad_line_send,
    grad_line_recv,
    onward_send,
    onward_recv,
    dense_send,
    dense_recv,
    own_sems,
):
    own = lax.axis_index("wide")
    layer = lax.axis_index("tp")
    per_layer = 8 // depth
    width = hidden.shape[-1]
    step = 32
    steps = BLK // step
    others = [
        ((own + side) % 8, (layer + up) % depth)
        for up in range(depth)
        for side in range(8)
        if up or side
    ]
    own_lanes = pl.ds(pl.multiple_of(own * BLK, BLK), BLK)

    for place, ref in enumerate((pre_gain, pre_shift, mid_gain, mid_shift, b_dense, b_down)):
        vec_wide[pl.ds(place, 1)] = ref[...].astype(F32)
    vec_line[...] = jnp.zeros_like(vec_line)
    vec_line[0 : b_up.shape[0], 0 : b_up.shape[1]] = b_up[...].astype(F32)
    vec_line[b_up.shape[0] :, 0:8] = b_query[...].astype(F32)
    vec_line[b_up.shape[0] :, 8:16] = b_value[...].astype(F32)
    first_row = own * BLK

    def token_mask(slot, rows, count):
        place = first_row + rows * count + lax.broadcasted_iota(jnp.int32, (count, BLK), 0)
        inside = place < lengths[layer * 2 + slot]
        return jnp.where(inside, 1.0, 0.0).astype(F32)[:, :1]

    def down_part(index, carry):
        rows = pl.ds(pl.multiple_of(index * step, step), step)
        for slot in range(2):
            values = token_mask(slot, index, step) * cotangent[slot, rows].astype(F32)
            down_own[slot, rows] = values.astype(BF)
        return carry

    lax.fori_loop(0, steps, down_part, 0)
    greet(wide_others(own) + line_others(depth))

    def block_rows(dev):
        return pl.ds(pl.multiple_of(dev * BLK, BLK), BLK)

    def gather_of(number, src, dst):
        return SquareGather(
            (src.at[0], src.at[1], src),
            lambda slot, dev: dst.at[slot, block_rows(dev)],
            lambda dev: dst.at[:, block_rows(dev)],
            gather_send.at[number],
            gather_recv.at[number],
            gather_local.at[number],
        )

    def wide_of(number, source, target):
        return WideExchange(source, target, wide_send.at[number], wide_recv.at[number])

    gains = wide_of(0, lambda dev: vec_wide, lambda dev: vec_wide_all.at[dev])
    gains.start()
    hid = gather_of(0, hidden, hidden_all)
    hid.start()
    line = LineGather(
        depth,
        [
            (w_query, lambda at: z_qkv.at[at, 0]),
            (w_key, lambda at: z_qkv.at[at, 1]),
            (w_value, lambda at: z_qkv.at[at, 2]),
            (w_dense, lambda at: dense_all.at[own, at]),
            (vec_line, lambda at: z_vec.at[at]),
        ],
        line_send,
        line_recv,
    )
    line.start(1)
    own_copies = [
        pltpu.make_async_copy(ref, place(layer), own_sems.at[number])
        for number, (ref, place) in enumerate(line.pieces)
    ]
    for copy in own_copies:
        copy.start()
    vec_wide_all[own] = vec_wide[...]
    gains.arrive()
    for dev in range(8):
        vectors[:, dev * BLK : (dev + 1) * BLK] = vec_wide_all[dev]

    def norm_block(index, carry):
        base = relation(index) * BLK

        def norm_part(part, carry):
            rows = pl.ds(pl.multiple_of(base + part * step, step), step)
            for slot in range(2):
                hat, _inverse = norm_stats(hidden_all[slot, rows].astype(F32))
                normed[slot, rows] = (hat * vectors[0:1] + vectors[1:2]).astype(BF)
            return carry

        return lax.fori_loop(0, steps, norm_part, carry)

    hid.arrive("p")
    hid.local.wait()
    lax.fori_loop(0, 2, norm_block, 0)
    hid.first()
    line.arrive(1)
    line.start(2)
    hid.second()
    ups = wide_of(
        3, lambda dev: w_up.at[:, block_rows(dev)], lambda dev: up_t.at[block_rows(dev)]
    )
    downs = wide_of(
        4, lambda dev: w_down.at[block_rows(dev)], lambda dev: down_t.at[:, block_rows(dev)]
    )
    unit_copies = [
        pltpu.make_async_copy(w_up.at[:, own_lanes], up_t.at[own_lanes], own_sems.at[6]),
        pltpu.make_async_copy(w_down.at[own_lanes], down_t.at[:, own_lanes], own_sems.at[7]),
    ]
    ups.start()
    downs.start()
    for copy in unit_copies:
        copy.start()
    line.arrive(2)
    line.start(3)
    hid.arrive("px0", "px1", "py0", "py1")
    lax.fori_loop(2, 6, norm_block, 0)
    hid.third()
    line.arrive(3)
    for copy in own_copies:
        copy.wait()

    def goal_lanes(dev):
        return pl.ds(pl.multiple_of((dev % per_layer) * BLK, BLK), BLK)

    heads = wide_of(
        1,
        lambda dev: z_qkv.at[dev // per_layer, :, :, goal_lanes(dev)],
        lambda dev: attn_in.at[dev],
    )
    biases = wide_of(2, lambda dev: z_vec, lambda dev: vec_line_all.at[dev])
    dense = SquareGather(
        (dense_all.at[own, pl.ds(0, 2)], dense_all.at[own, pl.ds(2, 2)], dense_all.at[own]),
        lambda half, dev: dense_all.at[dev, pl.ds(2 * half, 2)],
        lambda dev: dense_all.at[dev],
        gather_send.at[2],
        gather_recv.at[2],
    )
    biases.start()
    heads.start()
    dense.start()
    gd = gather_of(1, down_own, down_all)
    own_copies = [
        pltpu.make_async_copy(z_qkv.at[own // per_layer, :, :, goal_lanes(own)], attn_in.at[own], own_sems.at[5]),
    ]
    for copy in own_copies:
        copy.start()
    vec_line_all[own] = z_vec[...]
    hid.arrive("pd0", "pd1")
    lax.fori_loop(6, 8, norm_block, 0)
    biases.arrive()
    head_layer = own // per_layer
    piece = own % per_layer
    unit_row = own // 2
    for dev in range(8):
        for head in range(2):
            lanes = slice(head * HEAD + dev * 8, head * HEAD + dev * 8 + 8)
            row = pl.ds(b_up.shape[0] + 2 * piece + head, 1)
            values = vec_line_all[dev, head_layer, row]
            qkv_bias[:, lanes] = values[:, 0:8]
            lanes = slice(4 * HEAD + lanes.start, 4 * HEAD + lanes.stop)
            qkv_bias[:, lanes] = values[:, 8:16]
    qkv_bias[:, 2 * HEAD : 4 * HEAD] = jnp.zeros((1, 2 * HEAD), F32)
    for up in range(depth):
        for part in range(4):
            values = vec_line_all[4 * (own % 2) + part, up, pl.ds(unit_row, 1)]
            up_bias[:, up * BLK + part * 32 : up * BLK + part * 32 + 32] = values[:, 0:32]
    heads.arrive()
    hid.sent()
    for copy in own_copies + unit_copies:
        copy.wait()
    ups.arrive()
    downs.arrive()
    for dev in range(8):
        for kind in range(3):
            qkv_w[dev * BLK : (dev + 1) * BLK, kind * BLK : (kind + 1) * BLK] = attn_in[dev, kind]

    ffn_line = LineGather(
        depth,
        [
            (up_t, lambda at: up_w.at[:, pl.ds(pl.multiple_of(at * BLK, BLK), BLK)]),
            (down_t, lambda at: down_w.at[pl.ds(pl.multiple_of(at * BLK, BLK), BLK)]),
        ],
        ffn_line_send,
        ffn_line_recv,
    )
    ffn_line.start(1)
    unit_copies = [
        pltpu.make_async_copy(ref, place(layer), own_sems.at[8 + number])
        for number, (ref, place) in enumerate(ffn_line.pieces)
    ]
    for copy in unit_copies:
        copy.start()
    slopes = [
        jnp.exp2(-0.5 * (jnp.full((1, 1), 2 * own + head, jnp.int32).astype(F32) + 1.0)) * LOG2E
        for head in range(2)
    ]

    def att_exchange(slot):
        return wide_of(
            5 + slot,
            lambda dev: attention.at[slot, block_rows(dev)],
            lambda dev: att_own.at[slot, :, block_rows(dev)],
        )

    def att_local(slot):
        return pltpu.make_async_copy(
            attention.at[slot, block_rows(own)], att_own.at[slot, :, block_rows(own)], own_sems.at[10 + slot]
        )

    def one_slot(slot, carry):
        def block(index, carry):
            rows = pl.ds(pl.multiple_of(index * QB, QB), QB)
            qkv[slot, rows] = (dot_nn(normed[slot, rows], qkv_w[...]) + qkv_bias[...]).astype(BF)
            return carry

        lax.fori_loop(0, 8 * BLK // QB, block, 0)
        length = lengths[layer * 2 + slot]
        attend_head(slot, 0, length, slopes, qkv, attention, totals, bias)

        @pl.when(slot == 0)
        def _():
            dense.first()
            dense.second()

        attend_head(slot, 1, length, slopes, qkv, attention, totals, bias)
        att_exchange(slot).start()
        att_local(slot).start()

        @pl.when(slot == 0)
        def _():
            ffn_line.arrive(1)
            ffn_line.start(2)
            dense.third()
            gd.start()

        return carry

    lax.fori_loop(0, 2, one_slot, 0)
    gd.first()
    gd.second()
    ffn_line.arrive(2)
    ffn_line.start(3)
    dense.arrive("p", "px0", "px1", "py0", "py1", "pd0", "pd1")
    for slot in range(2):
        att_exchange(slot).arrive()
        att_local(slot).wait()

    for part in range(4):
        columns = [dense_all[2 * part + side].reshape(width, BLK) for side in range(2)]
        product = dot_nn(att_own[...].reshape(2 * BLK, width), jnp.concatenate(columns, 1))
        residual[:, :, part * QB : (part + 1) * QB] = product.reshape(2, BLK, QB)

    def scatter_of(number, share, out, buffers):
        summed, from_x, from_y = buffers
        return SquareScatter(
            lambda dev: share.at[:, block_rows(dev)],
            lambda slot, dev: share.at[slot, block_rows(dev)],
            out,
            lambda chip: summed.at[chip],
            lambda chip, slot: summed.at[chip, slot],
            lambda place: from_x.at[place],
            lambda place: from_y.at[place],
            scatter_send.at[number],
            scatter_recv.at[number],
        )

    def second_part(index, carry):
        rows = pl.ds(pl.multiple_of(index * step, step), step)
        for slot in range(2):
            values = hidden[slot, rows].astype(F32) + residual[slot, rows] + vectors[4:5]
            residual[slot, rows] = values
            hat, _inverse = norm_stats(values)
            own_rows[slot, rows] = (hat * vectors[2:3] + vectors[3:4]).astype(BF)
        return carry

    lax.fori_loop(0, steps, second_part, 0)
    second_all = hidden_all
    gather = gather_of(0, own_rows, second_all)
    gather.start()
    scatter = scatter_of(0, second_share, grad_second, (a_summed, a_x, a_y))
    gd.arrive("p")
    gd.local.wait()
    for copy in unit_copies:
        copy.wait()
    ffn_line.arrive(3)

    def compute(index, carry):
        source = relation(index)
        rows = pl.ds(pl.multiple_of(source * BLK, BLK), BLK)
        values = second_all[:, rows].reshape(2 * BLK, width)
        act_value, act_slope = gelu_parts(dot_nn(values, up_w[...]) + up_bias[...])
        activated = act_value.astype(BF)
        grad_rows = down_all[:, rows].reshape(2 * BLK, width)
        grad_pre = (dot_nt(grad_rows, down_w[...]) * act_slope).astype(BF)
        second_share[:, rows] = dot_nt(grad_pre, up_w[...]).astype(BF).reshape(2, BLK, width)
        down_share[:, rows] = dot_nn(activated, down_w[...]).astype(BF).reshape(2, BLK, width)
        up_sum[...] += jnp.sum(grad_pre.astype(F32), axis=0, keepdims=True)
        for slot in range(2):
            lanes = pl.ds(pl.multiple_of(slot * 8 * BLK + source * BLK, BLK), BLK)
            part = slice(slot * BLK, (slot + 1) * BLK)
            act_t[:, lanes] = activated[part].T
            pre_t[:, lanes] = grad_pre[part].T
        return carry

    up_sum[...] = jnp.zeros_like(up_sum)
    gather.arrive("p")
    gather.local.wait()
    lax.fori_loop(0, 2, compute, 0)
    scatter.pairs[3].start()
    gather.first()
    gd.third()
    gather.second()
    gd.arrive("px0", "px1", "py0", "py1")
    gather.arrive("px0", "px1", "py0", "py1")
    lax.fori_loop(2, 4, compute, 0)
    scatter.pairs[1].start()
    scatter.near(3)
    lax.fori_loop(4, 6, compute, 0)
    scatter.pairs[2].start()
    gather.third()
    scatter.near(1)
    gd.arrive("pd0", "pd1")
    gather.arrive("pd0", "pd1")
    lax.fori_loop(6, 8, compute, 0)
    scatter.pairs[0].start()
    scatter.near(2)
    scatter.near(0)

    def weight_grads(left, right, kind):
        def one(up, carry):
            rows = pl.ds(pl.multiple_of(up * BLK, BLK), BLK)
            total = dot_nn(left[rows, pl.ds(0, 8 * BLK)], right[0])
            total = total + dot_nn(left[rows, pl.ds(8 * BLK, 8 * BLK)], right[1])
            total = total.astype(BF)
            for blk in range(8):
                ffn_g[kind, up, blk] = total[:, blk * BLK : (blk + 1) * BLK]
            return carry

        lax.fori_loop(0, depth, one, 0)

    def line_copies(kind):
        return [
            remote(
                ffn_g.at[kind, (layer + up) % depth],
                ffn_in.at[kind, up - 1],
                grad_line_send.at[kind, up - 1],
                grad_line_recv.at[kind, up - 1],
                {"tp": (layer + up) % depth},
            )
            for up in range(1, depth)
        ]

    def line_sums(kind):
        for copy in line_copies(kind):
            copy.wait_recv()

        def add_block(blk, carry):
            total = ffn_g[kind, layer, blk].astype(F32)
            for up in range(depth - 1):
                total = total + ffn_in[kind, up, blk].astype(F32)
            ffn_sum[blk, kind] = total.astype(BF)
            return carry

        lax.fori_loop(0, 8, add_block, 0)

    weight_grads(pre_t, second_all, 0)
    for copy in line_copies(0):
        copy.start()
    scatter.middle()
    weight_grads(act_t, down_all, 1)
    for copy in line_copies(1):
        copy.start()
    scatter.finish()
    gather.sent()
    sums[...] = jnp.zeros_like(sums)

    def back_part(index, carry):
        rows = pl.ds(pl.multiple_of(index * step, step), step)
        for slot in range(2):
            hat, inverse = norm_stats(residual[slot, rows])
            grad = grad_second[slot, rows]
            grad_out = token_mask(slot, index, step) * cotangent[slot, rows].astype(F32)
            total = grad_out + norm_back_rows(grad, hat, inverse, vectors[2:3])
            grad_resid[slot, rows] = total
            own_rows[slot, rows] = total.astype(BF)
            for place, value in enumerate((total, grad * hat, grad, grad_out)):
                sums[pl.ds(place, 1)] += jnp.sum(value, axis=0, keepdims=True)
        return carry

    lax.fori_loop(0, steps, back_part, 0)
    for at in range(depth):
        columns = jnp.concatenate([dense_all[dev, at] for dev in range(8)], 1)
        product = dot_nt(own_rows[...].reshape(2 * BLK, width), columns).astype(BF)
        att_grad_own[:, :, at * QB : (at + 1) * QB] = product.reshape(2, BLK, QB)

    def att_back(slot):
        return wide_of(
            5 + slot,
            lambda dev: att_grad_own.at[slot, :, block_rows(dev)],
            lambda dev: grad_att.at[slot, block_rows(dev)],
        )

    def att_back_local(slot):
        return pltpu.make_async_copy(
            att_grad_own.at[slot, :, block_rows(own)], grad_att.at[slot, block_rows(own)], own_sems.at[12 + slot]
        )

    for sends in (gains, biases, heads, ups, downs, att_exchange(0), att_exchange(1)):
        sends.sent()
    dense.sent()
    for slot in range(2):
        att_back(slot).start()
        att_back_local(slot).start()
    down = scatter_of(1, down_share, down_out, (b_summed, b_x, b_y))
    down.start()

    half_lanes = pl.ds(0, width // 2)
    sum_lanes = pl.ds(width // 2, width // 2)
    for part in range(4):
        rows = slice(part * QB, (part + 1) * QB)
        left = own_rows[:, :, rows].reshape(2 * BLK, QB).T
        for half in range(2):
            lanes = slice(half * width // 2, (half + 1) * width // 2)
            product = dot_nn(left, att_own[:, :, lanes].reshape(2 * BLK, width // 2))
            second_all[half, rows, half_lanes] = product.astype(BF)
    dense_back = SquareScatter(
        lambda dev: second_all.at[:, block_rows(dev), half_lanes],
        lambda half, dev: second_all.at[half, block_rows(dev), half_lanes],
        dense_out,
        lambda chip: second_all.at[:, pl.ds(chip * BLK, BLK), sum_lanes],
        lambda chip, half: second_all.at[half, pl.ds(chip * BLK, BLK), sum_lanes],
        lambda place: second_all.at[0, pl.ds((4 + place) * BLK, BLK), sum_lanes],
        lambda place: second_all.at[1, pl.ds((4 + place) * BLK, BLK), sum_lanes],
        scatter_send.at[2],
        scatter_recv.at[2],
    )

    def dense_piece(at):
        return dense_out.at[at // 2, :, pl.ds(pl.multiple_of((at % 2) * QB, QB), QB)]

    def dense_copies():
        return [
            remote(
                dense_piece((layer + up) % depth),
                dense_in.at[up - 1],
                dense_send.at[up - 1],
                dense_recv.at[up - 1],
                {"tp": (layer + up) % depth},
            )
            for up in range(1, depth)
        ]

    att_back(0).arrive()
    att_back_local(0).wait()
    dense_back.start()
    for chip in range(3):
        down.near(chip)
    for chip in range(3):
        dense_back.near(chip)

    def ffn_exchange(kind):
        return wide_of(kind, lambda dev: ffn_sum.at[dev, kind], lambda dev: ffn_x.at[dev, kind])

    def slot_back(slot, carry):
        def one_head(head):
            attend_head_back(
                slot,
                head,
                lengths[layer * 2 + slot],
                slopes,
                qkv,
                attention,
                grad_att,
                totals,
                qkv,
                bias,
                key_sum,
                value_sum,
            )

        one_head(0)

        @pl.when(slot == 0)
        def _():
            down.near(3)
            down.middle()
            dense_back.near(3)

        @pl.when(slot == 1)
        def _():
            dense_back.finish()
            for copy in dense_copies():
                copy.start()
            line_sums(0)
            ffn_exchange(0).start()

        one_head(1)

        @pl.when(slot == 0)
        def _():
            dense_back.middle()
            att_back(1).arrive()
            att_back_local(1).wait()

        return carry

    lax.fori_loop(0, 2, slot_back, 0)
    grad_qkv = qkv
    weight_part = dot_nn(grad_qkv[0].T, normed[0]) + dot_nn(grad_qkv[1].T, normed[1])
    weight_part = weight_part.astype(BF)
    for kind in range(3):
        for blk in range(8):
            attn_g[blk, kind] = weight_part[
                kind * BLK : (kind + 1) * BLK, blk * BLK : (blk + 1) * BLK
            ]
    kinds = (pl.ds(0, 2), pl.ds(2, 1))
    exchanges = [
        wide_of(
            2 + group,
            lambda dev, kind=kind: attn_g.at[dev, kind],
            lambda dev, kind=kind: attn_in.at[dev, kind],
        )
        for group, kind in enumerate(kinds)
    ]

    def onward(group, index, source):
        pair = index
        return remote(
            source.at[index, kinds[group]],
            attn_z.at[layer, pair % per_layer, kinds[group]],
            onward_send.at[group, index],
            onward_recv.at[group, layer, pair % per_layer],
            {"tp": pair // per_layer},
        )

    def forward(group, index, source):
        @pl.when(index // per_layer != layer)
        def _():
            onward(group, index, source).start()

    def forward_all(group):
        for number in range(1, 8):
            exchanges[group].copies[number - 1].wait_recv()
            forward(group, (own + 8 - number) % 8, attn_in)

    exchanges[0].start()
    for group in range(2):
        forward(group, own, attn_g)
    share = second_share
    grad_normed = grad_second
    scatter = scatter_of(0, share, grad_normed, (a_summed, a_x, a_y))

    def normed_block(index, carry):
        rows = pl.ds(pl.multiple_of(relation(index) * BLK, BLK), BLK)
        values = grad_qkv[:, rows].reshape(2 * BLK, 6 * HEAD)
        share[:, rows] = dot_nt(values, qkv_w[...]).astype(BF).reshape(2, BLK, width)
        return carry

    for chip in range(4):
        start = (6, 2, 4, 0)[chip]
        lax.fori_loop(start, start + 2, normed_block, 0)
        scatter.pairs[chip].start()
        if chip:
            scatter.near(chip - 1)
    exchanges[1].start()
    line_sums(1)
    head_sum = jnp.sum(grad_qkv[0].astype(F32), axis=0, keepdims=True)
    head_sum = head_sum + jnp.sum(grad_qkv[1].astype(F32), axis=0, keepdims=True)
    down.finish()

    def out_part(index, carry):
        rows = pl.ds(pl.multiple_of(index * step, step), step)
        for slot in range(2):
            total = residual[slot, rows] + down_out[slot, rows] + vectors[5:6]
            output[slot, rows] = (token_mask(slot, index, step) * total).astype(BF)
        return carry

    lax.fori_loop(0, steps, out_part, 0)
    forward_all(0)
    scatter.near(3)
    scatter.middle()
    ffn_exchange(1).start()
    forward_all(1)
    for blk in range(8):
        lanes = slice(blk * BLK, (blk + 1) * BLK)
        for place in range(4):
            parts[blk, pl.ds(2 + place, 1)] = sums[place : place + 1, lanes]
        for place in range(depth):
            parts[blk, pl.ds(6 + place, 1)] = up_sum[:, place * BLK : (place + 1) * BLK]
        parts[blk, pl.ds(6 + depth, 1)] = head_sum[:, : 2 * HEAD]
        parts[blk, pl.ds(7 + depth, 1)] = head_sum[:, 4 * HEAD :]
    scatter.finish()

    def last_part(index, carry):
        gain_sum, shift_sum = carry
        rows = pl.ds(pl.multiple_of(index * step, step), step)
        for slot in range(2):
            hat, inverse = norm_stats(hidden[slot, rows].astype(F32))
            grad = grad_normed[slot, rows]
            total = grad_resid[slot, rows] + norm_back_rows(grad, hat, inverse, vectors[0:1])
            grad_in[slot, rows] = total.astype(BF)
            gain_sum = gain_sum + jnp.sum(grad * hat, axis=0, keepdims=True)
            shift_sum = shift_sum + jnp.sum(grad, axis=0, keepdims=True)
        return gain_sum, shift_sum

    zero = jnp.zeros((1, width), F32)
    gain_sum, shift_sum = lax.fori_loop(0, steps, last_part, (zero, zero))
    for blk in range(8):
        lanes = slice(blk * BLK, (blk + 1) * BLK)
        parts[blk, pl.ds(0, 1)] = gain_sum[:, lanes]
        parts[blk, pl.ds(1, 1)] = shift_sum[:, lanes]
    gd.sent()

    def sum_sems(index):
        if index < 7:
            return wide_send.at[4, index], wide_recv.at[4, index]
        number, place = 2 - (index - 7) // SquareGather.SENDS, (index - 7) % SquareGather.SENDS
        return gather_send.at[number, place], gather_recv.at[number, place]

    parts_bf[...] = parts[...].astype(BF)
    sum_copies = [
        remote(
            parts_bf.at[wide],
            gathered.at[own, layer],
            *sum_sems(index),
            {"wide": wide, "tp": tp},
        )
        for index, (wide, tp) in enumerate(others)
    ]
    for copy in sum_copies:
        copy.start()
    gathered[own, layer] = parts_bf[own]
    for group in range(2):
        for up in range(1, depth):
            source = (layer + up) % depth
            for number in range(per_layer):
                remote(
                    attn_in.at[number, kinds[group]],
                    attn_z.at[source, number, kinds[group]],
                    onward_send.at[group, number],
                    onward_recv.at[group, source, number],
                    {"tp": source},
                ).wait_recv()
    attn_in[own] = attn_g[own]
    for number in range(per_layer):
        for kind in range(3):
            total = attn_in[layer * per_layer + number, kind].astype(F32)
            for up in range(1, depth):
                total = total + attn_z[(layer + up) % depth, number, kind].astype(F32)
            attn_sum[number, kind] = total
    for copy in dense_copies():
        copy.wait_recv()
    total = dense_out[layer // 2, :, pl.ds(pl.multiple_of((layer % 2) * QB, QB), QB)].astype(F32)
    for up in range(1, depth):
        total = total + dense_in[up - 1].astype(F32)
    dense_sum[...] = total
    ffn_x[own] = ffn_sum[own]
    for kind in range(2):
        ffn_exchange(kind).arrive()
    for copy in sum_copies:
        copy.wait_recv()

    def unit_part(dev, carry):
        total = gathered[dev, 0].astype(F32)
        for up in range(1, depth):
            total = total + gathered[dev, up].astype(F32)
        unit_sums[dev] = total
        return carry + total

    vec_sums[...] = lax.fori_loop(0, 8, unit_part, jnp.zeros((16, BLK), F32))

    for copy in sum_copies:
        copy.wait_send()
    for slot in range(2):
        att_back(slot).sent()
        ffn_exchange(slot).sent()
    for sends in exchanges:
        sends.sent()
    for number in range(1, depth):
        line.sent(number)
        ffn_line.sent(number)
    for kind in range(2):
        for copy in line_copies(kind):
            copy.wait_send()
    for copy in dense_copies():
        copy.wait_send()
    for group in range(2):
        for index in range(8):

            @pl.when(index // per_layer != layer)
            def _(index=index, group=group):
                onward(group, index, attn_in).wait_send()


def layer_pass(depth, lengths, hidden, cotangent, *weights):
    width = hidden.shape[-1]
    units = depth * BLK
    per_layer = 8 // depth
    dma = pltpu.SemaphoreType.DMA
    rows = jax.ShapeDtypeStruct((2, BLK, width), BF)
    tokens = pltpu.VMEM((2, 8 * BLK, width), BF)
    own_f32 = pltpu.VMEM((2, BLK, width), F32)
    own_bf = pltpu.VMEM((2, BLK, width), BF)
    line_vec = (8, BLK)
    vectors = [part.reshape(1, BLK) for part in weights[6:12]]
    operands = (hidden, cotangent) + weights[:6] + tuple(vectors) + weights[12:]
    return pl.pallas_call(
        functools.partial(layer_body, depth),
        out_shape=[
            rows,
            rows,
            jax.ShapeDtypeStruct((per_layer, 3, BLK, BLK), F32),
            jax.ShapeDtypeStruct((BLK, per_layer * BLK), F32),
            jax.ShapeDtypeStruct((8, 2, BLK, BLK), BF),
            jax.ShapeDtypeStruct((16, BLK), F32),
            jax.ShapeDtypeStruct((8, 16, BLK), F32),
        ],
        in_specs=[pl.BlockSpec(memory_space=pltpu.SMEM)] + [vmem()] * len(operands),
        out_specs=[vmem()] * 7,
        scratch_shapes=[tokens] * 5
        + [
            pltpu.VMEM((2, 8 * BLK, 6 * HEAD), BF),
            pltpu.VMEM((2, 8 * BLK, 2 * HEAD), BF),
            pltpu.VMEM((2, 8 * BLK, 2 * HEAD), BF),
            pltpu.VMEM((units, 16 * BLK), BF),
            pltpu.VMEM((units, 16 * BLK), BF),
            pltpu.VMEM((2, 2, 8 * BLK), F32),
            pltpu.VMEM((8 * BLK, QB), F32),
            pltpu.VMEM((8 * BLK, HEAD), F32),
            pltpu.VMEM((8 * BLK, HEAD), F32),
            pltpu.VMEM((width, 6 * HEAD), BF),
            pltpu.VMEM((8, depth, per_layer * BLK, BLK), BF),
            own_bf,
            own_bf,
            pltpu.VMEM((width, BLK), BF),
            pltpu.VMEM((BLK, width), BF),
            pltpu.VMEM((width, units), BF),
            pltpu.VMEM((units, width), BF),
            pltpu.VMEM((depth, 3, BLK, per_layer * BLK), BF),
            pltpu.VMEM((depth,) + line_vec, F32),
            pltpu.VMEM((8, BLK), F32),
            pltpu.VMEM(line_vec, F32),
            pltpu.VMEM((8, 8, BLK), F32),
            pltpu.VMEM((8, depth) + line_vec, F32),
            pltpu.VMEM((8, width), F32),
            pltpu.VMEM((1, units), F32),
            pltpu.VMEM((1, 6 * HEAD), F32),
            own_bf,
            own_bf,
            own_f32,
            own_f32,
            own_f32,
            own_f32,
            pltpu.VMEM((8, width), F32),
            pltpu.VMEM((1, units), F32),
            pltpu.VMEM((2, depth, 8, BLK, BLK), BF),
            pltpu.VMEM((2, depth - 1, 8, BLK, BLK), BF),
            pltpu.VMEM((8, 2, BLK, BLK), BF),
            pltpu.VMEM((8, 3, BLK, BLK), BF),
            pltpu.VMEM((8, 3, BLK, BLK), BF),
            pltpu.VMEM((depth, per_layer, 3, BLK, BLK), BF),
            pltpu.VMEM((2, BLK, width // 2), BF),
            pltpu.VMEM((depth - 1, BLK, per_layer * BLK), BF),
            pltpu.VMEM((8, 16, BLK), F32),
            pltpu.VMEM((8, 16, BLK), BF),
            pltpu.VMEM((8, depth, 16, BLK), BF),
        ]
        + [
            pltpu.VMEM((4, 2, BLK, width), BF),
            pltpu.VMEM((3, BLK, width), BF),
            pltpu.VMEM((3, BLK, width), BF),
        ]
        * 2
        + [
            dma((3, SquareGather.SENDS)),
            dma((3, SquareGather.SENDS)),
            dma((2,)),
            dma((3, SquareScatter.SENDS)),
            dma((3, SquareScatter.SENDS)),
            dma((2, 5, depth - 1)),
            dma((2, 5, depth - 1)),
            dma((2, 2, depth - 1)),
            dma((2, 2, depth - 1)),
            dma((7, 7)),
            dma((7, 7)),
            dma((2, depth - 1)),
            dma((2, depth - 1)),
            dma((2, 8)),
            dma((2, depth, per_layer)),
            dma((depth - 1,)),
            dma((depth - 1,)),
            dma((14,)),
        ],
        compiler_params=pltpu.CompilerParams(
            collective_id=1, has_side_effects=True, vmem_limit_bytes=VMEM_MAX
        ),
        name="layer",
    )(lengths, *operands)


def write_body(
    depth,
    output_in,
    grad_in_in,
    attn_sum,
    dense_sum,
    ffn_x,
    vec_in,
    unit_sums,
    output,
    grad_in,
    grad_q,
    grad_k,
    grad_v,
    grad_d,
    grad_up,
    grad_down,
    up_b,
    query_b,
    value_b,
    *vec_rows,
):
    own = lax.axis_index("wide")
    layer = lax.axis_index("tp")
    per_layer = 8 // depth
    output[...] = output_in[...]
    grad_in[...] = grad_in_in[...]
    for number in range(per_layer):
        lanes = slice(number * BLK, (number + 1) * BLK)
        for kind, target in enumerate((grad_q, grad_k, grad_v)):
            target[:, lanes] = attn_sum[number, kind].T
    grad_d[...] = dense_sum[...].T
    for blk in range(8):
        lanes = slice(blk * BLK, (blk + 1) * BLK)
        grad_up[:, lanes] = ffn_x[blk, 0].astype(F32).T
        grad_down[lanes] = ffn_x[blk, 1].astype(F32)
    for row in range(up_b.shape[0]):
        unit = unit_sums[2 * row + own // 4, pl.ds(6 + layer, 1)]
        moved = pltpu.roll(unit, (BLK - 32 * (own % 4)) % BLK, 1)
        up_b[row : row + 1] = moved[:, :32]
        shift = (BLK - ((row % 2) * HEAD + 8 * own)) % BLK
        for place, target in enumerate((query_b, value_b)):
            unit = unit_sums[per_layer * layer + row // 2, pl.ds(6 + depth + place, 1)]
            target[row : row + 1] = pltpu.roll(unit, shift, 1)[:, :8]
    for place, target in enumerate(vec_rows):
        target[...] = vec_in[pl.ds(place, 1)]


def write_out(depth, *pieces):
    per_layer = 8 // depth
    width = pieces[0].shape[-1]
    rows = jax.ShapeDtypeStruct(pieces[0].shape, BF)
    square = jax.ShapeDtypeStruct((BLK, per_layer * BLK), F32)
    head = jax.ShapeDtypeStruct((4, 8), F32)
    return pl.pallas_call(
        functools.partial(write_body, depth),
        out_shape=[
            rows,
            rows,
            square,
            square,
            square,
            jax.ShapeDtypeStruct((per_layer * BLK, BLK), F32),
            jax.ShapeDtypeStruct((BLK, width), F32),
            jax.ShapeDtypeStruct((width, BLK), F32),
            jax.ShapeDtypeStruct((4, 32), F32),
            head,
            head,
        ]
        + [jax.ShapeDtypeStruct((1, BLK), F32)] * 6,
        in_specs=[vmem()] * 7,
        out_specs=[vmem()] * 17,
        name="write_out",
    )(*pieces)


def square_device(
    hidden_in,
    lengths,
    pre_gain,
    pre_shift,
    w_query,
    w_key,
    w_value,
    b_query,
    b_value,
    w_dense,
    b_dense,
    mid_gain,
    mid_shift,
    w_up,
    b_up,
    w_down,
    b_down,
    cotangent,
):
    depth = lax.axis_size("tp")
    pieces = layer_pass(
        depth,
        lengths,
        hidden_in,
        cotangent,
        w_query,
        w_key,
        w_value,
        w_dense,
        w_up,
        w_down,
        pre_gain,
        pre_shift,
        mid_gain,
        mid_shift,
        b_dense,
        b_down,
        b_up,
        b_query,
        b_value,
    )
    (
        output,
        grad_in,
        grad_q,
        grad_k,
        grad_v,
        grad_d,
        grad_up,
        grad_down,
        up_b,
        query_b,
        value_b,
        *vec_rows,
    ) = write_out(depth, *pieces)
    vec_sums = [row.reshape(BLK) for row in vec_rows]
    return (
        output,
        grad_in,
        vec_sums[0],
        vec_sums[1],
        grad_q,
        grad_k,
        grad_v,
        query_b,
        value_b,
        grad_d,
        vec_sums[2],
        vec_sums[3],
        vec_sums[4],
        grad_up,
        up_b,
        grad_down,
        vec_sums[5],
    )


def solution(mesh):
    square = mesh.shape["wide"] == 8 and mesh.shape["tp"] == 4
    return jax.shard_map(
        square_device if square else per_device,
        mesh=mesh,
        in_specs=(
            P("tp", "wide", None),
            P(),
            P("wide"),
            P("wide"),
            P("wide", "tp"),
            P("wide", "tp"),
            P("wide", "tp"),
            P("tp", "wide"),
            P("tp", "wide"),
            P("tp", "wide"),
            P("wide"),
            P("wide"),
            P("wide"),
            P("wide", "tp"),
            P("tp", "wide"),
            P("tp", "wide"),
            P("wide"),
            P("tp", "wide", None),
        ),
        out_specs=(
            P("tp", "wide", None),
            P("tp", "wide", None),
            P("wide"),
            P("wide"),
            P("wide", "tp"),
            P("wide", "tp"),
            P("wide", "tp"),
            P("tp", "wide"),
            P("tp", "wide"),
            P("tp", "wide"),
            P("wide"),
            P("wide"),
            P("wide"),
            P("wide", "tp"),
            P("tp", "wide"),
            P("tp", "wide"),
            P("wide"),
        ),
        check_vma=False,
    )
```

```python
import functools
import math

import jax
import jax.numpy as jnp
from jax import lax
from jax.experimental import pallas as pl
from jax.experimental.pallas import tpu as pltpu
from jax.sharding import PartitionSpec as P

HEAD = 64
MESH = pl.DeviceIdType.MESH


def norm_rows(values, gain_vec, shift_vec):
    middle = jnp.mean(values, axis=-1, keepdims=True)
    centred = values - middle
    spread = jnp.mean(centred * centred, axis=-1, keepdims=True)
    return centred * lax.rsqrt(spread + 1e-05) * gain_vec + shift_vec


def flatten_rows(tensor):
    return tensor.reshape(-1, tensor.shape[-1])


def row_product(first_op, second_op):
    return jnp.dot(first_op, second_op, preferred_element_type=jnp.float32)


def inner_rows(first_op, second_op):
    return lax.dot_general(
        flatten_rows(first_op),
        flatten_rows(second_op),
        (((0,), (0,)), ((), ())),
        preferred_element_type=jnp.float32,
    )


def times_transposed(first_op, second_op):
    return lax.dot_general(
        first_op,
        second_op,
        (((first_op.ndim - 1,), (1,)), ((), ())),
        preferred_element_type=jnp.float32,
    )


def activate(values):
    return jax.nn.gelu(values, approximate=True)


def masked_scores(query_blk, key_blk, lengths_blk, slopes, distance, causal_mask, key_places):
    raw_scores = (
        jnp.einsum("gihd,gjhd->ghij", query_blk, key_blk, preferred_element_type=jnp.float32)
        * 0.125
    )
    raw_scores = raw_scores - slopes[None, :, None, None] * distance[None, None]
    allowed = causal_mask[None] & (key_places[None, None, :] < lengths_blk[:, None, None])
    return jnp.where(allowed[:, None], raw_scores, -jnp.inf)


def per_device(
    hidden_in,
    lengths,
    pre_gain,
    pre_shift,
    w_query,
    w_key,
    w_value,
    b_query,
    b_value,
    w_dense,
    b_dense,
    mid_gain,
    mid_shift,
    w_up,
    b_up,
    w_down,
    b_down,
    cotangent,
):
    local_slots, block_len, _unused = hidden_in.shape
    heads_dev = b_query.shape[0]
    head_width = heads_dev * HEAD
    slot_total = local_slots * lax.axis_size("tp")
    slot_len = block_len * lax.axis_size("wide")
    wide_at = lax.axis_index("wide")
    tp_at = lax.axis_index("tp")
    vec_part = pre_gain.shape[0]
    (
        gain_one,
        shift_one,
        query_w,
        key_w,
        value_w,
        query_b,
        value_b,
        dense_w,
        dense_b,
        gain_two,
        shift_two,
        up_w,
        up_b,
        down_w,
        down_b,
    ) = (
        lax.all_gather(pre_gain, "wide", axis=0, tiled=True),
        lax.all_gather(pre_shift, "wide", axis=0, tiled=True),
        lax.all_gather(w_query, "wide", axis=0, tiled=True),
        lax.all_gather(w_key, "wide", axis=0, tiled=True),
        lax.all_gather(w_value, "wide", axis=0, tiled=True),
        lax.all_gather(b_query, "wide", axis=1, tiled=True),
        lax.all_gather(b_value, "wide", axis=1, tiled=True),
        lax.all_gather(w_dense, "wide", axis=1, tiled=True),
        lax.all_gather(b_dense, "wide", axis=0, tiled=True),
        lax.all_gather(mid_gain, "wide", axis=0, tiled=True),
        lax.all_gather(mid_shift, "wide", axis=0, tiled=True),
        lax.all_gather(w_up, "wide", axis=0, tiled=True),
        lax.all_gather(b_up, "wide", axis=1, tiled=True),
        lax.all_gather(w_down, "wide", axis=1, tiled=True),
        lax.all_gather(b_down, "wide", axis=0, tiled=True),
    )
    gain_one = gain_one.astype(jnp.float32)
    shift_one = shift_one.astype(jnp.float32)
    gain_two = gain_two.astype(jnp.float32)
    shift_two = shift_two.astype(jnp.float32)
    query_places = wide_at * block_len + jnp.arange(block_len, dtype=jnp.int32)
    key_places = jnp.arange(slot_len, dtype=jnp.int32)
    distance = (query_places[:, None] - key_places[None, :]).astype(jnp.float32)
    causal_mask = key_places[None, :] <= query_places[:, None]
    head_index = tp_at * heads_dev + jnp.arange(heads_dev, dtype=jnp.int32)
    slopes = jnp.exp2(-0.5 * (head_index.astype(jnp.float32) + 1.0))
    own_lengths = lax.dynamic_slice_in_dim(lengths, tp_at * local_slots, local_slots, 0)
    validity = (query_places[None, :] < own_lengths[:, None]).astype(jnp.float32)
    group_size = math.gcd(slot_total, max(1, 512 // block_len))
    group_count = slot_total // group_size
    grouped_lengths = lengths.reshape(group_count, group_size)
    hidden = hidden_in.astype(jnp.float32)

    def query_view(tensor):
        return tensor.reshape(group_count, group_size, block_len, heads_dev, HEAD)

    def pair_view(tensor):
        return tensor.reshape(group_count, group_size, slot_len, 2, heads_dev, HEAD)

    def forward_group(inputs):
        query_blk, pair_blk, lengths_blk = inputs
        masked = masked_scores(
            query_blk, pair_blk[:, :, 0], lengths_blk, slopes, distance, causal_mask, key_places
        )
        highest = jnp.max(masked, axis=-1, keepdims=True)
        totals = highest + jnp.log(jnp.sum(jnp.exp(masked - highest), axis=-1, keepdims=True))
        probabilities = jnp.exp(masked - totals).astype(jnp.bfloat16)
        summed = jnp.einsum(
            "ghij,gjhd->gihd", probabilities, pair_blk[:, :, 1], preferred_element_type=jnp.float32
        )
        return (totals[..., 0], summed)

    def attention_forward(hidden_rows):
        normed_f, norm_back = jax.vjp(norm_rows, hidden_rows, gain_one, shift_one)
        normed = normed_f.astype(jnp.bfloat16)
        normed_all = lax.all_gather(normed, "tp", axis=0, tiled=True)
        queries = (
            row_product(normed_all, query_w) + query_b.reshape(head_width).astype(jnp.float32)
        ).astype(jnp.bfloat16)
        keys_now = row_product(normed_all, key_w).astype(jnp.bfloat16)
        values_now = (
            row_product(normed_all, value_w) + value_b.reshape(head_width).astype(jnp.float32)
        ).astype(jnp.bfloat16)
        pairs = jnp.concatenate([keys_now, values_now], axis=-1)
        pairs_all = lax.all_gather(pairs, "wide", axis=1, tiled=True)
        totals, summed = lax.map(
            forward_group, (query_view(queries), pair_view(pairs_all), grouped_lengths)
        )
        return (
            normed_all,
            queries,
            pairs_all,
            totals,
            summed.reshape(slot_total, block_len, head_width),
            norm_back,
        )

    forward_parts = attention_forward(hidden)
    attention = forward_parts[4].astype(jnp.bfloat16)
    branch = lax.psum_scatter(
        row_product(attention, dense_w).astype(jnp.bfloat16), "tp", scatter_dimension=0, tiled=True
    ).astype(jnp.float32)
    residual = hidden + branch + dense_b.astype(jnp.float32)
    second_f, second_back = jax.vjp(norm_rows, residual, gain_two, shift_two)
    second = second_f.astype(jnp.bfloat16)
    grad_output = validity[:, :, None] * cotangent.astype(jnp.float32)
    grad_down = grad_output.astype(jnp.bfloat16)
    second_all, grad_down_all = (
        lax.all_gather(second, "tp", axis=0, tiled=True),
        lax.all_gather(grad_down, "tp", axis=0, tiled=True),
    )
    pre_act = row_product(second_all, up_w) + up_b.reshape(-1).astype(jnp.float32)
    act_value, act_back = jax.vjp(activate, pre_act)
    activated = act_value.astype(jnp.bfloat16)
    down_out = lax.psum_scatter(
        row_product(activated, down_w).astype(jnp.bfloat16), "tp", scatter_dimension=0, tiled=True
    ).astype(jnp.float32)
    grad_act = times_transposed(grad_down_all, down_w)
    grad_pre = act_back(grad_act)[0].astype(jnp.bfloat16)
    grad_up = inner_rows(second_all, grad_pre)
    grad_up_b = jnp.sum(flatten_rows(grad_pre), axis=0, dtype=jnp.float32).reshape(up_b.shape)
    grad_down_w = inner_rows(activated, grad_down_all)
    grad_second = lax.psum_scatter(
        times_transposed(grad_pre, up_w), "tp", scatter_dimension=0, tiled=True
    )
    output = (validity[:, :, None] * (residual + down_out + down_b.astype(jnp.float32))).astype(
        jnp.bfloat16
    )
    grad_resid_norm, grad_gain_two, grad_shift_two = second_back(grad_second)
    grad_resid = grad_output + grad_resid_norm
    grad_branch = grad_resid.astype(jnp.bfloat16)
    hidden_again, grad_branch = lax.optimization_barrier((hidden, grad_branch))
    forward_parts = attention_forward(hidden_again)
    normed_all, queries, pairs_all, totals, summed, norm_back = forward_parts
    attention_back = summed.astype(jnp.bfloat16)
    branch_all = lax.all_gather(grad_branch, "tp", axis=0, tiled=True)
    grad_dense_w = inner_rows(attention_back, branch_all)
    grad_attention = times_transposed(branch_all, dense_w).astype(jnp.bfloat16)

    def backward_group(inputs):
        query_blk, pair_blk, lengths_blk, totals_blk, grad_blk = inputs
        masked = masked_scores(
            query_blk, pair_blk[:, :, 0], lengths_blk, slopes, distance, causal_mask, key_places
        )
        probabilities = jnp.exp(masked - totals_blk[..., None])
        grad_probs = jnp.einsum(
            "gihd,gjhd->ghij", grad_blk, pair_blk[:, :, 1], preferred_element_type=jnp.float32
        )
        row_delta = jnp.sum(probabilities * grad_probs, axis=-1, keepdims=True)
        grad_scores = (probabilities * (grad_probs - row_delta)).astype(jnp.bfloat16)
        grad_query = (
            jnp.einsum(
                "ghij,gjhd->gihd",
                grad_scores,
                pair_blk[:, :, 0],
                preferred_element_type=jnp.float32,
            )
            * 0.125
        )
        grad_key = (
            jnp.einsum(
                "ghij,gihd->gjhd", grad_scores, query_blk, preferred_element_type=jnp.float32
            )
            * 0.125
        )
        grad_value = jnp.einsum(
            "ghij,gihd->gjhd",
            probabilities.astype(jnp.bfloat16),
            grad_blk,
            preferred_element_type=jnp.float32,
        )
        return (grad_query, jnp.stack([grad_key, grad_value], axis=2))

    grad_query_all, grad_pairs = lax.map(
        backward_group,
        (
            query_view(queries),
            pair_view(pairs_all),
            grouped_lengths,
            totals,
            query_view(grad_attention),
        ),
    )
    grad_pairs_local = lax.psum_scatter(
        grad_pairs.reshape(slot_total, slot_len, 2 * head_width).astype(jnp.bfloat16),
        "wide",
        scatter_dimension=1,
        tiled=True,
    ).astype(jnp.float32)
    grad_queries = grad_query_all.reshape(slot_total, block_len, head_width).astype(jnp.bfloat16)
    grad_keys = grad_pairs_local[:, :, :head_width].astype(jnp.bfloat16)
    grad_values = grad_pairs_local[:, :, head_width:].astype(jnp.bfloat16)
    grad_query_w = inner_rows(normed_all, grad_queries)
    grad_key_w = inner_rows(normed_all, grad_keys)
    grad_value_w = inner_rows(normed_all, grad_values)
    grad_query_b = jnp.sum(flatten_rows(grad_queries), axis=0, dtype=jnp.float32).reshape(
        heads_dev, HEAD
    )
    grad_value_b = jnp.sum(flatten_rows(grad_values), axis=0, dtype=jnp.float32).reshape(
        heads_dev, HEAD
    )
    grad_normed = lax.psum_scatter(
        (
            times_transposed(grad_queries, query_w)
            + times_transposed(grad_keys, key_w)
            + times_transposed(grad_values, value_w)
        ).astype(jnp.bfloat16),
        "tp",
        scatter_dimension=0,
        tiled=True,
    ).astype(jnp.float32)
    grad_hidden_norm, grad_gain_one, grad_shift_one = norm_back(grad_normed)
    grad_in = (grad_resid + grad_hidden_norm).astype(jnp.bfloat16)
    (
        sum_query_w,
        sum_key_w,
        sum_value_w,
        sum_query_b,
        sum_value_b,
        sum_dense_w,
        sum_up_w,
        sum_up_b,
        sum_down_w,
    ) = (
        lax.psum_scatter(
            grad_query_w.astype(jnp.bfloat16), "wide", scatter_dimension=0, tiled=True
        ).astype(jnp.float32),
        lax.psum_scatter(
            grad_key_w.astype(jnp.bfloat16), "wide", scatter_dimension=0, tiled=True
        ).astype(jnp.float32),
        lax.psum_scatter(
            grad_value_w.astype(jnp.bfloat16), "wide", scatter_dimension=0, tiled=True
        ).astype(jnp.float32),
        lax.psum_scatter(
            grad_query_b.astype(jnp.bfloat16), "wide", scatter_dimension=1, tiled=True
        ).astype(jnp.float32),
        lax.psum_scatter(
            grad_value_b.astype(jnp.bfloat16), "wide", scatter_dimension=1, tiled=True
        ).astype(jnp.float32),
        lax.psum_scatter(
            grad_dense_w.astype(jnp.bfloat16), "wide", scatter_dimension=1, tiled=True
        ).astype(jnp.float32),
        lax.psum_scatter(
            grad_up.astype(jnp.bfloat16), "wide", scatter_dimension=0, tiled=True
        ).astype(jnp.float32),
        lax.psum_scatter(
            grad_up_b.astype(jnp.bfloat16), "wide", scatter_dimension=1, tiled=True
        ).astype(jnp.float32),
        lax.psum_scatter(
            grad_down_w.astype(jnp.bfloat16), "wide", scatter_dimension=1, tiled=True
        ).astype(jnp.float32),
    )
    grad_dense_b = jnp.sum(grad_resid, axis=(0, 1))
    grad_down_b = jnp.sum(grad_output, axis=(0, 1))
    sum_gain_one, sum_shift_one, sum_dense_b, sum_gain_two, sum_shift_two, sum_down_b = lax.psum(
        (grad_gain_one, grad_shift_one, grad_dense_b, grad_gain_two, grad_shift_two, grad_down_b),
        ("wide", "tp"),
    )

    def own_part(tensor):
        return lax.dynamic_slice_in_dim(tensor, wide_at * vec_part, vec_part, 0)

    return (
        output,
        grad_in,
        own_part(sum_gain_one),
        own_part(sum_shift_one),
        sum_query_w,
        sum_key_w,
        sum_value_w,
        sum_query_b,
        sum_value_b,
        sum_dense_w,
        own_part(sum_dense_b),
        own_part(sum_gain_two),
        own_part(sum_shift_two),
        sum_up_w,
        sum_up_b,
        sum_down_w,
        own_part(sum_down_b),
    )


BF = jnp.bfloat16
F32 = jnp.float32
LOG2E = 1.4426950408889634
NEG = -1e30
BLK = 128


def hbm():
    return pl.BlockSpec(memory_space=pl.ANY)


def vmem():
    return pl.BlockSpec(memory_space=pltpu.VMEM)


def square_places():
    own = lax.axis_index("wide")
    core = own % 2
    col = (own // 2) % 2
    row = own // 4
    pair = own + 1 - 2 * core
    along_x = own + 2 - 4 * col
    along_y = own + 4 - 8 * row
    return own, pair, along_x, along_y, along_x + along_y - own


def greet(targets):
    barrier = pltpu.get_barrier_semaphore()
    for target in targets:
        pl.semaphore_signal(barrier, inc=1, device_id=target, device_id_type=MESH)
    pl.semaphore_wait(barrier, len(targets))


def remote(src, dst, send_sem, recv_sem, target):
    return pltpu.make_async_remote_copy(
        src_ref=src,
        dst_ref=dst,
        send_sem=send_sem,
        recv_sem=recv_sem,
        device_id=target,
        device_id_type=MESH,
    )


class SquareGather:
    SENDS = 13

    def __init__(self, src, place, both, send, recv, local=None):
        own, pair, ax, ay, dg = square_places()
        first, second, whole = src
        to_x, to_y, to_p = {"wide": ax}, {"wide": ay}, {"wide": pair}
        self.local = None if local is None else pltpu.make_async_copy(whole, both(own), local)
        copies = {}
        copies["x0"] = remote(first, place(0, own), send.at[0], recv.at[0], to_x)
        copies["x1"] = remote(second, place(1, own), send.at[1], recv.at[1], to_x)
        copies["y0"] = remote(first, place(0, own), send.at[2], recv.at[2], to_y)
        copies["y1"] = remote(second, place(1, own), send.at[3], recv.at[3], to_y)
        copies["d0"] = remote(place(0, ay), place(0, ay), send.at[4], recv.at[4], to_x)
        copies["d1"] = remote(place(1, ax), place(1, ax), send.at[5], recv.at[5], to_y)
        copies["p"] = remote(whole, both(own), send.at[6], recv.at[6], to_p)
        for index, (name, slot, dev) in enumerate(
            (("x0", 0, ax), ("x1", 1, ax), ("y0", 0, ay), ("y1", 1, ay), ("d0", 0, dg), ("d1", 1, dg))
        ):
            copies["p" + name] = remote(
                place(slot, dev), place(slot, dev), send.at[7 + index], recv.at[7 + index], to_p
            )
        self.copies = copies

    def start(self):
        for name in ("y0", "x1", "x0", "y1", "p"):
            self.copies[name].start()
        if self.local is not None:
            self.local.start()

    def pass_on(self, arrived, sends):
        self.copies[arrived].wait_recv()
        for name in sends:
            self.copies[name].start()

    def first(self):
        self.pass_on("y0", ("d0", "py0"))
        self.pass_on("x1", ("d1", "px1"))

    def second(self):
        self.pass_on("x0", ("px0",))
        self.pass_on("y1", ("py1",))

    def third(self):
        self.pass_on("d0", ("pd0",))
        self.pass_on("d1", ("pd1",))

    def arrive(self, *names):
        for name in names:
            self.copies[name].wait_recv()

    def sent(self):
        for copy in self.copies.values():
            copy.wait_send()


def wide_square(own_places):
    _own, pair, ax, ay, _dg = own_places
    return [{"wide": pair}, {"wide": ax}, {"wide": ay}]


def add_rows(dst, first, second, third=None):
    step = 16

    def body(index, carry):
        rows = pl.ds(pl.multiple_of(index * step, step), step)
        total = first[rows].astype(F32) + second[rows].astype(F32)
        if third is not None:
            total = total + third[rows].astype(F32)
        dst[rows] = total.astype(dst.dtype)
        return carry

    lax.fori_loop(0, BLK // step, body, 0)


class SquareScatter:
    SENDS = 10

    def __init__(self, both, half, out, summed_both, summed, from_x, from_y, send, recv):
        own, pair, ax, ay, dg = square_places()
        shift = pair - own
        to_x, to_y, to_p = {"wide": ax}, {"wide": ay}, {"wide": pair}
        self.half, self.out = half, out
        self.summed, self.from_x, self.from_y = summed, from_x, from_y
        self.dests = (dg, ax, ay, own)
        self.pairs = [
            remote(
                both(self.dests[chip] + shift), summed_both(chip), send.at[chip], recv.at[chip], to_p
            )
            for chip in range(4)
        ]
        self.dx = remote(summed(0, 0), from_x(0), send.at[4], recv.at[4], to_x)
        self.dy = remote(summed(0, 1), from_y(0), send.at[5], recv.at[5], to_y)
        self.xx = remote(summed(1, 0), from_x(1), send.at[6], recv.at[6], to_x)
        self.yy = remote(summed(2, 1), from_y(1), send.at[7], recv.at[7], to_y)
        self.ty = remote(summed(2, 0), from_y(2), send.at[8], recv.at[8], to_y)
        self.tx = remote(summed(1, 1), from_x(2), send.at[9], recv.at[9], to_x)

    def pair_sum(self, chip, slot, third=None):
        place = self.summed(chip, slot)
        add_rows(place, self.half(slot, self.dests[chip]), place, third)

    def near(self, chip):
        self.pairs[chip].wait_recv()
        if chip == 0:
            self.pair_sum(0, 0)
            self.dx.start()
            self.pair_sum(0, 1)
            self.dy.start()
        elif chip == 1:
            self.pair_sum(1, 0)
            self.xx.start()
        elif chip == 2:
            self.pair_sum(2, 1)
            self.yy.start()
        else:
            self.pair_sum(3, 0)
            self.pair_sum(3, 1)

    def middle(self):
        self.dx.wait_recv()
        self.pair_sum(2, 0, self.from_x(0))
        self.ty.start()
        self.dy.wait_recv()
        self.pair_sum(1, 1, self.from_y(0))
        self.tx.start()

    def start(self):
        for chip in range(4):
            self.pairs[chip].start()

    def finish(self):
        self.xx.wait_recv()
        self.ty.wait_recv()
        add_rows(self.out.at[0], self.summed(3, 0), self.from_x(1), self.from_y(2))
        self.yy.wait_recv()
        self.tx.wait_recv()
        add_rows(self.out.at[1], self.summed(3, 1), self.from_y(1), self.from_x(2))
        for copy in self.pairs:
            copy.wait_send()
        for copy in (self.dx, self.dy, self.xx, self.yy, self.ty, self.tx):
            copy.wait_send()


class LineGather:
    def __init__(self, depth, pieces, send, recv):
        self.depth, self.pieces, self.send, self.recv = depth, pieces, send, recv
        self.layer = lax.axis_index("tp")

    def copies(self, step, up):
        index = self.layer - step + 1 if up else self.layer + step - 1
        goal = {"tp": self.layer + 1 if up else self.layer - 1}
        side = 0 if up else 1
        made = []
        for number, (own, place) in enumerate(self.pieces):
            source = own if step == 1 else place(index)
            made.append(
                remote(
                    source,
                    place(index),
                    self.send.at[side, number, step - 1],
                    self.recv.at[side, number, step - 1],
                    goal,
                )
            )
        return made

    def each(self, step, act):
        layer = self.layer

        @pl.when((layer < self.depth - 1) & (layer - step + 1 >= 0))
        def _():
            for copy in self.copies(step, True):
                act(copy)

        @pl.when((layer > 0) & (layer + step - 1 < self.depth))
        def _():
            for copy in self.copies(step, False):
                act(copy)

    def start(self, step):
        self.each(step, lambda copy: copy.start())

    def sent(self, step):
        self.each(step, lambda copy: copy.wait_send())

    def arrive(self, step):
        layer = self.layer

        @pl.when(layer - step >= 0)
        def _():
            for copy in self.copies(step, True):
                copy.wait_recv()

        @pl.when(layer + step < self.depth)
        def _():
            for copy in self.copies(step, False):
                copy.wait_recv()


def wide_others(own):
    return [{"wide": (own + step) % 8} for step in range(1, 8)]


def head_bias(length, slope, rows):
    place = lax.broadcasted_iota(jnp.int32, (rows, QB), 0)
    return jnp.where(place < length, slope * place.astype(F32), NEG)


QB = 256


def dot_nt(first, second):
    return lax.dot_general(first, second, (((1,), (1,)), ((), ())), preferred_element_type=F32)


def dot_nn(first, second):
    return lax.dot_general(first, second, (((1,), (0,)), ((), ())), preferred_element_type=F32)


def later_key(size):
    key_place = lax.broadcasted_iota(jnp.int32, (size, size), 0)
    query_place = lax.broadcasted_iota(jnp.int32, (size, size), 1)
    return key_place > query_place


def slot_scores(key, query, bias, step):
    extent = (step + 1) * QB
    scores = dot_nt(key[:extent], query) * (0.125 * LOG2E) + bias[:extent]
    edge = jnp.where(later_key(QB), NEG, scores[extent - QB :])
    return edge if step == 0 else jnp.concatenate([scores[: extent - QB], edge], 0)


def attend_head(slot, head, length, slopes, qkv, out, totals, bias):
    rows = qkv.shape[1]
    lanes = pl.ds(head * HEAD, HEAD)
    bias[...] = head_bias(length, slopes[head], rows)
    key = qkv[slot, :, pl.ds(2 * HEAD + head * HEAD, HEAD)]
    value_t = qkv[slot, :, pl.ds(4 * HEAD + head * HEAD, HEAD)].T
    for step in range(rows // QB):
        here = pl.ds(step * QB, QB)
        scores = slot_scores(key, qkv[slot, here, lanes], bias, step)
        highest = jnp.max(scores, axis=0, keepdims=True)
        weights = jnp.exp2(scores - highest)
        total = jnp.sum(weights, axis=0, keepdims=True)
        mixed = dot_nn(value_t[:, : (step + 1) * QB], weights.astype(BF)) / total
        out[slot, here, lanes] = mixed.T.astype(BF)
        totals[slot, pl.ds(head, 1), here] = highest + jnp.log2(total)


def attend_head_back(
    slot, head, length, slopes, qkv, attention, grad, totals, out, bias, key_sum, value_sum
):
    rows = qkv.shape[1]
    lanes = pl.ds(head * HEAD, HEAD)
    key_lanes = pl.ds(2 * HEAD + head * HEAD, HEAD)
    value_lanes = pl.ds(4 * HEAD + head * HEAD, HEAD)
    bias[...] = head_bias(length, slopes[head], rows)
    key = qkv[slot, :, key_lanes]
    value = qkv[slot, :, value_lanes]
    key_t = key.T
    key_sum[...] = jnp.zeros_like(key_sum)
    value_sum[...] = jnp.zeros_like(value_sum)
    for step in range(rows // QB):
        here = pl.ds(step * QB, QB)
        extent = (step + 1) * QB
        query = qkv[slot, here, lanes]
        grad_rows = grad[slot, here, lanes]
        product = grad_rows.astype(F32) * attention[slot, here, lanes].astype(F32)
        delta = jnp.sum(product.T, axis=0, keepdims=True)
        scores = slot_scores(key, query, bias, step)
        probs = jnp.exp2(scores - totals[slot, pl.ds(head, 1), here])
        grad_probs = dot_nt(value[:extent], grad_rows)
        grad_scores = (probs * (grad_probs - delta)).astype(BF)
        span = pl.ds(0, extent)
        value_sum[span] += dot_nn(probs.astype(BF), grad_rows)
        key_sum[span] += dot_nn(grad_scores, query)
        grad_query = dot_nn(key_t[:, :extent], grad_scores)
        out[slot, here, lanes] = (grad_query.T * 0.125).astype(BF)
    out[slot, :, key_lanes] = (key_sum[...] * 0.125).astype(BF)
    out[slot, :, value_lanes] = value_sum[...].astype(BF)


def line_others(depth):
    layer = lax.axis_index("tp")
    return [{"tp": (layer + step) % depth} for step in range(1, depth)]


VMEM_MAX = 67043328


def norm_stats(values):
    middle = jnp.mean(values, axis=-1, keepdims=True)
    centred = values - middle
    spread = jnp.mean(centred * centred, axis=-1, keepdims=True)
    inverse = lax.rsqrt(spread + 1e-05)
    return centred * inverse, inverse


def norm_back_rows(grad, hat, inverse, gain):
    scaled = grad * gain
    first = jnp.mean(scaled, axis=-1, keepdims=True)
    second = jnp.mean(scaled * hat, axis=-1, keepdims=True)
    return (scaled - first - hat * second) * inverse


def gelu_parts(values):
    root = math.sqrt(2 / math.pi)
    squared = values * values
    inner = jnp.tanh(root * values * (1.0 + 0.044715 * squared))
    half = 0.5 * (1.0 + inner)
    slope = half + 0.5 * values * (1.0 - inner * inner) * root * (1.0 + 3 * 0.044715 * squared)
    return values * half, slope


def relation(index):
    own = lax.axis_index("wide")
    core = (own + index) % 2
    col = (own // 2 + index // 2) % 2
    row = (own // 4 + index // 4) % 2
    return row * 4 + col * 2 + core


class WideExchange:
    def __init__(self, source, target, send, recv):
        own = lax.axis_index("wide")
        self.copies = [
            remote(
                source((own + step) % 8),
                target(own),
                send.at[step - 1],
                recv.at[step - 1],
                {"wide": (own + step) % 8},
            )
            for step in range(1, 8)
        ]

    def start(self):
        for copy in self.copies:
            copy.start()

    def arrive(self):
        for copy in self.copies:
            copy.wait_recv()

    def sent(self):
        for copy in self.copies:
            copy.wait_send()


def layer_body(
    depth,
    lengths,
    hidden,
    cotangent,
    w_query,
    w_key,
    w_value,
    w_dense,
    w_up,
    w_down,
    pre_gain,
    pre_shift,
    mid_gain,
    mid_shift,
    b_dense,
    b_down,
    b_up,
    b_query,
    b_value,
    output,
    grad_in,
    attn_sum,
    dense_sum,
    ffn_x,
    vec_sums,
    unit_sums,
    hidden_all,
    normed,
    down_all,
    second_share,
    down_share,
    qkv,
    attention,
    grad_att,
    act_t,
    pre_t,
    totals,
    bias,
    key_sum,
    value_sum,
    qkv_w,
    dense_all,
    att_own,
    att_grad_own,
    up_t,
    down_t,
    up_w,
    down_w,
    z_qkv,
    z_vec,
    vec_wide,
    vec_line,
    vec_wide_all,
    vec_line_all,
    vectors,
    up_bias,
    qkv_bias,
    own_rows,
    down_own,
    residual,
    grad_second,
    grad_resid,
    down_out,
    sums,
    up_sum,
    ffn_g,
    ffn_in,
    ffn_sum,
    attn_g,
    attn_in,
    attn_z,
    dense_out,
    dense_in,
    parts,
    parts_bf,
    gathered,
    a_summed,
    a_x,
    a_y,
    b_summed,
    b_x,
    b_y,
    gather_send,
    gather_recv,
    gather_local,
    scatter_send,
    scatter_recv,
    line_send,
    line_recv,
    ffn_line_send,
    ffn_line_recv,
    wide_send,
    wide_recv,
    grad_line_send,
    grad_line_recv,
    onward_send,
    onward_recv,
    dense_send,
    dense_recv,
    own_sems,
):
    own = lax.axis_index("wide")
    layer = lax.axis_index("tp")
    per_layer = 8 // depth
    width = hidden.shape[-1]
    step = 32
    steps = BLK // step
    others = [
        ((own + side) % 8, (layer + up) % depth)
        for up in range(depth)
        for side in range(8)
        if up or side
    ]
    own_lanes = pl.ds(pl.multiple_of(own * BLK, BLK), BLK)

    for place, ref in enumerate((pre_gain, pre_shift, mid_gain, mid_shift, b_dense, b_down)):
        vec_wide[pl.ds(place, 1)] = ref[...].astype(F32)
    vec_line[...] = jnp.zeros_like(vec_line)
    vec_line[0 : b_up.shape[0], 0 : b_up.shape[1]] = b_up[...].astype(F32)
    vec_line[b_up.shape[0] :, 0:8] = b_query[...].astype(F32)
    vec_line[b_up.shape[0] :, 8:16] = b_value[...].astype(F32)
    first_row = own * BLK

    def token_mask(slot, rows, count):
        place = first_row + rows * count + lax.broadcasted_iota(jnp.int32, (count, BLK), 0)
        inside = place < lengths[layer * 2 + slot]
        return jnp.where(inside, 1.0, 0.0).astype(F32)[:, :1]

    def down_part(index, carry):
        rows = pl.ds(pl.multiple_of(index * step, step), step)
        for slot in range(2):
            values = token_mask(slot, index, step) * cotangent[slot, rows].astype(F32)
            down_own[slot, rows] = values.astype(BF)
        return carry

    lax.fori_loop(0, steps, down_part, 0)
    greet(wide_others(own) + line_others(depth))

    def block_rows(dev):
        return pl.ds(pl.multiple_of(dev * BLK, BLK), BLK)

    def gather_of(number, src, dst):
        return SquareGather(
            (src.at[0], src.at[1], src),
            lambda slot, dev: dst.at[slot, block_rows(dev)],
            lambda dev: dst.at[:, block_rows(dev)],
            gather_send.at[number],
            gather_recv.at[number],
            gather_local.at[number],
        )

    def wide_of(number, source, target):
        return WideExchange(source, target, wide_send.at[number], wide_recv.at[number])

    gains = wide_of(0, lambda dev: vec_wide, lambda dev: vec_wide_all.at[dev])
    gains.start()
    hid = gather_of(0, hidden, hidden_all)
    hid.start()
    line = LineGather(
        depth,
        [
            (w_query, lambda at: z_qkv.at[at, 0]),
            (w_key, lambda at: z_qkv.at[at, 1]),
            (w_value, lambda at: z_qkv.at[at, 2]),
            (w_dense, lambda at: dense_all.at[own, at]),
            (vec_line, lambda at: z_vec.at[at]),
        ],
        line_send,
        line_recv,
    )
    line.start(1)
    own_copies = [
        pltpu.make_async_copy(ref, place(layer), own_sems.at[number])
        for number, (ref, place) in enumerate(line.pieces)
    ]
    for copy in own_copies:
        copy.start()
    vec_wide_all[own] = vec_wide[...]
    gains.arrive()
    for dev in range(8):
        vectors[:, dev * BLK : (dev + 1) * BLK] = vec_wide_all[dev]

    def norm_block(index, carry):
        base = relation(index) * BLK

        def norm_part(part, carry):
            rows = pl.ds(pl.multiple_of(base + part * step, step), step)
            for slot in range(2):
                hat, _inverse = norm_stats(hidden_all[slot, rows].astype(F32))
                normed[slot, rows] = (hat * vectors[0:1] + vectors[1:2]).astype(BF)
            return carry

        return lax.fori_loop(0, steps, norm_part, carry)

    hid.arrive("p")
    hid.local.wait()
    lax.fori_loop(0, 2, norm_block, 0)
    hid.first()
    line.arrive(1)
    line.start(2)
    hid.second()
    ups = wide_of(
        3, lambda dev: w_up.at[:, block_rows(dev)], lambda dev: up_t.at[block_rows(dev)]
    )
    downs = wide_of(
        4, lambda dev: w_down.at[block_rows(dev)], lambda dev: down_t.at[:, block_rows(dev)]
    )
    unit_copies = [
        pltpu.make_async_copy(w_up.at[:, own_lanes], up_t.at[own_lanes], own_sems.at[6]),
        pltpu.make_async_copy(w_down.at[own_lanes], down_t.at[:, own_lanes], own_sems.at[7]),
    ]
    ups.start()
    downs.start()
    for copy in unit_copies:
        copy.start()
    line.arrive(2)
    line.start(3)
    hid.arrive("px0", "px1", "py0", "py1")
    lax.fori_loop(2, 6, norm_block, 0)
    hid.third()
    line.arrive(3)
    for copy in own_copies:
        copy.wait()

    def goal_lanes(dev):
        return pl.ds(pl.multiple_of((dev % per_layer) * BLK, BLK), BLK)

    heads = wide_of(
        1,
        lambda dev: z_qkv.at[dev // per_layer, :, :, goal_lanes(dev)],
        lambda dev: attn_in.at[dev],
    )
    biases = wide_of(2, lambda dev: z_vec, lambda dev: vec_line_all.at[dev])
    dense = SquareGather(
        (dense_all.at[own, pl.ds(0, 2)], dense_all.at[own, pl.ds(2, 2)], dense_all.at[own]),
        lambda half, dev: dense_all.at[dev, pl.ds(2 * half, 2)],
        lambda dev: dense_all.at[dev],
        gather_send.at[2],
        gather_recv.at[2],
    )
    biases.start()
    heads.start()
    dense.start()
    gd = gather_of(1, down_own, down_all)
    gd.start()
    own_copies = [
        pltpu.make_async_copy(z_qkv.at[own // per_layer, :, :, goal_lanes(own)], attn_in.at[own], own_sems.at[5]),
    ]
    for copy in own_copies:
        copy.start()
    vec_line_all[own] = z_vec[...]
    hid.arrive("pd0", "pd1")
    lax.fori_loop(6, 8, norm_block, 0)
    biases.arrive()
    head_layer = own // per_layer
    piece = own % per_layer
    unit_row = own // 2
    for dev in range(8):
        for head in range(2):
            lanes = slice(head * HEAD + dev * 8, head * HEAD + dev * 8 + 8)
            row = pl.ds(b_up.shape[0] + 2 * piece + head, 1)
            values = vec_line_all[dev, head_layer, row]
            qkv_bias[:, lanes] = values[:, 0:8]
            lanes = slice(4 * HEAD + lanes.start, 4 * HEAD + lanes.stop)
            qkv_bias[:, lanes] = values[:, 8:16]
    qkv_bias[:, 2 * HEAD : 4 * HEAD] = jnp.zeros((1, 2 * HEAD), F32)
    for up in range(depth):
        for part in range(4):
            values = vec_line_all[4 * (own % 2) + part, up, pl.ds(unit_row, 1)]
            up_bias[:, up * BLK + part * 32 : up * BLK + part * 32 + 32] = values[:, 0:32]
    heads.arrive()
    hid.sent()
    for copy in own_copies + unit_copies:
        copy.wait()
    ups.arrive()
    downs.arrive()
    for dev in range(8):
        for kind in range(3):
            qkv_w[dev * BLK : (dev + 1) * BLK, kind * BLK : (kind + 1) * BLK] = attn_in[dev, kind]

    ffn_line = LineGather(
        depth,
        [
            (up_t, lambda at: up_w.at[:, pl.ds(pl.multiple_of(at * BLK, BLK), BLK)]),
            (down_t, lambda at: down_w.at[pl.ds(pl.multiple_of(at * BLK, BLK), BLK)]),
        ],
        ffn_line_send,
        ffn_line_recv,
    )
    ffn_line.start(1)
    unit_copies = [
        pltpu.make_async_copy(ref, place(layer), own_sems.at[8 + number])
        for number, (ref, place) in enumerate(ffn_line.pieces)
    ]
    for copy in unit_copies:
        copy.start()
    slopes = [
        jnp.exp2(-0.5 * (jnp.full((1, 1), 2 * own + head, jnp.int32).astype(F32) + 1.0)) * LOG2E
        for head in range(2)
    ]

    def att_exchange(slot):
        return wide_of(
            5 + slot,
            lambda dev: attention.at[slot, block_rows(dev)],
            lambda dev: att_own.at[slot, :, block_rows(dev)],
        )

    def att_local(slot):
        return pltpu.make_async_copy(
            attention.at[slot, block_rows(own)], att_own.at[slot, :, block_rows(own)], own_sems.at[10 + slot]
        )

    def one_slot(slot, carry):
        def block(index, carry):
            rows = pl.ds(pl.multiple_of(index * QB, QB), QB)
            qkv[slot, rows] = (dot_nn(normed[slot, rows], qkv_w[...]) + qkv_bias[...]).astype(BF)
            return carry

        lax.fori_loop(0, 8 * BLK // QB, block, 0)
        length = lengths[layer * 2 + slot]
        @pl.when(slot == 0)
        def _():
            dense.first()
            dense.second()

        attend_head(slot, 0, length, slopes, qkv, attention, totals, bias)

        @pl.when(slot == 0)
        def _():
            dense.third()

        attend_head(slot, 1, length, slopes, qkv, attention, totals, bias)
        att_exchange(slot).start()
        att_local(slot).start()

        @pl.when(slot == 0)
        def _():
            ffn_line.arrive(1)
            ffn_line.start(2)

        return carry

    lax.fori_loop(0, 2, one_slot, 0)
    gd.first()
    gd.second()
    ffn_line.arrive(2)
    ffn_line.start(3)
    dense.arrive("p", "px0", "px1", "py0", "py1", "pd0", "pd1")
    for slot in range(2):
        att_exchange(slot).arrive()
        att_local(slot).wait()

    for part in range(4):
        columns = [dense_all[2 * part + side].reshape(width, BLK) for side in range(2)]
        product = dot_nn(att_own[...].reshape(2 * BLK, width), jnp.concatenate(columns, 1))
        residual[:, :, part * QB : (part + 1) * QB] = product.reshape(2, BLK, QB)

    def scatter_of(number, share, out, buffers):
        summed, from_x, from_y = buffers
        return SquareScatter(
            lambda dev: share.at[:, block_rows(dev)],
            lambda slot, dev: share.at[slot, block_rows(dev)],
            out,
            lambda chip: summed.at[chip],
            lambda chip, slot: summed.at[chip, slot],
            lambda place: from_x.at[place],
            lambda place: from_y.at[place],
            scatter_send.at[number],
            scatter_recv.at[number],
        )

    def second_part(index, carry):
        rows = pl.ds(pl.multiple_of(index * step, step), step)
        for slot in range(2):
            values = hidden[slot, rows].astype(F32) + residual[slot, rows] + vectors[4:5]
            residual[slot, rows] = values
            hat, _inverse = norm_stats(values)
            own_rows[slot, rows] = (hat * vectors[2:3] + vectors[3:4]).astype(BF)
        return carry

    lax.fori_loop(0, steps, second_part, 0)
    second_all = hidden_all
    gather = gather_of(0, own_rows, second_all)
    gather.start()
    scatter = scatter_of(0, second_share, grad_second, (a_summed, a_x, a_y))
    gd.arrive("p")
    gd.local.wait()
    for copy in unit_copies:
        copy.wait()
    ffn_line.arrive(3)

    def compute(index, carry):
        source = relation(index)
        rows = pl.ds(pl.multiple_of(source * BLK, BLK), BLK)
        values = second_all[:, rows].reshape(2 * BLK, width)
        act_value, act_slope = gelu_parts(dot_nn(values, up_w[...]) + up_bias[...])
        activated = act_value.astype(BF)
        grad_rows = down_all[:, rows].reshape(2 * BLK, width)
        grad_pre = (dot_nt(grad_rows, down_w[...]) * act_slope).astype(BF)
        second_share[:, rows] = dot_nt(grad_pre, up_w[...]).astype(BF).reshape(2, BLK, width)
        down_share[:, rows] = dot_nn(activated, down_w[...]).astype(BF).reshape(2, BLK, width)
        up_sum[...] += jnp.sum(grad_pre.astype(F32), axis=0, keepdims=True)
        for slot in range(2):
            lanes = pl.ds(pl.multiple_of(slot * 8 * BLK + source * BLK, BLK), BLK)
            part = slice(slot * BLK, (slot + 1) * BLK)
            act_t[:, lanes] = activated[part].T
            pre_t[:, lanes] = grad_pre[part].T
        return carry

    up_sum[...] = jnp.zeros_like(up_sum)
    gather.arrive("p")
    gather.local.wait()
    lax.fori_loop(0, 2, compute, 0)
    scatter.pairs[3].start()
    gather.first()
    gd.third()
    gather.second()
    gd.arrive("px0", "px1", "py0", "py1")
    gather.arrive("px0", "px1", "py0", "py1")
    lax.fori_loop(2, 4, compute, 0)
    scatter.pairs[1].start()
    scatter.near(3)
    lax.fori_loop(4, 6, compute, 0)
    scatter.pairs[2].start()
    gather.third()
    scatter.near(1)
    gd.arrive("pd0", "pd1")
    gather.arrive("pd0", "pd1")
    lax.fori_loop(6, 8, compute, 0)
    scatter.pairs[0].start()
    scatter.near(2)
    scatter.near(0)

    def weight_grads(left, right, kind):
        def one(up, carry):
            rows = pl.ds(pl.multiple_of(up * BLK, BLK), BLK)
            total = dot_nn(left[rows, pl.ds(0, 8 * BLK)], right[0])
            total = total + dot_nn(left[rows, pl.ds(8 * BLK, 8 * BLK)], right[1])
            total = total.astype(BF)
            for blk in range(8):
                ffn_g[kind, up, blk] = total[:, blk * BLK : (blk + 1) * BLK]
            return carry

        lax.fori_loop(0, depth, one, 0)

    def line_copies(kind):
        return [
            remote(
                ffn_g.at[kind, (layer + up) % depth],
                ffn_in.at[kind, up - 1],
                grad_line_send.at[kind, up - 1],
                grad_line_recv.at[kind, up - 1],
                {"tp": (layer + up) % depth},
            )
            for up in range(1, depth)
        ]

    def line_sums(kind):
        for copy in line_copies(kind):
            copy.wait_recv()

        def add_block(blk, carry):
            total = ffn_g[kind, layer, blk].astype(F32)
            for up in range(depth - 1):
                total = total + ffn_in[kind, up, blk].astype(F32)
            ffn_sum[blk, kind] = total.astype(BF)
            return carry

        lax.fori_loop(0, 8, add_block, 0)

    weight_grads(pre_t, second_all, 0)
    for copy in line_copies(0):
        copy.start()
    scatter.middle()
    weight_grads(act_t, down_all, 1)
    for copy in line_copies(1):
        copy.start()
    scatter.finish()
    gather.sent()
    sums[...] = jnp.zeros_like(sums)

    def back_part(index, carry):
        rows = pl.ds(pl.multiple_of(index * step, step), step)
        for slot in range(2):
            hat, inverse = norm_stats(residual[slot, rows])
            grad = grad_second[slot, rows]
            grad_out = token_mask(slot, index, step) * cotangent[slot, rows].astype(F32)
            total = grad_out + norm_back_rows(grad, hat, inverse, vectors[2:3])
            grad_resid[slot, rows] = total
            own_rows[slot, rows] = total.astype(BF)
            for place, value in enumerate((total, grad * hat, grad, grad_out)):
                sums[pl.ds(place, 1)] += jnp.sum(value, axis=0, keepdims=True)
        return carry

    lax.fori_loop(0, steps, back_part, 0)
    for at in range(depth):
        columns = jnp.concatenate([dense_all[dev, at] for dev in range(8)], 1)
        product = dot_nt(own_rows[...].reshape(2 * BLK, width), columns).astype(BF)
        att_grad_own[:, :, at * QB : (at + 1) * QB] = product.reshape(2, BLK, QB)

    def att_back(slot):
        return wide_of(
            5 + slot,
            lambda dev: att_grad_own.at[slot, :, block_rows(dev)],
            lambda dev: grad_att.at[slot, block_rows(dev)],
        )

    def att_back_local(slot):
        return pltpu.make_async_copy(
            att_grad_own.at[slot, :, block_rows(own)], grad_att.at[slot, block_rows(own)], own_sems.at[12 + slot]
        )

    for sends in (gains, biases, heads, ups, downs, att_exchange(0), att_exchange(1)):
        sends.sent()
    dense.sent()
    for slot in range(2):
        att_back(slot).start()
        att_back_local(slot).start()
    down = scatter_of(1, down_share, down_out, (b_summed, b_x, b_y))
    down.start()

    half_lanes = pl.ds(0, width // 2)
    sum_lanes = pl.ds(width // 2, width // 2)
    for part in range(4):
        rows = slice(part * QB, (part + 1) * QB)
        left = own_rows[:, :, rows].reshape(2 * BLK, QB).T
        for half in range(2):
            lanes = slice(half * width // 2, (half + 1) * width // 2)
            product = dot_nn(left, att_own[:, :, lanes].reshape(2 * BLK, width // 2))
            second_all[half, rows, half_lanes] = product.astype(BF)
    dense_back = SquareScatter(
        lambda dev: second_all.at[:, block_rows(dev), half_lanes],
        lambda half, dev: second_all.at[half, block_rows(dev), half_lanes],
        dense_out,
        lambda chip: second_all.at[:, pl.ds(chip * BLK, BLK), sum_lanes],
        lambda chip, half: second_all.at[half, pl.ds(chip * BLK, BLK), sum_lanes],
        lambda place: second_all.at[0, pl.ds((4 + place) * BLK, BLK), sum_lanes],
        lambda place: second_all.at[1, pl.ds((4 + place) * BLK, BLK), sum_lanes],
        scatter_send.at[2],
        scatter_recv.at[2],
    )

    def dense_piece(at):
        return dense_out.at[at // 2, :, pl.ds(pl.multiple_of((at % 2) * QB, QB), QB)]

    def dense_copies():
        return [
            remote(
                dense_piece((layer + up) % depth),
                dense_in.at[up - 1],
                dense_send.at[up - 1],
                dense_recv.at[up - 1],
                {"tp": (layer + up) % depth},
            )
            for up in range(1, depth)
        ]

    att_back(0).arrive()
    att_back_local(0).wait()
    dense_back.start()
    for chip in range(3):
        down.near(chip)
    for chip in range(3):
        dense_back.near(chip)

    def ffn_exchange(kind):
        return wide_of(kind, lambda dev: ffn_sum.at[dev, kind], lambda dev: ffn_x.at[dev, kind])

    def slot_back(slot, carry):
        def one_head(head):
            attend_head_back(
                slot,
                head,
                lengths[layer * 2 + slot],
                slopes,
                qkv,
                attention,
                grad_att,
                totals,
                qkv,
                bias,
                key_sum,
                value_sum,
            )

        one_head(0)

        @pl.when(slot == 0)
        def _():
            down.near(3)
            down.middle()
            dense_back.near(3)

        @pl.when(slot == 1)
        def _():
            dense_back.finish()
            for copy in dense_copies():
                copy.start()
            line_sums(0)
            ffn_exchange(0).start()

        one_head(1)

        @pl.when(slot == 0)
        def _():
            dense_back.middle()
            att_back(1).arrive()
            att_back_local(1).wait()

        return carry

    lax.fori_loop(0, 2, slot_back, 0)
    grad_qkv = qkv
    weight_part = dot_nn(grad_qkv[0].T, normed[0]) + dot_nn(grad_qkv[1].T, normed[1])
    weight_part = weight_part.astype(BF)
    for kind in range(3):
        for blk in range(8):
            attn_g[blk, kind] = weight_part[
                kind * BLK : (kind + 1) * BLK, blk * BLK : (blk + 1) * BLK
            ]
    kinds = (pl.ds(0, 2), pl.ds(2, 1))
    exchanges = [
        wide_of(
            2 + group,
            lambda dev, kind=kind: attn_g.at[dev, kind],
            lambda dev, kind=kind: attn_in.at[dev, kind],
        )
        for group, kind in enumerate(kinds)
    ]

    def onward(group, index, source):
        pair = index
        return remote(
            source.at[index, kinds[group]],
            attn_z.at[layer, pair % per_layer, kinds[group]],
            onward_send.at[group, index],
            onward_recv.at[group, layer, pair % per_layer],
            {"tp": pair // per_layer},
        )

    def forward(group, index, source):
        @pl.when(index // per_layer != layer)
        def _():
            onward(group, index, source).start()

    def forward_all(group):
        for number in range(1, 8):
            exchanges[group].copies[number - 1].wait_recv()
            forward(group, (own + 8 - number) % 8, attn_in)

    exchanges[0].start()
    for group in range(2):
        forward(group, own, attn_g)
    share = second_share
    grad_normed = grad_second
    scatter = scatter_of(0, share, grad_normed, (a_summed, a_x, a_y))

    def normed_block(index, carry):
        rows = pl.ds(pl.multiple_of(relation(index) * BLK, BLK), BLK)
        values = grad_qkv[:, rows].reshape(2 * BLK, 6 * HEAD)
        share[:, rows] = dot_nt(values, qkv_w[...]).astype(BF).reshape(2, BLK, width)
        return carry

    for chip in range(4):
        start = (6, 2, 4, 0)[chip]
        lax.fori_loop(start, start + 2, normed_block, 0)
        scatter.pairs[chip].start()
        if chip:
            scatter.near(chip - 1)
    exchanges[1].start()
    line_sums(1)
    head_sum = jnp.sum(grad_qkv[0].astype(F32), axis=0, keepdims=True)
    head_sum = head_sum + jnp.sum(grad_qkv[1].astype(F32), axis=0, keepdims=True)
    down.finish()

    def out_part(index, carry):
        rows = pl.ds(pl.multiple_of(index * step, step), step)
        for slot in range(2):
            total = residual[slot, rows] + down_out[slot, rows] + vectors[5:6]
            output[slot, rows] = (token_mask(slot, index, step) * total).astype(BF)
        return carry

    lax.fori_loop(0, steps, out_part, 0)
    forward_all(0)
    scatter.near(3)
    scatter.middle()
    ffn_exchange(1).start()
    forward_all(1)
    for blk in range(8):
        lanes = slice(blk * BLK, (blk + 1) * BLK)
        for place in range(4):
            parts[blk, pl.ds(2 + place, 1)] = sums[place : place + 1, lanes]
        for place in range(depth):
            parts[blk, pl.ds(6 + place, 1)] = up_sum[:, place * BLK : (place + 1) * BLK]
        parts[blk, pl.ds(6 + depth, 1)] = head_sum[:, : 2 * HEAD]
        parts[blk, pl.ds(7 + depth, 1)] = head_sum[:, 4 * HEAD :]
    scatter.finish()

    def last_part(index, carry):
        gain_sum, shift_sum = carry
        rows = pl.ds(pl.multiple_of(index * step, step), step)
        for slot in range(2):
            hat, inverse = norm_stats(hidden[slot, rows].astype(F32))
            grad = grad_normed[slot, rows]
            total = grad_resid[slot, rows] + norm_back_rows(grad, hat, inverse, vectors[0:1])
            grad_in[slot, rows] = total.astype(BF)
            gain_sum = gain_sum + jnp.sum(grad * hat, axis=0, keepdims=True)
            shift_sum = shift_sum + jnp.sum(grad, axis=0, keepdims=True)
        return gain_sum, shift_sum

    zero = jnp.zeros((1, width), F32)
    gain_sum, shift_sum = lax.fori_loop(0, steps, last_part, (zero, zero))
    for blk in range(8):
        lanes = slice(blk * BLK, (blk + 1) * BLK)
        parts[blk, pl.ds(0, 1)] = gain_sum[:, lanes]
        parts[blk, pl.ds(1, 1)] = shift_sum[:, lanes]
    gd.sent()

    def sum_sems(index):
        if index < 7:
            return wide_send.at[4, index], wide_recv.at[4, index]
        number, place = 2 - (index - 7) // SquareGather.SENDS, (index - 7) % SquareGather.SENDS
        return gather_send.at[number, place], gather_recv.at[number, place]

    parts_bf[...] = parts[...].astype(BF)
    sum_copies = [
        remote(
            parts_bf.at[wide],
            gathered.at[own, layer],
            *sum_sems(index),
            {"wide": wide, "tp": tp},
        )
        for index, (wide, tp) in enumerate(others)
    ]
    for copy in sum_copies:
        copy.start()
    gathered[own, layer] = parts_bf[own]
    for group in range(2):
        for up in range(1, depth):
            source = (layer + up) % depth
            for number in range(per_layer):
                remote(
                    attn_in.at[number, kinds[group]],
                    attn_z.at[source, number, kinds[group]],
                    onward_send.at[group, number],
                    onward_recv.at[group, source, number],
                    {"tp": source},
                ).wait_recv()
    attn_in[own] = attn_g[own]
    for number in range(per_layer):
        for kind in range(3):
            total = attn_in[layer * per_layer + number, kind].astype(F32)
            for up in range(1, depth):
                total = total + attn_z[(layer + up) % depth, number, kind].astype(F32)
            attn_sum[number, kind] = total
    for copy in dense_copies():
        copy.wait_recv()
    total = dense_out[layer // 2, :, pl.ds(pl.multiple_of((layer % 2) * QB, QB), QB)].astype(F32)
    for up in range(1, depth):
        total = total + dense_in[up - 1].astype(F32)
    dense_sum[...] = total
    ffn_x[own] = ffn_sum[own]
    for kind in range(2):
        ffn_exchange(kind).arrive()
    for copy in sum_copies:
        copy.wait_recv()

    def unit_part(dev, carry):
        total = gathered[dev, 0].astype(F32)
        for up in range(1, depth):
            total = total + gathered[dev, up].astype(F32)
        unit_sums[dev] = total
        return carry + total

    vec_sums[...] = lax.fori_loop(0, 8, unit_part, jnp.zeros((16, BLK), F32))

    for copy in sum_copies:
        copy.wait_send()
    for slot in range(2):
        att_back(slot).sent()
        ffn_exchange(slot).sent()
    for sends in exchanges:
        sends.sent()
    for number in range(1, depth):
        line.sent(number)
        ffn_line.sent(number)
    for kind in range(2):
        for copy in line_copies(kind):
            copy.wait_send()
    for copy in dense_copies():
        copy.wait_send()
    for group in range(2):
        for index in range(8):

            @pl.when(index // per_layer != layer)
            def _(index=index, group=group):
                onward(group, index, attn_in).wait_send()


def layer_pass(depth, lengths, hidden, cotangent, *weights):
    width = hidden.shape[-1]
    units = depth * BLK
    per_layer = 8 // depth
    dma = pltpu.SemaphoreType.DMA
    rows = jax.ShapeDtypeStruct((2, BLK, width), BF)
    tokens = pltpu.VMEM((2, 8 * BLK, width), BF)
    own_f32 = pltpu.VMEM((2, BLK, width), F32)
    own_bf = pltpu.VMEM((2, BLK, width), BF)
    line_vec = (8, BLK)
    vectors = [part.reshape(1, BLK) for part in weights[6:12]]
    operands = (hidden, cotangent) + weights[:6] + tuple(vectors) + weights[12:]
    return pl.pallas_call(
        functools.partial(layer_body, depth),
        out_shape=[
            rows,
            rows,
            jax.ShapeDtypeStruct((per_layer, 3, BLK, BLK), F32),
            jax.ShapeDtypeStruct((BLK, per_layer * BLK), F32),
            jax.ShapeDtypeStruct((8, 2, BLK, BLK), BF),
            jax.ShapeDtypeStruct((16, BLK), F32),
            jax.ShapeDtypeStruct((8, 16, BLK), F32),
        ],
        in_specs=[pl.BlockSpec(memory_space=pltpu.SMEM)] + [vmem()] * len(operands),
        out_specs=[vmem()] * 7,
        scratch_shapes=[tokens] * 5
        + [
            pltpu.VMEM((2, 8 * BLK, 6 * HEAD), BF),
            pltpu.VMEM((2, 8 * BLK, 2 * HEAD), BF),
            pltpu.VMEM((2, 8 * BLK, 2 * HEAD), BF),
            pltpu.VMEM((units, 16 * BLK), BF),
            pltpu.VMEM((units, 16 * BLK), BF),
            pltpu.VMEM((2, 2, 8 * BLK), F32),
            pltpu.VMEM((8 * BLK, QB), F32),
            pltpu.VMEM((8 * BLK, HEAD), F32),
            pltpu.VMEM((8 * BLK, HEAD), F32),
            pltpu.VMEM((width, 6 * HEAD), BF),
            pltpu.VMEM((8, depth, per_layer * BLK, BLK), BF),
            own_bf,
            own_bf,
            pltpu.VMEM((width, BLK), BF),
            pltpu.VMEM((BLK, width), BF),
            pltpu.VMEM((width, units), BF),
            pltpu.VMEM((units, width), BF),
            pltpu.VMEM((depth, 3, BLK, per_layer * BLK), BF),
            pltpu.VMEM((depth,) + line_vec, F32),
            pltpu.VMEM((8, BLK), F32),
            pltpu.VMEM(line_vec, F32),
            pltpu.VMEM((8, 8, BLK), F32),
            pltpu.VMEM((8, depth) + line_vec, F32),
            pltpu.VMEM((8, width), F32),
            pltpu.VMEM((1, units), F32),
            pltpu.VMEM((1, 6 * HEAD), F32),
            own_bf,
            own_bf,
            own_f32,
            own_f32,
            own_f32,
            own_f32,
            pltpu.VMEM((8, width), F32),
            pltpu.VMEM((1, units), F32),
            pltpu.VMEM((2, depth, 8, BLK, BLK), BF),
            pltpu.VMEM((2, depth - 1, 8, BLK, BLK), BF),
            pltpu.VMEM((8, 2, BLK, BLK), BF),
            pltpu.VMEM((8, 3, BLK, BLK), BF),
            pltpu.VMEM((8, 3, BLK, BLK), BF),
            pltpu.VMEM((depth, per_layer, 3, BLK, BLK), BF),
            pltpu.VMEM((2, BLK, width // 2), BF),
            pltpu.VMEM((depth - 1, BLK, per_layer * BLK), BF),
            pltpu.VMEM((8, 16, BLK), F32),
            pltpu.VMEM((8, 16, BLK), BF),
            pltpu.VMEM((8, depth, 16, BLK), BF),
        ]
        + [
            pltpu.VMEM((4, 2, BLK, width), BF),
            pltpu.VMEM((3, BLK, width), BF),
            pltpu.VMEM((3, BLK, width), BF),
        ]
        * 2
        + [
            dma((3, SquareGather.SENDS)),
            dma((3, SquareGather.SENDS)),
            dma((2,)),
            dma((3, SquareScatter.SENDS)),
            dma((3, SquareScatter.SENDS)),
            dma((2, 5, depth - 1)),
            dma((2, 5, depth - 1)),
            dma((2, 2, depth - 1)),
            dma((2, 2, depth - 1)),
            dma((7, 7)),
            dma((7, 7)),
            dma((2, depth - 1)),
            dma((2, depth - 1)),
            dma((2, 8)),
            dma((2, depth, per_layer)),
            dma((depth - 1,)),
            dma((depth - 1,)),
            dma((14,)),
        ],
        compiler_params=pltpu.CompilerParams(
            collective_id=1, has_side_effects=True, vmem_limit_bytes=VMEM_MAX
        ),
        name="layer",
    )(lengths, *operands)


def write_body(
    depth,
    output_in,
    grad_in_in,
    attn_sum,
    dense_sum,
    ffn_x,
    vec_in,
    unit_sums,
    output,
    grad_in,
    grad_q,
    grad_k,
    grad_v,
    grad_d,
    grad_up,
    grad_down,
    up_b,
    query_b,
    value_b,
    *vec_rows,
):
    own = lax.axis_index("wide")
    layer = lax.axis_index("tp")
    per_layer = 8 // depth
    output[...] = output_in[...]
    grad_in[...] = grad_in_in[...]
    for number in range(per_layer):
        lanes = slice(number * BLK, (number + 1) * BLK)
        for kind, target in enumerate((grad_q, grad_k, grad_v)):
            target[:, lanes] = attn_sum[number, kind].T
    grad_d[...] = dense_sum[...].T
    for blk in range(8):
        lanes = slice(blk * BLK, (blk + 1) * BLK)
        grad_up[:, lanes] = ffn_x[blk, 0].astype(F32).T
        grad_down[lanes] = ffn_x[blk, 1].astype(F32)
    for row in range(up_b.shape[0]):
        unit = unit_sums[2 * row + own // 4, pl.ds(6 + layer, 1)]
        moved = pltpu.roll(unit, (BLK - 32 * (own % 4)) % BLK, 1)
        up_b[row : row + 1] = moved[:, :32]
        shift = (BLK - ((row % 2) * HEAD + 8 * own)) % BLK
        for place, target in enumerate((query_b, value_b)):
            unit = unit_sums[per_layer * layer + row // 2, pl.ds(6 + depth + place, 1)]
            target[row : row + 1] = pltpu.roll(unit, shift, 1)[:, :8]
    for place, target in enumerate(vec_rows):
        target[...] = vec_in[pl.ds(place, 1)]


def write_out(depth, *pieces):
    per_layer = 8 // depth
    width = pieces[0].shape[-1]
    rows = jax.ShapeDtypeStruct(pieces[0].shape, BF)
    square = jax.ShapeDtypeStruct((BLK, per_layer * BLK), F32)
    head = jax.ShapeDtypeStruct((4, 8), F32)
    return pl.pallas_call(
        functools.partial(write_body, depth),
        out_shape=[
            rows,
            rows,
            square,
            square,
            square,
            jax.ShapeDtypeStruct((per_layer * BLK, BLK), F32),
            jax.ShapeDtypeStruct((BLK, width), F32),
            jax.ShapeDtypeStruct((width, BLK), F32),
            jax.ShapeDtypeStruct((4, 32), F32),
            head,
            head,
        ]
        + [jax.ShapeDtypeStruct((1, BLK), F32)] * 6,
        in_specs=[vmem()] * 7,
        out_specs=[vmem()] * 17,
        name="write_out",
    )(*pieces)


def square_device(
    hidden_in,
    lengths,
    pre_gain,
    pre_shift,
    w_query,
    w_key,
    w_value,
    b_query,
    b_value,
    w_dense,
    b_dense,
    mid_gain,
    mid_shift,
    w_up,
    b_up,
    w_down,
    b_down,
    cotangent,
):
    depth = lax.axis_size("tp")
    pieces = layer_pass(
        depth,
        lengths,
        hidden_in,
        cotangent,
        w_query,
        w_key,
        w_value,
        w_dense,
        w_up,
        w_down,
        pre_gain,
        pre_shift,
        mid_gain,
        mid_shift,
        b_dense,
        b_down,
        b_up,
        b_query,
        b_value,
    )
    (
        output,
        grad_in,
        grad_q,
        grad_k,
        grad_v,
        grad_d,
        grad_up,
        grad_down,
        up_b,
        query_b,
        value_b,
        *vec_rows,
    ) = write_out(depth, *pieces)
    vec_sums = [row.reshape(BLK) for row in vec_rows]
    return (
        output,
        grad_in,
        vec_sums[0],
        vec_sums[1],
        grad_q,
        grad_k,
        grad_v,
        query_b,
        value_b,
        grad_d,
        vec_sums[2],
        vec_sums[3],
        vec_sums[4],
        grad_up,
        up_b,
        grad_down,
        vec_sums[5],
    )


def solution(mesh):
    square = mesh.shape["wide"] == 8 and mesh.shape["tp"] == 4
    return jax.shard_map(
        square_device if square else per_device,
        mesh=mesh,
        in_specs=(
            P("tp", "wide", None),
            P(),
            P("wide"),
            P("wide"),
            P("wide", "tp"),
            P("wide", "tp"),
            P("wide", "tp"),
            P("tp", "wide"),
            P("tp", "wide"),
            P("tp", "wide"),
            P("wide"),
            P("wide"),
            P("wide"),
            P("wide", "tp"),
            P("tp", "wide"),
            P("tp", "wide"),
            P("wide"),
            P("tp", "wide", None),
        ),
        out_specs=(
            P("tp", "wide", None),
            P("tp", "wide", None),
            P("wide"),
            P("wide"),
            P("wide", "tp"),
            P("wide", "tp"),
            P("wide", "tp"),
            P("tp", "wide"),
            P("tp", "wide"),
            P("tp", "wide"),
            P("wide"),
            P("wide"),
            P("wide"),
            P("wide", "tp"),
            P("tp", "wide"),
            P("tp", "wide"),
            P("wide"),
        ),
        check_vma=False,
    )
```
